32 devices in a mesh: replica: 4 (over z), fsdp: 8 (over y, x, core).
Axes of the slice: x: 2, y: 2, z: 4, core: 2. Of those that a mesh axis runs over, the one named last changes fastest.
Arguments:
- prompt_hidden: bfloat16 [16, 1024, 1024], P('replica', 'fsdp'), may hold values from -6 to 6
- sequel_hidden: bfloat16 [128, 128, 1024], P(('replica', 'fsdp')), may hold values from -6 to 6
- parents: int32 [128], P(('replica', 'fsdp')), may hold values from 0 to 3, as said below
- prompt_cotangent: bfloat16 [16, 1024, 1024], P('replica', 'fsdp'), may hold values from -6 to 6
- sequel_cotangent: bfloat16 [128, 128, 1024], P(('replica', 'fsdp')), may hold values from -6 to 6
- norm_gain: bfloat16 [1024], P('fsdp'), may hold values from 0.5 to 1.5
- input_weight: bfloat16 [1024, 4096], P('fsdp'), may hold values from -0.1875 to 0.1875
- filter_weight: bfloat16 [4, 2048], P(None, 'fsdp'), may hold values from -3 to 3
- depthwise_filter_bias: bfloat16 [2048], P('fsdp'), may hold values from -0.5 to 0.5
- select_weight: bfloat16 [2048, 96], P('fsdp'), may hold values from -0.125 to 0.125
- step_weight: bfloat16 [64, 2048], P(None, 'fsdp'), may hold values from -0.75 to 0.75
- step_bias: bfloat16 [2048], P('fsdp'), may hold values from -7 to -2
- decay_log: bfloat16 [2048, 16], P('fsdp'), may hold values from 0 to 2.765625
- skip_gain: bfloat16 [2048], P('fsdp'), may hold values from 0.5 to 1.5
- output_weight: bfloat16 [2048, 1024], P('fsdp'), may hold values from -0.5 to 0.5
Outputs:
- prompt_output: bfloat16 [16, 1024, 1024], P('replica', 'fsdp')
- sequel_output: bfloat16 [128, 128, 1024], P(('replica', 'fsdp'))
- prompt_input_gradient: float32 [16, 1024, 1024], P('replica', 'fsdp')
- sequel_input_gradient: float32 [128, 128, 1024], P(('replica', 'fsdp'))
- norm_gain_gradient: float32 [1024], P('fsdp')
- input_weight_gradient: float32 [1024, 4096], P('fsdp')
- filter_weight_gradient: float32 [4, 2048], P(None, 'fsdp')
- filter_bias_gradient: float32 [2048], P('fsdp')
- select_weight_gradient: float32 [2048, 96], P('fsdp')
- step_weight_gradient: float32 [64, 2048], P(None, 'fsdp')
- step_bias_gradient: float32 [2048], P('fsdp')
- decay_log_gradient: float32 [2048, 16], P('fsdp')
- skip_gain_gradient: float32 [2048], P('fsdp')
- output_weight_gradient: float32 [2048, 1024], P('fsdp')
The draws below stay inside these ranges and needn't reach their ends.
Inputs may be any that keep to these rules, and one draw needn't show every extreme that they name: `parents`: in each aligned block of 32 continuations (those of one replica index) every value appears exactly 8 times; value p in block r names prompt r * 4 + p.
All inputs are finite; a program needn't handle non-finite values.
Results may differ from the reference program's by a relative error of at most 0.012.
Values may be sent and summed in bfloat16 or wider, within the bound.
A program may use at most 448 MiB of HBM per device.

```python
import math
import jax
import jax.numpy as jnp
from jax import lax

D = 1024
INNER = 2048
STATES = 16
RANK = 64
KERNEL = 4
PROMPTS = 4
CHILDREN = 8
PLEN = 1024
SLEN = 128
FAMILIES = 16
SEQUELS = 128


def draw_parents(key, part):

    def one_group(replica_row):
        shuffled = jax.random.permutation(jax.random.fold_in(key, replica_row), CHILDREN * PROMPTS)
        return (shuffled // CHILDREN).astype(jnp.int32)
    return jax.vmap(one_group)(jnp.arange(FAMILIES // PROMPTS, dtype=jnp.int32)).reshape(-1)


def level_of(rng, extent, cuts, least, top_value):
    def one(axis_at, parts):
        draws = jax.random.uniform(jax.random.fold_in(jax.random.fold_in(rng, 6), axis_at), (parts,), jnp.float32, least / len(cuts), top_value / len(cuts))
        return jnp.repeat(jnp.exp(draws), extent[axis_at] // parts).reshape((-1,) + (1,) * (len(extent) - axis_at - 1))

    gain = one(*cuts[0])
    for cut in cuts[1:]:
        gain = gain * one(*cut)
    return gain


def normal_values(own_key, dims, deviation, reach, shards=(), kind=jnp.bfloat16):
    drawn = deviation * jax.random.normal(own_key, dims, jnp.float32)
    if shards:
        drawn = drawn * level_of(own_key, dims, shards, -0.22, 0.18)
    return jnp.clip(drawn, -reach, reach).astype(kind)


def setup_inputs(seed: int = 0) -> dict:
    key_of = jax.random.split(jax.random.key(seed), 16)
    return {
        "prompt_hidden": normal_values(key_of[0], (FAMILIES, PLEN, D), 1.0, 6.0, ((0, 4), (1, 8))),
        "sequel_hidden": normal_values(key_of[1], (SEQUELS, SLEN, D), 1.0, 6.0, ((0, 32),)),
        "parents": draw_parents(jax.random.fold_in(key_of[15], 71), 0),
        "prompt_cotangent": normal_values(key_of[3], (FAMILIES, PLEN, D), 1.0, 6.0, ((0, 4), (1, 8))),
        "sequel_cotangent": normal_values(key_of[4], (SEQUELS, SLEN, D), 1.0, 6.0, ((0, 32),)),
        "norm_gain": jnp.clip(1.0 + 0.1 * jax.random.normal(key_of[5], (D,), jnp.float32), 0.5, 1.5).astype(jnp.bfloat16),
        "input_weight": normal_values(key_of[6], (D, 2 * INNER), D ** -0.5, 0.1875, ((0, 8),)),
        "filter_weight": normal_values(key_of[7], (KERNEL, INNER), KERNEL ** -0.5, 3.0, ((1, 8),)),
        "depthwise_filter_bias": jnp.clip(jax.random.uniform(key_of[8], (INNER,), jnp.float32, -0.5, 0.5) * level_of(key_of[8], (INNER,), ((0, 8),), -0.4, 0.0), -0.5, 0.5).astype(jnp.bfloat16),
        "select_weight": normal_values(key_of[9], (INNER, RANK + 2 * STATES), INNER ** -0.5, 0.125, ((0, 8),)),
        "step_weight": normal_values(key_of[10], (RANK, INNER), RANK ** -0.5, 0.75, ((1, 8),)),
        "step_bias": jnp.clip(-7.0 + 5.0 * jax.random.uniform(key_of[11], (INNER,), jnp.float32) ** level_of(key_of[11], (INNER,), ((0, 8),), -0.2, 0.2), -7.0, -2.0).astype(jnp.bfloat16),
        "decay_log": jnp.clip(2.765625 * jax.random.uniform(key_of[12], (INNER, STATES), jnp.float32) ** level_of(key_of[12], (INNER, STATES), ((0, 8),), -0.2, 0.2), 0.0, 2.765625).astype(jnp.bfloat16),
        "skip_gain": jnp.clip(0.5 + 1.0 * jax.random.uniform(key_of[13], (INNER,), jnp.float32) ** level_of(key_of[13], (INNER,), ((0, 8),), -0.2, 0.2), 0.5, 1.5).astype(jnp.bfloat16),
        "output_weight": normal_values(key_of[14], (INNER, D), (INNER // 16) ** -0.5, 0.5, ((0, 8),)),
    }


@jax.custom_vjp
def low(v):
    return lax.optimization_barrier(v.astype(jnp.bfloat16)).astype(jnp.float32)

@jax.custom_vjp
def low_back(v):
    return v

def low_keep(v):
    return (low(v), None)

def low_pass(kept, grad):
    return (grad,)

def back_keep(v):
    return (v, None)

def back_low(kept, grad):
    return (low(grad),)
low.defvjp(low_keep, low_pass)
low_back.defvjp(back_keep, back_low)

def matmul(left_side, right_side):
    return jnp.dot(left_side, right_side, precision=lax.Precision.HIGHEST, preferred_element_type=jnp.float32)

def selective(activated, pre_step, input_map, output_map, step_bias, decay_log, initial):
    step_size = jax.nn.softplus(pre_step + step_bias)
    decay_rate = -jnp.exp(decay_log)
    length = activated.shape[1]
    stride = math.gcd(length, 64)

    def blocks_of(values):
        swapped = jnp.swapaxes(values, 0, 1)
        return swapped.reshape((length // stride, stride) + swapped.shape[1:])
    inputs = (blocks_of(step_size), blocks_of(activated), blocks_of(input_map), blocks_of(output_map))

    def advance(carry_state, element):
        size_now, act_now, in_now, out_now = element
        carry_state = jnp.exp(size_now[..., None] * decay_rate) * carry_state + (size_now * act_now)[..., None] * in_now[:, None, :]
        return (carry_state, lax.optimization_barrier(jnp.sum(carry_state * out_now[:, None, :], axis=-1)))

    @jax.checkpoint
    def run_block(carry_state, element):
        return lax.scan(advance, carry_state, element)
    last_state, outputs_all = lax.scan(run_block, initial, inputs)
    outputs_all = outputs_all.reshape((length,) + outputs_all.shape[2:])
    return (jnp.swapaxes(outputs_all, 0, 1), last_state)

def reference(prompt_hidden, sequel_hidden, parents, prompt_cotangent, sequel_cotangent, norm_gain, input_weight, filter_weight, depthwise_filter_bias, select_weight, step_weight, step_bias, decay_log, skip_gain, output_weight):
    family = jnp.arange(SEQUELS, dtype=jnp.int32) // (CHILDREN * PROMPTS) * PROMPTS + parents.astype(jnp.int32)

    def forward(prompt_rows, sequel_rows, norm_gain, input_weight, filter_weight, depthwise_filter_bias, select_weight, step_weight, step_bias, decay_log, skip_gain, output_weight):

        def front_rows(hidden):
            scaled = hidden * lax.rsqrt(lax.optimization_barrier(jnp.mean(hidden * hidden, axis=-1, keepdims=True)) + 1e-05) * norm_gain
            mixture = low_back(matmul(low(scaled), input_weight))
            return (low(mixture[..., :INNER]), mixture[..., INNER:])

        def filtered(earlier, values):
            extended = jnp.concatenate([earlier, values], axis=1)
            length = values.shape[1]
            summed = sum((filter_weight[offset] * extended[:, offset:offset + length] for offset in range(KERNEL)))
            return jax.nn.silu(depthwise_filter_bias + summed)

        def select(activated):
            projected = low_back(matmul(low(activated), select_weight))
            rank_part = low(projected[..., :RANK])
            pre_step = low_back(matmul(rank_part, step_weight))
            return (pre_step, projected[..., RANK:RANK + STATES], projected[..., RANK + STATES:])

        def finish(hidden, state_out, activated, gate_input):
            gated = low((state_out + skip_gain * activated) * jax.nn.silu(gate_input))
            return hidden + matmul(gated, output_weight)
        prompt_filter, prompt_gate = front_rows(prompt_rows)
        sequel_filter, sequel_gate = front_rows(sequel_rows)
        zero_rim = jnp.zeros((FAMILIES, KERNEL - 1, INNER), jnp.float32)
        prompt_act = filtered(zero_rim, prompt_filter)
        prompt_tails = prompt_filter[:, PLEN - (KERNEL - 1):]
        sequel_act = filtered(prompt_tails[family], sequel_filter)
        prompt_pre, prompt_inmap, prompt_outmap = select(prompt_act)
        sequel_pre, sequel_inmap, sequel_outmap = select(sequel_act)
        zero_state = jnp.zeros((FAMILIES, INNER, STATES), jnp.float32)
        prompt_states, prompt_last = selective(prompt_act, prompt_pre, prompt_inmap, prompt_outmap, step_bias, decay_log, zero_state)
        sequel_states, sequel_last = selective(sequel_act, sequel_pre, sequel_inmap, sequel_outmap, step_bias, decay_log, prompt_last[family])
        return (finish(prompt_rows, prompt_states, prompt_act, prompt_gate), finish(sequel_rows, sequel_states, sequel_act, sequel_gate))
    primals = tuple((member.astype(jnp.float32) for member in (prompt_hidden, sequel_hidden, norm_gain, input_weight, filter_weight, depthwise_filter_bias, select_weight, step_weight, step_bias, decay_log, skip_gain, output_weight)))
    outputs, pullback = jax.vjp(forward, *primals)
    gradients = pullback((prompt_cotangent.astype(jnp.float32), sequel_cotangent.astype(jnp.float32)))
    return (outputs[0].astype(jnp.bfloat16), outputs[1].astype(jnp.bfloat16), gradients[0], gradients[1], gradients[2], gradients[3], gradients[4], gradients[5], gradients[6], gradients[7], gradients[8], gradients[9], gradients[10], gradients[11])
```

```python
import functools
import math

import jax
import jax.numpy as jnp
from jax import lax
from jax.experimental import pallas as pl
from jax.experimental.pallas import tpu as pltpu
from jax.sharding import PartitionSpec as P

D = 1024
INNER = 2048
STATES = 16
RANK = 64
KERNEL = 4
PROMPTS = 4

SEQS = 8
HALO = 4
LANES = 128
WIDE = 256
LOG2E = math.log2(math.e)
LN2 = math.log(2.0)
f32 = jnp.float32
bf16 = jnp.bfloat16

VMEM_LIMIT = 62 * 1024 * 1024


def cost(microseconds):
    return pl.CostEstimate(flops=int(microseconds * 1e9), bytes_accessed=0, transcendentals=0)


def params(**kw):
    return pltpu.CompilerParams(vmem_limit_bytes=VMEM_LIMIT, **kw)


def sigmoid(x):
    return 1.0 / (1.0 + jnp.exp(-x))


def softplus(x):
    return jnp.maximum(x, 0.0) + jnp.log1p(jnp.exp(-jnp.abs(x)))


def front_kernel(mix_ref, fw_ref, fb_ref, sel_ref, act_ref, proj_ref):
    j = pl.program_id(0)
    steps = act_ref.shape[0]
    chunk = 16
    taps = [fw_ref[k : k + 1, :] for k in range(KERNEL)]
    bias = fb_ref[0:1, :]

    @pl.when(j == 0)
    def _():
        proj_ref[...] = jnp.zeros_like(proj_ref)

    def step(i, _):
        t = i * chunk
        x = mix_ref[pl.ds(t, chunk + HALO)].astype(bf16).astype(f32)
        v = bias[None] + taps[0][None] * x[1 : 1 + chunk]
        for k in range(1, KERNEL):
            v = v + taps[k][None] * x[1 + k : 1 + k + chunk]
        act = v * sigmoid(v)
        act_ref[pl.ds(t, chunk)] = act
        low = act.reshape(chunk * SEQS, act.shape[-1]).astype(bf16)
        r = pl.multiple_of(t * SEQS, chunk * SEQS)
        proj_ref[pl.ds(r, chunk * SEQS), :] += jnp.dot(low, sel_ref[...], preferred_element_type=f32)
        return 0

    lax.fori_loop(0, steps // chunk, step, 0)


def front(mixture, fw, fb, select_pad, steps):
    channels = fw.shape[1]
    return pl.pallas_call(
        front_kernel,
        grid=(channels // WIDE,),
        in_specs=[
            pl.BlockSpec((steps + HALO, SEQS, WIDE), lambda j: (0, 0, j)),
            pl.BlockSpec((KERNEL, WIDE), lambda j: (0, j)),
            pl.BlockSpec((1, WIDE), lambda j: (0, j)),
            pl.BlockSpec((WIDE, LANES), lambda j: (j, 0)),
        ],
        out_specs=[
            pl.BlockSpec((steps, SEQS, WIDE), lambda j: (0, 0, j)),
            pl.BlockSpec((steps * SEQS, LANES), lambda j: (0, 0)),
        ],
        out_shape=[
            jax.ShapeDtypeStruct((steps, SEQS, channels), f32),
            jax.ShapeDtypeStruct((steps * SEQS, LANES), f32),
        ],
        compiler_params=params(),
        cost_estimate=cost(16),
        name="front",
    )(mixture, fw, fb, select_pad)


def pair(a, b):
    return jnp.concatenate([a, b], axis=0).astype(bf16)


def both(v):
    return pair(v, v)


def halves(v):
    v = v.astype(f32)
    return v[:SEQS], v[SEQS:]


def folded(v):
    a, b = halves(v)
    return a + b


def spread_maps(proj_ref, select_ref, first, count, store):
    steps = proj_ref.shape[0] // SEQS
    chunk = 32

    def step(i, _):
        r = pl.multiple_of(i * chunk * SEQS, chunk * SEQS)
        rows = proj_ref[pl.ds(r, chunk * SEQS), :].astype(bf16)
        for n in range(0, count, 2):
            at = (first - RANK + n) * LANES
            wide = jnp.dot(rows, select_ref[:, at : at + 2 * LANES], preferred_element_type=f32)
            wide = wide.reshape(chunk, SEQS, 2 * LANES)
            store(i * chunk, chunk, n, wide[:, :, :LANES], wide[:, :, LANES:])
        return 0

    lax.fori_loop(0, steps // chunk, step, 0)


def store_plain(ref):
    def store(t, count, n, a, b):
        ref[pl.ds(t, count), n] = a
        ref[pl.ds(t, count), n + 1] = b

    return store


def store_pairs(ref):
    def store(t, count, n, a, b):
        ref[pl.ds(t, count), n // 2] = jnp.concatenate([a, b], axis=1).astype(bf16)

    return store


PAIRS = STATES // 2
RUN = 8


def piece_kernel(
    proj_ref, act_ref, gate_ref, gg_ref, stepw_ref, sbias_ref, rate_ref, select_ref,
    dt_ref, sig_ref, yg_ref, silu_ref, slope_ref, fwd_ref, bwd_ref, tot_ref,
    b_scr, c_scr, time_scr, acc_scr,
):
    j = pl.program_id(0)
    steps = dt_ref.shape[0]
    half = SEQS // 2
    groups = fwd_ref.shape[0]

    @pl.when(j == 0)
    def _():
        def store_groups(t, count, n, a, b):
            for group in range(groups):
                rows = slice(group * half, (group + 1) * half)
                parts = [a[:, rows], a[:, rows], b[:, rows], b[:, rows]]
                b_scr[group, pl.ds(t, count), n // 2] = jnp.concatenate(parts, axis=1).astype(bf16)

        spread_maps(proj_ref, select_ref, RANK, STATES, store_groups)
        spread_maps(proj_ref, select_ref, RANK + STATES, STATES, store_pairs(c_scr))

    chunk = 8
    sbias = sbias_ref[0:1, :]

    def prep(i, total):
        t = i * chunk
        r = pl.multiple_of(t * SEQS, chunk * SEQS)
        rank = proj_ref[pl.ds(r, chunk * SEQS), :].astype(bf16)
        pre = jnp.dot(rank, stepw_ref[...], preferred_element_type=f32).reshape(chunk, SEQS, WIDE)
        pre = pre + sbias[None]
        small = jnp.exp2(jnp.abs(pre) * -LOG2E)
        one = 1.0 + small
        inverse = 1.0 / one
        dt = jnp.maximum(pre, 0.0) + (jnp.log(one) + (small - (one - 1.0)) * inverse)
        dt_ref[pl.ds(t, chunk)] = dt
        sig_ref[pl.ds(t, chunk)] = jnp.where(pre >= 0.0, inverse, small * inverse).astype(bf16)
        gate = gate_ref[pl.ds(t + HALO, chunk)]
        gg = gg_ref[pl.ds(t, chunk)]
        sig = sigmoid(gate)
        silu = gate * sig
        yg_ref[pl.ds(t, chunk)] = gg * silu
        silu_ref[pl.ds(t, chunk)] = silu.astype(bf16)
        slope_ref[pl.ds(t, chunk)] = (gg * (sig + silu * (1.0 - sig))).astype(bf16)
        for k in range(chunk):
            total = total + dt[k]
            time_scr[t + k] = total
        return total

    total = lax.fori_loop(0, steps // chunk, prep, jnp.zeros((SEQS, WIDE), f32))
    tot_ref[...] = total

    def weighted(rates, vectors, map_at, out):
        acc_scr[...] = jnp.zeros_like(acc_scr)

        def run(i, _):
            sums = [None] * PAIRS
            for k in range(RUN):
                t = i * RUN + k
                time, drive = vectors(t)
                for p in range(PAIRS):
                    term = jnp.exp2(time * rates[p]) * drive * map_at(t, p)
                    sums[p] = term if k == 0 else sums[p] + term
            for p in range(PAIRS):
                a, b = halves(sums[p])
                acc_scr[2 * p] += a
                acc_scr[2 * p + 1] += b
            return 0

        lax.fori_loop(0, steps // RUN, run, 0)
        for n in range(STATES):
            out(n, acc_scr[n])

    low = lax.broadcasted_iota(jnp.int32, (SEQS, LANES), 0) < half
    packed = [
        jnp.where(low, rate_ref[n : n + 1, :LANES], rate_ref[n : n + 1, LANES:])
        for n in range(STATES)
    ]
    packed = [pair(packed[2 * p], packed[2 * p + 1]) for p in range(PAIRS)]
    for group in range(groups):
        rows = slice(group * half, (group + 1) * half)

        def pack(v):
            return jnp.concatenate([v[rows, :LANES], v[rows, LANES:]], axis=0)

        whole = pack(total)

        def vectors(t):
            return both(whole - pack(time_scr[t])), both(pack(dt_ref[t] * act_ref[t]))

        def map_at(t, p):
            return b_scr[group, t, p]

        def out(n, value):
            fwd_ref[group, 0, n] = value

        weighted(packed, vectors, map_at, out)

    for part in range(WIDE // LANES):
        cols = slice(part * LANES, (part + 1) * LANES)
        mine = [jnp.broadcast_to(rate_ref[n : n + 1, cols], (SEQS, LANES)) for n in range(STATES)]
        mine = [pair(mine[2 * p], mine[2 * p + 1]) for p in range(PAIRS)]

        def vectors(t):
            return both(time_scr[t, :, cols]), both(yg_ref[t, :, cols])

        def map_at(t, p):
            return c_scr[t, p]

        def out(n, value):
            bwd_ref[n, :, cols] = value

        weighted(mine, vectors, map_at, out)


def piece(proj, act, mixture, gated_grad, step_pad, sbias, rate, select, groups):
    steps, _, channels = act.shape
    grid = channels // WIDE
    wide = lambda j: (0, 0, j)
    flat = pl.BlockSpec((steps, SEQS, WIDE), wide)
    shape = (steps, SEQS, channels)
    return pl.pallas_call(
        piece_kernel,
        grid=(grid,),
        in_specs=[
            pl.BlockSpec((steps * SEQS, LANES), lambda j: (0, 0)),
            flat,
            pl.BlockSpec((steps + HALO, SEQS, WIDE), lambda j: (0, 0, j + grid)),
            flat,
            pl.BlockSpec((LANES, WIDE), lambda j: (0, j)),
            pl.BlockSpec((1, WIDE), lambda j: (0, j)),
            pl.BlockSpec((STATES, WIDE), lambda j: (0, j)),
            pl.BlockSpec(select.shape, lambda j: (0, 0)),
        ],
        out_specs=[
            flat, flat, flat, flat, flat,
            pl.BlockSpec((groups, 1, STATES, SEQS, LANES), lambda j: (0, j, 0, 0, 0)),
            pl.BlockSpec((STATES, SEQS, WIDE), wide),
            pl.BlockSpec((SEQS, WIDE), lambda j: (0, j)),
        ],
        out_shape=[
            jax.ShapeDtypeStruct(shape, f32),
            jax.ShapeDtypeStruct(shape, bf16),
            jax.ShapeDtypeStruct(shape, f32),
            jax.ShapeDtypeStruct(shape, bf16),
            jax.ShapeDtypeStruct(shape, bf16),
            jax.ShapeDtypeStruct((groups, grid, STATES, SEQS, LANES), f32),
            jax.ShapeDtypeStruct((STATES, SEQS, channels), f32),
            jax.ShapeDtypeStruct((SEQS, channels), f32),
        ],
        scratch_shapes=[
            pltpu.VMEM((groups, steps, PAIRS, 2 * SEQS, LANES), bf16),
            pltpu.VMEM((steps, PAIRS, 2 * SEQS, LANES), bf16),
            pltpu.VMEM((steps, SEQS, WIDE), f32),
            pltpu.VMEM((STATES, SEQS, LANES), f32),
        ],
        compiler_params=params(),
        cost_estimate=cost(60),
        name="piece",
    )(proj, act, mixture, gated_grad, step_pad, sbias, rate, select)


TILES = [slice(k * LANES, (k + 1) * LANES) for k in range(WIDE // LANES)]


def forward_kernel(
    proj_ref, dt_ref, act_ref, yg_ref, silu_ref, slope_ref, rate_ref, start_ref, skip_ref, select_ref,
    gated_ref, hist_ref, gategrad_ref, skipg_ref,
    b_scr, c_scr,
):
    j = pl.program_id(0)
    steps = dt_ref.shape[0]

    @pl.when(j == 0)
    def _():
        spread_maps(proj_ref, select_ref, RANK, STATES, store_plain(b_scr))
        spread_maps(proj_ref, select_ref, RANK + STATES, STATES, store_pairs(c_scr))

    rates = [jnp.broadcast_to(rate_ref[n : n + 1, :], (SEQS, LANES)) for n in range(STATES)]
    skip = jnp.broadcast_to(skip_ref[0:1, :], (SEQS, LANES))
    unroll = 8

    def run(i, carry):
        h, skip_sum = carry
        for k in range(unroll):
            t = i * unroll + k
            dt = dt_ref[t]
            act = act_ref[t]
            u = dt * act
            new = []
            y = None
            for p in range(PAIRS):
                for n in (2 * p, 2 * p + 1):
                    new.append(jnp.exp2(dt * rates[n]) * h[n] + u * b_scr[t, n])
                low = pair(new[2 * p], new[2 * p + 1])
                hist_ref[t + 1, p] = low
                term = low * c_scr[t, p]
                y = term if p == 0 else y + term
            h = tuple(new)
            mixed = folded(y) + skip * act
            gated_ref[t] = (mixed * silu_ref[t].astype(f32)).astype(bf16)
            gategrad_ref[t] = (mixed * slope_ref[t].astype(f32)).astype(bf16)
            skip_sum = skip_sum + yg_ref[t] * act
        return h, skip_sum

    start = tuple(start_ref[n] for n in range(STATES))
    for p in range(PAIRS):
        hist_ref[0, p] = pair(start[2 * p], start[2 * p + 1])
    _, skip_sum = lax.fori_loop(0, steps // unroll, run, (start, jnp.zeros((SEQS, LANES), f32)))
    skipg_ref[...] = jnp.sum(skip_sum, axis=0, keepdims=True)


def forward(proj, dt, act, yg, silu, slope, rate, start, skip, select):
    steps, _, channels = act.shape
    grid = channels // LANES
    tile = lambda j: (0, 0, j)
    flat = pl.BlockSpec((steps, SEQS, LANES), tile)
    parts = len(TILES)
    return pl.pallas_call(
        forward_kernel,
        grid=(grid,),
        in_specs=[
            pl.BlockSpec((steps * SEQS, LANES), lambda j: (0, 0)),
            flat, flat, flat, flat, flat,
            pl.BlockSpec((STATES, LANES), lambda j: (0, j)),
            pl.BlockSpec((STATES, SEQS, LANES), tile),
            pl.BlockSpec((1, LANES), lambda j: (0, j)),
            pl.BlockSpec(select.shape, lambda j: (0, 0)),
        ],
        out_specs=[
            flat,
            pl.BlockSpec(
                (None, None, steps + 1, PAIRS, 2 * SEQS, LANES),
                lambda j: (j // parts, j % parts, 0, 0, 0, 0),
            ),
            flat,
            pl.BlockSpec((1, LANES), lambda j: (0, j)),
        ],
        out_shape=[
            jax.ShapeDtypeStruct((steps, SEQS, channels), bf16),
            jax.ShapeDtypeStruct((grid // parts, parts, steps + 1, PAIRS, 2 * SEQS, LANES), bf16),
            jax.ShapeDtypeStruct((steps, SEQS, channels), bf16),
            jax.ShapeDtypeStruct((1, channels), f32),
        ],
        scratch_shapes=[
            pltpu.VMEM((steps, STATES, SEQS, LANES), f32),
            pltpu.VMEM((steps, PAIRS, 2 * SEQS, LANES), bf16),
        ],
        compiler_params=params(),
        cost_estimate=cost(50),
        name="forward_scan",
    )(proj, dt, act, yg, silu, slope, rate, start, skip, select)


def backward_kernel(
    proj_ref, dt_ref, sig_ref, act_ref, yg_ref, rate_ref, end_ref, skip_ref,
    hist_ref, rank_t_ref, stepw_t_ref, pick_ref, select_ref,
    act_grad_ref, stepg_ref, biasg_ref, decayg_ref, projg_ref,
    b_scr, c_scr, db_scr, dc_scr, pre_scr, acc_scr, decay_scr, ge_scr, sum_scr,
):
    j = pl.program_id(0)
    steps = dt_ref.shape[0]

    @pl.when(j == 0)
    def _():
        spread_maps(proj_ref, select_ref, RANK, STATES, store_pairs(b_scr))
        spread_maps(proj_ref, select_ref, RANK + STATES, STATES, store_plain(c_scr))

        def clear(t, _):
            for p in range(PAIRS):
                db_scr[t, p] = jnp.zeros((2 * SEQS, LANES), bf16)
                dc_scr[t, p] = jnp.zeros((2 * SEQS, LANES), bf16)
            return 0

        lax.fori_loop(0, steps, clear, 0)
        acc_scr[...] = jnp.zeros_like(acc_scr)

    decay_scr[...] = jnp.zeros_like(decay_scr)
    sum_scr[...] = jnp.zeros_like(sum_scr)
    for n in range(STATES):
        ge_scr[n] = end_ref[n]

    def run(i, _):
        base = steps - (i + 1) * RUN
        db = [[None] * PAIRS for _ in range(RUN)]
        dc = [[None] * PAIRS for _ in range(RUN)]
        for part, cols in enumerate(TILES):
            rates = [jnp.broadcast_to(rate_ref[n : n + 1, cols], (SEQS, LANES)) for n in range(STATES)]
            low_rates = [pair(rates[2 * p], rates[2 * p + 1]) for p in range(PAIRS)]
            skip = jnp.broadcast_to(skip_ref[0:1, cols], (SEQS, LANES))
            ge = [ge_scr[n, :, cols] for n in range(STATES)]
            bias_sum = jnp.zeros((SEQS, LANES), f32)
            decay = [None] * PAIRS
            for k in range(RUN - 1, -1, -1):
                t = base + k
                dt = dt_ref[t, :, cols]
                act = act_ref[t, :, cols]
                yg = yg_ref[t, :, cols]
                u2 = both(dt * act)
                dt2 = both(dt)
                yg2 = both(yg)
                du = None
                ddt = None
                for p in range(PAIRS):
                    g = [ge[n] + yg * c_scr[t, n] for n in (2 * p, 2 * p + 1)]
                    g2 = pair(*g)
                    term = yg2 * hist_ref[part, t + 1, p]
                    dc[k][p] = term if part == 0 else dc[k][p] + term
                    term = g2 * u2
                    db[k][p] = term if part == 0 else db[k][p] + term
                    term = g2 * b_scr[t, p]
                    du = term if p == 0 else du + term
                    gn = [jnp.exp2(dt * rates[2 * p + m]) * g[m] for m in (0, 1)]
                    ge[2 * p], ge[2 * p + 1] = gn
                    q = pair(*gn) * hist_ref[part, t, p]
                    term = q * dt2
                    decay[p] = term if decay[p] is None else decay[p] + term
                    term = q * low_rates[p]
                    ddt = term if p == 0 else ddt + term
                du = folded(du)
                pre_grad = (du * act + folded(ddt) * LN2) * sig_ref[t, :, cols].astype(f32)
                pre_scr[t, :, cols] = pre_grad.astype(bf16)
                act_grad_ref[t, :, cols] = yg * skip + du * dt
                bias_sum = bias_sum + pre_grad
                if part == len(TILES) - 1:
                    for p in range(PAIRS):
                        dc_scr[t, p] = dc[k][p] + dc_scr[t, p]
                        db_scr[t, p] = db[k][p] + db_scr[t, p]
            for p in range(PAIRS):
                a, b = halves(decay[p])
                decay_scr[2 * p, :, cols] += a
                decay_scr[2 * p + 1, :, cols] += b
            for n in range(STATES):
                ge_scr[n, :, cols] = ge[n]
            sum_scr[:, cols] += bias_sum
        return 0

    lax.fori_loop(0, steps // RUN, run, 0)
    for n in range(STATES):
        decayg_ref[n : n + 1, :] = jnp.sum(decay_scr[n] * rate_ref[n : n + 1, :], axis=0, keepdims=True) * LN2
    biasg_ref[...] = jnp.sum(sum_scr[...], axis=0, keepdims=True)

    pre_low = pre_scr[...].reshape(steps * SEQS, WIDE)
    stepg_ref[...] = jnp.dot(rank_t_ref[...], pre_low, preferred_element_type=f32)
    acc_scr[...] += jnp.dot(pre_low, stepw_t_ref[...], preferred_element_type=f32)

    @pl.when(j == pl.num_programs(0) - 1)
    def _():
        chunk = 32
        even = lax.broadcasted_iota(jnp.int32, (chunk, SEQS, LANES), 2) % 2 == 0

        def step(i, _):
            t = i * chunk
            total = jnp.zeros((chunk * 2 * SEQS, LANES), f32)
            for p in range(PAIRS):
                rows = jnp.concatenate([db_scr[pl.ds(t, chunk), p], dc_scr[pl.ds(t, chunk), p]], axis=2)
                rows = rows.reshape(chunk * 2 * SEQS, 2 * LANES)
                total = total + jnp.dot(rows, pick_ref[p], preferred_element_type=f32)
            total = total.reshape(chunk, 2 * SEQS, LANES)
            total = jnp.where(even, total[:, :SEQS], total[:, SEQS:]).reshape(chunk * SEQS, LANES)
            r = pl.multiple_of(t * SEQS, chunk * SEQS)
            projg_ref[pl.ds(r, chunk * SEQS), :] = (acc_scr[pl.ds(r, chunk * SEQS), :] + total).astype(bf16)
            return 0

        lax.fori_loop(0, steps // chunk, step, 0)


def backward(proj, dt, sig, act, yg, rate, end, skip, hist, rank_t, stepw_t, pick, select):
    steps, _, channels = act.shape
    grid = channels // WIDE
    tile = lambda j: (0, 0, j)
    whole = lambda j: (0, 0)
    flat = pl.BlockSpec((steps, SEQS, WIDE), tile)
    sums = pltpu.VMEM((steps, PAIRS, 2 * SEQS, LANES), bf16)
    return pl.pallas_call(
        backward_kernel,
        grid=(grid,),
        in_specs=[
            pl.BlockSpec((steps * SEQS, LANES), whole),
            flat, flat, flat, flat,
            pl.BlockSpec((STATES, WIDE), lambda j: (0, j)),
            pl.BlockSpec((STATES, SEQS, WIDE), tile),
            pl.BlockSpec((1, WIDE), lambda j: (0, j)),
            pl.BlockSpec(
                (None, len(TILES), steps + 1, PAIRS, 2 * SEQS, LANES), lambda j: (j, 0, 0, 0, 0, 0)
            ),
            pl.BlockSpec((RANK, steps * SEQS), whole),
            pl.BlockSpec((WIDE, LANES), lambda j: (j, 0)),
            pl.BlockSpec(pick.shape, lambda j: (0, 0, 0)),
            pl.BlockSpec(select.shape, whole),
        ],
        out_specs=[
            flat,
            pl.BlockSpec((RANK, WIDE), lambda j: (0, j)),
            pl.BlockSpec((1, WIDE), lambda j: (0, j)),
            pl.BlockSpec((STATES, WIDE), lambda j: (0, j)),
            pl.BlockSpec((steps * SEQS, LANES), whole),
        ],
        out_shape=[
            jax.ShapeDtypeStruct((steps, SEQS, channels), f32),
            jax.ShapeDtypeStruct((RANK, channels), f32),
            jax.ShapeDtypeStruct((1, channels), f32),
            jax.ShapeDtypeStruct((STATES, channels), f32),
            jax.ShapeDtypeStruct((steps * SEQS, LANES), bf16),
        ],
        scratch_shapes=[
            sums,
            pltpu.VMEM((steps, STATES, SEQS, LANES), f32),
            sums, sums,
            pltpu.VMEM((steps, SEQS, WIDE), bf16),
            pltpu.VMEM((steps * SEQS, LANES), f32),
            pltpu.VMEM((STATES, SEQS, WIDE), f32),
            pltpu.VMEM((STATES, SEQS, WIDE), f32),
            pltpu.VMEM((SEQS, WIDE), f32),
        ],
        compiler_params=params(),
        cost_estimate=cost(90),
        name="backward_scan",
    )(proj, dt, sig, act, yg, rate, end, skip, hist, rank_t, stepw_t, pick, select)


def filter_back_kernel(
    mix_ref, act_ref, act_grad_ref, projg_ref, projg_t_ref, sel_t_ref, fw_ref, fb_ref,
    mixgrad_ref, selg_ref, fwg_ref, fbg_ref,
    dv_scr,
):
    steps = act_ref.shape[0]
    chunk = 16
    taps = [fw_ref[k : k + 1, :] for k in range(KERNEL)]
    bias = fb_ref[0:1, :]
    zero = jnp.zeros((HALO, SEQS, WIDE), f32)
    dv_scr[0:HALO] = zero
    dv_scr[steps + HALO :] = zero

    def step(i, sums):
        t = i * chunk
        x = mix_ref[pl.ds(t, chunk + HALO)].astype(bf16).astype(f32)
        v = bias[None] + taps[0][None] * x[1 : 1 + chunk]
        for k in range(1, KERNEL):
            v = v + taps[k][None] * x[1 + k : 1 + k + chunk]
        sig = sigmoid(v)
        r = pl.multiple_of(t * SEQS, chunk * SEQS)
        more = jnp.dot(projg_ref[pl.ds(r, chunk * SEQS), :], sel_t_ref[...], preferred_element_type=f32)
        total = act_grad_ref[pl.ds(t, chunk)] + more.reshape(chunk, SEQS, WIDE)
        dv = total * (sig * (1.0 + v * (1.0 - sig)))
        dv_scr[pl.ds(t + HALO, chunk)] = dv
        new = [sums[0] + jnp.sum(dv, axis=0)]
        for k in range(KERNEL):
            new.append(sums[1 + k] + jnp.sum(dv * x[1 + k : 1 + k + chunk], axis=0))
        return tuple(new)

    sums = lax.fori_loop(
        0, steps // chunk, step, tuple(jnp.zeros((SEQS, WIDE), f32) for _ in range(KERNEL + 1))
    )
    fbg_ref[...] = jnp.sum(sums[0], axis=0, keepdims=True)
    for k in range(KERNEL):
        fwg_ref[k : k + 1, :] = jnp.sum(sums[1 + k], axis=0, keepdims=True)

    def spread(t, count):
        dv = dv_scr[pl.ds(t, count + HALO)]
        out = taps[KERNEL - 1][None] * dv[0:count]
        for k in range(KERNEL - 1):
            s = KERNEL - 1 - k
            out = out + taps[k][None] * dv[s : s + count]
        mixgrad_ref[pl.ds(t, count)] = out.astype(bf16)

    def out_step(i, _):
        spread(i * chunk, chunk)
        return 0

    lax.fori_loop(0, steps // chunk, out_step, 0)
    spread(steps, HALO)
    low = act_ref[...].reshape(steps * SEQS, WIDE).astype(bf16)
    selg_ref[...] = jnp.dot(projg_t_ref[...], low, preferred_element_type=f32)


def filter_back(mixture, act, act_grad, projg, projg_t, sel_t, fw, fb):
    steps, _, channels = act.shape
    grid = channels // WIDE
    wide = lambda j: (0, 0, j)
    whole = lambda j: (0, 0)
    cols = lambda j: (0, j)
    return pl.pallas_call(
        filter_back_kernel,
        grid=(grid,),
        in_specs=[
            pl.BlockSpec((steps + HALO, SEQS, WIDE), wide),
            pl.BlockSpec((steps, SEQS, WIDE), wide),
            pl.BlockSpec((steps, SEQS, WIDE), wide),
            pl.BlockSpec((steps * SEQS, LANES), whole),
            pl.BlockSpec((LANES, steps * SEQS), whole),
            pl.BlockSpec((LANES, WIDE), cols),
            pl.BlockSpec((KERNEL, WIDE), cols),
            pl.BlockSpec((1, WIDE), cols),
        ],
        out_specs=[
            pl.BlockSpec((steps + HALO, SEQS, WIDE), wide),
            pl.BlockSpec((LANES, WIDE), cols),
            pl.BlockSpec((KERNEL, WIDE), cols),
            pl.BlockSpec((1, WIDE), cols),
        ],
        out_shape=[
            jax.ShapeDtypeStruct((steps + HALO, SEQS, channels), bf16),
            jax.ShapeDtypeStruct((LANES, channels), f32),
            jax.ShapeDtypeStruct((KERNEL, channels), f32),
            jax.ShapeDtypeStruct((1, channels), f32),
        ],
        scratch_shapes=[pltpu.VMEM((steps + 2 * HALO, SEQS, WIDE), f32)],
        compiler_params=params(),
        cost_estimate=cost(20),
        name="filter_back",
    )(mixture, act, act_grad, projg, projg_t, sel_t, fw, fb)


def normalized(hidden, norm_gain):
    return hidden * lax.rsqrt(jnp.mean(hidden * hidden, axis=-1, keepdims=True) + 1e-05) * norm_gain


def contract_rows(left_side, right_side):
    return lax.dot_general(
        left_side, right_side, (((0,), (0,)), ((), ())), preferred_element_type=f32
    )


def contract_cols(left_side, right_side):
    return lax.dot_general(
        left_side, right_side, (((1,), (1,)), ((), ())), preferred_element_type=f32
    )


def exchanged(block, axis, distance):
    return lax.ppermute(block, axis, [(i, i ^ distance) for i in range(lax.axis_size(axis))])


def pick_row(block, index, axis=0):
    return lax.dynamic_index_in_dim(block, index, axis, keepdims=False)


def over_cores(blocks):
    blocks = blocks.reshape((-1, 2) + blocks.shape[1:])
    core = lax.axis_index("fsdp") % 2
    got = exchanged(pick_row(blocks, 1 - core, 1), "fsdp", 1)
    return (pick_row(blocks, core, 1).astype(f32) + got.astype(f32)).astype(bf16)


def to_chips(blocks):
    chip = lax.axis_index("fsdp") // 2
    got = [exchanged(pick_row(blocks, chip ^ d), "fsdp", 2 * d) for d in range(1, blocks.shape[0])]
    return pick_row(blocks, chip), got


def summed(own, got):
    total = own.astype(f32)
    for block in got:
        total = total + block.astype(f32)
    return total


def to_replicas(block):
    size, here = lax.axis_size("replica"), lax.axis_index("replica")
    parts = block.astype(bf16).reshape((size, -1) + block.shape[1:])
    own = pick_row(block.reshape(parts.shape), here)
    return own, [exchanged(pick_row(parts, here ^ d), "replica", d) for d in range(1, size)]


def from_replicas(part):
    return [part] + [exchanged(part, "replica", d) for d in range(1, lax.axis_size("replica"))]


def joined(parts):
    here = lax.axis_index("replica")
    parts = jnp.stack(parts)
    return jnp.concatenate([pick_row(parts, here ^ i) for i in range(parts.shape[0])]).astype(f32)


def gathered(block, axis):
    return lax.all_gather(block, "fsdp", axis=axis, tiled=True)


def body(
    prompt_hidden, sequel_hidden, parents, prompt_cotangent, sequel_cotangent,
    norm_gain, input_weight, filter_weight, depthwise_filter_bias, select_weight,
    step_weight, step_bias, decay_log, skip_gain, output_weight,
):
    size, here = lax.axis_size("fsdp"), lax.axis_index("fsdp")
    prompts, steps = prompt_hidden.shape[:2]
    sequels, sequel_len = sequel_hidden.shape[:2]
    split = sequel_len // steps
    assert prompts == PROMPTS and sequels * split == SEQS - prompts
    rim = KERNEL - 1
    half = SEQS // 2
    rows = steps * SEQS

    small = jnp.concatenate(
        [
            filter_weight,
            depthwise_filter_bias[None],
            step_bias[None],
            skip_gain[None],
            decay_log.T,
            step_weight,
            select_weight.T,
            jnp.pad(norm_gain, (0, step_bias.shape[0] - norm_gain.shape[0]))[None],
        ],
        axis=0,
    )
    small = gathered(small, 1)
    at = 0

    def take(count):
        nonlocal at
        at += count
        return small[at - count : at]

    fw = take(KERNEL).astype(f32)
    fb = take(1).astype(f32)
    sbias = take(1).astype(f32)
    skip = take(1).astype(f32)
    rate = -jnp.exp(take(STATES).astype(f32)) * LOG2E
    step_full = take(RANK)
    sel_t = jnp.pad(take(RANK + 2 * STATES), ((0, LANES - RANK - 2 * STATES), (0, 0)))
    gain = take(1).reshape(size, -1)[:, : norm_gain.shape[0]].reshape(-1).astype(f32)
    select_pad = sel_t.T
    step_pad = jnp.pad(step_full, ((0, LANES - RANK), (0, 0)))
    full_output = gathered(output_weight, 0)
    full_input = gathered(input_weight, 0)

    tails = lax.all_gather(prompt_hidden[:, steps - rim :], "fsdp")
    before = jnp.where(here > 0, tails[jnp.maximum(here - 1, 0)], jnp.zeros_like(tails[0]))
    pieces = sequel_hidden.reshape(sequels, split, steps, D)
    inner = jnp.concatenate([tails[size - 1][parents][:, None], pieces[:, :-1, steps - rim :]], axis=1)
    halo = jnp.concatenate([before, inner.reshape(-1, rim, D)], axis=0)
    halo = jnp.pad(halo, ((0, 0), (HALO - rim, 0), (0, 0)))
    hidden = jnp.concatenate([prompt_hidden, sequel_hidden.reshape(-1, steps, D)], axis=0)
    hidden = jnp.swapaxes(jnp.concatenate([halo, hidden], axis=1), 0, 1).reshape(-1, D).astype(f32)
    cot = jnp.concatenate([prompt_cotangent, sequel_cotangent.reshape(-1, steps, D)], axis=0)
    cotangent = jnp.swapaxes(cot, 0, 1).reshape(rows, D)

    gated_grad = contract_cols(cotangent, full_output).reshape(steps, SEQS, INNER)
    scaled = normalized(hidden, gain).astype(bf16)
    mixture = jnp.dot(scaled, full_input, preferred_element_type=f32)
    mixture = mixture.reshape(steps + HALO, SEQS, 2 * INNER)
    act, proj = front(mixture, fw, fb, select_pad, steps)
    groups = 1 if split == 1 else 2
    lane = jnp.arange(2 * STATES * LANES)[None, :]
    select = (jnp.arange(LANES)[:, None] == RANK + lane // LANES).astype(bf16)
    dt, sig, yg, silu, slope, ahead, behind, total = piece(
        proj, act, mixture, gated_grad, step_pad, sbias, rate, select, groups
    )

    ahead = ahead.reshape(groups, -1, STATES, 2, half, LANES).transpose(2, 0, 4, 1, 3, 5)
    ahead = ahead.reshape(STATES, groups * half, INNER)
    one_hot = (parents[:, None] == jnp.arange(PROMPTS, dtype=jnp.int32)[None, :]).astype(f32)
    own = total[half:].reshape(sequels, split, INNER)
    own_behind = behind[:, half:].reshape(STATES, sequels, split, INNER)
    own_decay = jnp.exp2(rate[:, None, None, :] * own[None])
    back = jnp.zeros((STATES, sequels, INNER), f32)
    own_end = []
    for p in range(split - 1, -1, -1):
        own_end.insert(0, back)
        back = own_behind[:, :, p] + (own_decay[:, :, p] * back if p < split - 1 else 0.0)
    branch = jnp.sum(back[:, :, None, :] * one_hot[None, :, :, None], axis=1)
    branch = lax.psum(branch, "fsdp")
    moved = jnp.concatenate([ahead[:, :half], behind[:, :half]], axis=0)
    moved, totals = lax.all_gather((moved, total[:half]), "fsdp")
    decays = jnp.exp2(rate[None, :, None, :] * totals[:, None, :, :])
    state = jnp.zeros_like(branch)
    start = state
    for k in range(size):
        start = jnp.where(here == k, state, start)
        state = decays[k] * state + moved[k, :STATES]
    back = branch
    end = back
    for k in range(size - 1, -1, -1):
        end = jnp.where(here == k, back, end)
        back = decays[k] * back + moved[k, STATES:]
    state = jnp.sum(state[:, None] * one_hot[None, :, :, None], axis=2)
    own_start = [state]
    for p in range(split - 1):
        state = own_decay[:, :, p] * state + ahead[:, half:].reshape(STATES, sequels, split, INNER)[:, :, p]
        own_start.append(state)
    own_start = jnp.stack(own_start, axis=2).reshape(STATES, half, INNER)
    own_end = jnp.stack(own_end, axis=2).reshape(STATES, half, INNER)
    start = jnp.concatenate([start, own_start], axis=1)
    end = jnp.concatenate([end, own_end], axis=1)

    gated, hist, gate_grad, skip_grad = forward(
        proj, dt, act, yg, silu, slope, rate, start, skip, select
    )
    gated = gated.reshape(rows, INNER)
    gate_grad = gate_grad.reshape(rows, INNER)
    after = lax.optimization_barrier
    output_grad = contract_rows(gated, cotangent).astype(bf16).reshape(size, -1, D)
    gate_weight_grad = contract_rows(scaled[HALO * SEQS :], gate_grad).astype(bf16)
    early = [over_cores(output_grad), over_cores(gate_weight_grad.reshape(size, -1, INNER))]
    result = hidden[HALO * SEQS :] + jnp.dot(gated, full_output, preferred_element_type=f32)
    result = jnp.swapaxes(result.reshape(steps, SEQS, D), 0, 1).astype(bf16)
    end, early = after((end, early))
    early = [to_chips(block) for block in early]

    rank_t = proj[:, :RANK].astype(bf16).T
    lane = jnp.arange(LANES)[None, None, :]
    which = jnp.arange(PAIRS)[:, None, None]
    source = jnp.arange(2 * LANES)[None, :, None]
    pick = (lane // 2 == jnp.where(source < LANES, RANK, RANK + STATES) // 2 + which).astype(bf16)
    act_grad, step_grad, bias_grad, decay_grad, projg = backward(
        proj, dt, sig, act, yg, rate, end, skip, hist, rank_t, step_pad.T, pick, select
    )
    projg, early = after((projg, early))
    early = [summed(*block) for block in early]
    projg, early = after((projg, early))
    early = [to_replicas(block) for block in early]
    filter_in_grad, select_grad, filter_grad, filter_bias_grad = filter_back(
        mixture, act, act_grad, projg, projg.T, sel_t, fw, fb
    )
    filter_in_grad, early = after((filter_in_grad, early))
    early = [summed(*block).astype(bf16) for block in early]
    filter_in_grad = filter_in_grad.reshape(-1, INNER)
    filter_weight_grad = contract_rows(scaled, filter_in_grad).astype(bf16)
    late = [over_cores(filter_weight_grad.reshape(size, -1, INNER))]
    early = [from_replicas(block) for block in early]
    scaled_grad = contract_cols(filter_in_grad, full_input[:, :INNER])
    more = contract_cols(gate_grad, full_input[:, INNER:])
    scaled_grad = scaled_grad + jnp.pad(more, ((HALO * SEQS, 0), (0, 0)))
    unused_norm, norm_back = jax.vjp(normalized, hidden, gain)
    hidden_grad, gain_grad = norm_back(scaled_grad)
    hidden_grad = jnp.swapaxes(hidden_grad.reshape(steps + HALO, SEQS, D), 0, 1)
    main = hidden_grad[:, HALO:]
    extra = hidden_grad[:, HALO - rim : HALO]
    own_extra = extra[half:].reshape(sequels, split, rim, D)
    child = jnp.einsum("sp,srd->prd", one_hot, own_extra[:, 0], precision=lax.Precision.HIGHEST)
    shared = lax.all_gather(jnp.stack([extra[:half], child]), "fsdp")
    following = jnp.where(
        here < size - 1, shared[jnp.minimum(here + 1, size - 1), 0], jnp.sum(shared[:, 1], axis=0)
    )
    own_following = jnp.pad(own_extra[:, 1:], ((0, 0), (0, 1), (0, 0), (0, 0))).reshape(half, rim, D)
    tail = jnp.concatenate([following, own_following], axis=0)
    main = main + jnp.pad(tail, ((0, 0), (steps - rim, 0), (0, 0))) + cot.astype(f32)

    small_grad = jnp.concatenate(
        [
            filter_grad,
            filter_bias_grad,
            bias_grad,
            skip_grad,
            decay_grad,
            step_grad,
            select_grad[: RANK + 2 * STATES],
            jnp.pad(gain_grad.reshape(size, -1), ((0, 0), (0, (INNER - D) // size))).reshape(1, -1),
            jnp.zeros((8, INNER), f32),
        ],
        axis=0,
    )
    small_grad = jnp.swapaxes(small_grad.astype(bf16).reshape(small_grad.shape[0], size, -1), 0, 1)
    late = late + [over_cores(small_grad)]
    late = [summed(*to_chips(block)) for block in late]
    late = [summed(*to_replicas(block)).astype(bf16) for block in late]
    filter_weight_grad, small_grad = [joined(from_replicas(block)) for block in late]
    output_grad, gate_weight_grad = [joined(block) for block in early]
    input_grad = jnp.concatenate([filter_weight_grad, gate_weight_grad], axis=1)
    at = 0
    taken = []
    for count in (KERNEL, 1, 1, 1, STATES, RANK, RANK + 2 * STATES, 1):
        taken.append(small_grad[at : at + count])
        at += count
    g_filter, g_fbias, g_sbias, g_skip, g_decay, g_step, g_select, g_gain = taken
    return (
        result[:half],
        result[half:].reshape(sequel_hidden.shape),
        main[:half],
        main[half:].reshape(sequel_hidden.shape),
        g_gain[0, : norm_gain.shape[0]],
        input_grad,
        g_filter,
        g_fbias[0],
        g_select.T,
        g_step,
        g_sbias[0],
        g_decay.T,
        g_skip[0],
        output_grad,
    )


def solution(mesh):
    rows = P("replica", "fsdp", None)
    own = P(("replica", "fsdp"), None, None)
    return jax.shard_map(
        body,
        mesh=mesh,
        in_specs=(
            rows, own, P(("replica", "fsdp")), rows, own,
            P("fsdp"), P("fsdp", None), P(None, "fsdp"), P("fsdp"), P("fsdp", None),
            P(None, "fsdp"), P("fsdp"), P("fsdp", None), P("fsdp"), P("fsdp", None),
        ),
        out_specs=(
            rows, own, rows, own,
            P("fsdp"), P("fsdp", None), P(None, "fsdp"), P("fsdp"), P("fsdp", None),
            P(None, "fsdp"), P("fsdp"), P("fsdp", None), P("fsdp"), P("fsdp", None),
        ),
        check_vma=False,
    )
```

```python
import functools
import math

import jax
import jax.numpy as jnp
from jax import lax
from jax.experimental import pallas as pl
from jax.experimental.pallas import tpu as pltpu
from jax.sharding import PartitionSpec as P

D = 1024
INNER = 2048
STATES = 16
RANK = 64
KERNEL = 4
PROMPTS = 4

SEQS = 8
HALO = 4
LANES = 128
WIDE = 256
LOG2E = math.log2(math.e)
LN2 = math.log(2.0)
f32 = jnp.float32
bf16 = jnp.bfloat16

VMEM_LIMIT = 62 * 1024 * 1024


def cost(microseconds):
    return pl.CostEstimate(flops=int(microseconds * 1e9), bytes_accessed=0, transcendentals=0)


def params(**kw):
    return pltpu.CompilerParams(vmem_limit_bytes=VMEM_LIMIT, **kw)


def sigmoid(x):
    return 1.0 / (1.0 + jnp.exp(-x))


def softplus(x):
    return jnp.maximum(x, 0.0) + jnp.log1p(jnp.exp(-jnp.abs(x)))


def scale_of(rows):
    return lax.rsqrt(jnp.mean(rows * rows, axis=-1, keepdims=True) + 1e-05)


def by_time(prompt_ref, piece_ref):
    both_kinds = jnp.concatenate([prompt_ref[...], piece_ref[...]], axis=0).astype(f32)
    return jnp.swapaxes(both_kinds, 0, 1)


def prepare_kernel(prompt_ref, piece_ref, prompt_cot_ref, piece_cot_ref, halo_ref, gain_ref, scaled_ref, cot_ref):
    i = pl.program_id(0)
    gain = gain_ref[...]

    @pl.when(i == 0)
    def _():
        rows = halo_ref[...]
        scaled_ref[0 : HALO * SEQS, :] = (rows * scale_of(rows) * gain).astype(bf16)

    rows = by_time(prompt_ref, piece_ref)
    count = rows.shape[0] * SEQS
    rows = rows.reshape(count, D)
    at = pl.multiple_of(HALO * SEQS + i * count, HALO * SEQS)
    scaled_ref[pl.ds(at, count), :] = (rows * scale_of(rows) * gain).astype(bf16)
    cot_ref[...] = by_time(prompt_cot_ref, piece_cot_ref).reshape(count, D).astype(bf16)


CHUNK = 16


def prepare(prompt, piece, prompt_cot, piece_cot, halo, gain):
    steps = prompt.shape[1]
    part = pl.BlockSpec((SEQS // 2, CHUNK, D), lambda i: (0, i, 0))
    rows = steps * SEQS
    return pl.pallas_call(
        prepare_kernel,
        grid=(steps // CHUNK,),
        in_specs=[
            part, part, part, part,
            pl.BlockSpec((HALO * SEQS, D), lambda i: (0, 0)),
            pl.BlockSpec((1, D), lambda i: (0, 0)),
        ],
        out_specs=[
            pl.BlockSpec((HALO * SEQS + rows, D), lambda i: (0, 0)),
            pl.BlockSpec((CHUNK * SEQS, D), lambda i: (i, 0)),
        ],
        out_shape=[
            jax.ShapeDtypeStruct((HALO * SEQS + rows, D), bf16),
            jax.ShapeDtypeStruct((rows, D), bf16),
        ],
        compiler_params=params(),
        cost_estimate=cost(5),
        name="prepare",
    )(prompt, piece, prompt_cot, piece_cot, halo, gain)


def norm_back(rows, scaled_grad, gain):
    inverse = scale_of(rows)
    unit = rows * inverse
    grad = scaled_grad * gain
    back = inverse * (grad - unit * jnp.mean(grad * unit, axis=-1, keepdims=True))
    return back, scaled_grad * unit


def finish_kernel(
    mixed_ref, grad_ref, more_ref, grad_halo_ref, more_halo_ref,
    prompt_ref, piece_ref, prompt_cot_ref, piece_cot_ref, halo_ref, gain_ref,
    prompt_out, piece_out, prompt_grad, piece_grad, halo_grad, gain_grad,
):
    i = pl.program_id(0)
    gain = gain_ref[...]

    @pl.when(i == 0)
    def _():
        back, sums = norm_back(halo_ref[...], grad_halo_ref[...] + more_halo_ref[...], gain)
        halo_grad[...] = back
        gain_grad[...] = jnp.sum(sums, axis=0, keepdims=True)

    half = SEQS // 2
    rows = by_time(prompt_ref, piece_ref)
    shape = rows.shape
    rows = rows.reshape(-1, D)
    back, sums = norm_back(rows, grad_ref[...] + more_ref[...], gain)
    gain_grad[...] += jnp.sum(sums, axis=0, keepdims=True)
    back = jnp.swapaxes(back.reshape(shape), 0, 1)
    prompt_grad[...] = back[:half] + prompt_cot_ref[...].astype(f32)
    piece_grad[...] = back[half:] + piece_cot_ref[...].astype(f32)
    mixed = jnp.swapaxes((mixed_ref[...] + rows).reshape(shape), 0, 1)
    prompt_out[...] = mixed[:half].astype(bf16)
    piece_out[...] = mixed[half:].astype(bf16)


def finish(mixed, grad, more, prompt, piece, prompt_cot, piece_cot, halo, gain):
    steps = prompt.shape[1]
    part = pl.BlockSpec((SEQS // 2, CHUNK, D), lambda i: (0, i, 0))
    first = pl.BlockSpec((HALO * SEQS, D), lambda i: (0, 0))
    shifted = pl.BlockSpec(
        (pl.Element(CHUNK * SEQS), pl.Element(D)),
        lambda i: (pl.multiple_of(HALO * SEQS + i * (CHUNK * SEQS), HALO * SEQS), 0),
    )
    return pl.pallas_call(
        finish_kernel,
        grid=(steps // CHUNK,),
        in_specs=[
            pl.BlockSpec((CHUNK * SEQS, D), lambda i: (i, 0)),
            shifted, shifted, first, first,
            part, part, part, part,
            first,
            pl.BlockSpec((1, D), lambda i: (0, 0)),
        ],
        out_specs=[part, part, part, part, first, pl.BlockSpec((1, D), lambda i: (0, 0))],
        out_shape=[
            jax.ShapeDtypeStruct(prompt.shape, bf16),
            jax.ShapeDtypeStruct(piece.shape, bf16),
            jax.ShapeDtypeStruct(prompt.shape, f32),
            jax.ShapeDtypeStruct(piece.shape, f32),
            jax.ShapeDtypeStruct((HALO * SEQS, D), f32),
            jax.ShapeDtypeStruct((1, D), f32),
        ],
        compiler_params=params(),
        cost_estimate=cost(8),
        name="finish",
    )(mixed, grad, more, grad, more, prompt, piece, prompt_cot, piece_cot, halo, gain)


def front_kernel(mix_ref, fw_ref, fb_ref, sel_ref, act_ref, proj_ref):
    j = pl.program_id(0)
    steps = act_ref.shape[0]
    chunk = 16
    taps = [fw_ref[k : k + 1, :] for k in range(KERNEL)]
    bias = fb_ref[0:1, :]

    @pl.when(j == 0)
    def _():
        proj_ref[...] = jnp.zeros_like(proj_ref)

    def step(i, _):
        t = i * chunk
        x = mix_ref[pl.ds(t, chunk + HALO)].astype(f32)
        v = bias[None] + taps[0][None] * x[1 : 1 + chunk]
        for k in range(1, KERNEL):
            v = v + taps[k][None] * x[1 + k : 1 + k + chunk]
        act = v * sigmoid(v)
        act_ref[pl.ds(t, chunk)] = act
        low = act.reshape(chunk * SEQS, act.shape[-1]).astype(bf16)
        r = pl.multiple_of(t * SEQS, chunk * SEQS)
        proj_ref[pl.ds(r, chunk * SEQS), :] += jnp.dot(low, sel_ref[...], preferred_element_type=f32)
        return 0

    lax.fori_loop(0, steps // chunk, step, 0)


def front(mixture, fw, fb, select_pad, steps):
    channels = fw.shape[1]
    return pl.pallas_call(
        front_kernel,
        grid=(channels // WIDE,),
        in_specs=[
            pl.BlockSpec((steps + HALO, SEQS, WIDE), lambda j: (0, 0, j)),
            pl.BlockSpec((KERNEL, WIDE), lambda j: (0, j)),
            pl.BlockSpec((1, WIDE), lambda j: (0, j)),
            pl.BlockSpec((WIDE, LANES), lambda j: (j, 0)),
        ],
        out_specs=[
            pl.BlockSpec((steps, SEQS, WIDE), lambda j: (0, 0, j)),
            pl.BlockSpec((steps * SEQS, LANES), lambda j: (0, 0)),
        ],
        out_shape=[
            jax.ShapeDtypeStruct((steps, SEQS, channels), f32),
            jax.ShapeDtypeStruct((steps * SEQS, LANES), f32),
        ],
        compiler_params=params(),
        cost_estimate=cost(16),
        name="front",
    )(mixture, fw, fb, select_pad)


def pair(a, b):
    return jnp.concatenate([a, b], axis=0).astype(bf16)


def both(v):
    return pair(v, v)


def halves(v):
    v = v.astype(f32)
    return v[:SEQS], v[SEQS:]


def folded(v):
    a, b = halves(v)
    return a + b


def spread_maps(proj_ref, select_ref, first, count, store):
    steps = proj_ref.shape[0] // SEQS
    chunk = 32

    def step(i, _):
        r = pl.multiple_of(i * chunk * SEQS, chunk * SEQS)
        rows = proj_ref[pl.ds(r, chunk * SEQS), :].astype(bf16)
        for n in range(0, count, 2):
            at = (first - RANK + n) * LANES
            wide = jnp.dot(rows, select_ref[:, at : at + 2 * LANES], preferred_element_type=f32)
            wide = wide.reshape(chunk, SEQS, 2 * LANES)
            store(i * chunk, chunk, n, wide[:, :, :LANES], wide[:, :, LANES:])
        return 0

    lax.fori_loop(0, steps // chunk, step, 0)


def store_plain(ref):
    def store(t, count, n, a, b):
        ref[pl.ds(t, count), n] = a
        ref[pl.ds(t, count), n + 1] = b

    return store


def store_pairs(ref):
    def store(t, count, n, a, b):
        ref[pl.ds(t, count), n // 2] = jnp.concatenate([a, b], axis=1).astype(bf16)

    return store


PAIRS = STATES // 2
RUN = 8


def piece_kernel(
    proj_ref, act_ref, gate_ref, gg_ref, stepw_ref, sbias_ref, rate_ref, select_ref,
    dt_ref, sig_ref, yg_ref, silu_ref, slope_ref, fwd_ref, bwd_ref, tot_ref,
    b_scr, c_scr, time_scr, acc_scr,
):
    j = pl.program_id(0)
    steps = dt_ref.shape[0]
    half = SEQS // 2
    groups = fwd_ref.shape[0] // half

    @pl.when(j == 0)
    def _():
        def store_groups(t, count, n, a, b):
            for group in range(groups):
                rows = slice(group * half, (group + 1) * half)
                parts = [a[:, rows], a[:, rows], b[:, rows], b[:, rows]]
                b_scr[group, pl.ds(t, count), n // 2] = jnp.concatenate(parts, axis=1).astype(bf16)

        spread_maps(proj_ref, select_ref, RANK, STATES, store_groups)
        spread_maps(proj_ref, select_ref, RANK + STATES, STATES, store_pairs(c_scr))

    chunk = 8
    sbias = sbias_ref[0:1, :]

    def prep(i, total):
        t = i * chunk
        r = pl.multiple_of(t * SEQS, chunk * SEQS)
        rank = proj_ref[pl.ds(r, chunk * SEQS), :].astype(bf16)
        pre = jnp.dot(rank, stepw_ref[...], preferred_element_type=f32).reshape(chunk, SEQS, WIDE)
        pre = pre + sbias[None]
        small = jnp.exp2(jnp.abs(pre) * -LOG2E)
        one = 1.0 + small
        inverse = 1.0 / one
        dt = jnp.maximum(pre, 0.0) + (jnp.log(one) + (small - (one - 1.0)) * inverse)
        dt_ref[pl.ds(t, chunk)] = dt
        sig_ref[pl.ds(t, chunk)] = jnp.where(pre >= 0.0, inverse, small * inverse).astype(bf16)
        gate = gate_ref[pl.ds(t + HALO, chunk)]
        gg = gg_ref[pl.ds(t, chunk)]
        sig = sigmoid(gate)
        silu = gate * sig
        yg_ref[pl.ds(t, chunk)] = gg * silu
        silu_ref[pl.ds(t, chunk)] = silu.astype(bf16)
        slope_ref[pl.ds(t, chunk)] = (gg * (sig + silu * (1.0 - sig))).astype(bf16)
        for k in range(chunk):
            total = total + dt[k]
            time_scr[t + k] = total
        return total

    total = lax.fori_loop(0, steps // chunk, prep, jnp.zeros((SEQS, WIDE), f32))
    tot_ref[...] = total

    def weighted(rates, vectors, map_at, out):
        acc_scr[...] = jnp.zeros_like(acc_scr)

        def run(i, _):
            sums = [None] * PAIRS
            for k in range(RUN):
                t = i * RUN + k
                time, drive = vectors(t)
                for p in range(PAIRS):
                    term = jnp.exp2(time * rates[p]) * drive * map_at(t, p)
                    sums[p] = term if k == 0 else sums[p] + term
            for p in range(PAIRS):
                a, b = halves(sums[p])
                acc_scr[2 * p] += a
                acc_scr[2 * p + 1] += b
            return 0

        lax.fori_loop(0, steps // RUN, run, 0)
        for n in range(STATES):
            out(n, acc_scr[n])

    low = lax.broadcasted_iota(jnp.int32, (SEQS, LANES), 0) < half
    packed = [
        jnp.where(low, rate_ref[n : n + 1, :LANES], rate_ref[n : n + 1, LANES:])
        for n in range(STATES)
    ]
    packed = [pair(packed[2 * p], packed[2 * p + 1]) for p in range(PAIRS)]
    for group in range(groups):
        rows = slice(group * half, (group + 1) * half)

        def pack(v):
            return jnp.concatenate([v[rows, :LANES], v[rows, LANES:]], axis=0)

        whole = pack(total)

        def vectors(t):
            return both(whole - pack(time_scr[t])), both(pack(dt_ref[t] * act_ref[t]))

        def map_at(t, p):
            return b_scr[group, t, p]

        def out(n, value):
            fwd_ref[rows, n, :LANES] = value[:half]
            fwd_ref[rows, n, LANES:] = value[half:]

        weighted(packed, vectors, map_at, out)

    for part in range(WIDE // LANES):
        cols = slice(part * LANES, (part + 1) * LANES)
        mine = [jnp.broadcast_to(rate_ref[n : n + 1, cols], (SEQS, LANES)) for n in range(STATES)]
        mine = [pair(mine[2 * p], mine[2 * p + 1]) for p in range(PAIRS)]

        def vectors(t):
            return both(time_scr[t, :, cols]), both(yg_ref[t, :, cols])

        def map_at(t, p):
            return c_scr[t, p]

        def out(n, value):
            bwd_ref[:, n, cols] = value

        weighted(mine, vectors, map_at, out)


def piece(proj, act, gate, gated_grad, step_pad, sbias, rate, select, groups):
    steps, _, channels = act.shape
    grid = channels // WIDE
    wide = lambda j: (0, 0, j)
    flat = pl.BlockSpec((steps, SEQS, WIDE), wide)
    shape = (steps, SEQS, channels)
    return pl.pallas_call(
        piece_kernel,
        grid=(grid,),
        in_specs=[
            pl.BlockSpec((steps * SEQS, LANES), lambda j: (0, 0)),
            flat,
            pl.BlockSpec((steps + HALO, SEQS, WIDE), wide),
            flat,
            pl.BlockSpec((LANES, WIDE), lambda j: (0, j)),
            pl.BlockSpec((1, WIDE), lambda j: (0, j)),
            pl.BlockSpec((STATES, WIDE), lambda j: (0, j)),
            pl.BlockSpec(select.shape, lambda j: (0, 0)),
        ],
        out_specs=[
            flat, flat, flat, flat, flat,
            pl.BlockSpec((groups * SEQS // 2, STATES, WIDE), wide),
            pl.BlockSpec((SEQS, STATES, WIDE), wide),
            pl.BlockSpec((SEQS, WIDE), lambda j: (0, j)),
        ],
        out_shape=[
            jax.ShapeDtypeStruct(shape, f32),
            jax.ShapeDtypeStruct(shape, bf16),
            jax.ShapeDtypeStruct(shape, f32),
            jax.ShapeDtypeStruct(shape, bf16),
            jax.ShapeDtypeStruct(shape, bf16),
            jax.ShapeDtypeStruct((groups * SEQS // 2, STATES, channels), f32),
            jax.ShapeDtypeStruct((SEQS, STATES, channels), f32),
            jax.ShapeDtypeStruct((SEQS, channels), f32),
        ],
        scratch_shapes=[
            pltpu.VMEM((groups, steps, PAIRS, 2 * SEQS, LANES), bf16),
            pltpu.VMEM((steps, PAIRS, 2 * SEQS, LANES), bf16),
            pltpu.VMEM((steps, SEQS, WIDE), f32),
            pltpu.VMEM((STATES, SEQS, LANES), f32),
        ],
        compiler_params=params(),
        cost_estimate=cost(60),
        name="piece",
    )(proj, act, gate, gated_grad, step_pad, sbias, rate, select)


def chain_kernel(
    one_hot_ref, ahead_ref, behind_ref, branch_ref, time_ref, rate_ref, start_out, end_out,
    moved_ref, got, got_time, back, done, sems, time_sems, back_sems,
):
    size = got.shape[0]
    width = got.shape[2]
    count = PROMPTS * STATES
    sequels = branch_ref.shape[0]
    me = lax.axis_index("fsdp")
    for p in range(PROMPTS):
        rows = slice(p * STATES, (p + 1) * STATES)
        total = one_hot_ref[0, p] * branch_ref[0]
        for k in range(1, sequels):
            total = total + one_hot_ref[k, p] * branch_ref[k]
        moved_ref[0 * count + p * STATES : 0 * count + (p + 1) * STATES] = ahead_ref[p].astype(bf16)
        moved_ref[1 * count + p * STATES : 1 * count + (p + 1) * STATES] = behind_ref[p].astype(bf16)
        moved_ref[2 * count + p * STATES : 2 * count + (p + 1) * STATES] = total.astype(bf16)
    barrier = pltpu.get_barrier_semaphore()
    for d in range(1, size):
        peer = lax.rem(me + d, size)
        pl.semaphore_signal(barrier, inc=1, device_id={"fsdp": peer}, device_id_type=pl.DeviceIdType.MESH)
    pl.semaphore_wait(barrier, size - 1)

    def columns(device):
        return pl.ds(pl.multiple_of(device * width, width), width)

    copies = []
    for d in range(1, size):
        peer = lax.rem(me + d, size)
        for src, dst, sem in ((moved_ref, got, sems), (time_ref, got_time, time_sems)):
            copy = pltpu.make_async_remote_copy(
                src_ref=src.at[:, columns(peer)],
                dst_ref=dst.at[me],
                send_sem=sem.at[0, d],
                recv_sem=sem.at[1, d],
                device_id={"fsdp": peer},
                device_id_type=pl.DeviceIdType.MESH,
            )
            copy.start()
            copies.append(copy)
    got[me] = moved_ref[:, columns(me)]
    got_time[me] = time_ref[:, columns(me)]
    for copy in copies:
        copy.wait()

    rate = jnp.concatenate([rate_ref[...]] * PROMPTS, axis=0)
    branch = jnp.zeros((count, width), f32)
    state = jnp.zeros((count, width), f32)
    decays = []
    for k in range(size):
        time = jnp.concatenate(
            [jnp.broadcast_to(got_time[k, p : p + 1, :], (STATES, width)) for p in range(PROMPTS)], axis=0
        )
        decays.append(jnp.exp2(rate * time))
        back[k, 0:count] = state.astype(bf16)
        state = decays[k] * state + got[k, 0:count].astype(f32)
        branch = branch + got[k, 2 * count : 3 * count].astype(f32)
    grad = branch
    for k in range(size - 1, -1, -1):
        back[k, count : 2 * count] = grad.astype(bf16)
        grad = decays[k] * grad + got[k, count : 2 * count].astype(f32)
    last = state.astype(bf16)
    for k in range(size):
        back[k, 2 * count : 3 * count] = last
    copies = []
    for d in range(1, size):
        peer = lax.rem(me + d, size)
        copy = pltpu.make_async_remote_copy(
            src_ref=back.at[peer],
            dst_ref=done.at[me],
            send_sem=back_sems.at[0, d],
            recv_sem=back_sems.at[1, d],
            device_id={"fsdp": peer},
            device_id_type=pl.DeviceIdType.MESH,
        )
        copy.start()
        copies.append(copy)
    done[me] = back[me]
    for copy in copies:
        copy.wait()
    for k in range(size):
        columns_k = slice(k * width, (k + 1) * width)
        last = []
        for p in range(PROMPTS):
            rows = slice(p * STATES, (p + 1) * STATES)
            start_out[p, :, columns_k] = done[k, rows].astype(f32)
            rows = slice(count + p * STATES, count + (p + 1) * STATES)
            end_out[p, :, columns_k] = done[k, rows].astype(f32)
            rows = slice(2 * count + p * STATES, 2 * count + (p + 1) * STATES)
            last.append(done[k, rows].astype(f32))
        for q in range(sequels):
            total = one_hot_ref[q, 0] * last[0]
            for p in range(1, PROMPTS):
                total = total + one_hot_ref[q, p] * last[p]
            start_out[PROMPTS + q, :, columns_k] = total
            end_out[PROMPTS + q, :, columns_k] = jnp.zeros_like(total)


def chain(one_hot, ahead, behind, branch, time, rate):
    size = lax.axis_size("fsdp")
    channels = ahead.shape[2]
    rows = 3 * PROMPTS * STATES
    width = channels // size
    own = lax.dynamic_slice_in_dim(rate, lax.axis_index("fsdp") * width, width, 1)
    whole = pl.BlockSpec(memory_space=pltpu.VMEM)
    shape = (PROMPTS + branch.shape[0], STATES, channels)
    return pl.pallas_call(
        chain_kernel,
        in_specs=[pl.BlockSpec(memory_space=pltpu.SMEM)] + [whole] * 5,
        out_specs=[whole] * 2,
        out_shape=[jax.ShapeDtypeStruct(shape, f32)] * 2,
        scratch_shapes=[
            pltpu.VMEM((rows, channels), bf16),
            pltpu.VMEM((size, rows, width), bf16),
            pltpu.VMEM((size, SEQS, width), f32),
            pltpu.VMEM((size, rows, width), bf16),
            pltpu.VMEM((size, rows, width), bf16),
            pltpu.SemaphoreType.DMA((2, size)),
            pltpu.SemaphoreType.DMA((2, size)),
            pltpu.SemaphoreType.DMA((2, size)),
        ],
        compiler_params=params(collective_id=1, has_side_effects=True),
        cost_estimate=cost(25),
        name="chain",
    )(one_hot, ahead, behind, branch, time, own)


TILES = [slice(k * LANES, (k + 1) * LANES) for k in range(WIDE // LANES)]


def forward_kernel(
    proj_ref, dt_ref, act_ref, yg_ref, silu_ref, slope_ref, rate_ref, start_ref, skip_ref, select_ref,
    gated_ref, hist_ref, gategrad_ref, skipg_ref,
    b_scr, c_scr,
):
    j = pl.program_id(0)
    steps = dt_ref.shape[0]

    @pl.when(j == 0)
    def _():
        spread_maps(proj_ref, select_ref, RANK, STATES, store_plain(b_scr))
        spread_maps(proj_ref, select_ref, RANK + STATES, STATES, store_pairs(c_scr))

    rates = [jnp.broadcast_to(rate_ref[n : n + 1, :], (SEQS, LANES)) for n in range(STATES)]
    skip = jnp.broadcast_to(skip_ref[0:1, :], (SEQS, LANES))
    gategrad_ref[0:HALO] = jnp.zeros((HALO, SEQS, LANES), bf16)
    unroll = 8

    def run(i, carry):
        h, skip_sum = carry
        for k in range(unroll):
            t = i * unroll + k
            dt = dt_ref[t]
            act = act_ref[t]
            u = dt * act
            new = []
            y = None
            for p in range(PAIRS):
                for n in (2 * p, 2 * p + 1):
                    new.append(jnp.exp2(dt * rates[n]) * h[n] + u * b_scr[t, n])
                low = pair(new[2 * p], new[2 * p + 1])
                hist_ref[t + 1, p] = low
                term = low * c_scr[t, p]
                y = term if p == 0 else y + term
            h = tuple(new)
            mixed = folded(y) + skip * act
            gated_ref[t] = (mixed * silu_ref[t].astype(f32)).astype(bf16)
            gategrad_ref[t + HALO] = (mixed * slope_ref[t].astype(f32)).astype(bf16)
            skip_sum = skip_sum + yg_ref[t] * act
        return h, skip_sum

    start = tuple(start_ref[:, n, :] for n in range(STATES))
    for p in range(PAIRS):
        hist_ref[0, p] = pair(start[2 * p], start[2 * p + 1])
    _, skip_sum = lax.fori_loop(0, steps // unroll, run, (start, jnp.zeros((SEQS, LANES), f32)))
    skipg_ref[...] = jnp.sum(skip_sum, axis=0, keepdims=True)


def forward(proj, dt, act, yg, silu, slope, rate, start, skip, select):
    steps, _, channels = act.shape
    grid = channels // LANES
    tile = lambda j: (0, 0, j)
    flat = pl.BlockSpec((steps, SEQS, LANES), tile)
    parts = len(TILES)
    return pl.pallas_call(
        forward_kernel,
        grid=(grid,),
        in_specs=[
            pl.BlockSpec((steps * SEQS, LANES), lambda j: (0, 0)),
            flat, flat, flat, flat, flat,
            pl.BlockSpec((STATES, LANES), lambda j: (0, j)),
            pl.BlockSpec((SEQS, STATES, LANES), tile),
            pl.BlockSpec((1, LANES), lambda j: (0, j)),
            pl.BlockSpec(select.shape, lambda j: (0, 0)),
        ],
        out_specs=[
            flat,
            pl.BlockSpec(
                (None, None, steps + 1, PAIRS, 2 * SEQS, LANES),
                lambda j: (j // parts, j % parts, 0, 0, 0, 0),
            ),
            pl.BlockSpec((steps + HALO, SEQS, LANES), tile),
            pl.BlockSpec((1, LANES), lambda j: (0, j)),
        ],
        out_shape=[
            jax.ShapeDtypeStruct((steps, SEQS, channels), bf16),
            jax.ShapeDtypeStruct((grid // parts, parts, steps + 1, PAIRS, 2 * SEQS, LANES), bf16),
            jax.ShapeDtypeStruct((steps + HALO, SEQS, channels), bf16),
            jax.ShapeDtypeStruct((1, channels), f32),
        ],
        scratch_shapes=[
            pltpu.VMEM((steps, STATES, SEQS, LANES), f32),
            pltpu.VMEM((steps, PAIRS, 2 * SEQS, LANES), bf16),
        ],
        compiler_params=params(),
        cost_estimate=cost(50),
        name="forward_scan",
    )(proj, dt, act, yg, silu, slope, rate, start, skip, select)


def backward_kernel(
    proj_ref, dt_ref, sig_ref, act_ref, yg_ref, rate_ref, end_ref, skip_ref,
    hist_ref, rank_t_ref, stepw_t_ref, pick_ref, select_ref,
    act_grad_ref, stepg_ref, biasg_ref, decayg_ref, projg_ref,
    b_scr, c_scr, db_scr, dc_scr, pre_scr, acc_scr, decay_scr, ge_scr, sum_scr,
):
    j = pl.program_id(0)
    steps = dt_ref.shape[0]

    @pl.when(j == 0)
    def _():
        spread_maps(proj_ref, select_ref, RANK, STATES, store_pairs(b_scr))
        spread_maps(proj_ref, select_ref, RANK + STATES, STATES, store_plain(c_scr))

        def clear(t, _):
            for p in range(PAIRS):
                db_scr[t, p] = jnp.zeros((2 * SEQS, LANES), bf16)
                dc_scr[t, p] = jnp.zeros((2 * SEQS, LANES), bf16)
            return 0

        lax.fori_loop(0, steps, clear, 0)
        acc_scr[...] = jnp.zeros_like(acc_scr)

    decay_scr[...] = jnp.zeros_like(decay_scr)
    sum_scr[...] = jnp.zeros_like(sum_scr)
    for n in range(STATES):
        ge_scr[n] = end_ref[:, n, :]

    def run(i, _):
        base = steps - (i + 1) * RUN
        db = [[None] * PAIRS for _ in range(RUN)]
        dc = [[None] * PAIRS for _ in range(RUN)]
        for part, cols in enumerate(TILES):
            rates = [jnp.broadcast_to(rate_ref[n : n + 1, cols], (SEQS, LANES)) for n in range(STATES)]
            low_rates = [pair(rates[2 * p], rates[2 * p + 1]) for p in range(PAIRS)]
            skip = jnp.broadcast_to(skip_ref[0:1, cols], (SEQS, LANES))
            ge = [ge_scr[n, :, cols] for n in range(STATES)]
            bias_sum = jnp.zeros((SEQS, LANES), f32)
            decay = [None] * PAIRS
            for k in range(RUN - 1, -1, -1):
                t = base + k
                dt = dt_ref[t, :, cols]
                act = act_ref[t, :, cols]
                yg = yg_ref[t, :, cols]
                u2 = both(dt * act)
                dt2 = both(dt)
                yg2 = both(yg)
                du = None
                ddt = None
                for p in range(PAIRS):
                    g = [ge[n] + yg * c_scr[t, n] for n in (2 * p, 2 * p + 1)]
                    g2 = pair(*g)
                    term = yg2 * hist_ref[part, t + 1, p]
                    dc[k][p] = term if part == 0 else dc[k][p] + term
                    term = g2 * u2
                    db[k][p] = term if part == 0 else db[k][p] + term
                    term = g2 * b_scr[t, p]
                    du = term if p == 0 else du + term
                    gn = [jnp.exp2(dt * rates[2 * p + m]) * g[m] for m in (0, 1)]
                    ge[2 * p], ge[2 * p + 1] = gn
                    q = pair(*gn) * hist_ref[part, t, p]
                    term = q * dt2
                    decay[p] = term if decay[p] is None else decay[p] + term
                    term = q * low_rates[p]
                    ddt = term if p == 0 else ddt + term
                du = folded(du)
                pre_grad = (du * act + folded(ddt) * LN2) * sig_ref[t, :, cols].astype(f32)
                pre_scr[t, :, cols] = pre_grad.astype(bf16)
                act_grad_ref[t, :, cols] = yg * skip + du * dt
                bias_sum = bias_sum + pre_grad
                if part == len(TILES) - 1:
                    for p in range(PAIRS):
                        dc_scr[t, p] = dc[k][p] + dc_scr[t, p]
                        db_scr[t, p] = db[k][p] + db_scr[t, p]
            for p in range(PAIRS):
                a, b = halves(decay[p])
                decay_scr[2 * p, :, cols] += a
                decay_scr[2 * p + 1, :, cols] += b
            for n in range(STATES):
                ge_scr[n, :, cols] = ge[n]
            sum_scr[:, cols] += bias_sum
        return 0

    lax.fori_loop(0, steps // RUN, run, 0)
    for n in range(STATES):
        decayg_ref[n : n + 1, :] = jnp.sum(decay_scr[n] * rate_ref[n : n + 1, :], axis=0, keepdims=True) * LN2
    biasg_ref[...] = jnp.sum(sum_scr[...], axis=0, keepdims=True)

    pre_low = pre_scr[...].reshape(steps * SEQS, WIDE)
    stepg_ref[...] = jnp.dot(rank_t_ref[...], pre_low, preferred_element_type=f32)
    acc_scr[...] += jnp.dot(pre_low, stepw_t_ref[...], preferred_element_type=f32)

    @pl.when(j == pl.num_programs(0) - 1)
    def _():
        chunk = 32
        even = lax.broadcasted_iota(jnp.int32, (chunk, SEQS, LANES), 2) % 2 == 0

        def step(i, _):
            t = i * chunk
            total = jnp.zeros((chunk * 2 * SEQS, LANES), f32)
            for p in range(PAIRS):
                rows = jnp.concatenate([db_scr[pl.ds(t, chunk), p], dc_scr[pl.ds(t, chunk), p]], axis=2)
                rows = rows.reshape(chunk * 2 * SEQS, 2 * LANES)
                total = total + jnp.dot(rows, pick_ref[p], preferred_element_type=f32)
            total = total.reshape(chunk, 2 * SEQS, LANES)
            total = jnp.where(even, total[:, :SEQS], total[:, SEQS:]).reshape(chunk * SEQS, LANES)
            r = pl.multiple_of(t * SEQS, chunk * SEQS)
            projg_ref[pl.ds(r, chunk * SEQS), :] = (acc_scr[pl.ds(r, chunk * SEQS), :] + total).astype(bf16)
            return 0

        lax.fori_loop(0, steps // chunk, step, 0)


def backward(proj, dt, sig, act, yg, rate, end, skip, hist, rank_t, stepw_t, pick, select):
    steps, _, channels = act.shape
    grid = channels // WIDE
    tile = lambda j: (0, 0, j)
    whole = lambda j: (0, 0)
    flat = pl.BlockSpec((steps, SEQS, WIDE), tile)
    sums = pltpu.VMEM((steps, PAIRS, 2 * SEQS, LANES), bf16)
    return pl.pallas_call(
        backward_kernel,
        grid=(grid,),
        in_specs=[
            pl.BlockSpec((steps * SEQS, LANES), whole),
            flat, flat, flat, flat,
            pl.BlockSpec((STATES, WIDE), lambda j: (0, j)),
            pl.BlockSpec((SEQS, STATES, WIDE), tile),
            pl.BlockSpec((1, WIDE), lambda j: (0, j)),
            pl.BlockSpec(
                (None, len(TILES), steps + 1, PAIRS, 2 * SEQS, LANES), lambda j: (j, 0, 0, 0, 0, 0)
            ),
            pl.BlockSpec((RANK, steps * SEQS), whole),
            pl.BlockSpec((WIDE, LANES), lambda j: (j, 0)),
            pl.BlockSpec(pick.shape, lambda j: (0, 0, 0)),
            pl.BlockSpec(select.shape, whole),
        ],
        out_specs=[
            flat,
            pl.BlockSpec((RANK, WIDE), lambda j: (0, j)),
            pl.BlockSpec((1, WIDE), lambda j: (0, j)),
            pl.BlockSpec((STATES, WIDE), lambda j: (0, j)),
            pl.BlockSpec((steps * SEQS, LANES), whole),
        ],
        out_shape=[
            jax.ShapeDtypeStruct((steps, SEQS, channels), f32),
            jax.ShapeDtypeStruct((RANK, channels), f32),
            jax.ShapeDtypeStruct((1, channels), f32),
            jax.ShapeDtypeStruct((STATES, channels), f32),
            jax.ShapeDtypeStruct((steps * SEQS, LANES), bf16),
        ],
        scratch_shapes=[
            sums,
            pltpu.VMEM((steps, STATES, SEQS, LANES), f32),
            sums, sums,
            pltpu.VMEM((steps, SEQS, WIDE), bf16),
            pltpu.VMEM((steps * SEQS, LANES), f32),
            pltpu.VMEM((STATES, SEQS, WIDE), f32),
            pltpu.VMEM((STATES, SEQS, WIDE), f32),
            pltpu.VMEM((SEQS, WIDE), f32),
        ],
        compiler_params=params(),
        cost_estimate=cost(90),
        name="backward_scan",
    )(proj, dt, sig, act, yg, rate, end, skip, hist, rank_t, stepw_t, pick, select)


def filter_back_kernel(
    mix_ref, act_ref, act_grad_ref, projg_ref, projg_t_ref, sel_ref, fw_ref, fb_ref,
    mixgrad_ref, selg_ref, fwg_ref, fbg_ref,
    dv_scr,
):
    steps = act_ref.shape[0]
    chunk = 16
    taps = [fw_ref[k : k + 1, :] for k in range(KERNEL)]
    bias = fb_ref[0:1, :]
    zero = jnp.zeros((HALO, SEQS, WIDE), f32)
    dv_scr[0:HALO] = zero
    dv_scr[steps + HALO :] = zero

    def step(i, sums):
        t = i * chunk
        x = mix_ref[pl.ds(t, chunk + HALO)].astype(f32)
        v = bias[None] + taps[0][None] * x[1 : 1 + chunk]
        for k in range(1, KERNEL):
            v = v + taps[k][None] * x[1 + k : 1 + k + chunk]
        sig = sigmoid(v)
        r = pl.multiple_of(t * SEQS, chunk * SEQS)
        more = contract_cols(projg_ref[pl.ds(r, chunk * SEQS), :], sel_ref[...])
        total = act_grad_ref[pl.ds(t, chunk)] + more.reshape(chunk, SEQS, WIDE)
        dv = total * (sig * (1.0 + v * (1.0 - sig)))
        dv_scr[pl.ds(t + HALO, chunk)] = dv
        new = [sums[0] + jnp.sum(dv, axis=0)]
        for k in range(KERNEL):
            new.append(sums[1 + k] + jnp.sum(dv * x[1 + k : 1 + k + chunk], axis=0))
        return tuple(new)

    sums = lax.fori_loop(
        0, steps // chunk, step, tuple(jnp.zeros((SEQS, WIDE), f32) for _ in range(KERNEL + 1))
    )
    fbg_ref[...] = jnp.sum(sums[0], axis=0, keepdims=True)
    for k in range(KERNEL):
        fwg_ref[k : k + 1, :] = jnp.sum(sums[1 + k], axis=0, keepdims=True)

    def spread(t, count):
        dv = dv_scr[pl.ds(t, count + HALO)]
        out = taps[KERNEL - 1][None] * dv[0:count]
        for k in range(KERNEL - 1):
            s = KERNEL - 1 - k
            out = out + taps[k][None] * dv[s : s + count]
        mixgrad_ref[pl.ds(t, count)] = out.astype(bf16)

    def out_step(i, _):
        spread(i * chunk, chunk)
        return 0

    lax.fori_loop(0, steps // chunk, out_step, 0)
    spread(steps, HALO)
    low = act_ref[...].reshape(steps * SEQS, WIDE).astype(bf16)
    selg_ref[...] = jnp.dot(projg_t_ref[...], low, preferred_element_type=f32)


def filter_back(mixture, act, act_grad, projg, projg_t, select_pad, fw, fb):
    steps, _, channels = act.shape
    grid = channels // WIDE
    wide = lambda j: (0, 0, j)
    whole = lambda j: (0, 0)
    cols = lambda j: (0, j)
    return pl.pallas_call(
        filter_back_kernel,
        grid=(grid,),
        in_specs=[
            pl.BlockSpec((steps + HALO, SEQS, WIDE), wide),
            pl.BlockSpec((steps, SEQS, WIDE), wide),
            pl.BlockSpec((steps, SEQS, WIDE), wide),
            pl.BlockSpec((steps * SEQS, LANES), whole),
            pl.BlockSpec((LANES, steps * SEQS), whole),
            pl.BlockSpec((WIDE, LANES), lambda j: (j, 0)),
            pl.BlockSpec((KERNEL, WIDE), cols),
            pl.BlockSpec((1, WIDE), cols),
        ],
        out_specs=[
            pl.BlockSpec((steps + HALO, SEQS, WIDE), wide),
            pl.BlockSpec((LANES, WIDE), cols),
            pl.BlockSpec((KERNEL, WIDE), cols),
            pl.BlockSpec((1, WIDE), cols),
        ],
        out_shape=[
            jax.ShapeDtypeStruct((steps + HALO, SEQS, channels), bf16),
            jax.ShapeDtypeStruct((LANES, channels), f32),
            jax.ShapeDtypeStruct((KERNEL, channels), f32),
            jax.ShapeDtypeStruct((1, channels), f32),
        ],
        scratch_shapes=[pltpu.VMEM((steps + 2 * HALO, SEQS, WIDE), f32)],
        compiler_params=params(),
        cost_estimate=cost(20),
        name="filter_back",
    )(mixture, act, act_grad, projg, projg_t, select_pad, fw, fb)


def send(src, dst, send_sem, recv_sem, peer, axis="fsdp"):
    return pltpu.make_async_remote_copy(
        src_ref=src,
        dst_ref=dst,
        send_sem=send_sem,
        recv_sem=recv_sem,
        device_id={axis: peer},
        device_id_type=pl.DeviceIdType.MESH,
    )


def greet(others):
    barrier = pltpu.get_barrier_semaphore()
    for axis, peer in others:
        pl.semaphore_signal(barrier, inc=1, device_id={axis: peer}, device_id_type=pl.DeviceIdType.MESH)
    pl.semaphore_wait(barrier, len(others))


def flipped(index, bit):
    return index + (1 - 2 * (index // bit % 2)) * bit


FIRST, SECOND = (0, 1, 2, 3), (4, 5)


def gather_kernel(
    rows_ref, select_ref, out_ref, in_ref, all_rows, all_select, all_out, all_in,
    local_sems, own_send, own_recv, pass_send, pass_recv, core_send, core_recv,
):
    me = lax.axis_index("fsdp")
    a, b = flipped(me, 2), flipped(me, 4)
    corner = flipped(a, 4)
    twin = flipped(me, 1)
    greet([("fsdp", a), ("fsdp", b), ("fsdp", twin)])
    kinds = ((rows_ref, all_rows), (select_ref, all_select), (out_ref, all_out), (in_ref, all_in))
    table = [(0, 0, 1), (1, 0, 1), (2, 0, 2), (3, 0, 2), (2, 1, 2), (3, 1, 2)]

    def place(owner, piece):
        kind, part, parts = table[piece]
        count = kinds[kind][0].shape[0]
        step = count // parts
        return kinds[kind][1].at[pl.ds(pl.multiple_of(owner * count + part * step, step), step)]

    def mine(piece):
        kind, part, parts = table[piece]
        step = kinds[kind][0].shape[0] // parts
        return kinds[kind][0].at[pl.ds(part * step, step)]

    started = []

    def start(copy):
        copy.start()
        started.append(copy)

    def own_copy(piece, k, peer, owner):
        return send(mine(piece), place(owner, piece), own_send.at[k, piece], own_recv.at[k, piece], peer)

    def pass_copy(piece, peer, owner):
        return send(place(owner, piece), place(owner, piece), pass_send.at[piece], pass_recv.at[piece], peer)

    def core_copy(piece, k, owner):
        src = mine(piece) if k == 0 else place(owner, piece)
        return send(src, place(owner, piece), core_send.at[k, piece], core_recv.at[k, piece], twin)

    for piece in FIRST + SECOND:
        start(own_copy(piece, 0, a, me))
    for piece in SECOND + FIRST:
        start(own_copy(piece, 1, b, me))
    local = []
    for piece in FIRST + SECOND:
        start(core_copy(piece, 0, me))
        copy = pltpu.make_async_copy(mine(piece), place(me, piece), local_sems.at[piece])
        copy.start()
        local.append(copy)

    def arrived(piece, k):
        owner = (a, b, corner)[k]
        if k == 2:
            pass_copy(piece, a, owner).wait_recv()
        else:
            own_copy(piece, k, a, owner).wait_recv()
            if k == 0 and piece in FIRST:
                start(pass_copy(piece, b, owner))
            if k == 1 and piece in SECOND:
                start(pass_copy(piece, a, owner))
        start(core_copy(piece, k + 1, owner))

    for piece, k in (
        (0, 0), (1, 0), (2, 0), (4, 1), (3, 0), (5, 1), (4, 0), (0, 1), (1, 1), (2, 1), (0, 2), (1, 2), (2, 2),
        (4, 2), (5, 0), (3, 1), (3, 2), (5, 2),
    ):
        arrived(piece, k)
    for k, owner in enumerate((twin, flipped(twin, 2), flipped(twin, 4), flipped(corner, 1))):
        for piece in FIRST + SECOND:
            core_copy(piece, k, owner).wait_recv()
    for copy in started:
        copy.wait_send()
    for copy in local:
        copy.wait()


def gather(*shards):
    size = lax.axis_size("fsdp")
    if size != 8:
        return [lax.all_gather(shard, "fsdp", axis=0, tiled=True) for shard in shards]
    vmem = pl.BlockSpec(memory_space=pltpu.VMEM)
    hbm = pl.BlockSpec(memory_space=pl.ANY)
    pieces = len(FIRST + SECOND)
    dma = pltpu.SemaphoreType.DMA
    return pl.pallas_call(
        gather_kernel,
        in_specs=[vmem] * 4,
        out_specs=[hbm] * 4,
        out_shape=[jax.ShapeDtypeStruct((size * shard.shape[0], shard.shape[1]), bf16) for shard in shards],
        scratch_shapes=[
            dma((pieces,)), dma((2, pieces)), dma((2, pieces)), dma((pieces,)), dma((pieces,)),
            dma((4, pieces)), dma((4, pieces)),
        ],
        compiler_params=params(collective_id=2, has_side_effects=True),
        cost_estimate=cost(55),
        name="gather",
    )(*shards)


SMALL = (KERNEL, 1, 1, 1, STATES, RANK, RANK + 2 * STATES, 1)
SMALL_ROWS = 192


def xor(index, bits):
    for bit in (1, 2, 4, 8):
        if bits & bit:
            index = flipped(index, bit)
    return index


def tail_kernel(
    one_hot_ref, b0, b1, b2, b3, filter_ref, fbias_ref, sbias_ref, skip_ref, decay_ref, step_ref, select_ref,
    gain_ref, halo_ref, *rest,
):
    depth = lax.axis_size("replica")
    early_refs, rest = rest[:depth], rest[depth:]
    (
        in_out, out_out, filter_out, fbias_out, sbias_out, skip_out, decay_out, step_out, select_out, gain_out,
        rim_out,
        total, to_z, from_z, part, parts, small_f, small_ref, got_small, small_z, small_from_z, small_part,
        small_parts, rim, child, got_rim, got_child, early,
        sems_s, sems_z, sems_p, sems_sz, sems_sp, sems_r, sems_cs, sems_cr,
    ) = rest
    me, size = lax.axis_index("fsdp"), lax.axis_size("fsdp")
    mz = lax.axis_index("replica")
    last = size - 1
    near = [lax.rem(me + d, size) for d in range(1, size)]
    far = [lax.rem(mz + d, depth) for d in range(1, depth)]
    greet([("fsdp", peer) for peer in near] + [("replica", peer) for peer in far])

    def spread(src, dst, sems, peers, axis, index):
        copies = []
        for d, peer in enumerate(peers):
            source = src.at[peer] if src.shape[0] == len(peers) + 1 and len(src.shape) == len(dst.shape) else src
            copy = send(source, dst.at[index], sems.at[0, d], sems.at[1, d], peer, axis)
            copy.start()
            copies.append(copy)
        return copies

    width = small_f.shape[2]
    small_f[...] = jnp.zeros_like(small_f)
    refs = (filter_ref, fbias_ref, sbias_ref, skip_ref, decay_ref, step_ref, select_ref)
    for k in range(size):
        at = 0
        for ref, count in zip(refs, SMALL):
            small_f[k, at : at + count] = ref[0:count, k * width : (k + 1) * width]
            at += count
        some = gain_ref.shape[1] // size
        small_f[k, at : at + 1, 0:some] = gain_ref[:, k * some : (k + 1) * some]
    small_ref[...] = small_f[...].astype(bf16)
    sequels = one_hot_ref.shape[0]
    pieces = (SEQS - PROMPTS) // sequels
    for t in range(HALO):
        rim[t * PROMPTS : (t + 1) * PROMPTS] = halo_ref[t, 0:PROMPTS]
        for p in range(PROMPTS):
            sums = None
            for q in range(sequels):
                row = PROMPTS + q * pieces
                term = one_hot_ref[q, p] * halo_ref[t, row : row + 1]
                sums = term if q == 0 else sums + term
            child[t * PROMPTS + p : t * PROMPTS + p + 1] = sums
    block = b0[...].astype(f32) + b1[...].astype(f32) + b2[...].astype(f32) + b3[...].astype(f32)
    total[...] = block.reshape(total.shape)
    to_z[...] = total[...].astype(bf16)
    to_left = send(rim, got_rim, sems_r.at[0], sems_r.at[1], lax.rem(me + last, size))
    to_left.start()

    @pl.when(me != last)
    def _():
        send(child, got_child.at[me], sems_cs.at[me], sems_cr.at[me], last).start()

    copies = spread(small_ref, got_small, sems_s, near, "fsdp", me)
    z_copies = spread(to_z, from_z, sems_z, far, "replica", mz)
    small = small_ref[me].astype(f32)
    got_small[me] = jnp.zeros(got_small.shape[1:], bf16)
    from_z[mz] = jnp.zeros(from_z.shape[1:], bf16)
    small_from_z[mz] = jnp.zeros(small_from_z.shape[1:], bf16)
    for copy in copies:
        copy.wait()
    for k in range(size):
        small = small + got_small[k].astype(f32)
    small_z[...] = small.reshape(small_z.shape)
    small_to_z = small_part
    small_to_z[...] = small_z[...].astype(bf16)
    s_copies = spread(small_to_z, small_from_z, sems_sz, far, "replica", mz)
    for copy in z_copies:
        copy.wait()
    own = total[mz]
    for k in range(depth):
        own = own + from_z[k].astype(f32)
    part[...] = own.astype(bf16)
    p_copies = spread(part, parts, sems_p, far, "replica", mz)
    parts[mz] = part[...]
    for copy in s_copies:
        copy.wait()
    own = small_z[mz]
    for k in range(depth):
        own = own + small_from_z[k].astype(f32)
    small_parts[mz] = own.astype(bf16)
    small_own = small_to_z.at[mz]
    small_own[...] = own.astype(bf16)
    q_copies = []
    for d, peer in enumerate(far):
        copy = send(small_own, small_parts.at[mz], sems_sp.at[0, d], sems_sp.at[1, d], peer, "replica")
        copy.start()
        q_copies.append(copy)
    for copy in p_copies + q_copies:
        copy.wait()
    half = in_out.shape[1] // 2
    in_out[:, 0:half] = parts[...].reshape(in_out.shape[0], half).astype(f32)
    small = small_parts[...].reshape(SMALL_ROWS, width).astype(f32)
    at = 0
    for out, count in zip(
        (filter_out, fbias_out, sbias_out, skip_out, decay_out, step_out, select_out, gain_out), SMALL
    ):
        out[...] = small[at : at + count, 0 : out.shape[1]]
        at += count
    for d, ref in enumerate(early_refs):
        count = ref.shape[0]
        total_rows = pl.ds(pl.multiple_of(xor(mz, d) * count, count), count)
        early[total_rows, :] = ref[...].astype(f32)
    rows = out_out.shape[0] // 2
    features = out_out.shape[1]
    out_out[0:rows, :] = early[0:rows, 0:features]
    out_out[rows:, :] = early[0:rows, features:]
    in_out[:, half:] = early[rows:, :]
    to_left.wait()

    @pl.when(me != last)
    def _():
        send(child, got_child.at[me], sems_cs.at[me], sems_cr.at[me], last).wait_send()
        rim_out[...] = got_rim[...]

    @pl.when(me == last)
    def _():
        sums = child[...]
        for k in range(size - 1):
            send(child, got_child.at[k], sems_cs.at[k], sems_cr.at[k], 0).wait_recv()
            sums = sums + got_child[k]
        rim_out[...] = sums


def tail(one_hot, blocks, small, halo_grad, early):
    size, depth = lax.axis_size("fsdp"), lax.axis_size("replica")
    vmem = pl.BlockSpec(memory_space=pltpu.VMEM)
    dma = pltpu.SemaphoreType.DMA
    while len(blocks) > 4:
        blocks = blocks[:3] + [summed(blocks[3], blocks[4:5]).astype(bf16)] + blocks[5:]
    rows, channels = blocks[0].shape
    features = small[-1].shape[1]
    width = channels // size
    cut = (depth, rows // depth, channels)
    by_owner = (size, SMALL_ROWS, width)
    small_cut = (depth, SMALL_ROWS // depth, width)
    rim = (HALO * PROMPTS, features)
    counts = [(count, width) for count in SMALL[:-1]] + [(1, features // size)]
    return pl.pallas_call(
        tail_kernel,
        in_specs=[pl.BlockSpec(memory_space=pltpu.SMEM)] + [vmem] * (4 + len(small) + 1 + depth),
        out_specs=[vmem] * (3 + len(counts)),
        out_shape=[
            jax.ShapeDtypeStruct(shape, f32)
            for shape in [(rows, 2 * channels), (2 * rows, features)] + counts + [rim]
        ],
        scratch_shapes=[
            pltpu.VMEM(cut, f32), pltpu.VMEM(cut, bf16), pltpu.VMEM(cut, bf16),
            pltpu.VMEM(cut[1:], bf16), pltpu.VMEM(cut, bf16),
            pltpu.VMEM(by_owner, f32), pltpu.VMEM(by_owner, bf16), pltpu.VMEM(by_owner, bf16),
            pltpu.VMEM(small_cut, f32), pltpu.VMEM(small_cut, bf16),
            pltpu.VMEM(small_cut, bf16), pltpu.VMEM(small_cut, bf16),
            pltpu.VMEM(rim, f32), pltpu.VMEM(rim, f32), pltpu.VMEM(rim, f32), pltpu.VMEM((size,) + rim, f32),
            pltpu.VMEM((2 * rows, channels), f32),
            dma((2, size)), dma((2, depth)), dma((2, depth)), dma((2, depth)), dma((2, depth)),
            dma((2,)), dma((size,)), dma((size,)),
        ],
        compiler_params=params(collective_id=4, has_side_effects=True),
        cost_estimate=cost(30),
        name="tail",
    )(one_hot, *blocks, *small, halo_grad, *early)


def contract_rows(left_side, right_side):
    return lax.dot_general(
        left_side, right_side, (((0,), (0,)), ((), ())), preferred_element_type=f32
    )


def contract_cols(left_side, right_side):
    return lax.dot_general(
        left_side, right_side, (((1,), (1,)), ((), ())), preferred_element_type=f32
    )


def exchanged(block, axis, distance):
    return lax.ppermute(block, axis, [(i, i ^ distance) for i in range(lax.axis_size(axis))])


def pick_row(block, index, axis=0):
    return lax.dynamic_index_in_dim(block, index, axis, keepdims=False)


def over_cores(blocks):
    blocks = blocks.reshape((-1, 2) + blocks.shape[1:])
    core = lax.axis_index("fsdp") % 2
    got = exchanged(pick_row(blocks, 1 - core, 1), "fsdp", 1)
    return (pick_row(blocks, core, 1).astype(f32) + got.astype(f32)).astype(bf16)


def to_chips(blocks):
    chip = lax.axis_index("fsdp") // 2
    got = [exchanged(pick_row(blocks, chip ^ d), "fsdp", 2 * d) for d in range(1, blocks.shape[0])]
    return pick_row(blocks, chip), got


def summed(own, got):
    total = own.astype(f32)
    for block in got:
        total = total + block.astype(f32)
    return total


def to_replicas(block):
    size, here = lax.axis_size("replica"), lax.axis_index("replica")
    parts = block.astype(bf16).reshape((size, -1) + block.shape[1:])
    own = pick_row(block.reshape(parts.shape), here)
    return own, [exchanged(pick_row(parts, here ^ d), "replica", d) for d in range(1, size)]


def from_replicas(part):
    return [part] + [exchanged(part, "replica", d) for d in range(1, lax.axis_size("replica"))]


def joined(parts):
    here = lax.axis_index("replica")
    parts = jnp.stack(parts)
    return jnp.concatenate([pick_row(parts, here ^ i) for i in range(parts.shape[0])]).astype(f32)


def body(
    prompt_hidden, sequel_hidden, parents, prompt_cotangent, sequel_cotangent,
    norm_gain, input_weight, filter_weight, depthwise_filter_bias, select_weight,
    step_weight, step_bias, decay_log, skip_gain, output_weight,
):
    size, here = lax.axis_size("fsdp"), lax.axis_index("fsdp")
    prompts, steps = prompt_hidden.shape[:2]
    sequels, sequel_len = sequel_hidden.shape[:2]
    split = sequel_len // steps
    assert prompts == PROMPTS and sequels * split == SEQS - prompts
    rim = KERNEL - 1
    half = SEQS // 2
    rows = steps * SEQS

    after = lax.optimization_barrier
    width = step_bias.shape[0]
    tail_rows = prompt_hidden[:, steps - rim :]
    shard = jnp.concatenate(
        [
            step_weight,
            tail_rows.reshape(-1, width),
            filter_weight,
            depthwise_filter_bias[None],
            step_bias[None],
            skip_gain[None],
            jnp.pad(norm_gain, (0, width - norm_gain.shape[0]))[None],
        ],
        axis=0,
    )
    shard = jnp.pad(shard, ((0, -shard.shape[0] % 16), (0, 0)))
    lanes = jnp.concatenate([select_weight, decay_log], axis=1)
    lanes = jnp.pad(lanes, ((0, 0), (0, LANES - lanes.shape[1])))
    every, select_pad, full_output, full_input = gather(shard, lanes, output_weight, input_weight)
    every = every.reshape(size, shard.shape[0], width)
    at = RANK + tail_rows.size // width
    tails = every[:, RANK:at].reshape((size,) + tail_rows.shape)
    step_full = jnp.swapaxes(every[:, :RANK], 0, 1).reshape(RANK, -1)
    vectors = jnp.swapaxes(every[:, at : at + SEQS], 0, 1).astype(f32)
    gain = vectors[KERNEL + 3, :, : norm_gain.shape[0]].reshape(1, -1)
    vectors = vectors.reshape(SEQS, -1)
    fw, fb, sbias, skip = vectors[:KERNEL], vectors[4:5], vectors[5:6], vectors[6:7]
    first = RANK + 2 * STATES
    rate = -jnp.exp(select_pad[:, first : first + STATES].T.astype(f32)) * LOG2E
    step_pad = jnp.pad(step_full, ((0, LANES - RANK), (0, 0)))

    before = jnp.where(here > 0, tails[jnp.maximum(here - 1, 0)], jnp.zeros_like(tails[0]))
    cut = sequel_hidden.reshape(sequels, split, steps, D)
    inner = jnp.concatenate([tails[size - 1][parents][:, None], cut[:, :-1, steps - rim :]], axis=1)
    halo = jnp.concatenate([before, inner.reshape(-1, rim, D)], axis=0)
    halo = jnp.pad(jnp.swapaxes(halo, 0, 1), ((HALO - rim, 0), (0, 0), (0, 0))).reshape(-1, D).astype(f32)
    pieces = sequel_hidden.reshape(-1, steps, D)
    piece_cot = sequel_cotangent.reshape(-1, steps, D)
    scaled, cotangent = prepare(prompt_hidden, pieces, prompt_cotangent, piece_cot, halo, gain)

    mixture = jnp.dot(scaled, full_input[:, :INNER], preferred_element_type=f32).astype(bf16)
    gate = jnp.dot(scaled, full_input[:, INNER:], preferred_element_type=f32)
    mixture = mixture.reshape(steps + HALO, SEQS, INNER)
    gate = gate.reshape(steps + HALO, SEQS, INNER)
    gated_grad = contract_cols(cotangent, full_output).reshape(steps, SEQS, INNER)
    act, proj = front(mixture, fw, fb, select_pad, steps)
    groups = 1 if split == 1 else 2
    lane = jnp.arange(2 * STATES * LANES)[None, :]
    select = (jnp.arange(LANES)[:, None] == RANK + lane // LANES).astype(bf16)
    dt, sig, yg, silu, slope, ahead, behind, total = piece(
        proj, act, gate, gated_grad, step_pad, sbias, rate, select, groups
    )

    one_hot = (parents[:, None] == jnp.arange(PROMPTS, dtype=jnp.int32)[None, :]).astype(f32)
    own = total[half:].reshape(sequels, split, 1, INNER)
    own_behind = behind[half:].reshape(sequels, split, STATES, INNER)
    back = own_behind[:, split - 1]
    own_end = [jnp.zeros_like(back)]
    for p in range(split - 2, -1, -1):
        own_end.insert(0, back)
        back = own_behind[:, p] + jnp.exp2(rate * own[:, p]) * back
    start, end = chain(one_hot, ahead[:half], behind[:half], back, total, rate)
    if split > 1:
        state = start[half:]
        own_start = [state]
        for p in range(split - 1):
            state = jnp.exp2(rate * own[:, p]) * state + ahead[half:].reshape(own_behind.shape)[:, p]
            own_start.append(state)
        own_start = jnp.stack(own_start, axis=1).reshape(half, STATES, INNER)
        start = jnp.concatenate([start[:half], own_start], axis=0)
        end = jnp.concatenate([end[:half], jnp.stack(own_end, axis=1).reshape(half, STATES, INNER)], axis=0)

    gated, hist, gate_grad, skip_grad = forward(
        proj, dt, act, yg, silu, slope, rate, start, skip, select
    )
    gated = gated.reshape(rows, INNER)
    gate_grad = gate_grad.reshape(-1, INNER)
    output_grad = contract_rows(gated, cotangent).astype(bf16).reshape(size, -1, D)
    gate_weight_grad = contract_rows(scaled, gate_grad).astype(bf16)
    early = [over_cores(output_grad), over_cores(gate_weight_grad.reshape(size, -1, INNER))]
    wide = jnp.concatenate([early[0][:, : INNER // size // 2], early[0][:, INNER // size // 2 :]], axis=2)
    early = jnp.concatenate([wide, early[1]], axis=1)
    end, early = after((end, early))
    early = to_chips(early)

    rank_t = proj[:, :RANK].astype(bf16).T
    lane = jnp.arange(LANES)[None, None, :]
    which = jnp.arange(PAIRS)[:, None, None]
    source = jnp.arange(2 * LANES)[None, :, None]
    pick = (lane // 2 == jnp.where(source < LANES, RANK, RANK + STATES) // 2 + which).astype(bf16)
    act_grad, step_grad, bias_grad, decay_grad, projg = backward(
        proj, dt, sig, act, yg, rate, end, skip, hist, rank_t, step_pad.T, pick, select
    )
    projg, early = after((projg, early))
    early = summed(*early)
    projg, early = after((projg, early))
    early = to_replicas(early)
    filter_in_grad, select_grad, filter_grad, filter_bias_grad = filter_back(
        mixture, act, act_grad, projg, projg.T, select_pad, fw, fb
    )
    filter_in_grad, early = after((filter_in_grad, early))
    early = summed(*early).astype(bf16)
    filter_in_grad = filter_in_grad.reshape(-1, INNER)
    filter_weight_grad = contract_rows(scaled, filter_in_grad).astype(bf16)
    filter_weight_grad, early = after((filter_weight_grad, early))
    late = over_cores(filter_weight_grad.reshape(size, -1, INNER))
    early = from_replicas(early)
    more = contract_cols(gate_grad, full_input[:, INNER:])
    late, more, filter_in_grad, gated = after((late, more, filter_in_grad, gated))
    own_block, late = to_chips(late)
    scaled_grad = contract_cols(filter_in_grad, full_input[:, :INNER])
    mixed = jnp.dot(gated, full_output, preferred_element_type=f32)
    prompt_out, piece_out, prompt_grad, piece_grad, halo_grad, gain_grad = finish(
        mixed, scaled_grad, more, prompt_hidden, pieces, prompt_cotangent, piece_cot, halo, gain
    )
    halo_grad, own_block, late = after((halo_grad, own_block, late))
    halo_grad = halo_grad.reshape(HALO, SEQS, D)
    small = [
        filter_grad, filter_bias_grad, bias_grad, skip_grad, decay_grad, step_grad, select_grad, gain_grad,
    ]
    (
        input_grad, output_grad, g_filter, g_fbias, g_sbias, g_skip, g_decay, g_step, g_select, g_gain, following,
    ) = tail(one_hot, [own_block] + late, small, halo_grad, early)
    following = jnp.swapaxes(following.reshape(HALO, half, D), 0, 1)
    prompt_grad = prompt_grad.at[:, steps - HALO :].add(following)
    if split > 1:
        own = jnp.swapaxes(halo_grad[:, half:], 0, 1).reshape(sequels, split, HALO, D)
        own = jnp.pad(own[:, 1:], ((0, 0), (0, 1), (0, 0), (0, 0))).reshape(half, HALO, D)
        piece_grad = piece_grad.at[:, steps - HALO :].add(own)
    return (
        prompt_out,
        piece_out.reshape(sequel_hidden.shape),
        prompt_grad,
        piece_grad.reshape(sequel_hidden.shape),
        g_gain[0],
        input_grad,
        g_filter,
        g_fbias[0],
        g_select.T,
        g_step,
        g_sbias[0],
        g_decay.T,
        g_skip[0],
        output_grad,
    )


def solution(mesh):
    rows = P("replica", "fsdp", None)
    own = P(("replica", "fsdp"), None, None)
    return jax.shard_map(
        body,
        mesh=mesh,
        in_specs=(
            rows, own, P(("replica", "fsdp")), rows, own,
            P("fsdp"), P("fsdp", None), P(None, "fsdp"), P("fsdp"), P("fsdp", None),
            P(None, "fsdp"), P("fsdp"), P("fsdp", None), P("fsdp"), P("fsdp", None),
        ),
        out_specs=(
            rows, own, rows, own,
            P("fsdp"), P("fsdp", None), P(None, "fsdp"), P("fsdp"), P("fsdp", None),
            P(None, "fsdp"), P("fsdp"), P("fsdp", None), P("fsdp"), P("fsdp", None),
        ),
        check_vma=False,
    )
```

```python
import functools
import math

import jax
import jax.numpy as jnp
from jax import lax
from jax.experimental import pallas as pl
from jax.experimental.pallas import tpu as pltpu
from jax.sharding import PartitionSpec as P

D = 1024
INNER = 2048
STATES = 16
RANK = 64
KERNEL = 4
PROMPTS = 4

SEQS = 8
HALO = 4
LANES = 128
WIDE = 256
LOG2E = math.log2(math.e)
LN2 = math.log(2.0)
f32 = jnp.float32
bf16 = jnp.bfloat16

VMEM_LIMIT = 62 * 1024 * 1024


def cost(microseconds):
    return pl.CostEstimate(flops=int(microseconds * 1e9), bytes_accessed=0, transcendentals=0)


def params(**kw):
    return pltpu.CompilerParams(vmem_limit_bytes=VMEM_LIMIT, **kw)


def sigmoid(x):
    return 1.0 / (1.0 + jnp.exp(-x))


def softplus(x):
    return jnp.maximum(x, 0.0) + jnp.log1p(jnp.exp(-jnp.abs(x)))


def product_kernel(across, *refs):
    lefts, rhs_ref, out_ref = refs[:-2], refs[-2], refs[-1]
    total = None
    at = 0
    for left in lefts:
        depth = left.shape[1]
        rhs = rhs_ref[:, at : at + depth] if across else rhs_ref[at : at + depth]
        dims = (((1,), (1 if across else 0,)), ((), ()))
        term = lax.dot_general(left[...], rhs, dims, preferred_element_type=f32)
        total = term if total is None else total + term
        at += depth
    out_ref[...] = total.astype(out_ref.dtype)


def product(lefts, rhs, kind, across=False, part=0, parts=1):
    rows = lefts[0].shape[0]
    depth = sum(left.shape[1] for left in lefts)
    if across:
        columns = rhs.shape[0]
        rhs_spec = pl.BlockSpec((WIDE, depth), lambda j: (j, 0))
    else:
        columns = rhs.shape[1] // parts
        first = part * columns // WIDE
        rhs_spec = pl.BlockSpec((depth, WIDE), lambda j: (0, first + j))
    return pl.pallas_call(
        functools.partial(product_kernel, across),
        grid=(columns // WIDE,),
        in_specs=[pl.BlockSpec(left.shape, lambda j: (0, 0)) for left in lefts] + [rhs_spec],
        out_specs=pl.BlockSpec((rows, WIDE), lambda j: (0, j)),
        out_shape=jax.ShapeDtypeStruct((rows, columns), kind),
        compiler_params=params(),
        cost_estimate=cost(0.01),
        name="product",
    )(*lefts, rhs)


def scale_of(rows):
    return lax.rsqrt(jnp.mean(rows * rows, axis=-1, keepdims=True) + 1e-05)


def by_time(prompt_ref, piece_ref):
    both_kinds = jnp.concatenate([prompt_ref[...], piece_ref[...]], axis=0).astype(f32)
    return jnp.swapaxes(both_kinds, 0, 1)


def prepare_kernel(prompt_ref, piece_ref, prompt_cot_ref, piece_cot_ref, halo_ref, gain_ref, scaled_ref, cot_ref):
    i = pl.program_id(0)
    gain = gain_ref[...]

    @pl.when(i == 0)
    def _():
        rows = halo_ref[...]
        scaled_ref[0 : HALO * SEQS, :] = (rows * scale_of(rows) * gain).astype(bf16)

    rows = by_time(prompt_ref, piece_ref)
    count = rows.shape[0] * SEQS
    rows = rows.reshape(count, D)
    at = pl.multiple_of(HALO * SEQS + i * count, HALO * SEQS)
    scaled_ref[pl.ds(at, count), :] = (rows * scale_of(rows) * gain).astype(bf16)
    cot_ref[...] = by_time(prompt_cot_ref, piece_cot_ref).reshape(count, D).astype(bf16)


CHUNK = 16


def prepare(prompt, piece, prompt_cot, piece_cot, halo, gain):
    steps = prompt.shape[1]
    part = pl.BlockSpec((SEQS // 2, CHUNK, D), lambda i: (0, i, 0))
    rows = steps * SEQS
    return pl.pallas_call(
        prepare_kernel,
        grid=(steps // CHUNK,),
        in_specs=[
            part, part, part, part,
            pl.BlockSpec((HALO * SEQS, D), lambda i: (0, 0)),
            pl.BlockSpec((1, D), lambda i: (0, 0)),
        ],
        out_specs=[
            pl.BlockSpec((HALO * SEQS + rows, D), lambda i: (0, 0)),
            pl.BlockSpec((CHUNK * SEQS, D), lambda i: (i, 0)),
        ],
        out_shape=[
            jax.ShapeDtypeStruct((HALO * SEQS + rows, D), bf16),
            jax.ShapeDtypeStruct((rows, D), bf16),
        ],
        compiler_params=params(),
        cost_estimate=cost(5),
        name="prepare",
    )(prompt, piece, prompt_cot, piece_cot, halo, gain)


def norm_back(rows, scaled_grad, gain):
    inverse = scale_of(rows)
    unit = rows * inverse
    grad = scaled_grad * gain
    back = inverse * (grad - unit * jnp.mean(grad * unit, axis=-1, keepdims=True))
    return back, scaled_grad * unit


def finish_kernel(
    mixed_ref, grad_ref, grad_halo_ref,
    prompt_ref, piece_ref, prompt_cot_ref, piece_cot_ref, halo_ref, gain_ref,
    prompt_out, piece_out, prompt_grad, piece_grad, halo_grad, gain_grad,
):
    i = pl.program_id(0)
    gain = gain_ref[...]

    @pl.when(i == 0)
    def _():
        back, sums = norm_back(halo_ref[...], grad_halo_ref[...], gain)
        halo_grad[...] = back
        gain_grad[...] = jnp.sum(sums, axis=0, keepdims=True)

    half = SEQS // 2
    rows = by_time(prompt_ref, piece_ref)
    shape = rows.shape
    rows = rows.reshape(-1, D)
    back, sums = norm_back(rows, grad_ref[...], gain)
    gain_grad[...] += jnp.sum(sums, axis=0, keepdims=True)
    back = jnp.swapaxes(back.reshape(shape), 0, 1)
    prompt_grad[...] = back[:half] + prompt_cot_ref[...].astype(f32)
    piece_grad[...] = back[half:] + piece_cot_ref[...].astype(f32)
    mixed = jnp.swapaxes((mixed_ref[...] + rows).reshape(shape), 0, 1)
    prompt_out[...] = mixed[:half].astype(bf16)
    piece_out[...] = mixed[half:].astype(bf16)


def finish(mixed, grad, prompt, piece, prompt_cot, piece_cot, halo, gain):
    steps = prompt.shape[1]
    part = pl.BlockSpec((SEQS // 2, CHUNK, D), lambda i: (0, i, 0))
    first = pl.BlockSpec((HALO * SEQS, D), lambda i: (0, 0))
    shifted = pl.BlockSpec(
        (pl.Element(CHUNK * SEQS), pl.Element(D)),
        lambda i: (pl.multiple_of(HALO * SEQS + i * (CHUNK * SEQS), HALO * SEQS), 0),
    )
    return pl.pallas_call(
        finish_kernel,
        grid=(steps // CHUNK,),
        in_specs=[
            pl.BlockSpec((CHUNK * SEQS, D), lambda i: (i, 0)),
            shifted, first,
            part, part, part, part,
            first,
            pl.BlockSpec((1, D), lambda i: (0, 0)),
        ],
        out_specs=[part, part, part, part, first, pl.BlockSpec((1, D), lambda i: (0, 0))],
        out_shape=[
            jax.ShapeDtypeStruct(prompt.shape, bf16),
            jax.ShapeDtypeStruct(piece.shape, bf16),
            jax.ShapeDtypeStruct(prompt.shape, f32),
            jax.ShapeDtypeStruct(piece.shape, f32),
            jax.ShapeDtypeStruct((HALO * SEQS, D), f32),
            jax.ShapeDtypeStruct((1, D), f32),
        ],
        compiler_params=params(),
        cost_estimate=cost(0.01),
        name="finish",
    )(mixed, grad, grad, prompt, piece, prompt_cot, piece_cot, halo, gain)


def front_kernel(mix_ref, fw_ref, fb_ref, sel_ref, act_ref, proj_ref):
    j = pl.program_id(0)
    steps = act_ref.shape[0]
    chunk = 16
    taps = [fw_ref[k : k + 1, :] for k in range(KERNEL)]
    bias = fb_ref[0:1, :]

    @pl.when(j == 0)
    def _():
        proj_ref[...] = jnp.zeros_like(proj_ref)

    def step(i, _):
        t = i * chunk
        x = mix_ref[pl.ds(t, chunk + HALO)].astype(f32)
        v = bias[None] + taps[0][None] * x[1 : 1 + chunk]
        for k in range(1, KERNEL):
            v = v + taps[k][None] * x[1 + k : 1 + k + chunk]
        act = v * sigmoid(v)
        act_ref[pl.ds(t, chunk)] = act
        low = act.reshape(chunk * SEQS, act.shape[-1]).astype(bf16)
        r = pl.multiple_of(t * SEQS, chunk * SEQS)
        proj_ref[pl.ds(r, chunk * SEQS), :] += jnp.dot(low, sel_ref[...], preferred_element_type=f32)
        return 0

    lax.fori_loop(0, steps // chunk, step, 0)


def front(mixture, fw, fb, select_pad, steps):
    channels = fw.shape[1]
    return pl.pallas_call(
        front_kernel,
        grid=(channels // WIDE,),
        in_specs=[
            pl.BlockSpec((steps + HALO, SEQS, WIDE), lambda j: (0, 0, j)),
            pl.BlockSpec((KERNEL, WIDE), lambda j: (0, j)),
            pl.BlockSpec((1, WIDE), lambda j: (0, j)),
            pl.BlockSpec((WIDE, LANES), lambda j: (j, 0)),
        ],
        out_specs=[
            pl.BlockSpec((steps, SEQS, WIDE), lambda j: (0, 0, j)),
            pl.BlockSpec((steps * SEQS, LANES), lambda j: (0, 0)),
        ],
        out_shape=[
            jax.ShapeDtypeStruct((steps, SEQS, channels), f32),
            jax.ShapeDtypeStruct((steps * SEQS, LANES), f32),
        ],
        compiler_params=params(),
        cost_estimate=cost(16),
        name="front",
    )(mixture, fw, fb, select_pad)


def pair(a, b):
    return jnp.concatenate([a, b], axis=0).astype(bf16)


def both(v):
    return pair(v, v)


def halves(v):
    v = v.astype(f32)
    return v[:SEQS], v[SEQS:]


def folded(v):
    a, b = halves(v)
    return a + b


def spread_maps(proj_ref, select_ref, first, count, store):
    steps = proj_ref.shape[0] // SEQS
    chunk = 32

    def step(i, _):
        r = pl.multiple_of(i * chunk * SEQS, chunk * SEQS)
        rows = proj_ref[pl.ds(r, chunk * SEQS), :].astype(bf16)
        for n in range(0, count, 2):
            at = (first - RANK + n) * LANES
            wide = jnp.dot(rows, select_ref[:, at : at + 2 * LANES], preferred_element_type=f32)
            wide = wide.reshape(chunk, SEQS, 2 * LANES)
            store(i * chunk, chunk, n, wide[:, :, :LANES], wide[:, :, LANES:])
        return 0

    lax.fori_loop(0, steps // chunk, step, 0)


def store_plain(ref):
    def store(t, count, n, a, b):
        ref[pl.ds(t, count), n] = a
        ref[pl.ds(t, count), n + 1] = b

    return store


def store_pairs(ref):
    def store(t, count, n, a, b):
        ref[pl.ds(t, count), n // 2] = jnp.concatenate([a, b], axis=1).astype(bf16)

    return store


PAIRS = STATES // 2
RUN = 8


def piece_kernel(
    proj_ref, act_ref, gate_ref, gg_ref, stepw_ref, sbias_ref, rate_ref, select_ref,
    dt_ref, sig_ref, yg_ref, silu_ref, slope_ref, fwd_ref, bwd_ref, tot_ref,
    b_scr, c_scr, time_scr, acc_scr,
):
    j = pl.program_id(0)
    steps = dt_ref.shape[0]
    half = SEQS // 2
    groups = fwd_ref.shape[0] // half

    @pl.when(j == 0)
    def _():
        def store_groups(t, count, n, a, b):
            for group in range(groups):
                rows = slice(group * half, (group + 1) * half)
                parts = [a[:, rows], a[:, rows], b[:, rows], b[:, rows]]
                b_scr[group, pl.ds(t, count), n // 2] = jnp.concatenate(parts, axis=1).astype(bf16)

        spread_maps(proj_ref, select_ref, RANK, STATES, store_groups)
        spread_maps(proj_ref, select_ref, RANK + STATES, STATES, store_pairs(c_scr))

    chunk = 8
    sbias = sbias_ref[0:1, :]

    def prep(i, total):
        t = i * chunk
        r = pl.multiple_of(t * SEQS, chunk * SEQS)
        rank = proj_ref[pl.ds(r, chunk * SEQS), :].astype(bf16)
        pre = jnp.dot(rank, stepw_ref[...], preferred_element_type=f32).reshape(chunk, SEQS, WIDE)
        pre = pre + sbias[None]
        small = jnp.exp2(jnp.abs(pre) * -LOG2E)
        one = 1.0 + small
        inverse = 1.0 / one
        dt = jnp.maximum(pre, 0.0) + (jnp.log(one) + (small - (one - 1.0)) * inverse)
        dt_ref[pl.ds(t, chunk)] = dt
        sig_ref[pl.ds(t, chunk)] = jnp.where(pre >= 0.0, inverse, small * inverse).astype(bf16)
        gate = gate_ref[pl.ds(t + HALO, chunk)]
        gg = gg_ref[pl.ds(t, chunk)]
        sig = sigmoid(gate)
        silu = gate * sig
        yg_ref[pl.ds(t, chunk)] = gg * silu
        silu_ref[pl.ds(t, chunk)] = silu.astype(bf16)
        slope_ref[pl.ds(t, chunk)] = (gg * (sig + silu * (1.0 - sig))).astype(bf16)
        for k in range(chunk):
            total = total + dt[k]
            time_scr[t + k] = total
        return total

    total = lax.fori_loop(0, steps // chunk, prep, jnp.zeros((SEQS, WIDE), f32))
    tot_ref[...] = total

    units = []

    low = lax.broadcasted_iota(jnp.int32, (SEQS, LANES), 0) < half
    packed = [
        jnp.where(low, rate_ref[n : n + 1, :LANES], rate_ref[n : n + 1, LANES:])
        for n in range(STATES)
    ]
    packed = [pair(packed[2 * p], packed[2 * p + 1]) for p in range(PAIRS)]

    def forward_unit(group):
        rows = slice(group * half, (group + 1) * half)

        def pack(v):
            return jnp.concatenate([v[rows, :LANES], v[rows, LANES:]], axis=0)

        whole = pack(total)

        def vectors(t):
            return both(whole - pack(time_scr[t])), both(pack(dt_ref[t] * act_ref[t]))

        def out(n, value):
            fwd_ref[rows, n, :LANES] = value[:half]
            fwd_ref[rows, n, LANES:] = value[half:]

        return packed, vectors, lambda t, p: b_scr[group, t, p], out

    def backward_unit(cols):
        mine = [jnp.broadcast_to(rate_ref[n : n + 1, cols], (SEQS, LANES)) for n in range(STATES)]
        mine = [pair(mine[2 * p], mine[2 * p + 1]) for p in range(PAIRS)]

        def vectors(t):
            return both(time_scr[t, :, cols]), both(yg_ref[t, :, cols])

        def out(n, value):
            bwd_ref[:, n, cols] = value

        return mine, vectors, lambda t, p: c_scr[t, p], out

    for group in range(groups):
        units.append(forward_unit(group))
    for part in range(WIDE // LANES):
        units.append(backward_unit(slice(part * LANES, (part + 1) * LANES)))
    acc_scr[...] = jnp.zeros_like(acc_scr)

    def run(i, _):
        for k, (rates, vectors, map_at, _) in enumerate(units):
            sums = [None] * PAIRS
            for m in range(RUN):
                t = i * RUN + m
                time, drive = vectors(t)
                for p in range(PAIRS):
                    term = jnp.exp2(time * rates[p]) * drive * map_at(t, p)
                    sums[p] = term if m == 0 else sums[p] + term
            for p in range(PAIRS):
                a, b = halves(sums[p])
                acc_scr[k, 2 * p] += a
                acc_scr[k, 2 * p + 1] += b
        return 0

    lax.fori_loop(0, steps // RUN, run, 0)
    for k, (_, _, _, out) in enumerate(units):
        for n in range(STATES):
            out(n, acc_scr[k, n])


def piece(proj, act, gate, gated_grad, step_pad, sbias, rate, select, groups):
    steps, _, channels = act.shape
    grid = channels // WIDE
    wide = lambda j: (0, 0, j)
    flat = pl.BlockSpec((steps, SEQS, WIDE), wide)
    shape = (steps, SEQS, channels)
    return pl.pallas_call(
        piece_kernel,
        grid=(grid,),
        in_specs=[
            pl.BlockSpec((steps * SEQS, LANES), lambda j: (0, 0)),
            flat,
            pl.BlockSpec((steps + HALO, SEQS, WIDE), wide),
            flat,
            pl.BlockSpec((LANES, WIDE), lambda j: (0, j)),
            pl.BlockSpec((1, WIDE), lambda j: (0, j)),
            pl.BlockSpec((STATES, WIDE), lambda j: (0, j)),
            pl.BlockSpec(select.shape, lambda j: (0, 0)),
        ],
        out_specs=[
            flat, flat, flat, flat, flat,
            pl.BlockSpec((groups * SEQS // 2, STATES, WIDE), wide),
            pl.BlockSpec((SEQS, STATES, WIDE), wide),
            pl.BlockSpec((SEQS, WIDE), lambda j: (0, j)),
        ],
        out_shape=[
            jax.ShapeDtypeStruct(shape, f32),
            jax.ShapeDtypeStruct(shape, bf16),
            jax.ShapeDtypeStruct(shape, f32),
            jax.ShapeDtypeStruct(shape, bf16),
            jax.ShapeDtypeStruct(shape, bf16),
            jax.ShapeDtypeStruct((groups * SEQS // 2, STATES, channels), f32),
            jax.ShapeDtypeStruct((SEQS, STATES, channels), f32),
            jax.ShapeDtypeStruct((SEQS, channels), f32),
        ],
        scratch_shapes=[
            pltpu.VMEM((groups, steps, PAIRS, 2 * SEQS, LANES), bf16),
            pltpu.VMEM((steps, PAIRS, 2 * SEQS, LANES), bf16),
            pltpu.VMEM((steps, SEQS, WIDE), f32),
            pltpu.VMEM((groups + WIDE // LANES, STATES, SEQS, LANES), f32),
        ],
        compiler_params=params(),
        cost_estimate=cost(60),
        name="piece",
    )(proj, act, gate, gated_grad, step_pad, sbias, rate, select)


def chain_kernel(
    one_hot_ref, ahead_ref, behind_ref, branch_ref, time_ref, rate_ref, start_out, end_out,
    moved_ref, got, got_time, back, done, sems, time_sems, back_sems,
):
    size = got.shape[0]
    width = got.shape[2]
    count = PROMPTS * STATES
    sequels = branch_ref.shape[0]
    me = lax.axis_index("fsdp")
    for p in range(PROMPTS):
        rows = slice(p * STATES, (p + 1) * STATES)
        total = one_hot_ref[0, p] * branch_ref[0]
        for k in range(1, sequels):
            total = total + one_hot_ref[k, p] * branch_ref[k]
        moved_ref[0 * count + p * STATES : 0 * count + (p + 1) * STATES] = ahead_ref[p].astype(bf16)
        moved_ref[1 * count + p * STATES : 1 * count + (p + 1) * STATES] = behind_ref[p].astype(bf16)
        moved_ref[2 * count + p * STATES : 2 * count + (p + 1) * STATES] = total.astype(bf16)
    barrier = pltpu.get_barrier_semaphore()
    for d in range(1, size):
        peer = lax.rem(me + d, size)
        pl.semaphore_signal(barrier, inc=1, device_id={"fsdp": peer}, device_id_type=pl.DeviceIdType.MESH)
    pl.semaphore_wait(barrier, size - 1)

    def columns(device):
        return pl.ds(pl.multiple_of(device * width, width), width)

    copies = []
    for d in range(1, size):
        peer = lax.rem(me + d, size)
        for src, dst, sem in ((moved_ref, got, sems), (time_ref, got_time, time_sems)):
            copy = pltpu.make_async_remote_copy(
                src_ref=src.at[:, columns(peer)],
                dst_ref=dst.at[me],
                send_sem=sem.at[0, d],
                recv_sem=sem.at[1, d],
                device_id={"fsdp": peer},
                device_id_type=pl.DeviceIdType.MESH,
            )
            copy.start()
            copies.append(copy)
    got[me] = moved_ref[:, columns(me)]
    got_time[me] = time_ref[:, columns(me)]
    for copy in copies:
        copy.wait()

    rate = jnp.concatenate([rate_ref[...]] * PROMPTS, axis=0)
    branch = jnp.zeros((count, width), f32)
    state = jnp.zeros((count, width), f32)
    decays = []
    for k in range(size):
        time = jnp.concatenate(
            [jnp.broadcast_to(got_time[k, p : p + 1, :], (STATES, width)) for p in range(PROMPTS)], axis=0
        )
        decays.append(jnp.exp2(rate * time))
        back[k, 0:count] = state.astype(bf16)
        state = decays[k] * state + got[k, 0:count].astype(f32)
        branch = branch + got[k, 2 * count : 3 * count].astype(f32)
    grad = branch
    for k in range(size - 1, -1, -1):
        back[k, count : 2 * count] = grad.astype(bf16)
        grad = decays[k] * grad + got[k, count : 2 * count].astype(f32)
    last = state.astype(bf16)
    for k in range(size):
        back[k, 2 * count : 3 * count] = last
    copies = []
    for d in range(1, size):
        peer = lax.rem(me + d, size)
        copy = pltpu.make_async_remote_copy(
            src_ref=back.at[peer],
            dst_ref=done.at[me],
            send_sem=back_sems.at[0, d],
            recv_sem=back_sems.at[1, d],
            device_id={"fsdp": peer},
            device_id_type=pl.DeviceIdType.MESH,
        )
        copy.start()
        copies.append(copy)
    done[me] = back[me]
    for copy in copies:
        copy.wait()
    for k in range(size):
        columns_k = slice(k * width, (k + 1) * width)
        last = []
        for p in range(PROMPTS):
            rows = slice(p * STATES, (p + 1) * STATES)
            start_out[p, :, columns_k] = done[k, rows].astype(f32)
            rows = slice(count + p * STATES, count + (p + 1) * STATES)
            end_out[p, :, columns_k] = done[k, rows].astype(f32)
            rows = slice(2 * count + p * STATES, 2 * count + (p + 1) * STATES)
            last.append(done[k, rows].astype(f32))
        for q in range(sequels):
            total = one_hot_ref[q, 0] * last[0]
            for p in range(1, PROMPTS):
                total = total + one_hot_ref[q, p] * last[p]
            start_out[PROMPTS + q, :, columns_k] = total
            end_out[PROMPTS + q, :, columns_k] = jnp.zeros_like(total)


def chain(one_hot, ahead, behind, branch, time, rate):
    size = lax.axis_size("fsdp")
    channels = ahead.shape[2]
    rows = 3 * PROMPTS * STATES
    width = channels // size
    own = lax.dynamic_slice_in_dim(rate, lax.axis_index("fsdp") * width, width, 1)
    whole = pl.BlockSpec(memory_space=pltpu.VMEM)
    shape = (PROMPTS + branch.shape[0], STATES, channels)
    return pl.pallas_call(
        chain_kernel,
        in_specs=[pl.BlockSpec(memory_space=pltpu.SMEM)] + [whole] * 5,
        out_specs=[whole] * 2,
        out_shape=[jax.ShapeDtypeStruct(shape, f32)] * 2,
        scratch_shapes=[
            pltpu.VMEM((rows, channels), bf16),
            pltpu.VMEM((size, rows, width), bf16),
            pltpu.VMEM((size, SEQS, width), f32),
            pltpu.VMEM((size, rows, width), bf16),
            pltpu.VMEM((size, rows, width), bf16),
            pltpu.SemaphoreType.DMA((2, size)),
            pltpu.SemaphoreType.DMA((2, size)),
            pltpu.SemaphoreType.DMA((2, size)),
        ],
        compiler_params=params(collective_id=1, has_side_effects=True),
        cost_estimate=cost(25),
        name="chain",
    )(one_hot, ahead, behind, branch, time, own)


TILES = [slice(k * LANES, (k + 1) * LANES) for k in range(WIDE // LANES)]


def forward_kernel(
    proj_ref, dt_ref, act_ref, yg_ref, silu_ref, slope_ref, rate_ref, start_ref, skip_ref, select_ref,
    gated_ref, hist_ref, gategrad_ref, skipg_ref,
    b_scr, c_scr,
):
    j = pl.program_id(0)
    steps = dt_ref.shape[0]

    @pl.when(j == 0)
    def _():
        spread_maps(proj_ref, select_ref, RANK, STATES, store_plain(b_scr))
        spread_maps(proj_ref, select_ref, RANK + STATES, STATES, store_pairs(c_scr))

    rates = [jnp.broadcast_to(rate_ref[n : n + 1, :], (SEQS, LANES)) for n in range(STATES)]
    skip = jnp.broadcast_to(skip_ref[0:1, :], (SEQS, LANES))
    gategrad_ref[0:HALO] = jnp.zeros((HALO, SEQS, LANES), bf16)
    unroll = 8

    def run(i, carry):
        h, skip_sum = carry
        for k in range(unroll):
            t = i * unroll + k
            dt = dt_ref[t]
            act = act_ref[t]
            u = dt * act
            new = []
            y = None
            for p in range(PAIRS):
                for n in (2 * p, 2 * p + 1):
                    new.append(jnp.exp2(dt * rates[n]) * h[n] + u * b_scr[t, n])
                low = pair(new[2 * p], new[2 * p + 1])
                hist_ref[t + 1, p] = low
                term = low * c_scr[t, p]
                y = term if p == 0 else y + term
            h = tuple(new)
            mixed = folded(y) + skip * act
            gated_ref[t] = (mixed * silu_ref[t].astype(f32)).astype(bf16)
            gategrad_ref[t + HALO] = (mixed * slope_ref[t].astype(f32)).astype(bf16)
            skip_sum = skip_sum + yg_ref[t] * act
        return h, skip_sum

    start = tuple(start_ref[:, n, :] for n in range(STATES))
    for p in range(PAIRS):
        hist_ref[0, p] = pair(start[2 * p], start[2 * p + 1])
    _, skip_sum = lax.fori_loop(0, steps // unroll, run, (start, jnp.zeros((SEQS, LANES), f32)))
    skipg_ref[...] = jnp.sum(skip_sum, axis=0, keepdims=True)


def forward(proj, dt, act, yg, silu, slope, rate, start, skip, select):
    steps, _, channels = act.shape
    grid = channels // LANES
    tile = lambda j: (0, 0, j)
    flat = pl.BlockSpec((steps, SEQS, LANES), tile)
    parts = len(TILES)
    return pl.pallas_call(
        forward_kernel,
        grid=(grid,),
        in_specs=[
            pl.BlockSpec((steps * SEQS, LANES), lambda j: (0, 0)),
            flat, flat, flat, flat, flat,
            pl.BlockSpec((STATES, LANES), lambda j: (0, j)),
            pl.BlockSpec((SEQS, STATES, LANES), tile),
            pl.BlockSpec((1, LANES), lambda j: (0, j)),
            pl.BlockSpec(select.shape, lambda j: (0, 0)),
        ],
        out_specs=[
            flat,
            pl.BlockSpec(
                (None, None, steps + 1, PAIRS, 2 * SEQS, LANES),
                lambda j: (j // parts, j % parts, 0, 0, 0, 0),
            ),
            pl.BlockSpec((steps + HALO, SEQS, LANES), tile),
            pl.BlockSpec((1, LANES), lambda j: (0, j)),
        ],
        out_shape=[
            jax.ShapeDtypeStruct((steps, SEQS, channels), bf16),
            jax.ShapeDtypeStruct((grid // parts, parts, steps + 1, PAIRS, 2 * SEQS, LANES), bf16),
            jax.ShapeDtypeStruct((steps + HALO, SEQS, channels), bf16),
            jax.ShapeDtypeStruct((1, channels), f32),
        ],
        scratch_shapes=[
            pltpu.VMEM((steps, STATES, SEQS, LANES), f32),
            pltpu.VMEM((steps, PAIRS, 2 * SEQS, LANES), bf16),
        ],
        compiler_params=params(),
        cost_estimate=cost(50),
        name="forward_scan",
    )(proj, dt, act, yg, silu, slope, rate, start, skip, select)


def backward_kernel(
    proj_ref, dt_ref, sig_ref, act_ref, yg_ref, rate_ref, end_ref, skip_ref,
    hist_ref, rank_t_ref, stepw_t_ref, pick_ref, select_ref,
    act_grad_ref, stepg_ref, biasg_ref, decayg_ref, projg_ref,
    b_scr, c_scr, db_scr, dc_scr, pre_scr, acc_scr, decay_scr, ge_scr, sum_scr,
):
    j = pl.program_id(0)
    steps = dt_ref.shape[0]

    @pl.when(j == 0)
    def _():
        spread_maps(proj_ref, select_ref, RANK, STATES, store_pairs(b_scr))
        spread_maps(proj_ref, select_ref, RANK + STATES, STATES, store_plain(c_scr))

        def clear(t, _):
            for p in range(PAIRS):
                db_scr[t, p] = jnp.zeros((2 * SEQS, LANES), bf16)
                dc_scr[t, p] = jnp.zeros((2 * SEQS, LANES), bf16)
            return 0

        lax.fori_loop(0, steps, clear, 0)
        acc_scr[...] = jnp.zeros_like(acc_scr)

    decay_scr[...] = jnp.zeros_like(decay_scr)
    sum_scr[...] = jnp.zeros_like(sum_scr)
    for n in range(STATES):
        ge_scr[n] = end_ref[:, n, :]

    def run(i, _):
        base = steps - (i + 1) * RUN
        db = [[None] * PAIRS for _ in range(RUN)]
        dc = [[None] * PAIRS for _ in range(RUN)]
        for part, cols in enumerate(TILES):
            rates = [jnp.broadcast_to(rate_ref[n : n + 1, cols], (SEQS, LANES)) for n in range(STATES)]
            low_rates = [pair(rates[2 * p], rates[2 * p + 1]) for p in range(PAIRS)]
            skip = jnp.broadcast_to(skip_ref[0:1, cols], (SEQS, LANES))
            ge = [ge_scr[n, :, cols] for n in range(STATES)]
            bias_sum = jnp.zeros((SEQS, LANES), f32)
            decay = [None] * PAIRS
            for k in range(RUN - 1, -1, -1):
                t = base + k
                dt = dt_ref[t, :, cols]
                act = act_ref[t, :, cols]
                yg = yg_ref[t, :, cols]
                u2 = both(dt * act)
                dt2 = both(dt)
                yg2 = both(yg)
                du = None
                ddt = None
                for p in range(PAIRS):
                    g = [ge[n] + yg * c_scr[t, n] for n in (2 * p, 2 * p + 1)]
                    g2 = pair(*g)
                    term = yg2 * hist_ref[part, t + 1, p]
                    dc[k][p] = term if part == 0 else dc[k][p] + term
                    term = g2 * u2
                    db[k][p] = term if part == 0 else db[k][p] + term
                    term = g2 * b_scr[t, p]
                    du = term if p == 0 else du + term
                    gn = [jnp.exp2(dt * rates[2 * p + m]) * g[m] for m in (0, 1)]
                    ge[2 * p], ge[2 * p + 1] = gn
                    q = pair(*gn) * hist_ref[part, t, p]
                    term = q * dt2
                    decay[p] = term if decay[p] is None else decay[p] + term
                    term = q * low_rates[p]
                    ddt = term if p == 0 else ddt + term
                du = folded(du)
                pre_grad = (du * act + folded(ddt) * LN2) * sig_ref[t, :, cols].astype(f32)
                pre_scr[t, :, cols] = pre_grad.astype(bf16)
                act_grad_ref[t, :, cols] = yg * skip + du * dt
                bias_sum = bias_sum + pre_grad
                if part == len(TILES) - 1:
                    for p in range(PAIRS):
                        dc_scr[t, p] = dc[k][p] + dc_scr[t, p]
                        db_scr[t, p] = db[k][p] + db_scr[t, p]
            for p in range(PAIRS):
                a, b = halves(decay[p])
                decay_scr[2 * p, :, cols] += a
                decay_scr[2 * p + 1, :, cols] += b
            for n in range(STATES):
                ge_scr[n, :, cols] = ge[n]
            sum_scr[:, cols] += bias_sum
        return 0

    lax.fori_loop(0, steps // RUN, run, 0)
    for n in range(STATES):
        decayg_ref[n : n + 1, :] = jnp.sum(decay_scr[n] * rate_ref[n : n + 1, :], axis=0, keepdims=True) * LN2
    biasg_ref[...] = jnp.sum(sum_scr[...], axis=0, keepdims=True)

    pre_low = pre_scr[...].reshape(steps * SEQS, WIDE)
    stepg_ref[...] = jnp.dot(rank_t_ref[...], pre_low, preferred_element_type=f32)
    acc_scr[...] += jnp.dot(pre_low, stepw_t_ref[...], preferred_element_type=f32)

    @pl.when(j == pl.num_programs(0) - 1)
    def _():
        chunk = 32
        even = lax.broadcasted_iota(jnp.int32, (chunk, SEQS, LANES), 2) % 2 == 0

        def step(i, _):
            t = i * chunk
            total = jnp.zeros((chunk * 2 * SEQS, LANES), f32)
            for p in range(PAIRS):
                rows = jnp.concatenate([db_scr[pl.ds(t, chunk), p], dc_scr[pl.ds(t, chunk), p]], axis=2)
                rows = rows.reshape(chunk * 2 * SEQS, 2 * LANES)
                total = total + jnp.dot(rows, pick_ref[p], preferred_element_type=f32)
            total = total.reshape(chunk, 2 * SEQS, LANES)
            total = jnp.where(even, total[:, :SEQS], total[:, SEQS:]).reshape(chunk * SEQS, LANES)
            r = pl.multiple_of(t * SEQS, chunk * SEQS)
            projg_ref[pl.ds(r, chunk * SEQS), :] = (acc_scr[pl.ds(r, chunk * SEQS), :] + total).astype(bf16)
            return 0

        lax.fori_loop(0, steps // chunk, step, 0)


def backward(proj, dt, sig, act, yg, rate, end, skip, hist, rank_t, stepw_t, pick, select):
    steps, _, channels = act.shape
    grid = channels // WIDE
    tile = lambda j: (0, 0, j)
    whole = lambda j: (0, 0)
    flat = pl.BlockSpec((steps, SEQS, WIDE), tile)
    sums = pltpu.VMEM((steps, PAIRS, 2 * SEQS, LANES), bf16)
    return pl.pallas_call(
        backward_kernel,
        grid=(grid,),
        in_specs=[
            pl.BlockSpec((steps * SEQS, LANES), whole),
            flat, flat, flat, flat,
            pl.BlockSpec((STATES, WIDE), lambda j: (0, j)),
            pl.BlockSpec((SEQS, STATES, WIDE), tile),
            pl.BlockSpec((1, WIDE), lambda j: (0, j)),
            pl.BlockSpec(
                (None, len(TILES), steps + 1, PAIRS, 2 * SEQS, LANES), lambda j: (j, 0, 0, 0, 0, 0)
            ),
            pl.BlockSpec((RANK, steps * SEQS), whole),
            pl.BlockSpec((WIDE, LANES), lambda j: (j, 0)),
            pl.BlockSpec(pick.shape, lambda j: (0, 0, 0)),
            pl.BlockSpec(select.shape, whole),
        ],
        out_specs=[
            flat,
            pl.BlockSpec((RANK, WIDE), lambda j: (0, j)),
            pl.BlockSpec((1, WIDE), lambda j: (0, j)),
            pl.BlockSpec((STATES, WIDE), lambda j: (0, j)),
            pl.BlockSpec((steps * SEQS, LANES), whole),
        ],
        out_shape=[
            jax.ShapeDtypeStruct((steps, SEQS, channels), f32),
            jax.ShapeDtypeStruct((RANK, channels), f32),
            jax.ShapeDtypeStruct((1, channels), f32),
            jax.ShapeDtypeStruct((STATES, channels), f32),
            jax.ShapeDtypeStruct((steps * SEQS, LANES), bf16),
        ],
        scratch_shapes=[
            sums,
            pltpu.VMEM((steps, STATES, SEQS, LANES), f32),
            sums, sums,
            pltpu.VMEM((steps, SEQS, WIDE), bf16),
            pltpu.VMEM((steps * SEQS, LANES), f32),
            pltpu.VMEM((STATES, SEQS, WIDE), f32),
            pltpu.VMEM((STATES, SEQS, WIDE), f32),
            pltpu.VMEM((SEQS, WIDE), f32),
        ],
        compiler_params=params(),
        cost_estimate=cost(90),
        name="backward_scan",
    )(proj, dt, sig, act, yg, rate, end, skip, hist, rank_t, stepw_t, pick, select)


def filter_back_kernel(
    mix_ref, act_ref, act_grad_ref, projg_ref, projg_t_ref, sel_ref, fw_ref, fb_ref,
    mixgrad_ref, selg_ref, fwg_ref, fbg_ref,
    dv_scr,
):
    steps = act_ref.shape[0]
    chunk = 16
    taps = [fw_ref[k : k + 1, :] for k in range(KERNEL)]
    bias = fb_ref[0:1, :]
    zero = jnp.zeros((HALO, SEQS, WIDE), f32)
    dv_scr[0:HALO] = zero
    dv_scr[steps + HALO :] = zero

    def step(i, sums):
        t = i * chunk
        x = mix_ref[pl.ds(t, chunk + HALO)].astype(f32)
        v = bias[None] + taps[0][None] * x[1 : 1 + chunk]
        for k in range(1, KERNEL):
            v = v + taps[k][None] * x[1 + k : 1 + k + chunk]
        sig = sigmoid(v)
        r = pl.multiple_of(t * SEQS, chunk * SEQS)
        more = contract_cols(projg_ref[pl.ds(r, chunk * SEQS), :], sel_ref[...])
        total = act_grad_ref[pl.ds(t, chunk)] + more.reshape(chunk, SEQS, WIDE)
        dv = total * (sig * (1.0 + v * (1.0 - sig)))
        dv_scr[pl.ds(t + HALO, chunk)] = dv
        new = [sums[0] + jnp.sum(dv, axis=0)]
        for k in range(KERNEL):
            new.append(sums[1 + k] + jnp.sum(dv * x[1 + k : 1 + k + chunk], axis=0))
        return tuple(new)

    sums = lax.fori_loop(
        0, steps // chunk, step, tuple(jnp.zeros((SEQS, WIDE), f32) for _ in range(KERNEL + 1))
    )
    fbg_ref[...] = jnp.sum(sums[0], axis=0, keepdims=True)
    for k in range(KERNEL):
        fwg_ref[k : k + 1, :] = jnp.sum(sums[1 + k], axis=0, keepdims=True)

    def spread(t, count):
        dv = dv_scr[pl.ds(t, count + HALO)]
        out = taps[KERNEL - 1][None] * dv[0:count]
        for k in range(KERNEL - 1):
            s = KERNEL - 1 - k
            out = out + taps[k][None] * dv[s : s + count]
        mixgrad_ref[pl.ds(t, count)] = out.astype(bf16)

    def out_step(i, _):
        spread(i * chunk, chunk)
        return 0

    lax.fori_loop(0, steps // chunk, out_step, 0)
    spread(steps, HALO)
    low = act_ref[...].reshape(steps * SEQS, WIDE).astype(bf16)
    selg_ref[...] = jnp.dot(projg_t_ref[...], low, preferred_element_type=f32)


def filter_back(mixture, act, act_grad, projg, projg_t, select_pad, fw, fb):
    steps, _, channels = act.shape
    grid = channels // WIDE
    wide = lambda j: (0, 0, j)
    whole = lambda j: (0, 0)
    cols = lambda j: (0, j)
    return pl.pallas_call(
        filter_back_kernel,
        grid=(grid,),
        in_specs=[
            pl.BlockSpec((steps + HALO, SEQS, WIDE), wide),
            pl.BlockSpec((steps, SEQS, WIDE), wide),
            pl.BlockSpec((steps, SEQS, WIDE), wide),
            pl.BlockSpec((steps * SEQS, LANES), whole),
            pl.BlockSpec((LANES, steps * SEQS), whole),
            pl.BlockSpec((WIDE, LANES), lambda j: (j, 0)),
            pl.BlockSpec((KERNEL, WIDE), cols),
            pl.BlockSpec((1, WIDE), cols),
        ],
        out_specs=[
            pl.BlockSpec((steps + HALO, SEQS, WIDE), wide),
            pl.BlockSpec((LANES, WIDE), cols),
            pl.BlockSpec((KERNEL, WIDE), cols),
            pl.BlockSpec((1, WIDE), cols),
        ],
        out_shape=[
            jax.ShapeDtypeStruct((steps + HALO, SEQS, channels), bf16),
            jax.ShapeDtypeStruct((LANES, channels), f32),
            jax.ShapeDtypeStruct((KERNEL, channels), f32),
            jax.ShapeDtypeStruct((1, channels), f32),
        ],
        scratch_shapes=[pltpu.VMEM((steps + 2 * HALO, SEQS, WIDE), f32)],
        compiler_params=params(),
        cost_estimate=cost(20),
        name="filter_back",
    )(mixture, act, act_grad, projg, projg_t, select_pad, fw, fb)


def send(src, dst, send_sem, recv_sem, peer, axis="fsdp"):
    return pltpu.make_async_remote_copy(
        src_ref=src,
        dst_ref=dst,
        send_sem=send_sem,
        recv_sem=recv_sem,
        device_id={axis: peer},
        device_id_type=pl.DeviceIdType.MESH,
    )


def greet(others):
    barrier = pltpu.get_barrier_semaphore()
    for axis, peer in others:
        pl.semaphore_signal(barrier, inc=1, device_id={axis: peer}, device_id_type=pl.DeviceIdType.MESH)
    pl.semaphore_wait(barrier, len(others))


def flipped(index, bit):
    return index + (1 - 2 * (index // bit % 2)) * bit


FIRST, SECOND = (0, 1, 2, 3), (4, 5)


def gather_kernel(
    rows_ref, select_ref, out_ref, in_ref, all_rows, all_select, all_out, all_in,
    local_sems, own_send, own_recv, pass_send, pass_recv, core_send, core_recv,
):
    me = lax.axis_index("fsdp")
    a, b = flipped(me, 2), flipped(me, 4)
    corner = flipped(a, 4)
    twin = flipped(me, 1)
    greet([("fsdp", a), ("fsdp", b), ("fsdp", twin)])
    kinds = ((rows_ref, all_rows), (select_ref, all_select), (out_ref, all_out), (in_ref, all_in))
    table = [(0, 0, 1), (1, 0, 1), (2, 0, 2), (3, 0, 2), (2, 1, 2), (3, 1, 2)]

    def place(owner, piece):
        kind, part, parts = table[piece]
        count = kinds[kind][0].shape[0]
        step = count // parts
        return kinds[kind][1].at[pl.ds(pl.multiple_of(owner * count + part * step, step), step)]

    def mine(piece):
        kind, part, parts = table[piece]
        step = kinds[kind][0].shape[0] // parts
        return kinds[kind][0].at[pl.ds(part * step, step)]

    started = []

    def start(copy):
        copy.start()
        started.append(copy)

    def own_copy(piece, k, peer, owner):
        return send(mine(piece), place(owner, piece), own_send.at[k, piece], own_recv.at[k, piece], peer)

    def pass_copy(piece, peer, owner):
        return send(place(owner, piece), place(owner, piece), pass_send.at[piece], pass_recv.at[piece], peer)

    def core_copy(piece, k, owner):
        src = mine(piece) if k == 0 else place(owner, piece)
        return send(src, place(owner, piece), core_send.at[k, piece], core_recv.at[k, piece], twin)

    for piece in FIRST + SECOND:
        start(own_copy(piece, 0, a, me))
    for piece in SECOND + FIRST:
        start(own_copy(piece, 1, b, me))
    local = []
    for piece in FIRST + SECOND:
        start(core_copy(piece, 0, me))
        copy = pltpu.make_async_copy(mine(piece), place(me, piece), local_sems.at[piece])
        copy.start()
        local.append(copy)

    def arrived(piece, k):
        owner = (a, b, corner)[k]
        if k == 2:
            pass_copy(piece, a, owner).wait_recv()
        else:
            own_copy(piece, k, a, owner).wait_recv()
            if k == 0 and piece in FIRST:
                start(pass_copy(piece, b, owner))
            if k == 1 and piece in SECOND:
                start(pass_copy(piece, a, owner))
        start(core_copy(piece, k + 1, owner))

    for piece, k in (
        (0, 0), (1, 0), (2, 0), (4, 1), (3, 0), (5, 1), (4, 0), (0, 1), (1, 1), (2, 1), (0, 2), (1, 2), (2, 2),
        (4, 2), (5, 0), (3, 1), (3, 2), (5, 2),
    ):
        arrived(piece, k)
    for k, owner in enumerate((twin, flipped(twin, 2), flipped(twin, 4), flipped(corner, 1))):
        for piece in FIRST + SECOND:
            core_copy(piece, k, owner).wait_recv()
    for copy in started:
        copy.wait_send()
    for copy in local:
        copy.wait()


def gather(*shards):
    size = lax.axis_size("fsdp")
    if size != 8:
        return [lax.all_gather(shard, "fsdp", axis=0, tiled=True) for shard in shards]
    vmem = pl.BlockSpec(memory_space=pltpu.VMEM)
    hbm = pl.BlockSpec(memory_space=pl.ANY)
    pieces = len(FIRST + SECOND)
    dma = pltpu.SemaphoreType.DMA
    return pl.pallas_call(
        gather_kernel,
        in_specs=[vmem] * 4,
        out_specs=[hbm] * 4,
        out_shape=[jax.ShapeDtypeStruct((size * shard.shape[0], shard.shape[1]), bf16) for shard in shards],
        scratch_shapes=[
            dma((pieces,)), dma((2, pieces)), dma((2, pieces)), dma((pieces,)), dma((pieces,)),
            dma((4, pieces)), dma((4, pieces)),
        ],
        compiler_params=params(collective_id=2, has_side_effects=True),
        cost_estimate=cost(55),
        name="gather",
    )(*shards)


SMALL = (KERNEL, 1, 1, 1, STATES, RANK, RANK + 2 * STATES, 1)
SMALL_ROWS = 192


def xor(index, bits):
    for bit in (1, 2, 4, 8):
        if bits & bit:
            index = flipped(index, bit)
    return index


def tail_kernel(
    one_hot_ref, b0, b1, b2, b3, filter_ref, fbias_ref, sbias_ref, skip_ref, decay_ref, step_ref, select_ref,
    gain_ref, halo_ref, block_out, small_out, rim_out,
    total, to_z, from_z, part, parts, small_f, small_ref, got_small, small_z, small_from_z, small_part,
    small_parts, rim, child, got_rim, got_child,
    sems_s, sems_z, sems_p, sems_sz, sems_sp, sems_r, sems_cs, sems_cr,
):
    depth = lax.axis_size("replica")
    me, size = lax.axis_index("fsdp"), lax.axis_size("fsdp")
    mz = lax.axis_index("replica")
    last = size - 1
    near = [lax.rem(me + d, size) for d in range(1, size)]
    far = [lax.rem(mz + d, depth) for d in range(1, depth)]
    greet([("fsdp", peer) for peer in near] + [("replica", peer) for peer in far])

    def spread(src, dst, sems, peers, axis, index):
        copies = []
        for d, peer in enumerate(peers):
            source = src.at[peer] if src.shape[0] == len(peers) + 1 and len(src.shape) == len(dst.shape) else src
            copy = send(source, dst.at[index], sems.at[0, d], sems.at[1, d], peer, axis)
            copy.start()
            copies.append(copy)
        return copies

    width = small_f.shape[2]
    small_f[...] = jnp.zeros_like(small_f)
    refs = (filter_ref, fbias_ref, sbias_ref, skip_ref, decay_ref, step_ref, select_ref)
    for k in range(size):
        at = 0
        for ref, count in zip(refs, SMALL):
            small_f[k, at : at + count] = ref[0:count, k * width : (k + 1) * width]
            at += count
        some = gain_ref.shape[1] // size
        small_f[k, at : at + 1, 0:some] = gain_ref[:, k * some : (k + 1) * some]
    small_ref[...] = small_f[...].astype(bf16)
    sequels = one_hot_ref.shape[0]
    pieces = (SEQS - PROMPTS) // sequels
    for t in range(HALO):
        rim[t * PROMPTS : (t + 1) * PROMPTS] = halo_ref[t, 0:PROMPTS]
        for p in range(PROMPTS):
            sums = None
            for q in range(sequels):
                row = PROMPTS + q * pieces
                term = one_hot_ref[q, p] * halo_ref[t, row : row + 1]
                sums = term if q == 0 else sums + term
            child[t * PROMPTS + p : t * PROMPTS + p + 1] = sums
    block = b0[...].astype(f32) + b1[...].astype(f32) + b2[...].astype(f32) + b3[...].astype(f32)
    total[...] = block.reshape(total.shape)
    to_z[...] = total[...].astype(bf16)
    to_left = send(rim, got_rim, sems_r.at[0], sems_r.at[1], lax.rem(me + last, size))
    to_left.start()

    @pl.when(me != last)
    def _():
        send(child, got_child.at[me], sems_cs.at[me], sems_cr.at[me], last).start()

    copies = spread(small_ref, got_small, sems_s, near, "fsdp", me)
    z_copies = spread(to_z, from_z, sems_z, far, "replica", mz)
    small = small_ref[me].astype(f32)
    got_small[me] = jnp.zeros(got_small.shape[1:], bf16)
    from_z[mz] = jnp.zeros(from_z.shape[1:], bf16)
    small_from_z[mz] = jnp.zeros(small_from_z.shape[1:], bf16)
    for copy in copies:
        copy.wait()
    for k in range(size):
        small = small + got_small[k].astype(f32)
    small_z[...] = small.reshape(small_z.shape)
    small_to_z = small_part
    small_to_z[...] = small_z[...].astype(bf16)
    s_copies = spread(small_to_z, small_from_z, sems_sz, far, "replica", mz)
    for copy in z_copies:
        copy.wait()
    own = total[mz]
    for k in range(depth):
        own = own + from_z[k].astype(f32)
    part[...] = own.astype(bf16)
    p_copies = spread(part, parts, sems_p, far, "replica", mz)
    parts[mz] = part[...]
    for copy in s_copies:
        copy.wait()
    own = small_z[mz]
    for k in range(depth):
        own = own + small_from_z[k].astype(f32)
    small_parts[mz] = own.astype(bf16)
    small_own = small_to_z.at[mz]
    small_own[...] = own.astype(bf16)
    q_copies = []
    for d, peer in enumerate(far):
        copy = send(small_own, small_parts.at[mz], sems_sp.at[0, d], sems_sp.at[1, d], peer, "replica")
        copy.start()
        q_copies.append(copy)
    for copy in p_copies + q_copies:
        copy.wait()
    block_out[...] = parts[...].reshape(block_out.shape)
    small_out[...] = small_parts[...].reshape(small_out.shape)
    to_left.wait()

    @pl.when(me != last)
    def _():
        send(child, got_child.at[me], sems_cs.at[me], sems_cr.at[me], last).wait_send()
        rim_out[...] = got_rim[...]

    @pl.when(me == last)
    def _():
        sums = child[...]
        for k in range(size - 1):
            send(child, got_child.at[k], sems_cs.at[k], sems_cr.at[k], 0).wait_recv()
            sums = sums + got_child[k]
        rim_out[...] = sums


def tail(one_hot, blocks, small, halo_grad):
    size, depth = lax.axis_size("fsdp"), lax.axis_size("replica")
    vmem = pl.BlockSpec(memory_space=pltpu.VMEM)
    dma = pltpu.SemaphoreType.DMA
    while len(blocks) > 4:
        blocks = blocks[:3] + [summed(blocks[3], blocks[4:5]).astype(bf16)] + blocks[5:]
    rows, channels = blocks[0].shape
    features = small[-1].shape[1]
    width = channels // size
    cut = (depth, rows // depth, channels)
    by_owner = (size, SMALL_ROWS, width)
    small_cut = (depth, SMALL_ROWS // depth, width)
    rim = (HALO * PROMPTS, features)
    return pl.pallas_call(
        tail_kernel,
        in_specs=[pl.BlockSpec(memory_space=pltpu.SMEM)] + [vmem] * (4 + len(small) + 1),
        out_specs=[vmem] * 3,
        out_shape=[
            jax.ShapeDtypeStruct((rows, channels), bf16),
            jax.ShapeDtypeStruct((SMALL_ROWS, width), bf16),
            jax.ShapeDtypeStruct(rim, f32),
        ],
        scratch_shapes=[
            pltpu.VMEM(cut, f32), pltpu.VMEM(cut, bf16), pltpu.VMEM(cut, bf16),
            pltpu.VMEM(cut[1:], bf16), pltpu.VMEM(cut, bf16),
            pltpu.VMEM(by_owner, f32), pltpu.VMEM(by_owner, bf16), pltpu.VMEM(by_owner, bf16),
            pltpu.VMEM(small_cut, f32), pltpu.VMEM(small_cut, bf16),
            pltpu.VMEM(small_cut, bf16), pltpu.VMEM(small_cut, bf16),
            pltpu.VMEM(rim, f32), pltpu.VMEM(rim, f32), pltpu.VMEM(rim, f32), pltpu.VMEM((size,) + rim, f32),
            dma((2, size)), dma((2, depth)), dma((2, depth)), dma((2, depth)), dma((2, depth)),
            dma((2,)), dma((size,)), dma((size,)),
        ],
        compiler_params=params(collective_id=4, has_side_effects=True),
        cost_estimate=cost(30),
        name="tail",
    )(one_hot, *blocks, *small, halo_grad)


def deliver_kernel(block_ref, small_ref, rim_ref, prompt_ref, *rest):
    depth = lax.axis_size("replica")
    early_refs, outs = rest[:depth], rest[depth:-1]
    early = rest[-1]
    in_out, out_out, prompt_out = outs[:3]
    mz = lax.axis_index("replica")
    half = in_out.shape[1] // 2
    in_out[:, 0:half] = block_ref[...].astype(f32)
    small = small_ref[...].astype(f32)
    at = 0
    for k, (out, count) in enumerate(zip(outs[3:], SMALL)):
        rows = small[at : at + count]
        if k in (4, 6):
            rows = jnp.concatenate([rows, jnp.zeros((-count % LANES, rows.shape[1]), f32)], axis=0)
            out[...] = rows.T[:, :count]
        else:
            out[...] = rows[:, 0 : out.shape[1]]
        at += count
    for d, ref in enumerate(early_refs):
        count = ref.shape[0]
        early[pl.ds(pl.multiple_of(xor(mz, d) * count, count), count), :] = ref[...].astype(f32)
    rows = out_out.shape[0] // 2
    features = out_out.shape[1]
    out_out[0:rows, :] = early[0:rows, 0:features]
    out_out[rows:, :] = early[0:rows, features:]
    in_out[:, half:] = early[rows:, :]
    for p in range(PROMPTS):
        prompt_out[p, 0 : SEQS - HALO] = prompt_ref[p, 0 : SEQS - HALO]
        for t in range(HALO):
            row = SEQS - HALO + t
            prompt_out[p, row : row + 1] = (
                prompt_ref[p, row : row + 1] + rim_ref[t * PROMPTS + p : t * PROMPTS + p + 1]
            )


def deliver(block, small, rim, prompt_grad, early):
    size = lax.axis_size("fsdp")
    rows, channels = block.shape
    width = small.shape[1]
    features = prompt_grad.shape[2]
    vmem = pl.BlockSpec(memory_space=pltpu.VMEM)
    end = prompt_grad.shape[1] // SEQS - 1
    last = pl.BlockSpec((PROMPTS, SEQS, features), lambda i: (0, end, 0))
    shapes = [(count, width) for count in SMALL[:-1]] + [(1, features // size)]
    shapes[4], shapes[6] = shapes[4][::-1], shapes[6][::-1]
    shapes = [(rows, 2 * channels), (2 * rows, features), prompt_grad.shape] + shapes
    return pl.pallas_call(
        deliver_kernel,
        grid=(1,),
        in_specs=[vmem, vmem, vmem, last] + [vmem] * len(early),
        out_specs=[vmem, vmem, last] + [vmem] * len(SMALL),
        out_shape=[jax.ShapeDtypeStruct(shape, f32) for shape in shapes],
        scratch_shapes=[pltpu.VMEM((2 * rows, channels), f32)],
        input_output_aliases={3: 2},
        compiler_params=params(),
        cost_estimate=cost(4),
        name="deliver",
    )(block, small, rim, prompt_grad, *early)


def contract_rows(left_side, right_side):
    return lax.dot_general(
        left_side, right_side, (((0,), (0,)), ((), ())), preferred_element_type=f32
    )


def contract_cols(left_side, right_side):
    return lax.dot_general(
        left_side, right_side, (((1,), (1,)), ((), ())), preferred_element_type=f32
    )


def exchanged(block, axis, distance):
    return lax.ppermute(block, axis, [(i, i ^ distance) for i in range(lax.axis_size(axis))])


def pick_row(block, index, axis=0):
    return lax.dynamic_index_in_dim(block, index, axis, keepdims=False)


def over_cores(blocks):
    blocks = blocks.reshape((-1, 2) + blocks.shape[1:])
    core = lax.axis_index("fsdp") % 2
    got = exchanged(pick_row(blocks, 1 - core, 1), "fsdp", 1)
    return (pick_row(blocks, core, 1).astype(f32) + got.astype(f32)).astype(bf16)


def to_chips(blocks):
    chip = lax.axis_index("fsdp") // 2
    got = [exchanged(pick_row(blocks, chip ^ d), "fsdp", 2 * d) for d in range(1, blocks.shape[0])]
    return pick_row(blocks, chip), got


def summed(own, got):
    total = own.astype(f32)
    for block in got:
        total = total + block.astype(f32)
    return total


def to_replicas(block):
    size, here = lax.axis_size("replica"), lax.axis_index("replica")
    parts = block.astype(bf16).reshape((size, -1) + block.shape[1:])
    own = pick_row(block.reshape(parts.shape), here)
    return own, [exchanged(pick_row(parts, here ^ d), "replica", d) for d in range(1, size)]


def from_replicas(part):
    return [part] + [exchanged(part, "replica", d) for d in range(1, lax.axis_size("replica"))]


def body(
    prompt_hidden, sequel_hidden, parents, prompt_cotangent, sequel_cotangent,
    norm_gain, input_weight, filter_weight, depthwise_filter_bias, select_weight,
    step_weight, step_bias, decay_log, skip_gain, output_weight,
):
    size, here = lax.axis_size("fsdp"), lax.axis_index("fsdp")
    prompts, steps = prompt_hidden.shape[:2]
    sequels, sequel_len = sequel_hidden.shape[:2]
    split = sequel_len // steps
    assert prompts == PROMPTS and sequels * split == SEQS - prompts
    rim = KERNEL - 1
    half = SEQS // 2
    rows = steps * SEQS

    after = lax.optimization_barrier
    width = step_bias.shape[0]
    tail_rows = prompt_hidden[:, steps - rim :]
    shard = jnp.concatenate(
        [
            step_weight,
            tail_rows.reshape(-1, width),
            filter_weight,
            depthwise_filter_bias[None],
            step_bias[None],
            skip_gain[None],
            jnp.pad(norm_gain, (0, width - norm_gain.shape[0]))[None],
        ],
        axis=0,
    )
    shard = jnp.pad(shard, ((0, -shard.shape[0] % 16), (0, 0)))
    lanes = jnp.concatenate([select_weight, decay_log], axis=1)
    lanes = jnp.pad(lanes, ((0, 0), (0, LANES - lanes.shape[1])))
    every, select_pad, full_output, full_input = gather(shard, lanes, output_weight, input_weight)
    every = every.reshape(size, shard.shape[0], width)
    at = RANK + tail_rows.size // width
    tails = every[:, RANK:at].reshape((size,) + tail_rows.shape)
    step_full = jnp.swapaxes(every[:, :RANK], 0, 1).reshape(RANK, -1)
    vectors = jnp.swapaxes(every[:, at : at + SEQS], 0, 1).astype(f32)
    gain = vectors[KERNEL + 3, :, : norm_gain.shape[0]].reshape(1, -1)
    vectors = vectors.reshape(SEQS, -1)
    fw, fb, sbias, skip = vectors[:KERNEL], vectors[4:5], vectors[5:6], vectors[6:7]
    first = RANK + 2 * STATES
    rate = -jnp.exp(select_pad[:, first : first + STATES].T.astype(f32)) * LOG2E
    step_pad = jnp.pad(step_full, ((0, LANES - RANK), (0, 0)))

    before = jnp.where(here > 0, tails[jnp.maximum(here - 1, 0)], jnp.zeros_like(tails[0]))
    cut = sequel_hidden.reshape(sequels, split, steps, D)
    inner = jnp.concatenate([tails[size - 1][parents][:, None], cut[:, :-1, steps - rim :]], axis=1)
    halo = jnp.concatenate([before, inner.reshape(-1, rim, D)], axis=0)
    halo = jnp.pad(jnp.swapaxes(halo, 0, 1), ((HALO - rim, 0), (0, 0), (0, 0))).reshape(-1, D).astype(f32)
    pieces = sequel_hidden.reshape(-1, steps, D)
    piece_cot = sequel_cotangent.reshape(-1, steps, D)
    scaled, cotangent = prepare(prompt_hidden, pieces, prompt_cotangent, piece_cot, halo, gain)

    mixture = product([scaled], full_input, bf16, part=0, parts=2)
    gate = product([scaled], full_input, f32, part=1, parts=2)
    mixture = mixture.reshape(steps + HALO, SEQS, INNER)
    gate = gate.reshape(steps + HALO, SEQS, INNER)
    gated_grad = product([cotangent], full_output, f32, across=True).reshape(steps, SEQS, INNER)
    act, proj = front(mixture, fw, fb, select_pad, steps)
    groups = 1 if split == 1 else 2
    lane = jnp.arange(2 * STATES * LANES)[None, :]
    select = (jnp.arange(LANES)[:, None] == RANK + lane // LANES).astype(bf16)
    dt, sig, yg, silu, slope, ahead, behind, total = piece(
        proj, act, gate, gated_grad, step_pad, sbias, rate, select, groups
    )

    one_hot = (parents[:, None] == jnp.arange(PROMPTS, dtype=jnp.int32)[None, :]).astype(f32)
    own = total[half:].reshape(sequels, split, 1, INNER)
    own_behind = behind[half:].reshape(sequels, split, STATES, INNER)
    back = own_behind[:, split - 1]
    own_end = [jnp.zeros_like(back)]
    for p in range(split - 2, -1, -1):
        own_end.insert(0, back)
        back = own_behind[:, p] + jnp.exp2(rate * own[:, p]) * back
    start, end = chain(one_hot, ahead[:half], behind[:half], back, total, rate)
    if split > 1:
        state = start[half:]
        own_start = [state]
        for p in range(split - 1):
            state = jnp.exp2(rate * own[:, p]) * state + ahead[half:].reshape(own_behind.shape)[:, p]
            own_start.append(state)
        own_start = jnp.stack(own_start, axis=1).reshape(half, STATES, INNER)
        start = jnp.concatenate([start[:half], own_start], axis=0)
        end = jnp.concatenate([end[:half], jnp.stack(own_end, axis=1).reshape(half, STATES, INNER)], axis=0)

    gated, hist, gate_grad, skip_grad = forward(
        proj, dt, act, yg, silu, slope, rate, start, skip, select
    )
    gated = gated.reshape(rows, INNER)
    gate_grad = gate_grad.reshape(-1, INNER)
    output_grad = contract_rows(gated, cotangent).astype(bf16).reshape(size, -1, D)
    gate_weight_grad = contract_rows(scaled, gate_grad).astype(bf16)
    early = [over_cores(output_grad), over_cores(gate_weight_grad.reshape(size, -1, INNER))]
    wide = jnp.concatenate([early[0][:, : INNER // size // 2], early[0][:, INNER // size // 2 :]], axis=2)
    early = jnp.concatenate([wide, early[1]], axis=1)
    end, early = after((end, early))
    early = to_chips(early)

    rank_t = proj[:, :RANK].astype(bf16).T
    lane = jnp.arange(LANES)[None, None, :]
    which = jnp.arange(PAIRS)[:, None, None]
    source = jnp.arange(2 * LANES)[None, :, None]
    pick = (lane // 2 == jnp.where(source < LANES, RANK, RANK + STATES) // 2 + which).astype(bf16)
    act_grad, step_grad, bias_grad, decay_grad, projg = backward(
        proj, dt, sig, act, yg, rate, end, skip, hist, rank_t, step_pad.T, pick, select
    )
    projg, early = after((projg, early))
    early = summed(*early)
    projg, early = after((projg, early))
    early = to_replicas(early)
    filter_in_grad, select_grad, filter_grad, filter_bias_grad = filter_back(
        mixture, act, act_grad, projg, projg.T, select_pad, fw, fb
    )
    filter_in_grad, early = after((filter_in_grad, early))
    early = summed(*early).astype(bf16)
    filter_in_grad = filter_in_grad.reshape(-1, INNER)
    filter_weight_grad = contract_rows(scaled, filter_in_grad).astype(bf16)
    filter_weight_grad, early = after((filter_weight_grad, early))
    late = over_cores(filter_weight_grad.reshape(size, -1, INNER))
    early = from_replicas(early)
    mixed = jnp.dot(gated, full_output, preferred_element_type=f32)
    late, mixed, filter_in_grad = after((late, mixed, filter_in_grad))
    own_block, late = to_chips(late)
    scaled_grad = product([filter_in_grad, gate_grad], full_input, f32, across=True)
    prompt_out, piece_out, prompt_grad, piece_grad, halo_grad, gain_grad = finish(
        mixed, scaled_grad, prompt_hidden, pieces, prompt_cotangent, piece_cot, halo, gain
    )
    halo_grad, own_block, late = after((halo_grad, own_block, late))
    halo_grad = halo_grad.reshape(HALO, SEQS, D)
    small = [
        filter_grad, filter_bias_grad, bias_grad, skip_grad, decay_grad, step_grad, select_grad, gain_grad,
    ]
    block, small, following = tail(one_hot, [own_block] + late, small, halo_grad)
    (
        input_grad, output_grad, prompt_grad, g_filter, g_fbias, g_sbias, g_skip, g_decay, g_step, g_select, g_gain,
    ) = deliver(block, small, following, prompt_grad, early)
    if split > 1:
        own = jnp.swapaxes(halo_grad[:, half:], 0, 1).reshape(sequels, split, HALO, D)
        own = jnp.pad(own[:, 1:], ((0, 0), (0, 1), (0, 0), (0, 0))).reshape(half, HALO, D)
        piece_grad = piece_grad.at[:, steps - HALO :].add(own)
    return (
        prompt_out,
        piece_out.reshape(sequel_hidden.shape),
        prompt_grad,
        piece_grad.reshape(sequel_hidden.shape),
        g_gain[0],
        input_grad,
        g_filter,
        g_fbias[0],
        g_select,
        g_step,
        g_sbias[0],
        g_decay,
        g_skip[0],
        output_grad,
    )


def solution(mesh):
    rows = P("replica", "fsdp", None)
    own = P(("replica", "fsdp"), None, None)
    return jax.shard_map(
        body,
        mesh=mesh,
        in_specs=(
            rows, own, P(("replica", "fsdp")), rows, own,
            P("fsdp"), P("fsdp", None), P(None, "fsdp"), P("fsdp"), P("fsdp", None),
            P(None, "fsdp"), P("fsdp"), P("fsdp", None), P("fsdp"), P("fsdp", None),
        ),
        out_specs=(
            rows, own, rows, own,
            P("fsdp"), P("fsdp", None), P(None, "fsdp"), P("fsdp"), P("fsdp", None),
            P(None, "fsdp"), P("fsdp"), P("fsdp", None), P("fsdp"), P("fsdp", None),
        ),
        check_vma=False,
    )
```

```python
import functools
import math

import jax
import jax.numpy as jnp
from jax import lax
from jax.experimental import pallas as pl
from jax.experimental.pallas import tpu as pltpu
from jax.sharding import PartitionSpec as P

D = 1024
INNER = 2048
STATES = 16
RANK = 64
KERNEL = 4
PROMPTS = 4

SEQS = 8
HALO = 4
LANES = 128
WIDE = 256
LOG2E = math.log2(math.e)
LN2 = math.log(2.0)
f32 = jnp.float32
bf16 = jnp.bfloat16

VMEM_LIMIT = 62 * 1024 * 1024


def cost(microseconds):
    return pl.CostEstimate(flops=int(microseconds * 1e9), bytes_accessed=0, transcendentals=0)


def params(**kw):
    return pltpu.CompilerParams(vmem_limit_bytes=VMEM_LIMIT, **kw)


def sigmoid(x):
    return 1.0 / (1.0 + jnp.exp(-x))


def softplus(x):
    return jnp.maximum(x, 0.0) + jnp.log1p(jnp.exp(-jnp.abs(x)))


def product_kernel(across, *refs):
    lefts, rhs_ref, out_ref = refs[:-2], refs[-2], refs[-1]
    total = None
    at = 0
    for left in lefts:
        depth = left.shape[1]
        rhs = rhs_ref[:, at : at + depth] if across else rhs_ref[at : at + depth]
        dims = (((1,), (1 if across else 0,)), ((), ()))
        term = lax.dot_general(left[...], rhs, dims, preferred_element_type=f32)
        total = term if total is None else total + term
        at += depth
    out_ref[...] = total.astype(out_ref.dtype)


def product(lefts, rhs, kind, across=False, part=0, parts=1):
    rows = lefts[0].shape[0]
    depth = sum(left.shape[1] for left in lefts)
    tile = 2 * WIDE if len(lefts) == 1 else WIDE
    if across:
        columns = rhs.shape[0]
        rhs_spec = pl.BlockSpec((tile, depth), lambda j: (j, 0))
    else:
        columns = rhs.shape[1] // parts
        first = part * columns // tile
        rhs_spec = pl.BlockSpec((depth, tile), lambda j: (0, first + j))
    return pl.pallas_call(
        functools.partial(product_kernel, across),
        grid=(columns // tile,),
        in_specs=[pl.BlockSpec(left.shape, lambda j: (0, 0)) for left in lefts] + [rhs_spec],
        out_specs=pl.BlockSpec((rows, tile), lambda j: (0, j)),
        out_shape=jax.ShapeDtypeStruct((rows, columns), kind),
        compiler_params=params(),
        cost_estimate=cost(0.01),
        name="product",
    )(*lefts, rhs)


def scale_of(rows):
    return lax.rsqrt(jnp.mean(rows * rows, axis=-1, keepdims=True) + 1e-05)


def by_time(prompt_ref, piece_ref):
    both_kinds = jnp.concatenate([prompt_ref[...], piece_ref[...]], axis=0).astype(f32)
    return jnp.swapaxes(both_kinds, 0, 1)


def prepare_kernel(prompt_ref, piece_ref, prompt_cot_ref, piece_cot_ref, halo_ref, gain_ref, scaled_ref, cot_ref):
    i = pl.program_id(0)
    gain = gain_ref[...]

    @pl.when(i == 0)
    def _():
        rows = halo_ref[...]
        scaled_ref[0 : HALO * SEQS, :] = (rows * scale_of(rows) * gain).astype(bf16)

    rows = by_time(prompt_ref, piece_ref)
    count = rows.shape[0] * SEQS
    rows = rows.reshape(count, D)
    at = pl.multiple_of(HALO * SEQS + i * count, HALO * SEQS)
    scaled_ref[pl.ds(at, count), :] = (rows * scale_of(rows) * gain).astype(bf16)
    cot_ref[...] = by_time(prompt_cot_ref, piece_cot_ref).reshape(count, D).astype(bf16)


CHUNK = 16


def prepare(prompt, piece, prompt_cot, piece_cot, halo, gain):
    steps = prompt.shape[1]
    part = pl.BlockSpec((SEQS // 2, CHUNK, D), lambda i: (0, i, 0))
    rows = steps * SEQS
    return pl.pallas_call(
        prepare_kernel,
        grid=(steps // CHUNK,),
        in_specs=[
            part, part, part, part,
            pl.BlockSpec((HALO * SEQS, D), lambda i: (0, 0)),
            pl.BlockSpec((1, D), lambda i: (0, 0)),
        ],
        out_specs=[
            pl.BlockSpec((HALO * SEQS + rows, D), lambda i: (0, 0)),
            pl.BlockSpec((CHUNK * SEQS, D), lambda i: (i, 0)),
        ],
        out_shape=[
            jax.ShapeDtypeStruct((HALO * SEQS + rows, D), bf16),
            jax.ShapeDtypeStruct((rows, D), bf16),
        ],
        compiler_params=params(),
        cost_estimate=cost(5),
        name="prepare",
    )(prompt, piece, prompt_cot, piece_cot, halo, gain)


def norm_back(rows, scaled_grad, gain):
    inverse = scale_of(rows)
    unit = rows * inverse
    grad = scaled_grad * gain
    back = inverse * (grad - unit * jnp.mean(grad * unit, axis=-1, keepdims=True))
    return back, scaled_grad * unit


def finish_kernel(
    mixed_ref, grad_ref, grad_halo_ref,
    prompt_ref, piece_ref, prompt_cot_ref, piece_cot_ref, halo_ref, gain_ref,
    prompt_out, piece_out, prompt_grad, piece_grad, halo_grad, gain_grad,
):
    i = pl.program_id(0)
    gain = gain_ref[...]

    @pl.when(i == 0)
    def _():
        back, sums = norm_back(halo_ref[...], grad_halo_ref[...], gain)
        halo_grad[...] = back
        gain_grad[...] = jnp.sum(sums, axis=0, keepdims=True)

    half = SEQS // 2
    rows = by_time(prompt_ref, piece_ref)
    shape = rows.shape
    rows = rows.reshape(-1, D)
    back, sums = norm_back(rows, grad_ref[...], gain)
    gain_grad[...] += jnp.sum(sums, axis=0, keepdims=True)
    back = jnp.swapaxes(back.reshape(shape), 0, 1)
    prompt_grad[...] = back[:half] + prompt_cot_ref[...].astype(f32)
    piece_grad[...] = back[half:] + piece_cot_ref[...].astype(f32)
    mixed = jnp.swapaxes((mixed_ref[...] + rows).reshape(shape), 0, 1)
    prompt_out[...] = mixed[:half].astype(bf16)
    piece_out[...] = mixed[half:].astype(bf16)


def finish(mixed, grad, prompt, piece, prompt_cot, piece_cot, halo, gain):
    steps = prompt.shape[1]
    part = pl.BlockSpec((SEQS // 2, CHUNK, D), lambda i: (0, i, 0))
    first = pl.BlockSpec((HALO * SEQS, D), lambda i: (0, 0))
    shifted = pl.BlockSpec(
        (pl.Element(CHUNK * SEQS), pl.Element(D)),
        lambda i: (pl.multiple_of(HALO * SEQS + i * (CHUNK * SEQS), HALO * SEQS), 0),
    )
    return pl.pallas_call(
        finish_kernel,
        grid=(steps // CHUNK,),
        in_specs=[
            pl.BlockSpec((CHUNK * SEQS, D), lambda i: (i, 0)),
            shifted, first,
            part, part, part, part,
            first,
            pl.BlockSpec((1, D), lambda i: (0, 0)),
        ],
        out_specs=[part, part, part, part, first, pl.BlockSpec((1, D), lambda i: (0, 0))],
        out_shape=[
            jax.ShapeDtypeStruct(prompt.shape, bf16),
            jax.ShapeDtypeStruct(piece.shape, bf16),
            jax.ShapeDtypeStruct(prompt.shape, f32),
            jax.ShapeDtypeStruct(piece.shape, f32),
            jax.ShapeDtypeStruct((HALO * SEQS, D), f32),
            jax.ShapeDtypeStruct((1, D), f32),
        ],
        compiler_params=params(),
        cost_estimate=cost(0.01),
        name="finish",
    )(mixed, grad, grad, prompt, piece, prompt_cot, piece_cot, halo, gain)


def front_kernel(mix_ref, fw_ref, fb_ref, sel_ref, act_ref, proj_ref):
    j = pl.program_id(0)
    steps = act_ref.shape[0]
    chunk = 16
    taps = [fw_ref[k : k + 1, :] for k in range(KERNEL)]
    bias = fb_ref[0:1, :]

    @pl.when(j == 0)
    def _():
        proj_ref[...] = jnp.zeros_like(proj_ref)

    def step(i, _):
        t = i * chunk
        x = mix_ref[pl.ds(t, chunk + HALO)].astype(f32)
        v = bias[None] + taps[0][None] * x[1 : 1 + chunk]
        for k in range(1, KERNEL):
            v = v + taps[k][None] * x[1 + k : 1 + k + chunk]
        act = v * sigmoid(v)
        act_ref[pl.ds(t, chunk)] = act
        low = act.reshape(chunk * SEQS, act.shape[-1]).astype(bf16)
        r = pl.multiple_of(t * SEQS, chunk * SEQS)
        proj_ref[pl.ds(r, chunk * SEQS), :] += jnp.dot(low, sel_ref[...], preferred_element_type=f32)
        return 0

    lax.fori_loop(0, steps // chunk, step, 0)


def front(mixture, fw, fb, select_pad, steps):
    channels = fw.shape[1]
    return pl.pallas_call(
        front_kernel,
        grid=(channels // WIDE,),
        in_specs=[
            pl.BlockSpec((steps + HALO, SEQS, WIDE), lambda j: (0, 0, j)),
            pl.BlockSpec((KERNEL, WIDE), lambda j: (0, j)),
            pl.BlockSpec((1, WIDE), lambda j: (0, j)),
            pl.BlockSpec((WIDE, LANES), lambda j: (j, 0)),
        ],
        out_specs=[
            pl.BlockSpec((steps, SEQS, WIDE), lambda j: (0, 0, j)),
            pl.BlockSpec((steps * SEQS, LANES), lambda j: (0, 0)),
        ],
        out_shape=[
            jax.ShapeDtypeStruct((steps, SEQS, channels), f32),
            jax.ShapeDtypeStruct((steps * SEQS, LANES), f32),
        ],
        compiler_params=params(),
        cost_estimate=cost(16),
        name="front",
    )(mixture, fw, fb, select_pad)


def pair(a, b):
    return jnp.concatenate([a, b], axis=0).astype(bf16)


def both(v):
    return pair(v, v)


def halves(v):
    v = v.astype(f32)
    return v[:SEQS], v[SEQS:]


def folded(v):
    a, b = halves(v)
    return a + b


def spread_maps(proj_ref, select_ref, first, count, store):
    steps = proj_ref.shape[0] // SEQS
    chunk = 32

    def step(i, _):
        r = pl.multiple_of(i * chunk * SEQS, chunk * SEQS)
        rows = proj_ref[pl.ds(r, chunk * SEQS), :].astype(bf16)
        for n in range(0, count, 2):
            at = (first - RANK + n) * LANES
            wide = jnp.dot(rows, select_ref[:, at : at + 2 * LANES], preferred_element_type=f32)
            wide = wide.reshape(chunk, SEQS, 2 * LANES)
            store(i * chunk, chunk, n, wide[:, :, :LANES], wide[:, :, LANES:])
        return 0

    lax.fori_loop(0, steps // chunk, step, 0)


def store_plain(ref):
    def store(t, count, n, a, b):
        ref[pl.ds(t, count), n] = a
        ref[pl.ds(t, count), n + 1] = b

    return store


def store_pairs(ref):
    def store(t, count, n, a, b):
        ref[pl.ds(t, count), n // 2] = jnp.concatenate([a, b], axis=1).astype(bf16)

    return store


PAIRS = STATES // 2
RUN = 8


def piece_kernel(
    proj_ref, act_ref, gate_ref, gg_ref, stepw_ref, sbias_ref, rate_ref, select_ref,
    dt_ref, sig_ref, yg_ref, silu_ref, slope_ref, fwd_ref, bwd_ref, tot_ref,
    b_scr, c_scr, time_scr, acc_scr,
):
    j = pl.program_id(0)
    steps = dt_ref.shape[0]
    half = SEQS // 2
    groups = fwd_ref.shape[0] // half

    @pl.when(j == 0)
    def _():
        def store_groups(t, count, n, a, b):
            for group in range(groups):
                rows = slice(group * half, (group + 1) * half)
                parts = [a[:, rows], a[:, rows], b[:, rows], b[:, rows]]
                b_scr[group, pl.ds(t, count), n // 2] = jnp.concatenate(parts, axis=1).astype(bf16)

        spread_maps(proj_ref, select_ref, RANK, STATES, store_groups)
        spread_maps(proj_ref, select_ref, RANK + STATES, STATES, store_pairs(c_scr))

    chunk = 8
    sbias = sbias_ref[0:1, :]

    def prep(i, total):
        t = i * chunk
        r = pl.multiple_of(t * SEQS, chunk * SEQS)
        rank = proj_ref[pl.ds(r, chunk * SEQS), :].astype(bf16)
        pre = jnp.dot(rank, stepw_ref[...], preferred_element_type=f32).reshape(chunk, SEQS, WIDE)
        pre = pre + sbias[None]
        small = jnp.exp2(jnp.abs(pre) * -LOG2E)
        one = 1.0 + small
        inverse = 1.0 / one
        dt = jnp.maximum(pre, 0.0) + (jnp.log(one) + (small - (one - 1.0)) * inverse)
        dt_ref[pl.ds(t, chunk)] = dt
        sig_ref[pl.ds(t, chunk)] = jnp.where(pre >= 0.0, inverse, small * inverse).astype(bf16)
        gate = gate_ref[pl.ds(t + HALO, chunk)]
        gg = gg_ref[pl.ds(t, chunk)]
        sig = sigmoid(gate)
        silu = gate * sig
        yg_ref[pl.ds(t, chunk)] = gg * silu
        silu_ref[pl.ds(t, chunk)] = silu.astype(bf16)
        slope_ref[pl.ds(t, chunk)] = (gg * (sig + silu * (1.0 - sig))).astype(bf16)
        for k in range(chunk):
            total = total + dt[k]
            time_scr[t + k] = total
        return total

    total = lax.fori_loop(0, steps // chunk, prep, jnp.zeros((SEQS, WIDE), f32))
    tot_ref[...] = total

    units = []

    low = lax.broadcasted_iota(jnp.int32, (SEQS, LANES), 0) < half
    packed = [
        jnp.where(low, rate_ref[n : n + 1, :LANES], rate_ref[n : n + 1, LANES:])
        for n in range(STATES)
    ]
    packed = [pair(packed[2 * p], packed[2 * p + 1]) for p in range(PAIRS)]

    def forward_unit(group):
        rows = slice(group * half, (group + 1) * half)

        def pack(v):
            return jnp.concatenate([v[rows, :LANES], v[rows, LANES:]], axis=0)

        whole = pack(total)

        def vectors(t):
            return both(whole - pack(time_scr[t])), both(pack(dt_ref[t] * act_ref[t]))

        def out(n, value):
            fwd_ref[rows, n, :LANES] = value[:half]
            fwd_ref[rows, n, LANES:] = value[half:]

        return packed, vectors, lambda t, p: b_scr[group, t, p], out

    def backward_unit(cols):
        mine = [jnp.broadcast_to(rate_ref[n : n + 1, cols], (SEQS, LANES)) for n in range(STATES)]
        mine = [pair(mine[2 * p], mine[2 * p + 1]) for p in range(PAIRS)]

        def vectors(t):
            return both(time_scr[t, :, cols]), both(yg_ref[t, :, cols])

        def out(n, value):
            bwd_ref[:, n, cols] = value

        return mine, vectors, lambda t, p: c_scr[t, p], out

    for group in range(groups):
        units.append(forward_unit(group))
    for part in range(WIDE // LANES):
        units.append(backward_unit(slice(part * LANES, (part + 1) * LANES)))
    acc_scr[...] = jnp.zeros_like(acc_scr)

    def run(i, _):
        for k, (rates, vectors, map_at, _) in enumerate(units):
            sums = [None] * PAIRS
            for m in range(RUN):
                t = i * RUN + m
                time, drive = vectors(t)
                for p in range(PAIRS):
                    term = jnp.exp2(time * rates[p]) * drive * map_at(t, p)
                    sums[p] = term if m == 0 else sums[p] + term
            for p in range(PAIRS):
                a, b = halves(sums[p])
                acc_scr[k, 2 * p] += a
                acc_scr[k, 2 * p + 1] += b
        return 0

    lax.fori_loop(0, steps // RUN, run, 0)
    for k, (_, _, _, out) in enumerate(units):
        for n in range(STATES):
            out(n, acc_scr[k, n])


def piece(proj, act, gate, gated_grad, step_pad, sbias, rate, select, groups):
    steps, _, channels = act.shape
    grid = channels // WIDE
    wide = lambda j: (0, 0, j)
    flat = pl.BlockSpec((steps, SEQS, WIDE), wide)
    shape = (steps, SEQS, channels)
    return pl.pallas_call(
        piece_kernel,
        grid=(grid,),
        in_specs=[
            pl.BlockSpec((steps * SEQS, LANES), lambda j: (0, 0)),
            flat,
            pl.BlockSpec((steps + HALO, SEQS, WIDE), wide),
            flat,
            pl.BlockSpec((LANES, WIDE), lambda j: (0, j)),
            pl.BlockSpec((1, WIDE), lambda j: (0, j)),
            pl.BlockSpec((STATES, WIDE), lambda j: (0, j)),
            pl.BlockSpec(select.shape, lambda j: (0, 0)),
        ],
        out_specs=[
            flat, flat, flat, flat, flat,
            pl.BlockSpec((groups * SEQS // 2, STATES, WIDE), wide),
            pl.BlockSpec((SEQS, STATES, WIDE), wide),
            pl.BlockSpec((SEQS, WIDE), lambda j: (0, j)),
        ],
        out_shape=[
            jax.ShapeDtypeStruct(shape, f32),
            jax.ShapeDtypeStruct(shape, bf16),
            jax.ShapeDtypeStruct(shape, f32),
            jax.ShapeDtypeStruct(shape, bf16),
            jax.ShapeDtypeStruct(shape, bf16),
            jax.ShapeDtypeStruct((groups * SEQS // 2, STATES, channels), f32),
            jax.ShapeDtypeStruct((SEQS, STATES, channels), f32),
            jax.ShapeDtypeStruct((SEQS, channels), f32),
        ],
        scratch_shapes=[
            pltpu.VMEM((groups, steps, PAIRS, 2 * SEQS, LANES), bf16),
            pltpu.VMEM((steps, PAIRS, 2 * SEQS, LANES), bf16),
            pltpu.VMEM((steps, SEQS, WIDE), f32),
            pltpu.VMEM((groups + WIDE // LANES, STATES, SEQS, LANES), f32),
        ],
        compiler_params=params(),
        cost_estimate=cost(60),
        name="piece",
    )(proj, act, gate, gated_grad, step_pad, sbias, rate, select)


def chain_kernel(
    one_hot_ref, ahead_ref, behind_ref, branch_ref, time_ref, rate_ref, start_out, end_out,
    moved_ref, got, got_time, back, done, sems, time_sems, back_sems,
):
    size = got.shape[0]
    width = got.shape[2]
    count = PROMPTS * STATES
    sequels = branch_ref.shape[0]
    me = lax.axis_index("fsdp")
    for p in range(PROMPTS):
        rows = slice(p * STATES, (p + 1) * STATES)
        total = one_hot_ref[0, p] * branch_ref[0]
        for k in range(1, sequels):
            total = total + one_hot_ref[k, p] * branch_ref[k]
        moved_ref[0 * count + p * STATES : 0 * count + (p + 1) * STATES] = ahead_ref[p].astype(bf16)
        moved_ref[1 * count + p * STATES : 1 * count + (p + 1) * STATES] = behind_ref[p].astype(bf16)
        moved_ref[2 * count + p * STATES : 2 * count + (p + 1) * STATES] = total.astype(bf16)
    barrier = pltpu.get_barrier_semaphore()
    for d in range(1, size):
        peer = lax.rem(me + d, size)
        pl.semaphore_signal(barrier, inc=1, device_id={"fsdp": peer}, device_id_type=pl.DeviceIdType.MESH)
    pl.semaphore_wait(barrier, size - 1)

    def columns(device):
        return pl.ds(pl.multiple_of(device * width, width), width)

    copies = []
    for d in range(1, size):
        peer = lax.rem(me + d, size)
        for src, dst, sem in ((moved_ref, got, sems), (time_ref, got_time, time_sems)):
            copy = pltpu.make_async_remote_copy(
                src_ref=src.at[:, columns(peer)],
                dst_ref=dst.at[me],
                send_sem=sem.at[0, d],
                recv_sem=sem.at[1, d],
                device_id={"fsdp": peer},
                device_id_type=pl.DeviceIdType.MESH,
            )
            copy.start()
            copies.append(copy)
    got[me] = moved_ref[:, columns(me)]
    got_time[me] = time_ref[:, columns(me)]
    for copy in copies:
        copy.wait()

    rate = jnp.concatenate([rate_ref[...]] * PROMPTS, axis=0)
    branch = jnp.zeros((count, width), f32)
    state = jnp.zeros((count, width), f32)
    decays = []
    for k in range(size):
        time = jnp.concatenate(
            [jnp.broadcast_to(got_time[k, p : p + 1, :], (STATES, width)) for p in range(PROMPTS)], axis=0
        )
        decays.append(jnp.exp2(rate * time))
        back[k, 0:count] = state.astype(bf16)
        state = decays[k] * state + got[k, 0:count].astype(f32)
        branch = branch + got[k, 2 * count : 3 * count].astype(f32)
    grad = branch
    for k in range(size - 1, -1, -1):
        back[k, count : 2 * count] = grad.astype(bf16)
        grad = decays[k] * grad + got[k, count : 2 * count].astype(f32)
    last = state.astype(bf16)
    for k in range(size):
        back[k, 2 * count : 3 * count] = last
    copies = []
    for d in range(1, size):
        peer = lax.rem(me + d, size)
        copy = pltpu.make_async_remote_copy(
            src_ref=back.at[peer],
            dst_ref=done.at[me],
            send_sem=back_sems.at[0, d],
            recv_sem=back_sems.at[1, d],
            device_id={"fsdp": peer},
            device_id_type=pl.DeviceIdType.MESH,
        )
        copy.start()
        copies.append(copy)
    done[me] = back[me]
    for copy in copies:
        copy.wait()
    for k in range(size):
        columns_k = slice(k * width, (k + 1) * width)
        last = []
        for p in range(PROMPTS):
            rows = slice(p * STATES, (p + 1) * STATES)
            start_out[p, :, columns_k] = done[k, rows].astype(f32)
            rows = slice(count + p * STATES, count + (p + 1) * STATES)
            end_out[p, :, columns_k] = done[k, rows].astype(f32)
            rows = slice(2 * count + p * STATES, 2 * count + (p + 1) * STATES)
            last.append(done[k, rows].astype(f32))
        for q in range(sequels):
            total = one_hot_ref[q, 0] * last[0]
            for p in range(1, PROMPTS):
                total = total + one_hot_ref[q, p] * last[p]
            start_out[PROMPTS + q, :, columns_k] = total
            end_out[PROMPTS + q, :, columns_k] = jnp.zeros_like(total)


def chain(one_hot, ahead, behind, branch, time, rate):
    size = lax.axis_size("fsdp")
    channels = ahead.shape[2]
    rows = 3 * PROMPTS * STATES
    width = channels // size
    own = lax.dynamic_slice_in_dim(rate, lax.axis_index("fsdp") * width, width, 1)
    whole = pl.BlockSpec(memory_space=pltpu.VMEM)
    shape = (PROMPTS + branch.shape[0], STATES, channels)
    return pl.pallas_call(
        chain_kernel,
        in_specs=[pl.BlockSpec(memory_space=pltpu.SMEM)] + [whole] * 5,
        out_specs=[whole] * 2,
        out_shape=[jax.ShapeDtypeStruct(shape, f32)] * 2,
        scratch_shapes=[
            pltpu.VMEM((rows, channels), bf16),
            pltpu.VMEM((size, rows, width), bf16),
            pltpu.VMEM((size, SEQS, width), f32),
            pltpu.VMEM((size, rows, width), bf16),
            pltpu.VMEM((size, rows, width), bf16),
            pltpu.SemaphoreType.DMA((2, size)),
            pltpu.SemaphoreType.DMA((2, size)),
            pltpu.SemaphoreType.DMA((2, size)),
        ],
        compiler_params=params(collective_id=1, has_side_effects=True),
        cost_estimate=cost(25),
        name="chain",
    )(one_hot, ahead, behind, branch, time, own)


TILES = [slice(k * LANES, (k + 1) * LANES) for k in range(WIDE // LANES)]


def forward_kernel(
    proj_ref, dt_ref, act_ref, yg_ref, silu_ref, slope_ref, rate_ref, start_ref, skip_ref, select_ref,
    gated_ref, hist_ref, gategrad_ref, skipg_ref,
    b_scr, c_scr,
):
    j = pl.program_id(0)
    steps = dt_ref.shape[0]

    @pl.when(j == 0)
    def _():
        spread_maps(proj_ref, select_ref, RANK, STATES, store_plain(b_scr))
        spread_maps(proj_ref, select_ref, RANK + STATES, STATES, store_pairs(c_scr))

    rates = [jnp.broadcast_to(rate_ref[n : n + 1, :], (SEQS, LANES)) for n in range(STATES)]
    skip = jnp.broadcast_to(skip_ref[0:1, :], (SEQS, LANES))
    gategrad_ref[0:HALO] = jnp.zeros((HALO, SEQS, LANES), bf16)
    unroll = 8

    def run(i, carry):
        h, skip_sum = carry
        for k in range(unroll):
            t = i * unroll + k
            dt = dt_ref[t]
            act = act_ref[t]
            u = dt * act
            new = []
            y = None
            for p in range(PAIRS):
                for n in (2 * p, 2 * p + 1):
                    new.append(jnp.exp2(dt * rates[n]) * h[n] + u * b_scr[t, n])
                low = pair(new[2 * p], new[2 * p + 1])
                hist_ref[t + 1, p] = low
                term = low * c_scr[t, p]
                y = term if p == 0 else y + term
            h = tuple(new)
            mixed = folded(y) + skip * act
            gated_ref[t] = (mixed * silu_ref[t].astype(f32)).astype(bf16)
            gategrad_ref[t + HALO] = (mixed * slope_ref[t].astype(f32)).astype(bf16)
            skip_sum = skip_sum + yg_ref[t] * act
        return h, skip_sum

    start = tuple(start_ref[:, n, :] for n in range(STATES))
    for p in range(PAIRS):
        hist_ref[0, p] = pair(start[2 * p], start[2 * p + 1])
    _, skip_sum = lax.fori_loop(0, steps // unroll, run, (start, jnp.zeros((SEQS, LANES), f32)))
    skipg_ref[...] = jnp.sum(skip_sum, axis=0, keepdims=True)


def forward(proj, dt, act, yg, silu, slope, rate, start, skip, select):
    steps, _, channels = act.shape
    grid = channels // LANES
    tile = lambda j: (0, 0, j)
    flat = pl.BlockSpec((steps, SEQS, LANES), tile)
    parts = len(TILES)
    return pl.pallas_call(
        forward_kernel,
        grid=(grid,),
        in_specs=[
            pl.BlockSpec((steps * SEQS, LANES), lambda j: (0, 0)),
            flat, flat, flat, flat, flat,
            pl.BlockSpec((STATES, LANES), lambda j: (0, j)),
            pl.BlockSpec((SEQS, STATES, LANES), tile),
            pl.BlockSpec((1, LANES), lambda j: (0, j)),
            pl.BlockSpec(select.shape, lambda j: (0, 0)),
        ],
        out_specs=[
            flat,
            pl.BlockSpec(
                (None, None, steps + 1, PAIRS, 2 * SEQS, LANES),
                lambda j: (j // parts, j % parts, 0, 0, 0, 0),
            ),
            pl.BlockSpec((steps + HALO, SEQS, LANES), tile),
            pl.BlockSpec((1, LANES), lambda j: (0, j)),
        ],
        out_shape=[
            jax.ShapeDtypeStruct((steps, SEQS, channels), bf16),
            jax.ShapeDtypeStruct((grid // parts, parts, steps + 1, PAIRS, 2 * SEQS, LANES), bf16),
            jax.ShapeDtypeStruct((steps + HALO, SEQS, channels), bf16),
            jax.ShapeDtypeStruct((1, channels), f32),
        ],
        scratch_shapes=[
            pltpu.VMEM((steps, STATES, SEQS, LANES), f32),
            pltpu.VMEM((steps, PAIRS, 2 * SEQS, LANES), bf16),
        ],
        compiler_params=params(),
        cost_estimate=cost(50),
        name="forward_scan",
    )(proj, dt, act, yg, silu, slope, rate, start, skip, select)


def backward_kernel(
    proj_ref, dt_ref, sig_ref, act_ref, yg_ref, rate_ref, end_ref, skip_ref,
    hist_ref, rank_t_ref, stepw_t_ref, pick_ref, select_ref,
    act_grad_ref, stepg_ref, biasg_ref, decayg_ref, projg_ref,
    b_scr, c_scr, db_scr, dc_scr, pre_scr, acc_scr, decay_scr, ge_scr, sum_scr,
):
    j = pl.program_id(0)
    steps = dt_ref.shape[0]

    @pl.when(j == 0)
    def _():
        spread_maps(proj_ref, select_ref, RANK, STATES, store_pairs(b_scr))
        spread_maps(proj_ref, select_ref, RANK + STATES, STATES, store_plain(c_scr))

        def clear(t, _):
            for p in range(PAIRS):
                db_scr[t, p] = jnp.zeros((2 * SEQS, LANES), bf16)
                dc_scr[t, p] = jnp.zeros((2 * SEQS, LANES), bf16)
            return 0

        lax.fori_loop(0, steps, clear, 0)
        acc_scr[...] = jnp.zeros_like(acc_scr)

    decay_scr[...] = jnp.zeros_like(decay_scr)
    sum_scr[...] = jnp.zeros_like(sum_scr)
    for n in range(STATES):
        ge_scr[n] = end_ref[:, n, :]

    def run(i, _):
        base = steps - (i + 1) * RUN
        db = [[None] * PAIRS for _ in range(RUN)]
        dc = [[None] * PAIRS for _ in range(RUN)]
        for part, cols in enumerate(TILES):
            rates = [jnp.broadcast_to(rate_ref[n : n + 1, cols], (SEQS, LANES)) for n in range(STATES)]
            low_rates = [pair(rates[2 * p], rates[2 * p + 1]) for p in range(PAIRS)]
            skip = jnp.broadcast_to(skip_ref[0:1, cols], (SEQS, LANES))
            ge = [ge_scr[n, :, cols] for n in range(STATES)]
            bias_sum = jnp.zeros((SEQS, LANES), f32)
            decay = [None] * PAIRS
            for k in range(RUN - 1, -1, -1):
                t = base + k
                dt = dt_ref[t, :, cols]
                act = act_ref[t, :, cols]
                yg = yg_ref[t, :, cols]
                u2 = both(dt * act)
                dt2 = both(dt)
                yg2 = both(yg)
                du = None
                ddt = None
                for p in range(PAIRS):
                    g = [ge[n] + yg * c_scr[t, n] for n in (2 * p, 2 * p + 1)]
                    g2 = pair(*g)
                    term = yg2 * hist_ref[part, t + 1, p]
                    dc[k][p] = term if part == 0 else dc[k][p] + term
                    term = g2 * u2
                    db[k][p] = term if part == 0 else db[k][p] + term
                    term = g2 * b_scr[t, p]
                    du = term if p == 0 else du + term
                    gn = [jnp.exp2(dt * rates[2 * p + m]) * g[m] for m in (0, 1)]
                    ge[2 * p], ge[2 * p + 1] = gn
                    q = pair(*gn) * hist_ref[part, t, p]
                    term = q * dt2
                    decay[p] = term if decay[p] is None else decay[p] + term
                    term = q * low_rates[p]
                    ddt = term if p == 0 else ddt + term
                du = folded(du)
                pre_grad = (du * act + folded(ddt) * LN2) * sig_ref[t, :, cols].astype(f32)
                pre_scr[t, :, cols] = pre_grad.astype(bf16)
                act_grad_ref[t, :, cols] = yg * skip + du * dt
                bias_sum = bias_sum + pre_grad
                if part == len(TILES) - 1:
                    for p in range(PAIRS):
                        dc_scr[t, p] = dc[k][p] + dc_scr[t, p]
                        db_scr[t, p] = db[k][p] + db_scr[t, p]
            for p in range(PAIRS):
                a, b = halves(decay[p])
                decay_scr[2 * p, :, cols] += a
                decay_scr[2 * p + 1, :, cols] += b
            for n in range(STATES):
                ge_scr[n, :, cols] = ge[n]
            sum_scr[:, cols] += bias_sum
        return 0

    lax.fori_loop(0, steps // RUN, run, 0)
    for n in range(STATES):
        decayg_ref[n : n + 1, :] = jnp.sum(decay_scr[n] * rate_ref[n : n + 1, :], axis=0, keepdims=True) * LN2
    biasg_ref[...] = jnp.sum(sum_scr[...], axis=0, keepdims=True)

    pre_low = pre_scr[...].reshape(steps * SEQS, WIDE)
    stepg_ref[...] = jnp.dot(rank_t_ref[...], pre_low, preferred_element_type=f32)
    acc_scr[...] += jnp.dot(pre_low, stepw_t_ref[...], preferred_element_type=f32)

    @pl.when(j == pl.num_programs(0) - 1)
    def _():
        chunk = 32
        even = lax.broadcasted_iota(jnp.int32, (chunk, SEQS, LANES), 2) % 2 == 0

        def step(i, _):
            t = i * chunk
            total = jnp.zeros((chunk * 2 * SEQS, LANES), f32)
            for p in range(PAIRS):
                rows = jnp.concatenate([db_scr[pl.ds(t, chunk), p], dc_scr[pl.ds(t, chunk), p]], axis=2)
                rows = rows.reshape(chunk * 2 * SEQS, 2 * LANES)
                total = total + jnp.dot(rows, pick_ref[p], preferred_element_type=f32)
            total = total.reshape(chunk, 2 * SEQS, LANES)
            total = jnp.where(even, total[:, :SEQS], total[:, SEQS:]).reshape(chunk * SEQS, LANES)
            r = pl.multiple_of(t * SEQS, chunk * SEQS)
            projg_ref[pl.ds(r, chunk * SEQS), :] = (acc_scr[pl.ds(r, chunk * SEQS), :] + total).astype(bf16)
            return 0

        lax.fori_loop(0, steps // chunk, step, 0)


def backward(proj, dt, sig, act, yg, rate, end, skip, hist, rank_t, stepw_t, pick, select):
    steps, _, channels = act.shape
    grid = channels // WIDE
    tile = lambda j: (0, 0, j)
    whole = lambda j: (0, 0)
    flat = pl.BlockSpec((steps, SEQS, WIDE), tile)
    sums = pltpu.VMEM((steps, PAIRS, 2 * SEQS, LANES), bf16)
    return pl.pallas_call(
        backward_kernel,
        grid=(grid,),
        in_specs=[
            pl.BlockSpec((steps * SEQS, LANES), whole),
            flat, flat, flat, flat,
            pl.BlockSpec((STATES, WIDE), lambda j: (0, j)),
            pl.BlockSpec((SEQS, STATES, WIDE), tile),
            pl.BlockSpec((1, WIDE), lambda j: (0, j)),
            pl.BlockSpec(
                (None, len(TILES), steps + 1, PAIRS, 2 * SEQS, LANES), lambda j: (j, 0, 0, 0, 0, 0)
            ),
            pl.BlockSpec((RANK, steps * SEQS), whole),
            pl.BlockSpec((WIDE, LANES), lambda j: (j, 0)),
            pl.BlockSpec(pick.shape, lambda j: (0, 0, 0)),
            pl.BlockSpec(select.shape, whole),
        ],
        out_specs=[
            flat,
            pl.BlockSpec((RANK, WIDE), lambda j: (0, j)),
            pl.BlockSpec((1, WIDE), lambda j: (0, j)),
            pl.BlockSpec((STATES, WIDE), lambda j: (0, j)),
            pl.BlockSpec((steps * SEQS, LANES), whole),
        ],
        out_shape=[
            jax.ShapeDtypeStruct((steps, SEQS, channels), f32),
            jax.ShapeDtypeStruct((RANK, channels), f32),
            jax.ShapeDtypeStruct((1, channels), f32),
            jax.ShapeDtypeStruct((STATES, channels), f32),
            jax.ShapeDtypeStruct((steps * SEQS, LANES), bf16),
        ],
        scratch_shapes=[
            sums,
            pltpu.VMEM((steps, STATES, SEQS, LANES), f32),
            sums, sums,
            pltpu.VMEM((steps, SEQS, WIDE), bf16),
            pltpu.VMEM((steps * SEQS, LANES), f32),
            pltpu.VMEM((STATES, SEQS, WIDE), f32),
            pltpu.VMEM((STATES, SEQS, WIDE), f32),
            pltpu.VMEM((SEQS, WIDE), f32),
        ],
        compiler_params=params(),
        cost_estimate=cost(90),
        name="backward_scan",
    )(proj, dt, sig, act, yg, rate, end, skip, hist, rank_t, stepw_t, pick, select)


def filter_back_kernel(
    mix_ref, act_ref, act_grad_ref, projg_ref, projg_t_ref, sel_ref, fw_ref, fb_ref,
    mixgrad_ref, selg_ref, fwg_ref, fbg_ref,
    dv_scr,
):
    steps = act_ref.shape[0]
    chunk = 16
    taps = [fw_ref[k : k + 1, :] for k in range(KERNEL)]
    bias = fb_ref[0:1, :]
    zero = jnp.zeros((HALO, SEQS, WIDE), f32)
    dv_scr[0:HALO] = zero
    dv_scr[steps + HALO :] = zero

    def step(i, sums):
        t = i * chunk
        x = mix_ref[pl.ds(t, chunk + HALO)].astype(f32)
        v = bias[None] + taps[0][None] * x[1 : 1 + chunk]
        for k in range(1, KERNEL):
            v = v + taps[k][None] * x[1 + k : 1 + k + chunk]
        sig = sigmoid(v)
        r = pl.multiple_of(t * SEQS, chunk * SEQS)
        more = contract_cols(projg_ref[pl.ds(r, chunk * SEQS), :], sel_ref[...])
        total = act_grad_ref[pl.ds(t, chunk)] + more.reshape(chunk, SEQS, WIDE)
        dv = total * (sig * (1.0 + v * (1.0 - sig)))
        dv_scr[pl.ds(t + HALO, chunk)] = dv
        new = [sums[0] + jnp.sum(dv, axis=0)]
        for k in range(KERNEL):
            new.append(sums[1 + k] + jnp.sum(dv * x[1 + k : 1 + k + chunk], axis=0))
        return tuple(new)

    sums = lax.fori_loop(
        0, steps // chunk, step, tuple(jnp.zeros((SEQS, WIDE), f32) for _ in range(KERNEL + 1))
    )
    fbg_ref[...] = jnp.sum(sums[0], axis=0, keepdims=True)
    for k in range(KERNEL):
        fwg_ref[k : k + 1, :] = jnp.sum(sums[1 + k], axis=0, keepdims=True)

    def spread(t, count):
        dv = dv_scr[pl.ds(t, count + HALO)]
        out = taps[KERNEL - 1][None] * dv[0:count]
        for k in range(KERNEL - 1):
            s = KERNEL - 1 - k
            out = out + taps[k][None] * dv[s : s + count]
        mixgrad_ref[pl.ds(t, count)] = out.astype(bf16)

    def out_step(i, _):
        spread(i * chunk, chunk)
        return 0

    lax.fori_loop(0, steps // chunk, out_step, 0)
    spread(steps, HALO)
    low = act_ref[...].reshape(steps * SEQS, WIDE).astype(bf16)
    selg_ref[...] = jnp.dot(projg_t_ref[...], low, preferred_element_type=f32)


def filter_back(mixture, act, act_grad, projg, projg_t, select_pad, fw, fb):
    steps, _, channels = act.shape
    grid = channels // WIDE
    wide = lambda j: (0, 0, j)
    whole = lambda j: (0, 0)
    cols = lambda j: (0, j)
    return pl.pallas_call(
        filter_back_kernel,
        grid=(grid,),
        in_specs=[
            pl.BlockSpec((steps + HALO, SEQS, WIDE), wide),
            pl.BlockSpec((steps, SEQS, WIDE), wide),
            pl.BlockSpec((steps, SEQS, WIDE), wide),
            pl.BlockSpec((steps * SEQS, LANES), whole),
            pl.BlockSpec((LANES, steps * SEQS), whole),
            pl.BlockSpec((WIDE, LANES), lambda j: (j, 0)),
            pl.BlockSpec((KERNEL, WIDE), cols),
            pl.BlockSpec((1, WIDE), cols),
        ],
        out_specs=[
            pl.BlockSpec((steps + HALO, SEQS, WIDE), wide),
            pl.BlockSpec((LANES, WIDE), cols),
            pl.BlockSpec((KERNEL, WIDE), cols),
            pl.BlockSpec((1, WIDE), cols),
        ],
        out_shape=[
            jax.ShapeDtypeStruct((steps + HALO, SEQS, channels), bf16),
            jax.ShapeDtypeStruct((LANES, channels), f32),
            jax.ShapeDtypeStruct((KERNEL, channels), f32),
            jax.ShapeDtypeStruct((1, channels), f32),
        ],
        scratch_shapes=[pltpu.VMEM((steps + 2 * HALO, SEQS, WIDE), f32)],
        compiler_params=params(),
        cost_estimate=cost(20),
        name="filter_back",
    )(mixture, act, act_grad, projg, projg_t, select_pad, fw, fb)


def send(src, dst, send_sem, recv_sem, peer, axis="fsdp"):
    return pltpu.make_async_remote_copy(
        src_ref=src,
        dst_ref=dst,
        send_sem=send_sem,
        recv_sem=recv_sem,
        device_id={axis: peer},
        device_id_type=pl.DeviceIdType.MESH,
    )


def greet(others):
    barrier = pltpu.get_barrier_semaphore()
    for axis, peer in others:
        pl.semaphore_signal(barrier, inc=1, device_id={axis: peer}, device_id_type=pl.DeviceIdType.MESH)
    pl.semaphore_wait(barrier, len(others))


def flipped(index, bit):
    return index + (1 - 2 * (index // bit % 2)) * bit


FIRST, SECOND = (0, 1, 2, 3), (4, 5)
TRADED = (2, 3, 4, 5)


def gather_kernel(
    rows_ref, select_ref, out_ref, in_ref, all_rows, all_select, all_out, all_in,
    local_sems, own_send, own_recv, pass_send, pass_recv, core_send, core_recv, trade_send, trade_recv,
):
    me = lax.axis_index("fsdp")
    mz = lax.axis_index("replica")
    a, b = flipped(me, 2), flipped(me, 4)
    corner = flipped(a, 4)
    twin = flipped(me, 1)
    mate = flipped(mz, 1)
    greet([("fsdp", a), ("fsdp", b), ("fsdp", twin), ("replica", mate)])
    kinds = ((rows_ref, all_rows), (select_ref, all_select), (out_ref, all_out), (in_ref, all_in))

    def span(piece, side):
        if piece < 2:
            return piece, 0, kinds[piece][0].shape[0]
        kind = 2 + piece % 2
        quarter = kinds[kind][0].shape[0] // 4
        return kind, side * (2 * quarter) + (quarter if piece in SECOND else 0), quarter

    def place(owner, piece, side):
        kind, start, count = span(piece, side)
        first = owner * kinds[kind][0].shape[0] + start
        return kinds[kind][1].at[pl.ds(pl.multiple_of(first, 16), count)]

    def mine(piece, side):
        kind, start, count = span(piece, side)
        return kinds[kind][0].at[pl.ds(pl.multiple_of(start, 16), count) if piece in TRADED else pl.ds(0, count)]

    side = mz % 2
    other = 1 - side
    started = []

    def start(copy):
        copy.start()
        started.append(copy)

    def own_copy(piece, k, peer, owner):
        return send(mine(piece, side), place(owner, piece, side), own_send.at[k, piece], own_recv.at[k, piece], peer)

    def pass_copy(piece, peer, owner, far=False):
        ref = place(owner, piece, other if far else side)
        at = piece + len(FIRST + SECOND) * far
        return send(ref, ref, pass_send.at[at], pass_recv.at[at], peer)

    def trade_copy(piece, k, owner, whose):
        ref = place(owner, piece, whose)
        return send(ref, ref, trade_send.at[k, piece], trade_recv.at[k, piece], mate, "replica")

    def core_copy(piece, k, owner, whose=None):
        if whose is None:
            return send(
                place(owner, piece, side), place(owner, piece, side), core_send.at[k, piece], core_recv.at[k, piece], twin
            )
        at = len(FIRST + SECOND) + piece
        ref = place(owner, piece, whose)
        return send(ref, ref, core_send.at[k, at], core_recv.at[k, at], twin)

    def whole_copy(kind, owner):
        src, dst = kinds[kind]
        count = src.shape[0]
        rows = dst.at[pl.ds(pl.multiple_of(owner * count, count), count)]
        return send(src, rows, core_send.at[3, kind], core_recv.at[3, kind], twin)

    for piece in FIRST + SECOND:
        start(own_copy(piece, 0, a, me))
    for piece in SECOND + (2, 3, 0, 1):
        start(own_copy(piece, 1, b, me))
    local = []
    for kind, (src, dst) in enumerate(kinds):
        start(whole_copy(kind, me))
        count = src.shape[0]
        rows = dst.at[pl.ds(pl.multiple_of(me * count, count), count)]
        copy = pltpu.make_async_copy(src, rows, local_sems.at[kind])
        copy.start()
        local.append(copy)
    owners = (a, b, corner)

    def arrived(piece, k):
        owner = owners[k]
        if k == 2:
            pass_copy(piece, a, owner).wait_recv()
        else:
            own_copy(piece, k, a, owner).wait_recv()
            if k == 0 and piece in FIRST:
                start(pass_copy(piece, b, owner))
            if k == 1 and piece in SECOND:
                start(pass_copy(piece, a, owner))
        if piece in TRADED and k < 2:
            start(trade_copy(piece, k, owner, side))
        start(core_copy(piece, k, owner))

    def traded(piece, k):
        owner = owners[k]
        trade_copy(piece, k, owner, other).wait_recv()
        if k == 0 and piece in FIRST:
            start(pass_copy(piece, b, owner, True))
        if k == 1 and piece in SECOND:
            start(pass_copy(piece, a, owner, True))
        start(core_copy(piece, k, owner, other))

    for piece, k in ((0, 0), (4, 1), (1, 0), (2, 0), (5, 1), (3, 0)):
        arrived(piece, k)
    traded(2, 0)
    traded(4, 1)
    arrived(4, 0)
    arrived(2, 1)
    traded(3, 0)
    traded(5, 1)
    for piece, k in ((5, 0), (3, 1), (0, 1), (1, 1), (0, 2), (1, 2), (2, 2), (4, 2), (3, 2), (5, 2)):
        arrived(piece, k)
    for piece, k in ((4, 0), (2, 1), (5, 0), (3, 1)):
        traded(piece, k)
    for piece in (2, 4, 3, 5):
        pass_copy(piece, a, corner, True).wait_recv()
        start(core_copy(piece, 2, corner, other))
    for kind in range(len(kinds)):
        whole_copy(kind, twin).wait_recv()
    for k, owner in enumerate((flipped(twin, 2), flipped(twin, 4), flipped(corner, 1))):
        for piece in FIRST + SECOND:
            core_copy(piece, k, owner).wait_recv()
        for piece in TRADED:
            core_copy(piece, k, owner, other).wait_recv()
    for copy in started:
        copy.wait_send()
    for copy in local:
        copy.wait()


def gather(*shards):
    size = lax.axis_size("fsdp")
    if size != 8 or lax.axis_size("replica") % 2:
        return [lax.all_gather(shard, "fsdp", axis=0, tiled=True) for shard in shards]
    vmem = pl.BlockSpec(memory_space=pltpu.VMEM)
    hbm = pl.BlockSpec(memory_space=pl.ANY)
    pieces = len(FIRST + SECOND)
    dma = pltpu.SemaphoreType.DMA
    return pl.pallas_call(
        gather_kernel,
        in_specs=[vmem] * 4,
        out_specs=[hbm] * 4,
        out_shape=[jax.ShapeDtypeStruct((size * shard.shape[0], shard.shape[1]), bf16) for shard in shards],
        scratch_shapes=[
            dma((len(shards),)), dma((2, pieces)), dma((2, pieces)), dma((2 * pieces,)), dma((2 * pieces,)),
            dma((4, 2 * pieces)), dma((4, 2 * pieces)), dma((3, pieces)), dma((3, pieces)),
        ],
        compiler_params=params(collective_id=2, has_side_effects=True),
        cost_estimate=cost(55),
        name="gather",
    )(*shards)


SMALL = (KERNEL, 1, 1, 1, STATES, RANK, RANK + 2 * STATES, 1)
SMALL_ROWS = 192


def xor(index, bits):
    for bit in (1, 2, 4, 8):
        if bits & bit:
            index = flipped(index, bit)
    return index


def tail_kernel(
    one_hot_ref, b0, b1, b2, b3, filter_ref, fbias_ref, sbias_ref, skip_ref, decay_ref, step_ref, select_ref,
    gain_ref, halo_ref, block_out, small_out, rim_out,
    total, to_z, from_z, part, parts, small_f, small_ref, got_small, small_z, small_from_z, small_part,
    small_parts, rim, child, got_rim, got_child,
    sems_s, sems_z, sems_p, sems_sz, sems_sp, sems_r, sems_cs, sems_cr,
):
    depth = lax.axis_size("replica")
    me, size = lax.axis_index("fsdp"), lax.axis_size("fsdp")
    mz = lax.axis_index("replica")
    last = size - 1
    near = [lax.rem(me + d, size) for d in range(1, size)]
    far = [lax.rem(mz + d, depth) for d in range(1, depth)]
    greet([("fsdp", peer) for peer in near] + [("replica", peer) for peer in far])

    def spread(src, dst, sems, peers, axis, index):
        copies = []
        for d, peer in enumerate(peers):
            source = src.at[peer] if src.shape[0] == len(peers) + 1 and len(src.shape) == len(dst.shape) else src
            copy = send(source, dst.at[index], sems.at[0, d], sems.at[1, d], peer, axis)
            copy.start()
            copies.append(copy)
        return copies

    width = small_f.shape[2]
    small_f[...] = jnp.zeros_like(small_f)
    refs = (filter_ref, fbias_ref, sbias_ref, skip_ref, decay_ref, step_ref, select_ref)
    for k in range(size):
        at = 0
        for ref, count in zip(refs, SMALL):
            small_f[k, at : at + count] = ref[0:count, k * width : (k + 1) * width]
            at += count
        some = gain_ref.shape[1] // size
        small_f[k, at : at + 1, 0:some] = gain_ref[:, k * some : (k + 1) * some]
    small_ref[...] = small_f[...].astype(bf16)
    sequels = one_hot_ref.shape[0]
    pieces = (SEQS - PROMPTS) // sequels
    for t in range(HALO):
        rim[t * PROMPTS : (t + 1) * PROMPTS] = halo_ref[t, 0:PROMPTS]
        for p in range(PROMPTS):
            sums = None
            for q in range(sequels):
                row = PROMPTS + q * pieces
                term = one_hot_ref[q, p] * halo_ref[t, row : row + 1]
                sums = term if q == 0 else sums + term
            child[t * PROMPTS + p : t * PROMPTS + p + 1] = sums
    block = b0[...].astype(f32) + b1[...].astype(f32) + b2[...].astype(f32) + b3[...].astype(f32)
    total[...] = block.reshape(total.shape)
    to_z[...] = total[...].astype(bf16)
    to_left = send(rim, got_rim, sems_r.at[0], sems_r.at[1], lax.rem(me + last, size))
    to_left.start()

    @pl.when(me != last)
    def _():
        send(child, got_child.at[me], sems_cs.at[me], sems_cr.at[me], last).start()

    copies = spread(small_ref, got_small, sems_s, near, "fsdp", me)
    z_copies = spread(to_z, from_z, sems_z, far, "replica", mz)
    small = small_ref[me].astype(f32)
    got_small[me] = jnp.zeros(got_small.shape[1:], bf16)
    from_z[mz] = jnp.zeros(from_z.shape[1:], bf16)
    small_from_z[mz] = jnp.zeros(small_from_z.shape[1:], bf16)
    for copy in copies:
        copy.wait()
    for k in range(size):
        small = small + got_small[k].astype(f32)
    small_z[...] = small.reshape(small_z.shape)
    small_to_z = small_part
    small_to_z[...] = small_z[...].astype(bf16)
    s_copies = spread(small_to_z, small_from_z, sems_sz, far, "replica", mz)
    for copy in z_copies:
        copy.wait()
    own = total[mz]
    for k in range(depth):
        own = own + from_z[k].astype(f32)
    part[...] = own.astype(bf16)
    p_copies = spread(part, parts, sems_p, far, "replica", mz)
    parts[mz] = part[...]
    for copy in s_copies:
        copy.wait()
    own = small_z[mz]
    for k in range(depth):
        own = own + small_from_z[k].astype(f32)
    small_parts[mz] = own.astype(bf16)
    small_own = small_to_z.at[mz]
    small_own[...] = own.astype(bf16)
    q_copies = []
    for d, peer in enumerate(far):
        copy = send(small_own, small_parts.at[mz], sems_sp.at[0, d], sems_sp.at[1, d], peer, "replica")
        copy.start()
        q_copies.append(copy)
    for copy in p_copies + q_copies:
        copy.wait()
    block_out[...] = parts[...].reshape(block_out.shape)
    small_out[...] = small_parts[...].reshape(small_out.shape)
    to_left.wait()

    @pl.when(me != last)
    def _():
        send(child, got_child.at[me], sems_cs.at[me], sems_cr.at[me], last).wait_send()
        rim_out[...] = got_rim[...]

    @pl.when(me == last)
    def _():
        sums = child[...]
        for k in range(size - 1):
            send(child, got_child.at[k], sems_cs.at[k], sems_cr.at[k], 0).wait_recv()
            sums = sums + got_child[k]
        rim_out[...] = sums


def tail(one_hot, blocks, small, halo_grad):
    size, depth = lax.axis_size("fsdp"), lax.axis_size("replica")
    vmem = pl.BlockSpec(memory_space=pltpu.VMEM)
    dma = pltpu.SemaphoreType.DMA
    while len(blocks) > 4:
        blocks = blocks[:3] + [summed(blocks[3], blocks[4:5]).astype(bf16)] + blocks[5:]
    rows, channels = blocks[0].shape
    features = small[-1].shape[1]
    width = channels // size
    cut = (depth, rows // depth, channels)
    by_owner = (size, SMALL_ROWS, width)
    small_cut = (depth, SMALL_ROWS // depth, width)
    rim = (HALO * PROMPTS, features)
    return pl.pallas_call(
        tail_kernel,
        in_specs=[pl.BlockSpec(memory_space=pltpu.SMEM)] + [vmem] * (4 + len(small) + 1),
        out_specs=[vmem] * 3,
        out_shape=[
            jax.ShapeDtypeStruct((rows, channels), bf16),
            jax.ShapeDtypeStruct((SMALL_ROWS, width), bf16),
            jax.ShapeDtypeStruct(rim, f32),
        ],
        scratch_shapes=[
            pltpu.VMEM(cut, f32), pltpu.VMEM(cut, bf16), pltpu.VMEM(cut, bf16),
            pltpu.VMEM(cut[1:], bf16), pltpu.VMEM(cut, bf16),
            pltpu.VMEM(by_owner, f32), pltpu.VMEM(by_owner, bf16), pltpu.VMEM(by_owner, bf16),
            pltpu.VMEM(small_cut, f32), pltpu.VMEM(small_cut, bf16),
            pltpu.VMEM(small_cut, bf16), pltpu.VMEM(small_cut, bf16),
            pltpu.VMEM(rim, f32), pltpu.VMEM(rim, f32), pltpu.VMEM(rim, f32), pltpu.VMEM((size,) + rim, f32),
            dma((2, size)), dma((2, depth)), dma((2, depth)), dma((2, depth)), dma((2, depth)),
            dma((2,)), dma((size,)), dma((size,)),
        ],
        compiler_params=params(collective_id=4, has_side_effects=True),
        cost_estimate=cost(30),
        name="tail",
    )(one_hot, *blocks, *small, halo_grad)


def deliver_kernel(block_ref, small_ref, rim_ref, prompt_ref, *rest):
    depth = lax.axis_size("replica")
    early_refs, outs = rest[:depth], rest[depth:-1]
    early = rest[-1]
    in_out, out_out, prompt_out = outs[:3]
    mz = lax.axis_index("replica")
    half = in_out.shape[1] // 2
    in_out[:, 0:half] = block_ref[...].astype(f32)
    small = small_ref[...].astype(f32)
    at = 0
    for out, count in zip(outs[3:], SMALL):
        rows = small[at : at + count]
        out[...] = rows[:, 0 : out.shape[1]]
        at += count
    for d, ref in enumerate(early_refs):
        count = ref.shape[0]
        early[pl.ds(pl.multiple_of(xor(mz, d) * count, count), count), :] = ref[...].astype(f32)
    rows = out_out.shape[0] // 2
    features = out_out.shape[1]
    out_out[0:rows, :] = early[0:rows, 0:features]
    out_out[rows:, :] = early[0:rows, features:]
    in_out[:, half:] = early[rows:, :]
    for p in range(PROMPTS):
        prompt_out[p, 0 : SEQS - HALO] = prompt_ref[p, 0 : SEQS - HALO]
        for t in range(HALO):
            row = SEQS - HALO + t
            prompt_out[p, row : row + 1] = (
                prompt_ref[p, row : row + 1] + rim_ref[t * PROMPTS + p : t * PROMPTS + p + 1]
            )


def deliver(block, small, rim, prompt_grad, early):
    size = lax.axis_size("fsdp")
    rows, channels = block.shape
    width = small.shape[1]
    features = prompt_grad.shape[2]
    vmem = pl.BlockSpec(memory_space=pltpu.VMEM)
    end = prompt_grad.shape[1] // SEQS - 1
    last = pl.BlockSpec((PROMPTS, SEQS, features), lambda i: (0, end, 0))
    shapes = [(count, width) for count in SMALL[:-1]] + [(1, features // size)]
    shapes = [(rows, 2 * channels), (2 * rows, features), prompt_grad.shape] + shapes
    return pl.pallas_call(
        deliver_kernel,
        grid=(1,),
        in_specs=[vmem, vmem, vmem, last] + [vmem] * len(early),
        out_specs=[vmem, vmem, last] + [vmem] * len(SMALL),
        out_shape=[jax.ShapeDtypeStruct(shape, f32) for shape in shapes],
        scratch_shapes=[pltpu.VMEM((2 * rows, channels), f32)],
        input_output_aliases={3: 2},
        compiler_params=params(),
        cost_estimate=cost(4),
        name="deliver",
    )(block, small, rim, prompt_grad, *early)


def contract_rows(left_side, right_side):
    return lax.dot_general(
        left_side, right_side, (((0,), (0,)), ((), ())), preferred_element_type=f32
    )


def contract_cols(left_side, right_side):
    return lax.dot_general(
        left_side, right_side, (((1,), (1,)), ((), ())), preferred_element_type=f32
    )


def exchanged(block, axis, distance):
    return lax.ppermute(block, axis, [(i, i ^ distance) for i in range(lax.axis_size(axis))])


def pick_row(block, index, axis=0):
    return lax.dynamic_index_in_dim(block, index, axis, keepdims=False)


def over_cores(blocks):
    blocks = blocks.reshape((-1, 2) + blocks.shape[1:])
    core = lax.axis_index("fsdp") % 2
    got = exchanged(pick_row(blocks, 1 - core, 1), "fsdp", 1)
    return (pick_row(blocks, core, 1).astype(f32) + got.astype(f32)).astype(bf16)


def to_chips(blocks):
    chip = lax.axis_index("fsdp") // 2
    got = [exchanged(pick_row(blocks, chip ^ d), "fsdp", 2 * d) for d in range(1, blocks.shape[0])]
    return pick_row(blocks, chip), got


def summed(own, got):
    total = own.astype(f32)
    for block in got:
        total = total + block.astype(f32)
    return total


def to_replicas(block):
    size, here = lax.axis_size("replica"), lax.axis_index("replica")
    parts = block.astype(bf16).reshape((size, -1) + block.shape[1:])
    own = pick_row(block.reshape(parts.shape), here)
    return own, [exchanged(pick_row(parts, here ^ d), "replica", d) for d in range(1, size)]


def from_replicas(part):
    return [part] + [exchanged(part, "replica", d) for d in range(1, lax.axis_size("replica"))]


def body(
    prompt_hidden, sequel_hidden, parents, prompt_cotangent, sequel_cotangent,
    norm_gain, input_weight, filter_weight, depthwise_filter_bias, select_weight,
    step_weight, step_bias, decay_log, skip_gain, output_weight,
):
    size, here = lax.axis_size("fsdp"), lax.axis_index("fsdp")
    prompts, steps = prompt_hidden.shape[:2]
    sequels, sequel_len = sequel_hidden.shape[:2]
    split = sequel_len // steps
    assert prompts == PROMPTS and sequels * split == SEQS - prompts
    rim = KERNEL - 1
    half = SEQS // 2
    rows = steps * SEQS

    after = lax.optimization_barrier
    width = step_bias.shape[0]
    tail_rows = prompt_hidden[:, steps - rim :]
    shard = jnp.concatenate(
        [
            step_weight,
            tail_rows.reshape(-1, width),
            filter_weight,
            depthwise_filter_bias[None],
            step_bias[None],
            skip_gain[None],
            jnp.pad(norm_gain, (0, width - norm_gain.shape[0]))[None],
        ],
        axis=0,
    )
    shard = jnp.pad(shard, ((0, -shard.shape[0] % 16), (0, 0)))
    lanes = jnp.concatenate([select_weight, decay_log], axis=1)
    lanes = jnp.pad(lanes, ((0, 0), (0, LANES - lanes.shape[1])))
    every, select_pad, full_output, full_input = gather(shard, lanes, output_weight, input_weight)
    every = every.reshape(size, shard.shape[0], width)
    at = RANK + tail_rows.size // width
    tails = every[:, RANK:at].reshape((size,) + tail_rows.shape)
    step_full = jnp.swapaxes(every[:, :RANK], 0, 1).reshape(RANK, -1)
    vectors = jnp.swapaxes(every[:, at : at + SEQS], 0, 1).astype(f32)
    gain = vectors[KERNEL + 3, :, : norm_gain.shape[0]].reshape(1, -1)
    vectors = vectors.reshape(SEQS, -1)
    fw, fb, sbias, skip = vectors[:KERNEL], vectors[4:5], vectors[5:6], vectors[6:7]
    first = RANK + 2 * STATES
    rate = -jnp.exp(select_pad[:, first : first + STATES].T.astype(f32)) * LOG2E
    step_pad = jnp.pad(step_full, ((0, LANES - RANK), (0, 0)))

    before = jnp.where(here > 0, tails[jnp.maximum(here - 1, 0)], jnp.zeros_like(tails[0]))
    cut = sequel_hidden.reshape(sequels, split, steps, D)
    inner = jnp.concatenate([tails[size - 1][parents][:, None], cut[:, :-1, steps - rim :]], axis=1)
    halo = jnp.concatenate([before, inner.reshape(-1, rim, D)], axis=0)
    halo = jnp.pad(jnp.swapaxes(halo, 0, 1), ((HALO - rim, 0), (0, 0), (0, 0))).reshape(-1, D).astype(f32)
    pieces = sequel_hidden.reshape(-1, steps, D)
    piece_cot = sequel_cotangent.reshape(-1, steps, D)
    scaled, cotangent = prepare(prompt_hidden, pieces, prompt_cotangent, piece_cot, halo, gain)

    mixture = product([scaled], full_input, bf16, part=0, parts=2)
    gate = product([scaled], full_input, f32, part=1, parts=2)
    mixture = mixture.reshape(steps + HALO, SEQS, INNER)
    gate = gate.reshape(steps + HALO, SEQS, INNER)
    gated_grad = product([cotangent], full_output, f32, across=True).reshape(steps, SEQS, INNER)
    act, proj = front(mixture, fw, fb, select_pad, steps)
    groups = 1 if split == 1 else 2
    lane = jnp.arange(2 * STATES * LANES)[None, :]
    select = (jnp.arange(LANES)[:, None] == RANK + lane // LANES).astype(bf16)
    dt, sig, yg, silu, slope, ahead, behind, total = piece(
        proj, act, gate, gated_grad, step_pad, sbias, rate, select, groups
    )

    one_hot = (parents[:, None] == jnp.arange(PROMPTS, dtype=jnp.int32)[None, :]).astype(f32)
    own = total[half:].reshape(sequels, split, 1, INNER)
    own_behind = behind[half:].reshape(sequels, split, STATES, INNER)
    back = own_behind[:, split - 1]
    own_end = [jnp.zeros_like(back)]
    for p in range(split - 2, -1, -1):
        own_end.insert(0, back)
        back = own_behind[:, p] + jnp.exp2(rate * own[:, p]) * back
    start, end = chain(one_hot, ahead[:half], behind[:half], back, total, rate)
    if split > 1:
        state = start[half:]
        own_start = [state]
        for p in range(split - 1):
            state = jnp.exp2(rate * own[:, p]) * state + ahead[half:].reshape(own_behind.shape)[:, p]
            own_start.append(state)
        own_start = jnp.stack(own_start, axis=1).reshape(half, STATES, INNER)
        start = jnp.concatenate([start[:half], own_start], axis=0)
        end = jnp.concatenate([end[:half], jnp.stack(own_end, axis=1).reshape(half, STATES, INNER)], axis=0)

    gated, hist, gate_grad, skip_grad = forward(
        proj, dt, act, yg, silu, slope, rate, start, skip, select
    )
    gated = gated.reshape(rows, INNER)
    gate_grad = gate_grad.reshape(-1, INNER)
    output_grad = contract_rows(gated, cotangent).astype(bf16).reshape(size, -1, D)
    gate_weight_grad = contract_rows(scaled, gate_grad).astype(bf16)
    early = [over_cores(output_grad), over_cores(gate_weight_grad.reshape(size, -1, INNER))]
    wide = jnp.concatenate([early[0][:, : INNER // size // 2], early[0][:, INNER // size // 2 :]], axis=2)
    early = jnp.concatenate([wide, early[1]], axis=1)
    end, early = after((end, early))
    early = to_chips(early)

    rank_t = proj[:, :RANK].astype(bf16).T
    lane = jnp.arange(LANES)[None, None, :]
    which = jnp.arange(PAIRS)[:, None, None]
    source = jnp.arange(2 * LANES)[None, :, None]
    pick = (lane // 2 == jnp.where(source < LANES, RANK, RANK + STATES) // 2 + which).astype(bf16)
    act_grad, step_grad, bias_grad, decay_grad, projg = backward(
        proj, dt, sig, act, yg, rate, end, skip, hist, rank_t, step_pad.T, pick, select
    )
    projg, early = after((projg, early))
    early = summed(*early)
    projg, early = after((projg, early))
    early = to_replicas(early)
    filter_in_grad, select_grad, filter_grad, filter_bias_grad = filter_back(
        mixture, act, act_grad, projg, projg.T, select_pad, fw, fb
    )
    filter_in_grad, early = after((filter_in_grad, early))
    early = summed(*early).astype(bf16)
    filter_in_grad = filter_in_grad.reshape(-1, INNER)
    filter_weight_grad = contract_rows(scaled, filter_in_grad).astype(bf16)
    filter_weight_grad, early = after((filter_weight_grad, early))
    late = over_cores(filter_weight_grad.reshape(size, -1, INNER))
    early = from_replicas(early)
    mixed = jnp.dot(gated, full_output, preferred_element_type=f32)
    late, mixed, filter_in_grad = after((late, mixed, filter_in_grad))
    own_block, late = to_chips(late)
    scaled_grad = product([filter_in_grad, gate_grad], full_input, f32, across=True)
    prompt_out, piece_out, prompt_grad, piece_grad, halo_grad, gain_grad = finish(
        mixed, scaled_grad, prompt_hidden, pieces, prompt_cotangent, piece_cot, halo, gain
    )
    halo_grad, own_block, late = after((halo_grad, own_block, late))
    halo_grad = halo_grad.reshape(HALO, SEQS, D)
    small = [
        filter_grad, filter_bias_grad, bias_grad, skip_grad, decay_grad, step_grad, select_grad, gain_grad,
    ]
    block, small, following = tail(one_hot, [own_block] + late, small, halo_grad)
    (
        input_grad, output_grad, prompt_grad, g_filter, g_fbias, g_sbias, g_skip, g_decay, g_step, g_select, g_gain,
    ) = deliver(block, small, following, prompt_grad, early)
    if split > 1:
        own = jnp.swapaxes(halo_grad[:, half:], 0, 1).reshape(sequels, split, HALO, D)
        own = jnp.pad(own[:, 1:], ((0, 0), (0, 1), (0, 0), (0, 0))).reshape(half, HALO, D)
        piece_grad = piece_grad.at[:, steps - HALO :].add(own)
    return (
        prompt_out,
        piece_out.reshape(sequel_hidden.shape),
        prompt_grad,
        piece_grad.reshape(sequel_hidden.shape),
        g_gain[0],
        input_grad,
        g_filter,
        g_fbias[0],
        g_select.T,
        g_step,
        g_sbias[0],
        g_decay.T,
        g_skip[0],
        output_grad,
    )


def solution(mesh):
    rows = P("replica", "fsdp", None)
    own = P(("replica", "fsdp"), None, None)
    return jax.shard_map(
        body,
        mesh=mesh,
        in_specs=(
            rows, own, P(("replica", "fsdp")), rows, own,
            P("fsdp"), P("fsdp", None), P(None, "fsdp"), P("fsdp"), P("fsdp", None),
            P(None, "fsdp"), P("fsdp"), P("fsdp", None), P("fsdp"), P("fsdp", None),
        ),
        out_specs=(
            rows, own, rows, own,
            P("fsdp"), P("fsdp", None), P(None, "fsdp"), P("fsdp"), P("fsdp", None),
            P(None, "fsdp"), P("fsdp"), P("fsdp", None), P("fsdp"), P("fsdp", None),
        ),
        check_vma=False,
    )
```

```python
import functools
import math

import jax
import jax.numpy as jnp
from jax import lax
from jax.experimental import pallas as pl
from jax.experimental.pallas import tpu as pltpu
from jax.sharding import PartitionSpec as P

D = 1024
INNER = 2048
STATES = 16
RANK = 64
KERNEL = 4
PROMPTS = 4

SEQS = 8
HALO = 4
LANES = 128
WIDE = 256
LOG2E = math.log2(math.e)
LN2 = math.log(2.0)
f32 = jnp.float32
bf16 = jnp.bfloat16

VMEM_LIMIT = 62 * 1024 * 1024


def cost(microseconds):
    return pl.CostEstimate(flops=int(microseconds * 1e9), bytes_accessed=0, transcendentals=0)


def params(**kw):
    return pltpu.CompilerParams(vmem_limit_bytes=VMEM_LIMIT, **kw)


def sigmoid(x):
    return 1.0 / (1.0 + jnp.exp(-x))


def softplus(x):
    return jnp.maximum(x, 0.0) + jnp.log1p(jnp.exp(-jnp.abs(x)))


def product_kernel(across, *refs):
    lefts, rhs_ref, out_ref = refs[:-2], refs[-2], refs[-1]
    total = None
    at = 0
    for left in lefts:
        depth = left.shape[1]
        rhs = rhs_ref[:, at : at + depth] if across else rhs_ref[at : at + depth]
        dims = (((1,), (1 if across else 0,)), ((), ()))
        term = lax.dot_general(left[...], rhs, dims, preferred_element_type=f32)
        total = term if total is None else total + term
        at += depth
    if len(out_ref.shape) == 2:
        out_ref[...] = total.astype(out_ref.dtype)
    else:
        for k in range(out_ref.shape[0]):
            out_ref[k] = total[:, k * WIDE : (k + 1) * WIDE].astype(out_ref.dtype)


def product(lefts, rhs, kind, across=False, part=0, parts=1, tiled=False):
    rows = lefts[0].shape[0]
    depth = sum(left.shape[1] for left in lefts)
    tile = 2 * WIDE if len(lefts) == 1 else WIDE
    if across:
        columns = rhs.shape[0]
        rhs_spec = pl.BlockSpec((tile, depth), lambda j: (j, 0))
    else:
        columns = rhs.shape[1] // parts
        first = part * columns // tile
        rhs_spec = pl.BlockSpec((depth, tile), lambda j: (0, first + j))
    return pl.pallas_call(
        functools.partial(product_kernel, across),
        grid=(columns // tile,),
        in_specs=[pl.BlockSpec(left.shape, lambda j: (0, 0)) for left in lefts] + [rhs_spec],
        out_specs=pl.BlockSpec((tile // WIDE, rows, WIDE), lambda j: (j, 0, 0))
        if tiled
        else pl.BlockSpec((rows, tile), lambda j: (0, j)),
        out_shape=jax.ShapeDtypeStruct((columns // WIDE, rows, WIDE) if tiled else (rows, columns), kind),
        compiler_params=params(),
        cost_estimate=cost(0.01),
        name="product",
    )(*lefts, rhs)


def scale_of(rows):
    return lax.rsqrt(jnp.mean(rows * rows, axis=-1, keepdims=True) + 1e-05)


def by_time(prompt_ref, piece_ref):
    both_kinds = jnp.concatenate([prompt_ref[...], piece_ref[...]], axis=0).astype(f32)
    return jnp.swapaxes(both_kinds, 0, 1)


def prepare_kernel(prompt_ref, piece_ref, prompt_cot_ref, piece_cot_ref, halo_ref, gain_ref, scaled_ref, cot_ref):
    i = pl.program_id(0)
    gain = gain_ref[...]

    @pl.when(i == 0)
    def _():
        rows = halo_ref[...]
        scaled_ref[0 : HALO * SEQS, :] = (rows * scale_of(rows) * gain).astype(bf16)

    rows = by_time(prompt_ref, piece_ref)
    count = rows.shape[0] * SEQS
    rows = rows.reshape(count, D)
    at = pl.multiple_of(HALO * SEQS + i * count, HALO * SEQS)
    scaled_ref[pl.ds(at, count), :] = (rows * scale_of(rows) * gain).astype(bf16)
    cot_ref[...] = by_time(prompt_cot_ref, piece_cot_ref).reshape(count, D).astype(bf16)


CHUNK = 16


def prepare(prompt, piece, prompt_cot, piece_cot, halo, gain):
    steps = prompt.shape[1]
    part = pl.BlockSpec((SEQS // 2, CHUNK, D), lambda i: (0, i, 0))
    rows = steps * SEQS
    return pl.pallas_call(
        prepare_kernel,
        grid=(steps // CHUNK,),
        in_specs=[
            part, part, part, part,
            pl.BlockSpec((HALO * SEQS, D), lambda i: (0, 0)),
            pl.BlockSpec((1, D), lambda i: (0, 0)),
        ],
        out_specs=[
            pl.BlockSpec((HALO * SEQS + rows, D), lambda i: (0, 0)),
            pl.BlockSpec((CHUNK * SEQS, D), lambda i: (i, 0)),
        ],
        out_shape=[
            jax.ShapeDtypeStruct((HALO * SEQS + rows, D), bf16),
            jax.ShapeDtypeStruct((rows, D), bf16),
        ],
        compiler_params=params(),
        cost_estimate=cost(5),
        name="prepare",
    )(prompt, piece, prompt_cot, piece_cot, halo, gain)


def norm_back(rows, scaled_grad, gain):
    inverse = scale_of(rows)
    unit = rows * inverse
    grad = scaled_grad * gain
    back = inverse * (grad - unit * jnp.mean(grad * unit, axis=-1, keepdims=True))
    return back, scaled_grad * unit


def finish_kernel(
    mixed_ref, grad_ref, grad_halo_ref,
    prompt_ref, piece_ref, prompt_cot_ref, piece_cot_ref, halo_ref, gain_ref,
    prompt_out, piece_out, prompt_grad, piece_grad, halo_grad, gain_grad,
):
    i = pl.program_id(0)
    gain = gain_ref[...]

    @pl.when(i == 0)
    def _():
        back, sums = norm_back(halo_ref[...], grad_halo_ref[...], gain)
        halo_grad[...] = back
        gain_grad[...] = jnp.sum(sums, axis=0, keepdims=True)

    half = SEQS // 2
    rows = by_time(prompt_ref, piece_ref)
    shape = rows.shape
    rows = rows.reshape(-1, D)
    back, sums = norm_back(rows, grad_ref[...], gain)
    gain_grad[...] += jnp.sum(sums, axis=0, keepdims=True)
    back = jnp.swapaxes(back.reshape(shape), 0, 1)
    prompt_grad[...] = back[:half] + prompt_cot_ref[...].astype(f32)
    piece_grad[...] = back[half:] + piece_cot_ref[...].astype(f32)
    mixed = jnp.swapaxes((mixed_ref[...] + rows).reshape(shape), 0, 1)
    prompt_out[...] = mixed[:half].astype(bf16)
    piece_out[...] = mixed[half:].astype(bf16)


def finish(mixed, grad, prompt, piece, prompt_cot, piece_cot, halo, gain):
    steps = prompt.shape[1]
    part = pl.BlockSpec((SEQS // 2, CHUNK, D), lambda i: (0, i, 0))
    first = pl.BlockSpec((HALO * SEQS, D), lambda i: (0, 0))
    shifted = pl.BlockSpec(
        (pl.Element(CHUNK * SEQS), pl.Element(D)),
        lambda i: (pl.multiple_of(HALO * SEQS + i * (CHUNK * SEQS), HALO * SEQS), 0),
    )
    return pl.pallas_call(
        finish_kernel,
        grid=(steps // CHUNK,),
        in_specs=[
            pl.BlockSpec((CHUNK * SEQS, D), lambda i: (i, 0)),
            shifted, first,
            part, part, part, part,
            first,
            pl.BlockSpec((1, D), lambda i: (0, 0)),
        ],
        out_specs=[part, part, part, part, first, pl.BlockSpec((1, D), lambda i: (0, 0))],
        out_shape=[
            jax.ShapeDtypeStruct(prompt.shape, bf16),
            jax.ShapeDtypeStruct(piece.shape, bf16),
            jax.ShapeDtypeStruct(prompt.shape, f32),
            jax.ShapeDtypeStruct(piece.shape, f32),
            jax.ShapeDtypeStruct((HALO * SEQS, D), f32),
            jax.ShapeDtypeStruct((1, D), f32),
        ],
        compiler_params=params(),
        cost_estimate=cost(0.01),
        name="finish",
    )(mixed, grad, grad, prompt, piece, prompt_cot, piece_cot, halo, gain)


def front_kernel(mix_ref, fw_ref, fb_ref, sel_ref, act_ref, bend_ref, proj_ref):
    j = pl.program_id(0)
    steps = act_ref.shape[0]
    chunk = 16
    taps = [fw_ref[k : k + 1, :] for k in range(KERNEL)]
    bias = fb_ref[0:1, :]

    @pl.when(j == 0)
    def _():
        proj_ref[...] = jnp.zeros_like(proj_ref)

    def step(i, _):
        t = i * chunk
        x = mix_ref[pl.ds(t, chunk + HALO)].astype(f32)
        v = bias[None] + taps[0][None] * x[1 : 1 + chunk]
        for k in range(1, KERNEL):
            v = v + taps[k][None] * x[1 + k : 1 + k + chunk]
        sig = sigmoid(v)
        act = v * sig
        act_ref[pl.ds(t, chunk)] = act
        bend_ref[pl.ds(t, chunk)] = (sig + act * (1.0 - sig)).astype(bf16)
        low = act.reshape(chunk * SEQS, act.shape[-1]).astype(bf16)
        r = pl.multiple_of(t * SEQS, chunk * SEQS)
        proj_ref[pl.ds(r, chunk * SEQS), :] += jnp.dot(low, sel_ref[...], preferred_element_type=f32)
        return 0

    lax.fori_loop(0, steps // chunk, step, 0)


def front(mixture, fw, fb, select_pad, steps):
    channels = fw.shape[1]
    return pl.pallas_call(
        front_kernel,
        grid=(channels // WIDE,),
        in_specs=[
            pl.BlockSpec((None, steps + HALO, SEQS, WIDE), lambda j: (j, 0, 0, 0)),
            pl.BlockSpec((KERNEL, WIDE), lambda j: (0, j)),
            pl.BlockSpec((1, WIDE), lambda j: (0, j)),
            pl.BlockSpec((WIDE, LANES), lambda j: (j, 0)),
        ],
        out_specs=[
            pl.BlockSpec((None, steps, SEQS, WIDE), lambda j: (j, 0, 0, 0)),
            pl.BlockSpec((None, steps, SEQS, WIDE), lambda j: (j, 0, 0, 0)),
            pl.BlockSpec((steps * SEQS, LANES), lambda j: (0, 0)),
        ],
        out_shape=[
            jax.ShapeDtypeStruct((channels // WIDE, steps, SEQS, WIDE), f32),
            jax.ShapeDtypeStruct((channels // WIDE, steps, SEQS, WIDE), bf16),
            jax.ShapeDtypeStruct((steps * SEQS, LANES), f32),
        ],
        compiler_params=params(),
        cost_estimate=cost(16),
        name="front",
    )(mixture, fw, fb, select_pad)


def pair(a, b):
    return jnp.concatenate([a, b], axis=0).astype(bf16)


def both(v):
    return pair(v, v)


def halves(v):
    v = v.astype(f32)
    return v[:SEQS], v[SEQS:]


def folded(v):
    a, b = halves(v)
    return a + b


def spread_maps(proj_ref, select_ref, first, count, store):
    steps = proj_ref.shape[0] // SEQS
    chunk = 32

    def step(i, _):
        r = pl.multiple_of(i * chunk * SEQS, chunk * SEQS)
        rows = proj_ref[pl.ds(r, chunk * SEQS), :].astype(bf16)
        for n in range(0, count, 2):
            at = (first - RANK + n) * LANES
            wide = jnp.dot(rows, select_ref[:, at : at + 2 * LANES], preferred_element_type=f32)
            wide = wide.reshape(chunk, SEQS, 2 * LANES)
            store(i * chunk, chunk, n, wide[:, :, :LANES], wide[:, :, LANES:])
        return 0

    lax.fori_loop(0, steps // chunk, step, 0)


def store_plain(ref):
    def store(t, count, n, a, b):
        ref[pl.ds(t, count), n] = a
        ref[pl.ds(t, count), n + 1] = b

    return store


def store_pairs(ref):
    def store(t, count, n, a, b):
        ref[pl.ds(t, count), n // 2] = jnp.concatenate([a, b], axis=1).astype(bf16)

    return store


PAIRS = STATES // 2
RUN = 8


def piece_kernel(
    proj_ref, act_ref, gate_ref, gg_ref, stepw_ref, sbias_ref, rate_ref, select_ref,
    dt_ref, sig_ref, yg_ref, silu_ref, slope_ref, fwd_ref, bwd_ref, tot_ref,
    b_scr, c_scr, time_scr, acc_scr,
):
    j = pl.program_id(0)
    steps = dt_ref.shape[0]
    half = SEQS // 2
    groups = fwd_ref.shape[0] // half

    @pl.when(j == 0)
    def _():
        def store_groups(t, count, n, a, b):
            for group in range(groups):
                rows = slice(group * half, (group + 1) * half)
                parts = [a[:, rows], a[:, rows], b[:, rows], b[:, rows]]
                b_scr[group, pl.ds(t, count), n // 2] = jnp.concatenate(parts, axis=1).astype(bf16)

        spread_maps(proj_ref, select_ref, RANK, STATES, store_groups)
        spread_maps(proj_ref, select_ref, RANK + STATES, STATES, store_pairs(c_scr))

    chunk = 8
    sbias = sbias_ref[0:1, :]

    def prep(i, total):
        t = i * chunk
        r = pl.multiple_of(t * SEQS, chunk * SEQS)
        rank = proj_ref[pl.ds(r, chunk * SEQS), :].astype(bf16)
        pre = jnp.dot(rank, stepw_ref[...], preferred_element_type=f32).reshape(chunk, SEQS, WIDE)
        pre = pre + sbias[None]
        small = jnp.exp2(jnp.abs(pre) * -LOG2E)
        one = 1.0 + small
        inverse = 1.0 / one
        dt = jnp.maximum(pre, 0.0) + (jnp.log(one) + (small - (one - 1.0)) * inverse)
        dt_ref[pl.ds(t, chunk)] = dt
        sig_ref[pl.ds(t, chunk)] = jnp.where(pre >= 0.0, inverse, small * inverse).astype(bf16)
        gate = gate_ref[pl.ds(t + HALO, chunk)]
        gg = gg_ref[pl.ds(t, chunk)]
        sig = sigmoid(gate)
        silu = gate * sig
        yg_ref[pl.ds(t, chunk)] = gg * silu
        silu_ref[pl.ds(t, chunk)] = silu.astype(bf16)
        slope_ref[pl.ds(t, chunk)] = (gg * (sig + silu * (1.0 - sig))).astype(bf16)
        for k in range(chunk):
            total = total + dt[k]
            time_scr[t + k] = total
        return total

    total = lax.fori_loop(0, steps // chunk, prep, jnp.zeros((SEQS, WIDE), f32))
    tot_ref[...] = total

    units = []

    low = lax.broadcasted_iota(jnp.int32, (SEQS, LANES), 0) < half
    packed = [
        jnp.where(low, rate_ref[n : n + 1, :LANES], rate_ref[n : n + 1, LANES:])
        for n in range(STATES)
    ]
    packed = [pair(packed[2 * p], packed[2 * p + 1]) for p in range(PAIRS)]

    def forward_unit(group):
        rows = slice(group * half, (group + 1) * half)

        def pack(v):
            return jnp.concatenate([v[rows, :LANES], v[rows, LANES:]], axis=0)

        whole = pack(total)

        def vectors(t):
            return both(whole - pack(time_scr[t])), both(pack(dt_ref[t] * act_ref[t]))

        def out(n, value):
            fwd_ref[rows, n, :LANES] = value[:half]
            fwd_ref[rows, n, LANES:] = value[half:]

        return packed, vectors, lambda t, p: b_scr[group, t, p], out

    def backward_unit(cols):
        mine = [jnp.broadcast_to(rate_ref[n : n + 1, cols], (SEQS, LANES)) for n in range(STATES)]
        mine = [pair(mine[2 * p], mine[2 * p + 1]) for p in range(PAIRS)]

        def vectors(t):
            return both(time_scr[t, :, cols]), both(yg_ref[t, :, cols])

        def out(n, value):
            bwd_ref[:, n, cols] = value

        return mine, vectors, lambda t, p: c_scr[t, p], out

    for group in range(groups):
        units.append(forward_unit(group))
    for part in range(WIDE // LANES):
        units.append(backward_unit(slice(part * LANES, (part + 1) * LANES)))
    acc_scr[...] = jnp.zeros_like(acc_scr)

    def run(i, _):
        for k, (rates, vectors, map_at, _) in enumerate(units):
            sums = [None] * PAIRS
            for m in range(RUN):
                t = i * RUN + m
                time, drive = vectors(t)
                for p in range(PAIRS):
                    term = jnp.exp2(time * rates[p]) * drive * map_at(t, p)
                    sums[p] = term if m == 0 else sums[p] + term
            for p in range(PAIRS):
                a, b = halves(sums[p])
                acc_scr[k, 2 * p] += a
                acc_scr[k, 2 * p + 1] += b
        return 0

    lax.fori_loop(0, steps // RUN, run, 0)
    for k, (_, _, _, out) in enumerate(units):
        for n in range(STATES):
            out(n, acc_scr[k, n])


def piece(proj, act, gate, gated_grad, step_pad, sbias, rate, select, groups):
    grid, steps, _, _ = act.shape
    channels = grid * WIDE
    wide = lambda j: (0, 0, j)
    flat = pl.BlockSpec((None, steps, SEQS, WIDE), lambda j: (j, 0, 0, 0))
    shape = act.shape
    return pl.pallas_call(
        piece_kernel,
        grid=(grid,),
        in_specs=[
            pl.BlockSpec((steps * SEQS, LANES), lambda j: (0, 0)),
            flat,
            pl.BlockSpec((None, steps + HALO, SEQS, WIDE), lambda j: (j, 0, 0, 0)),
            flat,
            pl.BlockSpec((LANES, WIDE), lambda j: (0, j)),
            pl.BlockSpec((1, WIDE), lambda j: (0, j)),
            pl.BlockSpec((STATES, WIDE), lambda j: (0, j)),
            pl.BlockSpec(select.shape, lambda j: (0, 0)),
        ],
        out_specs=[
            flat, flat, flat, flat, flat,
            pl.BlockSpec((groups * SEQS // 2, STATES, WIDE), wide),
            pl.BlockSpec((SEQS, STATES, WIDE), wide),
            pl.BlockSpec((SEQS, WIDE), lambda j: (0, j)),
        ],
        out_shape=[
            jax.ShapeDtypeStruct(shape, f32),
            jax.ShapeDtypeStruct(shape, bf16),
            jax.ShapeDtypeStruct(shape, f32),
            jax.ShapeDtypeStruct(shape, bf16),
            jax.ShapeDtypeStruct(shape, bf16),
            jax.ShapeDtypeStruct((groups * SEQS // 2, STATES, channels), f32),
            jax.ShapeDtypeStruct((SEQS, STATES, channels), f32),
            jax.ShapeDtypeStruct((SEQS, channels), f32),
        ],
        scratch_shapes=[
            pltpu.VMEM((groups, steps, PAIRS, 2 * SEQS, LANES), bf16),
            pltpu.VMEM((steps, PAIRS, 2 * SEQS, LANES), bf16),
            pltpu.VMEM((steps, SEQS, WIDE), f32),
            pltpu.VMEM((groups + WIDE // LANES, STATES, SEQS, LANES), f32),
        ],
        compiler_params=params(),
        cost_estimate=cost(60),
        name="piece",
    )(proj, act, gate, gated_grad, step_pad, sbias, rate, select)


def chain_kernel(
    one_hot_ref, ahead_ref, behind_ref, time_ref, rate_ref, start_out, end_out,
    moved_ref, got, got_time, back, done, sems, time_sems, back_sems,
):
    size = got.shape[0]
    width = got.shape[2]
    count = PROMPTS * STATES
    sequels = one_hot_ref.shape[0]
    me = lax.axis_index("fsdp")
    for p in range(PROMPTS):
        rows = slice(p * STATES, (p + 1) * STATES)
        total = one_hot_ref[0, p] * behind_ref[PROMPTS]
        for k in range(1, sequels):
            total = total + one_hot_ref[k, p] * behind_ref[PROMPTS + k]
        moved_ref[0 * count + p * STATES : 0 * count + (p + 1) * STATES] = ahead_ref[p].astype(bf16)
        moved_ref[1 * count + p * STATES : 1 * count + (p + 1) * STATES] = behind_ref[p].astype(bf16)
        moved_ref[2 * count + p * STATES : 2 * count + (p + 1) * STATES] = total.astype(bf16)
    barrier = pltpu.get_barrier_semaphore()
    for d in range(1, size):
        peer = lax.rem(me + d, size)
        pl.semaphore_signal(barrier, inc=1, device_id={"fsdp": peer}, device_id_type=pl.DeviceIdType.MESH)
    pl.semaphore_wait(barrier, size - 1)

    def columns(device):
        return pl.ds(pl.multiple_of(device * width, width), width)

    copies = []
    for d in range(1, size):
        peer = lax.rem(me + d, size)
        for src, dst, sem in ((moved_ref, got, sems), (time_ref, got_time, time_sems)):
            copy = pltpu.make_async_remote_copy(
                src_ref=src.at[:, columns(peer)],
                dst_ref=dst.at[me],
                send_sem=sem.at[0, d],
                recv_sem=sem.at[1, d],
                device_id={"fsdp": peer},
                device_id_type=pl.DeviceIdType.MESH,
            )
            copy.start()
            copies.append(copy)
    got[me] = moved_ref[:, columns(me)]
    got_time[me] = time_ref[:, columns(me)]
    for copy in copies:
        copy.wait()

    rate = jnp.concatenate([rate_ref[...]] * PROMPTS, axis=0)
    branch = jnp.zeros((count, width), f32)
    state = jnp.zeros((count, width), f32)
    decays = []
    for k in range(size):
        time = jnp.concatenate(
            [jnp.broadcast_to(got_time[k, p : p + 1, :], (STATES, width)) for p in range(PROMPTS)], axis=0
        )
        decays.append(jnp.exp2(rate * time))
        back[k, 0:count] = state.astype(bf16)
        state = decays[k] * state + got[k, 0:count].astype(f32)
        branch = branch + got[k, 2 * count : 3 * count].astype(f32)
    grad = branch
    for k in range(size - 1, -1, -1):
        back[k, count : 2 * count] = grad.astype(bf16)
        grad = decays[k] * grad + got[k, count : 2 * count].astype(f32)
    last = state.astype(bf16)
    for k in range(size):
        back[k, 2 * count : 3 * count] = last
    copies = []
    for d in range(1, size):
        peer = lax.rem(me + d, size)
        copy = pltpu.make_async_remote_copy(
            src_ref=back.at[peer],
            dst_ref=done.at[me],
            send_sem=back_sems.at[0, d],
            recv_sem=back_sems.at[1, d],
            device_id={"fsdp": peer},
            device_id_type=pl.DeviceIdType.MESH,
        )
        copy.start()
        copies.append(copy)
    done[me] = back[me]
    for copy in copies:
        copy.wait()
    for k in range(size):
        columns_k = slice(k * width, (k + 1) * width)
        last = []
        for p in range(PROMPTS):
            rows = slice(p * STATES, (p + 1) * STATES)
            start_out[p, :, columns_k] = done[k, rows].astype(f32)
            rows = slice(count + p * STATES, count + (p + 1) * STATES)
            end_out[p, :, columns_k] = done[k, rows].astype(f32)
            rows = slice(2 * count + p * STATES, 2 * count + (p + 1) * STATES)
            last.append(done[k, rows].astype(f32))
        for q in range(sequels):
            total = one_hot_ref[q, 0] * last[0]
            for p in range(1, PROMPTS):
                total = total + one_hot_ref[q, p] * last[p]
            start_out[PROMPTS + q, :, columns_k] = total
            end_out[PROMPTS + q, :, columns_k] = jnp.zeros_like(total)


def chain(one_hot, ahead, behind, time, rate):
    size = lax.axis_size("fsdp")
    channels = ahead.shape[2]
    rows = 3 * PROMPTS * STATES
    width = channels // size
    own = lax.dynamic_slice_in_dim(rate, lax.axis_index("fsdp") * width, width, 1)
    whole = pl.BlockSpec(memory_space=pltpu.VMEM)
    shape = (PROMPTS + one_hot.shape[0], STATES, channels)
    return pl.pallas_call(
        chain_kernel,
        in_specs=[pl.BlockSpec(memory_space=pltpu.SMEM)] + [whole] * 4,
        out_specs=[whole] * 2,
        out_shape=[jax.ShapeDtypeStruct(shape, f32)] * 2,
        scratch_shapes=[
            pltpu.VMEM((rows, channels), bf16),
            pltpu.VMEM((size, rows, width), bf16),
            pltpu.VMEM((size, SEQS, width), f32),
            pltpu.VMEM((size, rows, width), bf16),
            pltpu.VMEM((size, rows, width), bf16),
            pltpu.SemaphoreType.DMA((2, size)),
            pltpu.SemaphoreType.DMA((2, size)),
            pltpu.SemaphoreType.DMA((2, size)),
        ],
        compiler_params=params(collective_id=1, has_side_effects=True),
        cost_estimate=cost(25),
        name="chain",
    )(one_hot, ahead, behind, time, own)


TILES = [slice(k * LANES, (k + 1) * LANES) for k in range(WIDE // LANES)]


def forward_kernel(
    proj_ref, dt_ref, act_ref, yg_ref, silu_ref, slope_ref, rate_ref, start_ref, skip_ref, select_ref,
    gated_ref, hist_ref, gategrad_ref, skipg_ref,
    b_scr, c_scr,
):
    j = pl.program_id(0)
    steps = dt_ref.shape[0]

    @pl.when(j == 0)
    def _():
        spread_maps(proj_ref, select_ref, RANK, STATES, store_plain(b_scr))
        spread_maps(proj_ref, select_ref, RANK + STATES, STATES, store_pairs(c_scr))

    gategrad_ref[0:HALO] = jnp.zeros((HALO, SEQS, WIDE), bf16)
    unroll = 8

    for part, cols in enumerate(TILES):
        rates = [jnp.broadcast_to(rate_ref[n : n + 1, cols], (SEQS, LANES)) for n in range(STATES)]
        skip = jnp.broadcast_to(skip_ref[0:1, cols], (SEQS, LANES))

        def run(i, carry):
            h, skip_sum = carry
            for k in range(unroll):
                t = i * unroll + k
                dt = dt_ref[t, :, cols]
                act = act_ref[t, :, cols]
                u = dt * act
                new = []
                y = None
                for p in range(PAIRS):
                    for n in (2 * p, 2 * p + 1):
                        new.append(jnp.exp2(dt * rates[n]) * h[n] + u * b_scr[t, n])
                    low = pair(new[2 * p], new[2 * p + 1])
                    hist_ref[part, t + 1, p] = low
                    term = low * c_scr[t, p]
                    y = term if p == 0 else y + term
                h = tuple(new)
                mixed = folded(y) + skip * act
                gated_ref[t, :, cols] = (mixed * silu_ref[t, :, cols].astype(f32)).astype(bf16)
                gategrad_ref[t + HALO, :, cols] = (mixed * slope_ref[t, :, cols].astype(f32)).astype(bf16)
                skip_sum = skip_sum + yg_ref[t, :, cols] * act
            return h, skip_sum

        start = tuple(start_ref[:, n, cols] for n in range(STATES))
        for p in range(PAIRS):
            hist_ref[part, 0, p] = pair(start[2 * p], start[2 * p + 1])
        _, skip_sum = lax.fori_loop(0, steps // unroll, run, (start, jnp.zeros((SEQS, LANES), f32)))
        skipg_ref[:, cols] = jnp.sum(skip_sum, axis=0, keepdims=True)


def forward(proj, dt, act, yg, silu, slope, rate, start, skip, select):
    grid, steps, _, _ = act.shape
    channels = grid * WIDE
    tile = lambda j: (0, 0, j)
    flat = pl.BlockSpec((None, steps, SEQS, WIDE), lambda j: (j, 0, 0, 0))
    parts = len(TILES)
    return pl.pallas_call(
        forward_kernel,
        grid=(grid,),
        in_specs=[
            pl.BlockSpec((steps * SEQS, LANES), lambda j: (0, 0)),
            flat, flat, flat, flat, flat,
            pl.BlockSpec((STATES, WIDE), lambda j: (0, j)),
            pl.BlockSpec((SEQS, STATES, WIDE), tile),
            pl.BlockSpec((1, WIDE), lambda j: (0, j)),
            pl.BlockSpec(select.shape, lambda j: (0, 0)),
        ],
        out_specs=[
            pl.BlockSpec((steps, SEQS, WIDE), tile),
            pl.BlockSpec((None, parts, steps + 1, PAIRS, 2 * SEQS, LANES), lambda j: (j, 0, 0, 0, 0, 0)),
            pl.BlockSpec((steps + HALO, SEQS, WIDE), tile),
            pl.BlockSpec((1, WIDE), lambda j: (0, j)),
        ],
        out_shape=[
            jax.ShapeDtypeStruct((steps, SEQS, channels), bf16),
            jax.ShapeDtypeStruct((grid, parts, steps + 1, PAIRS, 2 * SEQS, LANES), bf16),
            jax.ShapeDtypeStruct((steps + HALO, SEQS, channels), bf16),
            jax.ShapeDtypeStruct((1, channels), f32),
        ],
        scratch_shapes=[
            pltpu.VMEM((steps, STATES, SEQS, LANES), f32),
            pltpu.VMEM((steps, PAIRS, 2 * SEQS, LANES), bf16),
        ],
        compiler_params=params(),
        cost_estimate=cost(50),
        name="forward_scan",
    )(proj, dt, act, yg, silu, slope, rate, start, skip, select)


def backward_kernel(
    proj_ref, dt_ref, sig_ref, act_ref, yg_ref, rate_ref, end_ref, skip_ref,
    hist_ref, rank_t_ref, stepw_t_ref, pick_ref, select_ref,
    act_grad_ref, stepg_ref, biasg_ref, decayg_ref, projg_ref,
    b_scr, c_scr, db_scr, dc_scr, pre_scr, acc_scr, decay_scr, ge_scr, sum_scr,
):
    j = pl.program_id(0)
    steps = dt_ref.shape[0]

    @pl.when(j == 0)
    def _():
        spread_maps(proj_ref, select_ref, RANK, STATES, store_pairs(b_scr))
        spread_maps(proj_ref, select_ref, RANK + STATES, STATES, store_plain(c_scr))

        def clear(t, _):
            for p in range(PAIRS):
                db_scr[t, p] = jnp.zeros((2 * SEQS, LANES), bf16)
                dc_scr[t, p] = jnp.zeros((2 * SEQS, LANES), bf16)
            return 0

        lax.fori_loop(0, steps, clear, 0)
        acc_scr[...] = jnp.zeros_like(acc_scr)

    decay_scr[...] = jnp.zeros_like(decay_scr)
    sum_scr[...] = jnp.zeros_like(sum_scr)
    for n in range(STATES):
        ge_scr[n] = end_ref[:, n, :]

    def run(i, _):
        base = steps - (i + 1) * RUN
        db = [[None] * PAIRS for _ in range(RUN)]
        dc = [[None] * PAIRS for _ in range(RUN)]
        for part, cols in enumerate(TILES):
            rates = [jnp.broadcast_to(rate_ref[n : n + 1, cols], (SEQS, LANES)) for n in range(STATES)]
            low_rates = [pair(rates[2 * p], rates[2 * p + 1]) for p in range(PAIRS)]
            skip = jnp.broadcast_to(skip_ref[0:1, cols], (SEQS, LANES))
            ge = [ge_scr[n, :, cols] for n in range(STATES)]
            bias_sum = jnp.zeros((SEQS, LANES), f32)
            decay = [None] * PAIRS
            for k in range(RUN - 1, -1, -1):
                t = base + k
                dt = dt_ref[t, :, cols]
                act = act_ref[t, :, cols]
                yg = yg_ref[t, :, cols]
                u2 = both(dt * act)
                dt2 = both(dt)
                yg2 = both(yg)
                du = None
                ddt = None
                for p in range(PAIRS):
                    g = [ge[n] + yg * c_scr[t, n] for n in (2 * p, 2 * p + 1)]
                    g2 = pair(*g)
                    term = yg2 * hist_ref[part, t + 1, p]
                    dc[k][p] = term if part == 0 else dc[k][p] + term
                    term = g2 * u2
                    db[k][p] = term if part == 0 else db[k][p] + term
                    term = g2 * b_scr[t, p]
                    du = term if p == 0 else du + term
                    gn = [jnp.exp2(dt * rates[2 * p + m]) * g[m] for m in (0, 1)]
                    ge[2 * p], ge[2 * p + 1] = gn
                    q = pair(*gn) * hist_ref[part, t, p]
                    term = q * dt2
                    decay[p] = term if decay[p] is None else decay[p] + term
                    term = q * low_rates[p]
                    ddt = term if p == 0 else ddt + term
                du = folded(du)
                pre_grad = (du * act + folded(ddt) * LN2) * sig_ref[t, :, cols].astype(f32)
                pre_scr[t, :, cols] = pre_grad.astype(bf16)
                act_grad_ref[t, :, cols] = yg * skip + du * dt
                bias_sum = bias_sum + pre_grad
                if part == len(TILES) - 1:
                    for p in range(PAIRS):
                        dc_scr[t, p] = dc[k][p] + dc_scr[t, p]
                        db_scr[t, p] = db[k][p] + db_scr[t, p]
            for p in range(PAIRS):
                a, b = halves(decay[p])
                decay_scr[2 * p, :, cols] += a
                decay_scr[2 * p + 1, :, cols] += b
            for n in range(STATES):
                ge_scr[n, :, cols] = ge[n]
            sum_scr[:, cols] += bias_sum
        return 0

    lax.fori_loop(0, steps // RUN, run, 0)
    for n in range(STATES):
        decayg_ref[n : n + 1, :] = jnp.sum(decay_scr[n] * rate_ref[n : n + 1, :], axis=0, keepdims=True) * LN2
    biasg_ref[...] = jnp.sum(sum_scr[...], axis=0, keepdims=True)

    pre_low = pre_scr[...].reshape(steps * SEQS, WIDE)
    stepg_ref[...] = jnp.dot(rank_t_ref[...], pre_low, preferred_element_type=f32)
    acc_scr[...] += jnp.dot(pre_low, stepw_t_ref[...], preferred_element_type=f32)

    @pl.when(j == pl.num_programs(0) - 1)
    def _():
        chunk = 32
        even = lax.broadcasted_iota(jnp.int32, (chunk, SEQS, LANES), 2) % 2 == 0

        def step(i, _):
            t = i * chunk
            total = jnp.zeros((chunk * 2 * SEQS, LANES), f32)
            for p in range(PAIRS):
                rows = jnp.concatenate([db_scr[pl.ds(t, chunk), p], dc_scr[pl.ds(t, chunk), p]], axis=2)
                rows = rows.reshape(chunk * 2 * SEQS, 2 * LANES)
                total = total + jnp.dot(rows, pick_ref[p], preferred_element_type=f32)
            total = total.reshape(chunk, 2 * SEQS, LANES)
            total = jnp.where(even, total[:, :SEQS], total[:, SEQS:]).reshape(chunk * SEQS, LANES)
            r = pl.multiple_of(t * SEQS, chunk * SEQS)
            projg_ref[pl.ds(r, chunk * SEQS), :] = (acc_scr[pl.ds(r, chunk * SEQS), :] + total).astype(bf16)
            return 0

        lax.fori_loop(0, steps // chunk, step, 0)


def backward(proj, dt, sig, act, yg, rate, end, skip, hist, rank_t, stepw_t, pick, select):
    grid, steps, _, _ = act.shape
    channels = grid * WIDE
    tile = lambda j: (0, 0, j)
    whole = lambda j: (0, 0)
    flat = pl.BlockSpec((None, steps, SEQS, WIDE), lambda j: (j, 0, 0, 0))
    sums = pltpu.VMEM((steps, PAIRS, 2 * SEQS, LANES), bf16)
    return pl.pallas_call(
        backward_kernel,
        grid=(grid,),
        in_specs=[
            pl.BlockSpec((steps * SEQS, LANES), whole),
            flat, flat, flat, flat,
            pl.BlockSpec((STATES, WIDE), lambda j: (0, j)),
            pl.BlockSpec((SEQS, STATES, WIDE), tile),
            pl.BlockSpec((1, WIDE), lambda j: (0, j)),
            pl.BlockSpec(
                (None, len(TILES), steps + 1, PAIRS, 2 * SEQS, LANES), lambda j: (j, 0, 0, 0, 0, 0)
            ),
            pl.BlockSpec((RANK, steps * SEQS), whole),
            pl.BlockSpec((WIDE, LANES), lambda j: (j, 0)),
            pl.BlockSpec(pick.shape, lambda j: (0, 0, 0)),
            pl.BlockSpec(select.shape, whole),
        ],
        out_specs=[
            flat,
            pl.BlockSpec((RANK, WIDE), lambda j: (0, j)),
            pl.BlockSpec((1, WIDE), lambda j: (0, j)),
            pl.BlockSpec((STATES, WIDE), lambda j: (0, j)),
            pl.BlockSpec((steps * SEQS, LANES), whole),
        ],
        out_shape=[
            jax.ShapeDtypeStruct(act.shape, f32),
            jax.ShapeDtypeStruct((RANK, channels), f32),
            jax.ShapeDtypeStruct((1, channels), f32),
            jax.ShapeDtypeStruct((STATES, channels), f32),
            jax.ShapeDtypeStruct((steps * SEQS, LANES), bf16),
        ],
        scratch_shapes=[
            sums,
            pltpu.VMEM((steps, STATES, SEQS, LANES), f32),
            sums, sums,
            pltpu.VMEM((steps, SEQS, WIDE), bf16),
            pltpu.VMEM((steps * SEQS, LANES), f32),
            pltpu.VMEM((STATES, SEQS, WIDE), f32),
            pltpu.VMEM((STATES, SEQS, WIDE), f32),
            pltpu.VMEM((SEQS, WIDE), f32),
        ],
        compiler_params=params(),
        cost_estimate=cost(90),
        name="backward_scan",
    )(proj, dt, sig, act, yg, rate, end, skip, hist, rank_t, stepw_t, pick, select)


def filter_back_kernel(
    mix_ref, act_ref, bend_ref, act_grad_ref, projg_ref, projg_t_ref, sel_ref, fw_ref,
    mixgrad_ref, selg_ref, fwg_ref, fbg_ref,
    dv_scr,
):
    steps = act_ref.shape[0]
    chunk = 16
    taps = [fw_ref[k : k + 1, :] for k in range(KERNEL)]
    zero = jnp.zeros((HALO, SEQS, WIDE), f32)
    dv_scr[0:HALO] = zero
    dv_scr[steps + HALO :] = zero

    def step(i, sums):
        t = i * chunk
        x = mix_ref[pl.ds(t, chunk + HALO)].astype(f32)
        r = pl.multiple_of(t * SEQS, chunk * SEQS)
        more = contract_cols(projg_ref[pl.ds(r, chunk * SEQS), :], sel_ref[...])
        total = act_grad_ref[pl.ds(t, chunk)] + more.reshape(chunk, SEQS, WIDE)
        dv = total * bend_ref[pl.ds(t, chunk)].astype(f32)
        dv_scr[pl.ds(t + HALO, chunk)] = dv
        new = [sums[0] + jnp.sum(dv, axis=0)]
        for k in range(KERNEL):
            new.append(sums[1 + k] + jnp.sum(dv * x[1 + k : 1 + k + chunk], axis=0))
        return tuple(new)

    sums = lax.fori_loop(
        0, steps // chunk, step, tuple(jnp.zeros((SEQS, WIDE), f32) for _ in range(KERNEL + 1))
    )
    fbg_ref[...] = jnp.sum(sums[0], axis=0, keepdims=True)
    for k in range(KERNEL):
        fwg_ref[k : k + 1, :] = jnp.sum(sums[1 + k], axis=0, keepdims=True)

    def spread(t, count):
        dv = dv_scr[pl.ds(t, count + HALO)]
        out = taps[KERNEL - 1][None] * dv[0:count]
        for k in range(KERNEL - 1):
            s = KERNEL - 1 - k
            out = out + taps[k][None] * dv[s : s + count]
        mixgrad_ref[pl.ds(t, count)] = out.astype(bf16)

    def out_step(i, _):
        spread(i * chunk, chunk)
        return 0

    lax.fori_loop(0, steps // chunk, out_step, 0)
    spread(steps, HALO)
    low = act_ref[...].reshape(steps * SEQS, WIDE).astype(bf16)
    selg_ref[...] = jnp.dot(projg_t_ref[...], low, preferred_element_type=f32)


def filter_back(mixture, act, bend, act_grad, projg, projg_t, select_pad, fw):
    grid, steps, _, _ = act.shape
    channels = grid * WIDE
    wide = lambda j: (0, 0, j)
    whole = lambda j: (0, 0)
    cols = lambda j: (0, j)
    return pl.pallas_call(
        filter_back_kernel,
        grid=(grid,),
        in_specs=[
            pl.BlockSpec((None, steps + HALO, SEQS, WIDE), lambda j: (j, 0, 0, 0)),
            pl.BlockSpec((None, steps, SEQS, WIDE), lambda j: (j, 0, 0, 0)),
            pl.BlockSpec((None, steps, SEQS, WIDE), lambda j: (j, 0, 0, 0)),
            pl.BlockSpec((None, steps, SEQS, WIDE), lambda j: (j, 0, 0, 0)),
            pl.BlockSpec((steps * SEQS, LANES), whole),
            pl.BlockSpec((LANES, steps * SEQS), whole),
            pl.BlockSpec((WIDE, LANES), lambda j: (j, 0)),
            pl.BlockSpec((KERNEL, WIDE), cols),
        ],
        out_specs=[
            pl.BlockSpec((steps + HALO, SEQS, WIDE), wide),
            pl.BlockSpec((LANES, WIDE), cols),
            pl.BlockSpec((KERNEL, WIDE), cols),
            pl.BlockSpec((1, WIDE), cols),
        ],
        out_shape=[
            jax.ShapeDtypeStruct((steps + HALO, SEQS, channels), bf16),
            jax.ShapeDtypeStruct((LANES, channels), f32),
            jax.ShapeDtypeStruct((KERNEL, channels), f32),
            jax.ShapeDtypeStruct((1, channels), f32),
        ],
        scratch_shapes=[pltpu.VMEM((steps + 2 * HALO, SEQS, WIDE), f32)],
        compiler_params=params(),
        cost_estimate=cost(20),
        name="filter_back",
    )(mixture, act, bend, act_grad, projg, projg_t, select_pad, fw)


def send(src, dst, send_sem, recv_sem, peer, axis="fsdp"):
    return pltpu.make_async_remote_copy(
        src_ref=src,
        dst_ref=dst,
        send_sem=send_sem,
        recv_sem=recv_sem,
        device_id={axis: peer},
        device_id_type=pl.DeviceIdType.MESH,
    )


def greet(others):
    barrier = pltpu.get_barrier_semaphore()
    for axis, peer in others:
        pl.semaphore_signal(barrier, inc=1, device_id={axis: peer}, device_id_type=pl.DeviceIdType.MESH)
    pl.semaphore_wait(barrier, len(others))


def flipped(index, bit):
    return index + (1 - 2 * (index // bit % 2)) * bit


FIRST, SECOND = (0, 1, 2, 3), (4, 5)
TRADED = (2, 3, 4, 5)


def gather_kernel(
    rows_ref, select_ref, out_ref, in_ref, all_rows, all_select, all_out, all_in,
    local_sems, own_send, own_recv, pass_send, pass_recv, core_send, core_recv, trade_send, trade_recv,
):
    me = lax.axis_index("fsdp")
    mz = lax.axis_index("replica")
    a, b = flipped(me, 2), flipped(me, 4)
    corner = flipped(a, 4)
    twin = flipped(me, 1)
    mate = flipped(mz, 1)
    greet([("fsdp", a), ("fsdp", b), ("fsdp", twin), ("replica", mate)])
    kinds = ((rows_ref, all_rows), (select_ref, all_select), (out_ref, all_out), (in_ref, all_in))

    def span(piece, side):
        if piece < 2:
            return piece, 0, kinds[piece][0].shape[0]
        kind = 2 + piece % 2
        quarter = kinds[kind][0].shape[0] // 4
        return kind, side * (2 * quarter) + (quarter if piece in SECOND else 0), quarter

    def place(owner, piece, side):
        kind, start, count = span(piece, side)
        first = owner * kinds[kind][0].shape[0] + start
        return kinds[kind][1].at[pl.ds(pl.multiple_of(first, 16), count)]

    def mine(piece, side):
        kind, start, count = span(piece, side)
        return kinds[kind][0].at[pl.ds(pl.multiple_of(start, 16), count) if piece in TRADED else pl.ds(0, count)]

    side = mz % 2
    other = 1 - side
    started = []

    def start(copy):
        copy.start()
        started.append(copy)

    def own_copy(piece, k, peer, owner):
        return send(mine(piece, side), place(owner, piece, side), own_send.at[k, piece], own_recv.at[k, piece], peer)

    def pass_copy(piece, peer, owner, far=False):
        ref = place(owner, piece, other if far else side)
        at = piece + len(FIRST + SECOND) * far
        return send(ref, ref, pass_send.at[at], pass_recv.at[at], peer)

    def trade_copy(piece, k, owner, whose):
        ref = place(owner, piece, whose)
        return send(ref, ref, trade_send.at[k, piece], trade_recv.at[k, piece], mate, "replica")

    def core_copy(piece, k, owner, whose=None):
        if whose is None:
            return send(
                place(owner, piece, side), place(owner, piece, side), core_send.at[k, piece], core_recv.at[k, piece], twin
            )
        at = len(FIRST + SECOND) + piece
        ref = place(owner, piece, whose)
        return send(ref, ref, core_send.at[k, at], core_recv.at[k, at], twin)

    def whole_copy(kind, owner):
        src, dst = kinds[kind]
        count = src.shape[0]
        rows = dst.at[pl.ds(pl.multiple_of(owner * count, count), count)]
        return send(src, rows, core_send.at[3, kind], core_recv.at[3, kind], twin)

    for piece in FIRST + SECOND:
        start(own_copy(piece, 0, a, me))
    for piece in SECOND + (2, 3, 0, 1):
        start(own_copy(piece, 1, b, me))
    local = []
    for kind, (src, dst) in enumerate(kinds):
        start(whole_copy(kind, me))
        count = src.shape[0]
        rows = dst.at[pl.ds(pl.multiple_of(me * count, count), count)]
        copy = pltpu.make_async_copy(src, rows, local_sems.at[kind])
        copy.start()
        local.append(copy)
    owners = (a, b, corner)

    def arrived(piece, k):
        owner = owners[k]
        if k == 2:
            pass_copy(piece, a, owner).wait_recv()
        else:
            own_copy(piece, k, a, owner).wait_recv()
            if k == 0 and piece in FIRST:
                start(pass_copy(piece, b, owner))
            if k == 1 and piece in SECOND:
                start(pass_copy(piece, a, owner))
        if piece in TRADED and k < 2:
            start(trade_copy(piece, k, owner, side))
        start(core_copy(piece, k, owner))

    def traded(piece, k):
        owner = owners[k]
        trade_copy(piece, k, owner, other).wait_recv()
        if k == 0 and piece in FIRST:
            start(pass_copy(piece, b, owner, True))
        if k == 1 and piece in SECOND:
            start(pass_copy(piece, a, owner, True))
        start(core_copy(piece, k, owner, other))

    for piece, k in ((0, 0), (4, 1), (1, 0), (2, 0), (5, 1), (3, 0)):
        arrived(piece, k)
    traded(2, 0)
    traded(4, 1)
    arrived(4, 0)
    arrived(2, 1)
    traded(3, 0)
    traded(5, 1)
    for piece, k in ((5, 0), (3, 1), (0, 1), (1, 1), (0, 2), (1, 2), (2, 2), (4, 2), (3, 2), (5, 2)):
        arrived(piece, k)
    for piece, k in ((4, 0), (2, 1), (5, 0), (3, 1)):
        traded(piece, k)
    for piece in (2, 4, 3, 5):
        pass_copy(piece, a, corner, True).wait_recv()
        start(core_copy(piece, 2, corner, other))
    for kind in range(len(kinds)):
        whole_copy(kind, twin).wait_recv()
    for k, owner in enumerate((flipped(twin, 2), flipped(twin, 4), flipped(corner, 1))):
        for piece in FIRST + SECOND:
            core_copy(piece, k, owner).wait_recv()
        for piece in TRADED:
            core_copy(piece, k, owner, other).wait_recv()
    for copy in started:
        copy.wait_send()
    for copy in local:
        copy.wait()


def gather(*shards):
    size = lax.axis_size("fsdp")
    if size != 8 or lax.axis_size("replica") % 2:
        return [lax.all_gather(shard, "fsdp", axis=0, tiled=True) for shard in shards]
    vmem = pl.BlockSpec(memory_space=pltpu.VMEM)
    hbm = pl.BlockSpec(memory_space=pl.ANY)
    pieces = len(FIRST + SECOND)
    dma = pltpu.SemaphoreType.DMA
    return pl.pallas_call(
        gather_kernel,
        in_specs=[vmem] * 4,
        out_specs=[hbm] * 4,
        out_shape=[jax.ShapeDtypeStruct((size * shard.shape[0], shard.shape[1]), bf16) for shard in shards],
        scratch_shapes=[
            dma((len(shards),)), dma((2, pieces)), dma((2, pieces)), dma((2 * pieces,)), dma((2 * pieces,)),
            dma((4, 2 * pieces)), dma((4, 2 * pieces)), dma((3, pieces)), dma((3, pieces)),
        ],
        compiler_params=params(collective_id=2, has_side_effects=True),
        cost_estimate=cost(55),
        name="gather",
    )(*shards)


SMALL = (KERNEL, 1, 1, 1, STATES, RANK, RANK + 2 * STATES, 1)
SMALL_ROWS = 192


def xor(index, bits):
    for bit in (1, 2, 4, 8):
        if bits & bit:
            index = flipped(index, bit)
    return index


def tail_kernel(
    one_hot_ref, b0, b1, b2, b3, filter_ref, fbias_ref, sbias_ref, skip_ref, decay_ref, step_ref, select_ref,
    gain_ref, halo_ref, block_out, small_out, rim_out,
    total, to_z, from_z, part, parts, small_f, small_ref, got_small, small_z, small_from_z, small_part,
    small_parts, rim, child, got_rim, got_child,
    sems_s, sems_z, sems_p, sems_sz, sems_sp, sems_r, sems_cs, sems_cr,
):
    depth = lax.axis_size("replica")
    me, size = lax.axis_index("fsdp"), lax.axis_size("fsdp")
    mz = lax.axis_index("replica")
    last = size - 1
    near = [lax.rem(me + d, size) for d in range(1, size)]
    far = [lax.rem(mz + d, depth) for d in range(1, depth)]
    greet([("fsdp", peer) for peer in near] + [("replica", peer) for peer in far])

    def spread(src, dst, sems, peers, axis, index):
        copies = []
        for d, peer in enumerate(peers):
            source = src.at[peer] if src.shape[0] == len(peers) + 1 and len(src.shape) == len(dst.shape) else src
            copy = send(source, dst.at[index], sems.at[0, d], sems.at[1, d], peer, axis)
            copy.start()
            copies.append(copy)
        return copies

    width = small_f.shape[2]
    small_f[...] = jnp.zeros_like(small_f)
    refs = (filter_ref, fbias_ref, sbias_ref, skip_ref, decay_ref, step_ref, select_ref)
    for k in range(size):
        at = 0
        for ref, count in zip(refs, SMALL):
            small_f[k, at : at + count] = ref[0:count, k * width : (k + 1) * width]
            at += count
        some = gain_ref.shape[1] // size
        small_f[k, at : at + 1, 0:some] = gain_ref[:, k * some : (k + 1) * some]
    small_ref[...] = small_f[...].astype(bf16)
    sequels = one_hot_ref.shape[0]
    pieces = (SEQS - PROMPTS) // sequels
    for t in range(HALO):
        rim[t * PROMPTS : (t + 1) * PROMPTS] = halo_ref[t, 0:PROMPTS]
        for p in range(PROMPTS):
            sums = None
            for q in range(sequels):
                row = PROMPTS + q * pieces
                term = one_hot_ref[q, p] * halo_ref[t, row : row + 1]
                sums = term if q == 0 else sums + term
            child[t * PROMPTS + p : t * PROMPTS + p + 1] = sums
    block = b0[...].astype(f32) + b1[...].astype(f32) + b2[...].astype(f32) + b3[...].astype(f32)
    total[...] = block.reshape(total.shape)
    to_z[...] = total[...].astype(bf16)
    to_left = send(rim, got_rim, sems_r.at[0], sems_r.at[1], lax.rem(me + last, size))
    to_left.start()

    @pl.when(me != last)
    def _():
        send(child, got_child.at[me], sems_cs.at[me], sems_cr.at[me], last).start()

    copies = spread(small_ref, got_small, sems_s, near, "fsdp", me)
    z_copies = spread(to_z, from_z, sems_z, far, "replica", mz)
    small = small_ref[me].astype(f32)
    got_small[me] = jnp.zeros(got_small.shape[1:], bf16)
    from_z[mz] = jnp.zeros(from_z.shape[1:], bf16)
    small_from_z[mz] = jnp.zeros(small_from_z.shape[1:], bf16)
    for copy in copies:
        copy.wait()
    for k in range(size):
        small = small + got_small[k].astype(f32)
    small_z[...] = small.reshape(small_z.shape)
    small_to_z = small_part
    small_to_z[...] = small_z[...].astype(bf16)
    s_copies = spread(small_to_z, small_from_z, sems_sz, far, "replica", mz)
    for copy in z_copies:
        copy.wait()
    own = total[mz]
    for k in range(depth):
        own = own + from_z[k].astype(f32)
    part[...] = own.astype(bf16)
    p_copies = spread(part, parts, sems_p, far, "replica", mz)
    parts[mz] = part[...]
    for copy in s_copies:
        copy.wait()
    own = small_z[mz]
    for k in range(depth):
        own = own + small_from_z[k].astype(f32)
    small_parts[mz] = own.astype(bf16)
    small_own = small_to_z.at[mz]
    small_own[...] = own.astype(bf16)
    q_copies = []
    for d, peer in enumerate(far):
        copy = send(small_own, small_parts.at[mz], sems_sp.at[0, d], sems_sp.at[1, d], peer, "replica")
        copy.start()
        q_copies.append(copy)
    for copy in p_copies + q_copies:
        copy.wait()
    block_out[...] = parts[...].reshape(block_out.shape)
    small_out[...] = small_parts[...].reshape(small_out.shape)
    to_left.wait()

    @pl.when(me != last)
    def _():
        send(child, got_child.at[me], sems_cs.at[me], sems_cr.at[me], last).wait_send()
        rim_out[...] = got_rim[...]

    @pl.when(me == last)
    def _():
        sums = child[...]
        for k in range(size - 1):
            send(child, got_child.at[k], sems_cs.at[k], sems_cr.at[k], 0).wait_recv()
            sums = sums + got_child[k]
        rim_out[...] = sums


def tail(one_hot, blocks, small, halo_grad):
    size, depth = lax.axis_size("fsdp"), lax.axis_size("replica")
    vmem = pl.BlockSpec(memory_space=pltpu.VMEM)
    dma = pltpu.SemaphoreType.DMA
    while len(blocks) > 4:
        blocks = blocks[:3] + [summed(blocks[3], blocks[4:5]).astype(bf16)] + blocks[5:]
    rows, channels = blocks[0].shape
    features = small[-1].shape[1]
    width = channels // size
    cut = (depth, rows // depth, channels)
    by_owner = (size, SMALL_ROWS, width)
    small_cut = (depth, SMALL_ROWS // depth, width)
    rim = (HALO * PROMPTS, features)
    return pl.pallas_call(
        tail_kernel,
        in_specs=[pl.BlockSpec(memory_space=pltpu.SMEM)] + [vmem] * (4 + len(small) + 1),
        out_specs=[vmem] * 3,
        out_shape=[
            jax.ShapeDtypeStruct((rows, channels), bf16),
            jax.ShapeDtypeStruct((SMALL_ROWS, width), bf16),
            jax.ShapeDtypeStruct(rim, f32),
        ],
        scratch_shapes=[
            pltpu.VMEM(cut, f32), pltpu.VMEM(cut, bf16), pltpu.VMEM(cut, bf16),
            pltpu.VMEM(cut[1:], bf16), pltpu.VMEM(cut, bf16),
            pltpu.VMEM(by_owner, f32), pltpu.VMEM(by_owner, bf16), pltpu.VMEM(by_owner, bf16),
            pltpu.VMEM(small_cut, f32), pltpu.VMEM(small_cut, bf16),
            pltpu.VMEM(small_cut, bf16), pltpu.VMEM(small_cut, bf16),
            pltpu.VMEM(rim, f32), pltpu.VMEM(rim, f32), pltpu.VMEM(rim, f32), pltpu.VMEM((size,) + rim, f32),
            dma((2, size)), dma((2, depth)), dma((2, depth)), dma((2, depth)), dma((2, depth)),
            dma((2,)), dma((size,)), dma((size,)),
        ],
        compiler_params=params(collective_id=4, has_side_effects=True),
        cost_estimate=cost(30),
        name="tail",
    )(one_hot, *blocks, *small, halo_grad)


def deliver_kernel(block_ref, small_ref, rim_ref, prompt_ref, *rest):
    depth = lax.axis_size("replica")
    early_refs, outs = rest[:depth], rest[depth:-1]
    early = rest[-1]
    in_out, out_out, prompt_out = outs[:3]
    mz = lax.axis_index("replica")
    half = in_out.shape[1] // 2
    in_out[:, 0:half] = block_ref[...].astype(f32)
    small = small_ref[...].astype(f32)
    at = 0
    for out, count in zip(outs[3:], SMALL):
        rows = small[at : at + count]
        out[...] = rows[:, 0 : out.shape[1]]
        at += count
    for d, ref in enumerate(early_refs):
        count = ref.shape[0]
        early[pl.ds(pl.multiple_of(xor(mz, d) * count, count), count), :] = ref[...].astype(f32)
    rows = out_out.shape[0] // 2
    features = out_out.shape[1]
    out_out[0:rows, :] = early[0:rows, 0:features]
    out_out[rows:, :] = early[0:rows, features:]
    in_out[:, half:] = early[rows:, :]
    for p in range(PROMPTS):
        prompt_out[p, 0 : SEQS - HALO] = prompt_ref[p, 0 : SEQS - HALO]
        for t in range(HALO):
            row = SEQS - HALO + t
            prompt_out[p, row : row + 1] = (
                prompt_ref[p, row : row + 1] + rim_ref[t * PROMPTS + p : t * PROMPTS + p + 1]
            )


def deliver(block, small, rim, prompt_grad, early):
    size = lax.axis_size("fsdp")
    rows, channels = block.shape
    width = small.shape[1]
    features = prompt_grad.shape[2]
    vmem = pl.BlockSpec(memory_space=pltpu.VMEM)
    end = prompt_grad.shape[1] // SEQS - 1
    last = pl.BlockSpec((PROMPTS, SEQS, features), lambda i: (0, end, 0))
    shapes = [(count, width) for count in SMALL[:-1]] + [(1, features // size)]
    shapes = [(rows, 2 * channels), (2 * rows, features), prompt_grad.shape] + shapes
    return pl.pallas_call(
        deliver_kernel,
        grid=(1,),
        in_specs=[vmem, vmem, vmem, last] + [vmem] * len(early),
        out_specs=[vmem, vmem, last] + [vmem] * len(SMALL),
        out_shape=[jax.ShapeDtypeStruct(shape, f32) for shape in shapes],
        scratch_shapes=[pltpu.VMEM((2 * rows, channels), f32)],
        input_output_aliases={3: 2},
        compiler_params=params(),
        cost_estimate=cost(4),
        name="deliver",
    )(block, small, rim, prompt_grad, *early)


def contract_rows(left_side, right_side):
    return lax.dot_general(
        left_side, right_side, (((0,), (0,)), ((), ())), preferred_element_type=f32
    )


def contract_cols(left_side, right_side):
    return lax.dot_general(
        left_side, right_side, (((1,), (1,)), ((), ())), preferred_element_type=f32
    )


def exchanged(block, axis, distance):
    return lax.ppermute(block, axis, [(i, i ^ distance) for i in range(lax.axis_size(axis))])


def pick_row(block, index, axis=0):
    return lax.dynamic_index_in_dim(block, index, axis, keepdims=False)


def over_cores(blocks):
    blocks = blocks.reshape((-1, 2) + blocks.shape[1:])
    core = lax.axis_index("fsdp") % 2
    got = exchanged(pick_row(blocks, 1 - core, 1), "fsdp", 1)
    return (pick_row(blocks, core, 1).astype(f32) + got.astype(f32)).astype(bf16)


def to_chips(blocks):
    chip = lax.axis_index("fsdp") // 2
    got = [exchanged(pick_row(blocks, chip ^ d), "fsdp", 2 * d) for d in range(1, blocks.shape[0])]
    return pick_row(blocks, chip), got


def summed(own, got):
    total = own.astype(f32)
    for block in got:
        total = total + block.astype(f32)
    return total


def to_replicas(block):
    size, here = lax.axis_size("replica"), lax.axis_index("replica")
    parts = block.astype(bf16).reshape((size, -1) + block.shape[1:])
    own = pick_row(block.reshape(parts.shape), here)
    return own, [exchanged(pick_row(parts, here ^ d), "replica", d) for d in range(1, size)]


def from_replicas(part):
    return [part] + [exchanged(part, "replica", d) for d in range(1, lax.axis_size("replica"))]


def body(
    prompt_hidden, sequel_hidden, parents, prompt_cotangent, sequel_cotangent,
    norm_gain, input_weight, filter_weight, depthwise_filter_bias, select_weight,
    step_weight, step_bias, decay_log, skip_gain, output_weight,
):
    size, here = lax.axis_size("fsdp"), lax.axis_index("fsdp")
    prompts, steps = prompt_hidden.shape[:2]
    sequels, sequel_len = sequel_hidden.shape[:2]
    split = sequel_len // steps
    assert prompts == PROMPTS and sequels * split == SEQS - prompts
    rim = KERNEL - 1
    half = SEQS // 2
    rows = steps * SEQS

    after = lax.optimization_barrier
    width = step_bias.shape[0]
    tail_rows = prompt_hidden[:, steps - rim :]
    shard = jnp.concatenate(
        [
            step_weight,
            tail_rows.reshape(-1, width),
            filter_weight,
            depthwise_filter_bias[None],
            step_bias[None],
            skip_gain[None],
            jnp.pad(norm_gain, (0, width - norm_gain.shape[0]))[None],
        ],
        axis=0,
    )
    shard = jnp.pad(shard, ((0, -shard.shape[0] % 16), (0, 0)))
    lanes = jnp.concatenate([select_weight, decay_log], axis=1)
    lanes = jnp.pad(lanes, ((0, 0), (0, LANES - lanes.shape[1])))
    every, select_pad, full_output, full_input = gather(shard, lanes, output_weight, input_weight)
    every = every.reshape(size, shard.shape[0], width)
    at = RANK + tail_rows.size // width
    tails = every[:, RANK:at].reshape((size,) + tail_rows.shape)
    step_full = jnp.swapaxes(every[:, :RANK], 0, 1).reshape(RANK, -1)
    vectors = jnp.swapaxes(every[:, at : at + SEQS], 0, 1).astype(f32)
    gain = vectors[KERNEL + 3, :, : norm_gain.shape[0]].reshape(1, -1)
    vectors = vectors.reshape(SEQS, -1)
    fw, fb, sbias, skip = vectors[:KERNEL], vectors[4:5], vectors[5:6], vectors[6:7]
    first = RANK + 2 * STATES
    rate = -jnp.exp(select_pad[:, first : first + STATES].T.astype(f32)) * LOG2E
    step_pad = jnp.pad(step_full, ((0, LANES - RANK), (0, 0)))

    before = jnp.where(here > 0, tails[jnp.maximum(here - 1, 0)], jnp.zeros_like(tails[0]))
    cut = sequel_hidden.reshape(sequels, split, steps, D)
    inner = jnp.concatenate([tails[size - 1][parents][:, None], cut[:, :-1, steps - rim :]], axis=1)
    halo = jnp.concatenate([before, inner.reshape(-1, rim, D)], axis=0)
    halo = jnp.pad(jnp.swapaxes(halo, 0, 1), ((HALO - rim, 0), (0, 0), (0, 0))).reshape(-1, D).astype(f32)
    pieces = sequel_hidden.reshape(-1, steps, D)
    piece_cot = sequel_cotangent.reshape(-1, steps, D)
    scaled, cotangent = prepare(prompt_hidden, pieces, prompt_cotangent, piece_cot, halo, gain)

    mixture = product([scaled], full_input, bf16, part=0, parts=2, tiled=True)
    gate = product([scaled], full_input, f32, part=1, parts=2, tiled=True)
    mixture = mixture.reshape(-1, steps + HALO, SEQS, WIDE)
    gate = gate.reshape(-1, steps + HALO, SEQS, WIDE)
    gated_grad = product([cotangent], full_output, f32, across=True, tiled=True)
    gated_grad = gated_grad.reshape(-1, steps, SEQS, WIDE)
    act, bend, proj = front(mixture, fw, fb, select_pad, steps)
    groups = 1 if split == 1 else 2
    lane = jnp.arange(2 * STATES * LANES)[None, :]
    select = (jnp.arange(LANES)[:, None] == RANK + lane // LANES).astype(bf16)
    dt, sig, yg, silu, slope, ahead, behind, total = piece(
        proj, act, gate, gated_grad, step_pad, sbias, rate, select, groups
    )

    one_hot = (parents[:, None] == jnp.arange(PROMPTS, dtype=jnp.int32)[None, :]).astype(f32)
    own = total[half:].reshape(sequels, split, 1, INNER)
    own_behind = behind[half:].reshape(sequels, split, STATES, INNER)
    back = own_behind[:, split - 1]
    own_end = [jnp.zeros_like(back)]
    for p in range(split - 2, -1, -1):
        own_end.insert(0, back)
        back = own_behind[:, p] + jnp.exp2(rate * own[:, p]) * back
    joint = behind if split == 1 else jnp.concatenate([behind[:half], back], axis=0)
    start, end = chain(one_hot, ahead, joint, total, rate)
    if split > 1:
        state = start[half:]
        own_start = [state]
        for p in range(split - 1):
            state = jnp.exp2(rate * own[:, p]) * state + ahead[half:].reshape(own_behind.shape)[:, p]
            own_start.append(state)
        own_start = jnp.stack(own_start, axis=1).reshape(half, STATES, INNER)
        start = jnp.concatenate([start[:half], own_start], axis=0)
        end = jnp.concatenate([end[:half], jnp.stack(own_end, axis=1).reshape(half, STATES, INNER)], axis=0)

    gated, hist, gate_grad, skip_grad = forward(
        proj, dt, act, yg, silu, slope, rate, start, skip, select
    )
    gated = gated.reshape(rows, INNER)
    gate_grad = gate_grad.reshape(-1, INNER)
    output_grad = contract_rows(gated, cotangent).astype(bf16).reshape(size, -1, D)
    gate_weight_grad = contract_rows(scaled, gate_grad).astype(bf16)
    early = [over_cores(output_grad), over_cores(gate_weight_grad.reshape(size, -1, INNER))]
    wide = jnp.concatenate([early[0][:, : INNER // size // 2], early[0][:, INNER // size // 2 :]], axis=2)
    early = jnp.concatenate([wide, early[1]], axis=1)
    end, early = after((end, early))
    early = to_chips(early)

    rank_t = proj[:, :RANK].astype(bf16).T
    lane = jnp.arange(LANES)[None, None, :]
    which = jnp.arange(PAIRS)[:, None, None]
    source = jnp.arange(2 * LANES)[None, :, None]
    pick = (lane // 2 == jnp.where(source < LANES, RANK, RANK + STATES) // 2 + which).astype(bf16)
    act_grad, step_grad, bias_grad, decay_grad, projg = backward(
        proj, dt, sig, act, yg, rate, end, skip, hist, rank_t, step_pad.T, pick, select
    )
    projg, early = after((projg, early))
    early = summed(*early)
    projg, early = after((projg, early))
    early = to_replicas(early)
    filter_in_grad, select_grad, filter_grad, filter_bias_grad = filter_back(
        mixture, act, bend, act_grad, projg, projg.T, select_pad, fw
    )
    filter_in_grad, early = after((filter_in_grad, early))
    early = summed(*early).astype(bf16)
    filter_in_grad = filter_in_grad.reshape(-1, INNER)
    filter_weight_grad = contract_rows(scaled, filter_in_grad).astype(bf16)
    filter_weight_grad, early = after((filter_weight_grad, early))
    late = over_cores(filter_weight_grad.reshape(size, -1, INNER))
    early = from_replicas(early)
    mixed = jnp.dot(gated, full_output, preferred_element_type=f32)
    late, mixed, filter_in_grad = after((late, mixed, filter_in_grad))
    own_block, late = to_chips(late)
    scaled_grad = product([filter_in_grad, gate_grad], full_input, f32, across=True)
    prompt_out, piece_out, prompt_grad, piece_grad, halo_grad, gain_grad = finish(
        mixed, scaled_grad, prompt_hidden, pieces, prompt_cotangent, piece_cot, halo, gain
    )
    halo_grad, own_block, late = after((halo_grad, own_block, late))
    halo_grad = halo_grad.reshape(HALO, SEQS, D)
    small = [
        filter_grad, filter_bias_grad, bias_grad, skip_grad, decay_grad, step_grad, select_grad, gain_grad,
    ]
    block, small, following = tail(one_hot, [own_block] + late, small, halo_grad)
    (
        input_grad, output_grad, prompt_grad, g_filter, g_fbias, g_sbias, g_skip, g_decay, g_step, g_select, g_gain,
    ) = deliver(block, small, following, prompt_grad, early)
    if split > 1:
        own = jnp.swapaxes(halo_grad[:, half:], 0, 1).reshape(sequels, split, HALO, D)
        own = jnp.pad(own[:, 1:], ((0, 0), (0, 1), (0, 0), (0, 0))).reshape(half, HALO, D)
        piece_grad = piece_grad.at[:, steps - HALO :].add(own)
    return (
        prompt_out,
        piece_out.reshape(sequel_hidden.shape),
        prompt_grad,
        piece_grad.reshape(sequel_hidden.shape),
        g_gain[0],
        input_grad,
        g_filter,
        g_fbias[0],
        g_select.T,
        g_step,
        g_sbias[0],
        g_decay.T,
        g_skip[0],
        output_grad,
    )


def solution(mesh):
    rows = P("replica", "fsdp", None)
    own = P(("replica", "fsdp"), None, None)
    return jax.shard_map(
        body,
        mesh=mesh,
        in_specs=(
            rows, own, P(("replica", "fsdp")), rows, own,
            P("fsdp"), P("fsdp", None), P(None, "fsdp"), P("fsdp"), P("fsdp", None),
            P(None, "fsdp"), P("fsdp"), P("fsdp", None), P("fsdp"), P("fsdp", None),
        ),
        out_specs=(
            rows, own, rows, own,
            P("fsdp"), P("fsdp", None), P(None, "fsdp"), P("fsdp"), P("fsdp", None),
            P(None, "fsdp"), P("fsdp"), P("fsdp", None), P("fsdp"), P("fsdp", None),
        ),
        check_vma=False,
    )
```

```python
import functools
import math

import jax
import jax.numpy as jnp
from jax import lax
from jax.experimental import pallas as pl
from jax.experimental.pallas import tpu as pltpu
from jax.sharding import PartitionSpec as P

D = 1024
INNER = 2048
STATES = 16
RANK = 64
KERNEL = 4
PROMPTS = 4

SEQS = 8
HALO = 4
LANES = 128
WIDE = 256
LOG2E = math.log2(math.e)
LN2 = math.log(2.0)
f32 = jnp.float32
bf16 = jnp.bfloat16

VMEM_LIMIT = 62 * 1024 * 1024


def cost(microseconds):
    return pl.CostEstimate(flops=int(microseconds * 1e9), bytes_accessed=0, transcendentals=0)


def params(**kw):
    return pltpu.CompilerParams(vmem_limit_bytes=VMEM_LIMIT, **kw)


def sigmoid(x):
    return 1.0 / (1.0 + jnp.exp(-x))


def softplus(x):
    return jnp.maximum(x, 0.0) + jnp.log1p(jnp.exp(-jnp.abs(x)))


def product_kernel(across, *refs):
    lefts, rhs_ref, out_ref = refs[:-2], refs[-2], refs[-1]
    total = None
    at = 0
    for left in lefts:
        depth = left.shape[1]
        rhs = rhs_ref[:, at : at + depth] if across else rhs_ref[at : at + depth]
        dims = (((1,), (1 if across else 0,)), ((), ()))
        term = lax.dot_general(left[...], rhs, dims, preferred_element_type=f32)
        total = term if total is None else total + term
        at += depth
    if len(out_ref.shape) == 2:
        out_ref[...] = total.astype(out_ref.dtype)
    else:
        for k in range(out_ref.shape[0]):
            out_ref[k] = total[:, k * WIDE : (k + 1) * WIDE].astype(out_ref.dtype)


def product(lefts, rhs, kind, across=False, part=0, parts=1, tiled=False):
    rows = lefts[0].shape[0]
    depth = sum(left.shape[1] for left in lefts)
    tile = 2 * WIDE if len(lefts) == 1 else WIDE
    if across:
        columns = rhs.shape[0]
        rhs_spec = pl.BlockSpec((tile, depth), lambda j: (j, 0))
    else:
        columns = rhs.shape[1] // parts
        first = part * columns // tile
        rhs_spec = pl.BlockSpec((depth, tile), lambda j: (0, first + j))
    return pl.pallas_call(
        functools.partial(product_kernel, across),
        grid=(columns // tile,),
        in_specs=[pl.BlockSpec(left.shape, lambda j: (0, 0)) for left in lefts] + [rhs_spec],
        out_specs=pl.BlockSpec((tile // WIDE, rows, WIDE), lambda j: (j, 0, 0))
        if tiled
        else pl.BlockSpec((rows, tile), lambda j: (0, j)),
        out_shape=jax.ShapeDtypeStruct((columns // WIDE, rows, WIDE) if tiled else (rows, columns), kind),
        compiler_params=params(),
        cost_estimate=cost(0.01),
        name="product",
    )(*lefts, rhs)


def scale_of(rows):
    return lax.rsqrt(jnp.mean(rows * rows, axis=-1, keepdims=True) + 1e-05)


def by_time(prompt_ref, piece_ref):
    both_kinds = jnp.concatenate([prompt_ref[...], piece_ref[...]], axis=0).astype(f32)
    return jnp.swapaxes(both_kinds, 0, 1)


def prepare_kernel(prompt_ref, piece_ref, prompt_cot_ref, piece_cot_ref, halo_ref, gain_ref, scaled_ref, cot_ref):
    i = pl.program_id(0)
    gain = gain_ref[...]

    @pl.when(i == 0)
    def _():
        rows = halo_ref[...]
        scaled_ref[0 : HALO * SEQS, :] = (rows * scale_of(rows) * gain).astype(bf16)

    rows = by_time(prompt_ref, piece_ref)
    count = rows.shape[0] * SEQS
    rows = rows.reshape(count, D)
    at = pl.multiple_of(HALO * SEQS + i * count, HALO * SEQS)
    scaled_ref[pl.ds(at, count), :] = (rows * scale_of(rows) * gain).astype(bf16)
    cot_ref[...] = by_time(prompt_cot_ref, piece_cot_ref).reshape(count, D).astype(bf16)


CHUNK = 16


def prepare(prompt, piece, prompt_cot, piece_cot, halo, gain):
    steps = prompt.shape[1]
    part = pl.BlockSpec((SEQS // 2, CHUNK, D), lambda i: (0, i, 0))
    rows = steps * SEQS
    return pl.pallas_call(
        prepare_kernel,
        grid=(steps // CHUNK,),
        in_specs=[
            part, part, part, part,
            pl.BlockSpec((HALO * SEQS, D), lambda i: (0, 0)),
            pl.BlockSpec((1, D), lambda i: (0, 0)),
        ],
        out_specs=[
            pl.BlockSpec((HALO * SEQS + rows, D), lambda i: (0, 0)),
            pl.BlockSpec((CHUNK * SEQS, D), lambda i: (i, 0)),
        ],
        out_shape=[
            jax.ShapeDtypeStruct((HALO * SEQS + rows, D), bf16),
            jax.ShapeDtypeStruct((rows, D), bf16),
        ],
        compiler_params=params(),
        cost_estimate=cost(5),
        name="prepare",
    )(prompt, piece, prompt_cot, piece_cot, halo, gain)


def norm_back(rows, scaled_grad, gain):
    inverse = scale_of(rows)
    unit = rows * inverse
    grad = scaled_grad * gain
    back = inverse * (grad - unit * jnp.mean(grad * unit, axis=-1, keepdims=True))
    return back, scaled_grad * unit


def finish_kernel(
    mixed_ref, grad_ref, grad_halo_ref,
    prompt_ref, piece_ref, prompt_cot_ref, piece_cot_ref, halo_ref, gain_ref,
    prompt_out, piece_out, prompt_grad, piece_grad, halo_grad, gain_grad,
):
    i = pl.program_id(0)
    gain = gain_ref[...]

    @pl.when(i == 0)
    def _():
        back, sums = norm_back(halo_ref[...], grad_halo_ref[...], gain)
        halo_grad[...] = back
        gain_grad[...] = jnp.sum(sums, axis=0, keepdims=True)

    half = SEQS // 2
    rows = by_time(prompt_ref, piece_ref)
    shape = rows.shape
    rows = rows.reshape(-1, D)
    back, sums = norm_back(rows, grad_ref[...], gain)
    gain_grad[...] += jnp.sum(sums, axis=0, keepdims=True)
    back = jnp.swapaxes(back.reshape(shape), 0, 1)
    prompt_grad[...] = back[:half] + prompt_cot_ref[...].astype(f32)
    piece_grad[...] = back[half:] + piece_cot_ref[...].astype(f32)
    mixed = jnp.swapaxes((mixed_ref[...] + rows).reshape(shape), 0, 1)
    prompt_out[...] = mixed[:half].astype(bf16)
    piece_out[...] = mixed[half:].astype(bf16)


def finish(mixed, grad, prompt, piece, prompt_cot, piece_cot, halo, gain):
    steps = prompt.shape[1]
    part = pl.BlockSpec((SEQS // 2, CHUNK, D), lambda i: (0, i, 0))
    first = pl.BlockSpec((HALO * SEQS, D), lambda i: (0, 0))
    shifted = pl.BlockSpec(
        (pl.Element(CHUNK * SEQS), pl.Element(D)),
        lambda i: (pl.multiple_of(HALO * SEQS + i * (CHUNK * SEQS), HALO * SEQS), 0),
    )
    return pl.pallas_call(
        finish_kernel,
        grid=(steps // CHUNK,),
        in_specs=[
            pl.BlockSpec((CHUNK * SEQS, D), lambda i: (i, 0)),
            shifted, first,
            part, part, part, part,
            first,
            pl.BlockSpec((1, D), lambda i: (0, 0)),
        ],
        out_specs=[part, part, part, part, first, pl.BlockSpec((1, D), lambda i: (0, 0))],
        out_shape=[
            jax.ShapeDtypeStruct(prompt.shape, bf16),
            jax.ShapeDtypeStruct(piece.shape, bf16),
            jax.ShapeDtypeStruct(prompt.shape, f32),
            jax.ShapeDtypeStruct(piece.shape, f32),
            jax.ShapeDtypeStruct((HALO * SEQS, D), f32),
            jax.ShapeDtypeStruct((1, D), f32),
        ],
        compiler_params=params(),
        cost_estimate=cost(0.01),
        name="finish",
    )(mixed, grad, grad, prompt, piece, prompt_cot, piece_cot, halo, gain)


def front_kernel(mix_ref, fw_ref, fb_ref, sel_ref, act_ref, bend_ref, proj_ref, low_scr):
    j = pl.program_id(0)
    steps = act_ref.shape[0]
    chunk = 16
    taps = [fw_ref[k : k + 1, :] for k in range(KERNEL)]
    bias = fb_ref[0:1, :]

    @pl.when(j == 0)
    def _():
        proj_ref[...] = jnp.zeros_like(proj_ref)

    def step(i, _):
        t = i * chunk
        x = mix_ref[pl.ds(t, chunk + HALO)].astype(f32)
        v = bias[None] + taps[0][None] * x[1 : 1 + chunk]
        for k in range(1, KERNEL):
            v = v + taps[k][None] * x[1 + k : 1 + k + chunk]
        sig = sigmoid(v)
        act = v * sig
        act_ref[pl.ds(t, chunk)] = act
        bend_ref[pl.ds(t, chunk)] = (sig + act * (1.0 - sig)).astype(bf16)
        r = pl.multiple_of(t * SEQS, chunk * SEQS)
        low_scr[pl.ds(r, chunk * SEQS), :] = act.reshape(chunk * SEQS, act.shape[-1]).astype(bf16)
        return 0

    lax.fori_loop(0, steps // chunk, step, 0)
    proj_ref[...] += jnp.dot(low_scr[...], sel_ref[...], preferred_element_type=f32)


def front(mixture, fw, fb, select_pad, steps):
    channels = fw.shape[1]
    return pl.pallas_call(
        front_kernel,
        grid=(channels // WIDE,),
        in_specs=[
            pl.BlockSpec((None, steps + HALO, SEQS, WIDE), lambda j: (j, 0, 0, 0)),
            pl.BlockSpec((KERNEL, WIDE), lambda j: (0, j)),
            pl.BlockSpec((1, WIDE), lambda j: (0, j)),
            pl.BlockSpec((WIDE, LANES), lambda j: (j, 0)),
        ],
        out_specs=[
            pl.BlockSpec((None, steps, SEQS, WIDE), lambda j: (j, 0, 0, 0)),
            pl.BlockSpec((None, steps, SEQS, WIDE), lambda j: (j, 0, 0, 0)),
            pl.BlockSpec((steps * SEQS, LANES), lambda j: (0, 0)),
        ],
        out_shape=[
            jax.ShapeDtypeStruct((channels // WIDE, steps, SEQS, WIDE), f32),
            jax.ShapeDtypeStruct((channels // WIDE, steps, SEQS, WIDE), bf16),
            jax.ShapeDtypeStruct((steps * SEQS, LANES), f32),
        ],
        scratch_shapes=[pltpu.VMEM((steps * SEQS, WIDE), bf16)],
        compiler_params=params(),
        cost_estimate=cost(16),
        name="front",
    )(mixture, fw, fb, select_pad)


def pair(a, b):
    return jnp.concatenate([a, b], axis=0).astype(bf16)


def both(v):
    return pair(v, v)


def halves(v):
    v = v.astype(f32)
    return v[:SEQS], v[SEQS:]


def folded(v):
    a, b = halves(v)
    return a + b


def spread_maps(proj_ref, select_ref, first, count, store):
    steps = proj_ref.shape[0] // SEQS
    chunk = 32

    def step(i, _):
        r = pl.multiple_of(i * chunk * SEQS, chunk * SEQS)
        rows = proj_ref[pl.ds(r, chunk * SEQS), :].astype(bf16)
        for n in range(0, count, 2):
            at = (first - RANK + n) * LANES
            wide = jnp.dot(rows, select_ref[:, at : at + 2 * LANES], preferred_element_type=f32)
            wide = wide.reshape(chunk, SEQS, 2 * LANES)
            store(i * chunk, chunk, n, wide[:, :, :LANES], wide[:, :, LANES:])
        return 0

    lax.fori_loop(0, steps // chunk, step, 0)


def store_plain(ref):
    def store(t, count, n, a, b):
        ref[pl.ds(t, count), n] = a
        ref[pl.ds(t, count), n + 1] = b

    return store


def store_pairs(ref):
    def store(t, count, n, a, b):
        ref[pl.ds(t, count), n // 2] = jnp.concatenate([a, b], axis=1).astype(bf16)

    return store


PAIRS = STATES // 2
RUN = 8


def piece_kernel(
    proj_ref, act_ref, gate_ref, gg_ref, stepw_ref, sbias_ref, rate_ref, select_ref,
    dt_ref, sig_ref, yg_ref, silu_ref, slope_ref, fwd_ref, bwd_ref, tot_ref,
    b_scr, c_scr, time_scr, acc_scr,
):
    j = pl.program_id(0)
    steps = dt_ref.shape[0]
    half = SEQS // 2
    groups = fwd_ref.shape[0] // half

    @pl.when(j == 0)
    def _():
        def store_groups(t, count, n, a, b):
            for group in range(groups):
                rows = slice(group * half, (group + 1) * half)
                parts = [a[:, rows], a[:, rows], b[:, rows], b[:, rows]]
                b_scr[group, pl.ds(t, count), n // 2] = jnp.concatenate(parts, axis=1).astype(bf16)

        spread_maps(proj_ref, select_ref, RANK, STATES, store_groups)
        spread_maps(proj_ref, select_ref, RANK + STATES, STATES, store_pairs(c_scr))

    chunk = 8
    sbias = sbias_ref[0:1, :]
    pre = jnp.dot(proj_ref[...].astype(bf16), stepw_ref[...], preferred_element_type=f32)
    time_scr[...] = pre.reshape(steps, SEQS, WIDE)

    def prep(i, total):
        t = i * chunk
        pre = time_scr[pl.ds(t, chunk)] + sbias[None]
        small = jnp.exp2(jnp.abs(pre) * -LOG2E)
        one = 1.0 + small
        inverse = 1.0 / one
        dt = jnp.maximum(pre, 0.0) + (jnp.log(one) + (small - (one - 1.0)) * inverse)
        dt_ref[pl.ds(t, chunk)] = dt
        sig_ref[pl.ds(t, chunk)] = jnp.where(pre >= 0.0, inverse, small * inverse).astype(bf16)
        gate = gate_ref[pl.ds(t + HALO, chunk)]
        gg = gg_ref[pl.ds(t, chunk)]
        sig = sigmoid(gate)
        silu = gate * sig
        yg_ref[pl.ds(t, chunk)] = gg * silu
        silu_ref[pl.ds(t, chunk)] = silu.astype(bf16)
        slope_ref[pl.ds(t, chunk)] = (gg * (sig + silu * (1.0 - sig))).astype(bf16)
        for k in range(chunk):
            total = total + dt[k]
            time_scr[t + k] = total
        return total

    total = lax.fori_loop(0, steps // chunk, prep, jnp.zeros((SEQS, WIDE), f32))
    tot_ref[...] = total

    units = []

    low = lax.broadcasted_iota(jnp.int32, (SEQS, LANES), 0) < half
    packed = [
        jnp.where(low, rate_ref[n : n + 1, :LANES], rate_ref[n : n + 1, LANES:])
        for n in range(STATES)
    ]
    packed = [pair(packed[2 * p], packed[2 * p + 1]) for p in range(PAIRS)]

    def forward_unit(group):
        rows = slice(group * half, (group + 1) * half)

        def pack(v):
            return jnp.concatenate([v[rows, :LANES], v[rows, LANES:]], axis=0)

        whole = pack(total)

        def vectors(t):
            return both(whole - pack(time_scr[t])), both(pack(dt_ref[t] * act_ref[t]))

        def out(n, value):
            fwd_ref[rows, n, :LANES] = value[:half]
            fwd_ref[rows, n, LANES:] = value[half:]

        return packed, vectors, lambda t, p: b_scr[group, t, p], out

    def backward_unit(cols):
        mine = [jnp.broadcast_to(rate_ref[n : n + 1, cols], (SEQS, LANES)) for n in range(STATES)]
        mine = [pair(mine[2 * p], mine[2 * p + 1]) for p in range(PAIRS)]

        def vectors(t):
            return both(time_scr[t, :, cols]), both(yg_ref[t, :, cols])

        def out(n, value):
            bwd_ref[:, n, cols] = value

        return mine, vectors, lambda t, p: c_scr[t, p], out

    for group in range(groups):
        units.append(forward_unit(group))
    for part in range(WIDE // LANES):
        units.append(backward_unit(slice(part * LANES, (part + 1) * LANES)))
    acc_scr[...] = jnp.zeros_like(acc_scr)

    def run(i, _):
        for k, (rates, vectors, map_at, _) in enumerate(units):
            sums = [None] * PAIRS
            for m in range(RUN):
                t = i * RUN + m
                time, drive = vectors(t)
                for p in range(PAIRS):
                    term = jnp.exp2(time * rates[p]) * drive * map_at(t, p)
                    sums[p] = term if m == 0 else sums[p] + term
            for p in range(PAIRS):
                a, b = halves(sums[p])
                acc_scr[k, 2 * p] += a
                acc_scr[k, 2 * p + 1] += b
        return 0

    lax.fori_loop(0, steps // RUN, run, 0)
    for k, (_, _, _, out) in enumerate(units):
        for n in range(STATES):
            out(n, acc_scr[k, n])


def piece(proj, act, gate, gated_grad, step_pad, sbias, rate, select, groups):
    grid, steps, _, _ = act.shape
    channels = grid * WIDE
    wide = lambda j: (0, 0, j)
    flat = pl.BlockSpec((None, steps, SEQS, WIDE), lambda j: (j, 0, 0, 0))
    shape = act.shape
    return pl.pallas_call(
        piece_kernel,
        grid=(grid,),
        in_specs=[
            pl.BlockSpec((steps * SEQS, LANES), lambda j: (0, 0)),
            flat,
            pl.BlockSpec((None, steps + HALO, SEQS, WIDE), lambda j: (j, 0, 0, 0)),
            flat,
            pl.BlockSpec((LANES, WIDE), lambda j: (0, j)),
            pl.BlockSpec((1, WIDE), lambda j: (0, j)),
            pl.BlockSpec((STATES, WIDE), lambda j: (0, j)),
            pl.BlockSpec(select.shape, lambda j: (0, 0)),
        ],
        out_specs=[
            flat, flat, flat, flat, flat,
            pl.BlockSpec((groups * SEQS // 2, STATES, WIDE), wide),
            pl.BlockSpec((SEQS, STATES, WIDE), wide),
            pl.BlockSpec((SEQS, WIDE), lambda j: (0, j)),
        ],
        out_shape=[
            jax.ShapeDtypeStruct(shape, f32),
            jax.ShapeDtypeStruct(shape, bf16),
            jax.ShapeDtypeStruct(shape, f32),
            jax.ShapeDtypeStruct(shape, bf16),
            jax.ShapeDtypeStruct(shape, bf16),
            jax.ShapeDtypeStruct((groups * SEQS // 2, STATES, channels), f32),
            jax.ShapeDtypeStruct((SEQS, STATES, channels), f32),
            jax.ShapeDtypeStruct((SEQS, channels), f32),
        ],
        scratch_shapes=[
            pltpu.VMEM((groups, steps, PAIRS, 2 * SEQS, LANES), bf16),
            pltpu.VMEM((steps, PAIRS, 2 * SEQS, LANES), bf16),
            pltpu.VMEM((steps, SEQS, WIDE), f32),
            pltpu.VMEM((groups + WIDE // LANES, STATES, SEQS, LANES), f32),
        ],
        compiler_params=params(),
        cost_estimate=cost(60),
        name="piece",
    )(proj, act, gate, gated_grad, step_pad, sbias, rate, select)


def chain_kernel(
    one_hot_ref, ahead_ref, behind_ref, time_ref, rate_ref, start_out, end_out,
    moved_ref, got, got_time, back, done, sems, time_sems, back_sems,
):
    size = got.shape[0]
    width = got.shape[2]
    count = PROMPTS * STATES
    sequels = one_hot_ref.shape[0]
    me = lax.axis_index("fsdp")
    for p in range(PROMPTS):
        rows = slice(p * STATES, (p + 1) * STATES)
        total = one_hot_ref[0, p] * behind_ref[PROMPTS]
        for k in range(1, sequels):
            total = total + one_hot_ref[k, p] * behind_ref[PROMPTS + k]
        moved_ref[0 * count + p * STATES : 0 * count + (p + 1) * STATES] = ahead_ref[p].astype(bf16)
        moved_ref[1 * count + p * STATES : 1 * count + (p + 1) * STATES] = behind_ref[p].astype(bf16)
        moved_ref[2 * count + p * STATES : 2 * count + (p + 1) * STATES] = total.astype(bf16)
    barrier = pltpu.get_barrier_semaphore()
    for d in range(1, size):
        peer = lax.rem(me + d, size)
        pl.semaphore_signal(barrier, inc=1, device_id={"fsdp": peer}, device_id_type=pl.DeviceIdType.MESH)
    pl.semaphore_wait(barrier, size - 1)

    def columns(device):
        return pl.ds(pl.multiple_of(device * width, width), width)

    copies = []
    for d in range(1, size):
        peer = lax.rem(me + d, size)
        for src, dst, sem in ((moved_ref, got, sems), (time_ref, got_time, time_sems)):
            copy = pltpu.make_async_remote_copy(
                src_ref=src.at[:, columns(peer)],
                dst_ref=dst.at[me],
                send_sem=sem.at[0, d],
                recv_sem=sem.at[1, d],
                device_id={"fsdp": peer},
                device_id_type=pl.DeviceIdType.MESH,
            )
            copy.start()
            copies.append(copy)
    got[me] = moved_ref[:, columns(me)]
    got_time[me] = time_ref[:, columns(me)]
    for copy in copies:
        copy.wait()

    rate = jnp.concatenate([rate_ref[...]] * PROMPTS, axis=0)
    branch = jnp.zeros((count, width), f32)
    state = jnp.zeros((count, width), f32)
    decays = []
    for k in range(size):
        time = jnp.concatenate(
            [jnp.broadcast_to(got_time[k, p : p + 1, :], (STATES, width)) for p in range(PROMPTS)], axis=0
        )
        decays.append(jnp.exp2(rate * time))
        back[k, 0:count] = state.astype(bf16)
        state = decays[k] * state + got[k, 0:count].astype(f32)
        branch = branch + got[k, 2 * count : 3 * count].astype(f32)
    grad = branch
    for k in range(size - 1, -1, -1):
        back[k, count : 2 * count] = grad.astype(bf16)
        grad = decays[k] * grad + got[k, count : 2 * count].astype(f32)
    last = state.astype(bf16)
    for k in range(size):
        back[k, 2 * count : 3 * count] = last
    copies = []
    for d in range(1, size):
        peer = lax.rem(me + d, size)
        copy = pltpu.make_async_remote_copy(
            src_ref=back.at[peer],
            dst_ref=done.at[me],
            send_sem=back_sems.at[0, d],
            recv_sem=back_sems.at[1, d],
            device_id={"fsdp": peer},
            device_id_type=pl.DeviceIdType.MESH,
        )
        copy.start()
        copies.append(copy)
    done[me] = back[me]
    for copy in copies:
        copy.wait()
    for k in range(size):
        columns_k = slice(k * width, (k + 1) * width)
        last = []
        for p in range(PROMPTS):
            rows = slice(p * STATES, (p + 1) * STATES)
            start_out[p, :, columns_k] = done[k, rows].astype(f32)
            rows = slice(count + p * STATES, count + (p + 1) * STATES)
            end_out[p, :, columns_k] = done[k, rows].astype(f32)
            rows = slice(2 * count + p * STATES, 2 * count + (p + 1) * STATES)
            last.append(done[k, rows].astype(f32))
        for q in range(sequels):
            total = one_hot_ref[q, 0] * last[0]
            for p in range(1, PROMPTS):
                total = total + one_hot_ref[q, p] * last[p]
            start_out[PROMPTS + q, :, columns_k] = total
            end_out[PROMPTS + q, :, columns_k] = jnp.zeros_like(total)


def chain(one_hot, ahead, behind, time, rate):
    size = lax.axis_size("fsdp")
    channels = ahead.shape[2]
    rows = 3 * PROMPTS * STATES
    width = channels // size
    own = lax.dynamic_slice_in_dim(rate, lax.axis_index("fsdp") * width, width, 1)
    whole = pl.BlockSpec(memory_space=pltpu.VMEM)
    shape = (PROMPTS + one_hot.shape[0], STATES, channels)
    return pl.pallas_call(
        chain_kernel,
        in_specs=[pl.BlockSpec(memory_space=pltpu.SMEM)] + [whole] * 4,
        out_specs=[whole] * 2,
        out_shape=[jax.ShapeDtypeStruct(shape, f32)] * 2,
        scratch_shapes=[
            pltpu.VMEM((rows, channels), bf16),
            pltpu.VMEM((size, rows, width), bf16),
            pltpu.VMEM((size, SEQS, width), f32),
            pltpu.VMEM((size, rows, width), bf16),
            pltpu.VMEM((size, rows, width), bf16),
            pltpu.SemaphoreType.DMA((2, size)),
            pltpu.SemaphoreType.DMA((2, size)),
            pltpu.SemaphoreType.DMA((2, size)),
        ],
        compiler_params=params(collective_id=1, has_side_effects=True),
        cost_estimate=cost(25),
        name="chain",
    )(one_hot, ahead, behind, time, own)


TILES = [slice(k * LANES, (k + 1) * LANES) for k in range(WIDE // LANES)]


def forward_kernel(
    proj_ref, dt_ref, act_ref, yg_ref, silu_ref, slope_ref, rate_ref, start_ref, skip_ref, select_ref,
    gated_ref, hist_ref, gategrad_ref, skipg_ref,
    b_scr, c_scr,
):
    j = pl.program_id(0)
    steps = dt_ref.shape[0]

    @pl.when(j == 0)
    def _():
        spread_maps(proj_ref, select_ref, RANK, STATES, store_plain(b_scr))
        spread_maps(proj_ref, select_ref, RANK + STATES, STATES, store_pairs(c_scr))

    gategrad_ref[0:HALO] = jnp.zeros((HALO, SEQS, WIDE), bf16)
    unroll = 8

    for part, cols in enumerate(TILES):
        rates = [jnp.broadcast_to(rate_ref[n : n + 1, cols], (SEQS, LANES)) for n in range(STATES)]
        skip = jnp.broadcast_to(skip_ref[0:1, cols], (SEQS, LANES))

        def run(i, carry):
            h, skip_sum = carry
            for k in range(unroll):
                t = i * unroll + k
                dt = dt_ref[t, :, cols]
                act = act_ref[t, :, cols]
                u = dt * act
                new = []
                y = None
                for p in range(PAIRS):
                    for n in (2 * p, 2 * p + 1):
                        new.append(jnp.exp2(dt * rates[n]) * h[n] + u * b_scr[t, n])
                    low = pair(new[2 * p], new[2 * p + 1])
                    hist_ref[part, t + 1, p] = low
                    term = low * c_scr[t, p]
                    y = term if p == 0 else y + term
                h = tuple(new)
                mixed = folded(y) + skip * act
                gated_ref[t, :, cols] = (mixed * silu_ref[t, :, cols].astype(f32)).astype(bf16)
                gategrad_ref[t + HALO, :, cols] = (mixed * slope_ref[t, :, cols].astype(f32)).astype(bf16)
                skip_sum = skip_sum + yg_ref[t, :, cols] * act
            return h, skip_sum

        start = tuple(start_ref[:, n, cols] for n in range(STATES))
        for p in range(PAIRS):
            hist_ref[part, 0, p] = pair(start[2 * p], start[2 * p + 1])
        _, skip_sum = lax.fori_loop(0, steps // unroll, run, (start, jnp.zeros((SEQS, LANES), f32)))
        skipg_ref[:, cols] = jnp.sum(skip_sum, axis=0, keepdims=True)


def forward(proj, dt, act, yg, silu, slope, rate, start, skip, select):
    grid, steps, _, _ = act.shape
    channels = grid * WIDE
    tile = lambda j: (0, 0, j)
    flat = pl.BlockSpec((None, steps, SEQS, WIDE), lambda j: (j, 0, 0, 0))
    parts = len(TILES)
    return pl.pallas_call(
        forward_kernel,
        grid=(grid,),
        in_specs=[
            pl.BlockSpec((steps * SEQS, LANES), lambda j: (0, 0)),
            flat, flat, flat, flat, flat,
            pl.BlockSpec((STATES, WIDE), lambda j: (0, j)),
            pl.BlockSpec((SEQS, STATES, WIDE), tile),
            pl.BlockSpec((1, WIDE), lambda j: (0, j)),
            pl.BlockSpec(select.shape, lambda j: (0, 0)),
        ],
        out_specs=[
            pl.BlockSpec((steps, SEQS, WIDE), tile),
            pl.BlockSpec((None, parts, steps + 1, PAIRS, 2 * SEQS, LANES), lambda j: (j, 0, 0, 0, 0, 0)),
            pl.BlockSpec((steps + HALO, SEQS, WIDE), tile),
            pl.BlockSpec((1, WIDE), lambda j: (0, j)),
        ],
        out_shape=[
            jax.ShapeDtypeStruct((steps, SEQS, channels), bf16),
            jax.ShapeDtypeStruct((grid, parts, steps + 1, PAIRS, 2 * SEQS, LANES), bf16),
            jax.ShapeDtypeStruct((steps + HALO, SEQS, channels), bf16),
            jax.ShapeDtypeStruct((1, channels), f32),
        ],
        scratch_shapes=[
            pltpu.VMEM((steps, STATES, SEQS, LANES), f32),
            pltpu.VMEM((steps, PAIRS, 2 * SEQS, LANES), bf16),
        ],
        compiler_params=params(),
        cost_estimate=cost(50),
        name="forward_scan",
    )(proj, dt, act, yg, silu, slope, rate, start, skip, select)


def backward_kernel(
    proj_ref, dt_ref, sig_ref, act_ref, yg_ref, rate_ref, end_ref, skip_ref,
    hist_ref, rank_t_ref, stepw_t_ref, pick_ref, select_ref,
    act_grad_ref, stepg_ref, biasg_ref, decayg_ref, projg_ref,
    b_scr, c_scr, db_scr, dc_scr, pre_scr, acc_scr, decay_scr, ge_scr, sum_scr,
):
    j = pl.program_id(0)
    steps = dt_ref.shape[0]

    @pl.when(j == 0)
    def _():
        spread_maps(proj_ref, select_ref, RANK, STATES, store_pairs(b_scr))
        spread_maps(proj_ref, select_ref, RANK + STATES, STATES, store_plain(c_scr))

        def clear(t, _):
            for p in range(PAIRS):
                db_scr[t, p] = jnp.zeros((2 * SEQS, LANES), bf16)
                dc_scr[t, p] = jnp.zeros((2 * SEQS, LANES), bf16)
            return 0

        lax.fori_loop(0, steps, clear, 0)
        acc_scr[...] = jnp.zeros_like(acc_scr)

    decay_scr[...] = jnp.zeros_like(decay_scr)
    sum_scr[...] = jnp.zeros_like(sum_scr)
    for n in range(STATES):
        ge_scr[n] = end_ref[:, n, :]

    def run(i, _):
        base = steps - (i + 1) * RUN
        db = [[None] * PAIRS for _ in range(RUN)]
        dc = [[None] * PAIRS for _ in range(RUN)]
        for part, cols in enumerate(TILES):
            rates = [jnp.broadcast_to(rate_ref[n : n + 1, cols], (SEQS, LANES)) for n in range(STATES)]
            low_rates = [pair(rates[2 * p], rates[2 * p + 1]) for p in range(PAIRS)]
            skip = jnp.broadcast_to(skip_ref[0:1, cols], (SEQS, LANES))
            ge = [ge_scr[n, :, cols] for n in range(STATES)]
            bias_sum = jnp.zeros((SEQS, LANES), f32)
            decay = [None] * PAIRS
            for k in range(RUN - 1, -1, -1):
                t = base + k
                dt = dt_ref[t, :, cols]
                act = act_ref[t, :, cols]
                yg = yg_ref[t, :, cols]
                u2 = both(dt * act)
                dt2 = both(dt)
                yg2 = both(yg)
                du = None
                ddt = None
                for p in range(PAIRS):
                    g = [ge[n] + yg * c_scr[t, n] for n in (2 * p, 2 * p + 1)]
                    g2 = pair(*g)
                    term = yg2 * hist_ref[part, t + 1, p]
                    dc[k][p] = term if part == 0 else dc[k][p] + term
                    term = g2 * u2
                    db[k][p] = term if part == 0 else db[k][p] + term
                    term = g2 * b_scr[t, p]
                    du = term if p == 0 else du + term
                    gn = [jnp.exp2(dt * rates[2 * p + m]) * g[m] for m in (0, 1)]
                    ge[2 * p], ge[2 * p + 1] = gn
                    q = pair(*gn) * hist_ref[part, t, p]
                    term = q * dt2
                    decay[p] = term if decay[p] is None else decay[p] + term
                    term = q * low_rates[p]
                    ddt = term if p == 0 else ddt + term
                du = folded(du)
                pre_grad = (du * act + folded(ddt) * LN2) * sig_ref[t, :, cols].astype(f32)
                pre_scr[t, :, cols] = pre_grad.astype(bf16)
                act_grad_ref[t, :, cols] = yg * skip + du * dt
                bias_sum = bias_sum + pre_grad
                if part == len(TILES) - 1:
                    for p in range(PAIRS):
                        dc_scr[t, p] = dc[k][p] + dc_scr[t, p]
                        db_scr[t, p] = db[k][p] + db_scr[t, p]
            for p in range(PAIRS):
                a, b = halves(decay[p])
                decay_scr[2 * p, :, cols] += a
                decay_scr[2 * p + 1, :, cols] += b
            for n in range(STATES):
                ge_scr[n, :, cols] = ge[n]
            sum_scr[:, cols] += bias_sum
        return 0

    lax.fori_loop(0, steps // RUN, run, 0)
    for n in range(STATES):
        decayg_ref[n : n + 1, :] = jnp.sum(decay_scr[n] * rate_ref[n : n + 1, :], axis=0, keepdims=True) * LN2
    biasg_ref[...] = jnp.sum(sum_scr[...], axis=0, keepdims=True)

    pre_low = pre_scr[...].reshape(steps * SEQS, WIDE)
    stepg_ref[...] = jnp.dot(rank_t_ref[...], pre_low, preferred_element_type=f32)
    acc_scr[...] += jnp.dot(pre_low, stepw_t_ref[...], preferred_element_type=f32)

    @pl.when(j == pl.num_programs(0) - 1)
    def _():
        chunk = 32
        even = lax.broadcasted_iota(jnp.int32, (chunk, SEQS, LANES), 2) % 2 == 0

        def step(i, _):
            t = i * chunk
            total = jnp.zeros((chunk * 2 * SEQS, LANES), f32)
            for p in range(PAIRS):
                rows = jnp.concatenate([db_scr[pl.ds(t, chunk), p], dc_scr[pl.ds(t, chunk), p]], axis=2)
                rows = rows.reshape(chunk * 2 * SEQS, 2 * LANES)
                total = total + jnp.dot(rows, pick_ref[p], preferred_element_type=f32)
            total = total.reshape(chunk, 2 * SEQS, LANES)
            total = jnp.where(even, total[:, :SEQS], total[:, SEQS:]).reshape(chunk * SEQS, LANES)
            r = pl.multiple_of(t * SEQS, chunk * SEQS)
            projg_ref[pl.ds(r, chunk * SEQS), :] = (acc_scr[pl.ds(r, chunk * SEQS), :] + total).astype(bf16)
            return 0

        lax.fori_loop(0, steps // chunk, step, 0)


def backward(proj, dt, sig, act, yg, rate, end, skip, hist, rank_t, stepw_t, pick, select):
    grid, steps, _, _ = act.shape
    channels = grid * WIDE
    tile = lambda j: (0, 0, j)
    whole = lambda j: (0, 0)
    flat = pl.BlockSpec((None, steps, SEQS, WIDE), lambda j: (j, 0, 0, 0))
    sums = pltpu.VMEM((steps, PAIRS, 2 * SEQS, LANES), bf16)
    return pl.pallas_call(
        backward_kernel,
        grid=(grid,),
        in_specs=[
            pl.BlockSpec((steps * SEQS, LANES), whole),
            flat, flat, flat, flat,
            pl.BlockSpec((STATES, WIDE), lambda j: (0, j)),
            pl.BlockSpec((SEQS, STATES, WIDE), tile),
            pl.BlockSpec((1, WIDE), lambda j: (0, j)),
            pl.BlockSpec(
                (None, len(TILES), steps + 1, PAIRS, 2 * SEQS, LANES), lambda j: (j, 0, 0, 0, 0, 0)
            ),
            pl.BlockSpec((RANK, steps * SEQS), whole),
            pl.BlockSpec((WIDE, LANES), lambda j: (j, 0)),
            pl.BlockSpec(pick.shape, lambda j: (0, 0, 0)),
            pl.BlockSpec(select.shape, whole),
        ],
        out_specs=[
            flat,
            pl.BlockSpec((RANK, WIDE), lambda j: (0, j)),
            pl.BlockSpec((1, WIDE), lambda j: (0, j)),
            pl.BlockSpec((STATES, WIDE), lambda j: (0, j)),
            pl.BlockSpec((steps * SEQS, LANES), whole),
        ],
        out_shape=[
            jax.ShapeDtypeStruct(act.shape, f32),
            jax.ShapeDtypeStruct((RANK, channels), f32),
            jax.ShapeDtypeStruct((1, channels), f32),
            jax.ShapeDtypeStruct((STATES, channels), f32),
            jax.ShapeDtypeStruct((steps * SEQS, LANES), bf16),
        ],
        scratch_shapes=[
            sums,
            pltpu.VMEM((steps, STATES, SEQS, LANES), f32),
            sums, sums,
            pltpu.VMEM((steps, SEQS, WIDE), bf16),
            pltpu.VMEM((steps * SEQS, LANES), f32),
            pltpu.VMEM((STATES, SEQS, WIDE), f32),
            pltpu.VMEM((STATES, SEQS, WIDE), f32),
            pltpu.VMEM((SEQS, WIDE), f32),
        ],
        compiler_params=params(),
        cost_estimate=cost(90),
        name="backward_scan",
    )(proj, dt, sig, act, yg, rate, end, skip, hist, rank_t, stepw_t, pick, select)


def filter_back_kernel(
    mix_ref, act_ref, bend_ref, act_grad_ref, projg_ref, projg_t_ref, sel_ref, fw_ref,
    mixgrad_ref, selg_ref, fwg_ref, fbg_ref,
    dv_scr, more_scr,
):
    steps = act_ref.shape[0]
    chunk = 16
    taps = [fw_ref[k : k + 1, :] for k in range(KERNEL)]
    zero = jnp.zeros((HALO, SEQS, WIDE), f32)
    dv_scr[0:HALO] = zero
    dv_scr[steps + HALO :] = zero

    more = contract_cols(projg_ref[...], sel_ref[...])
    more_scr[...] = more.reshape(steps, SEQS, WIDE)

    def step(i, sums):
        t = i * chunk
        x = mix_ref[pl.ds(t, chunk + HALO)].astype(f32)
        total = act_grad_ref[pl.ds(t, chunk)] + more_scr[pl.ds(t, chunk)]
        dv = total * bend_ref[pl.ds(t, chunk)].astype(f32)
        dv_scr[pl.ds(t + HALO, chunk)] = dv
        new = [sums[0] + jnp.sum(dv, axis=0)]
        for k in range(KERNEL):
            new.append(sums[1 + k] + jnp.sum(dv * x[1 + k : 1 + k + chunk], axis=0))
        return tuple(new)

    sums = lax.fori_loop(
        0, steps // chunk, step, tuple(jnp.zeros((SEQS, WIDE), f32) for _ in range(KERNEL + 1))
    )
    fbg_ref[...] = jnp.sum(sums[0], axis=0, keepdims=True)
    for k in range(KERNEL):
        fwg_ref[k : k + 1, :] = jnp.sum(sums[1 + k], axis=0, keepdims=True)

    def spread(t, count):
        dv = dv_scr[pl.ds(t, count + HALO)]
        out = taps[KERNEL - 1][None] * dv[0:count]
        for k in range(KERNEL - 1):
            s = KERNEL - 1 - k
            out = out + taps[k][None] * dv[s : s + count]
        mixgrad_ref[pl.ds(t, count)] = out.astype(bf16)

    def out_step(i, _):
        spread(i * chunk, chunk)
        return 0

    lax.fori_loop(0, steps // chunk, out_step, 0)
    spread(steps, HALO)
    low = act_ref[...].reshape(steps * SEQS, WIDE).astype(bf16)
    selg_ref[...] = jnp.dot(projg_t_ref[...], low, preferred_element_type=f32)


def filter_back(mixture, act, bend, act_grad, projg, projg_t, select_pad, fw):
    grid, steps, _, _ = act.shape
    channels = grid * WIDE
    wide = lambda j: (0, 0, j)
    whole = lambda j: (0, 0)
    cols = lambda j: (0, j)
    return pl.pallas_call(
        filter_back_kernel,
        grid=(grid,),
        in_specs=[
            pl.BlockSpec((None, steps + HALO, SEQS, WIDE), lambda j: (j, 0, 0, 0)),
            pl.BlockSpec((None, steps, SEQS, WIDE), lambda j: (j, 0, 0, 0)),
            pl.BlockSpec((None, steps, SEQS, WIDE), lambda j: (j, 0, 0, 0)),
            pl.BlockSpec((None, steps, SEQS, WIDE), lambda j: (j, 0, 0, 0)),
            pl.BlockSpec((steps * SEQS, LANES), whole),
            pl.BlockSpec((LANES, steps * SEQS), whole),
            pl.BlockSpec((WIDE, LANES), lambda j: (j, 0)),
            pl.BlockSpec((KERNEL, WIDE), cols),
        ],
        out_specs=[
            pl.BlockSpec((steps + HALO, SEQS, WIDE), wide),
            pl.BlockSpec((LANES, WIDE), cols),
            pl.BlockSpec((KERNEL, WIDE), cols),
            pl.BlockSpec((1, WIDE), cols),
        ],
        out_shape=[
            jax.ShapeDtypeStruct((steps + HALO, SEQS, channels), bf16),
            jax.ShapeDtypeStruct((LANES, channels), f32),
            jax.ShapeDtypeStruct((KERNEL, channels), f32),
            jax.ShapeDtypeStruct((1, channels), f32),
        ],
        scratch_shapes=[
            pltpu.VMEM((steps + 2 * HALO, SEQS, WIDE), f32),
            pltpu.VMEM((steps, SEQS, WIDE), f32),
        ],
        compiler_params=params(),
        cost_estimate=cost(20),
        name="filter_back",
    )(mixture, act, bend, act_grad, projg, projg_t, select_pad, fw)


def send(src, dst, send_sem, recv_sem, peer, axis="fsdp"):
    return pltpu.make_async_remote_copy(
        src_ref=src,
        dst_ref=dst,
        send_sem=send_sem,
        recv_sem=recv_sem,
        device_id={axis: peer},
        device_id_type=pl.DeviceIdType.MESH,
    )


def greet(others):
    barrier = pltpu.get_barrier_semaphore()
    for axis, peer in others:
        pl.semaphore_signal(barrier, inc=1, device_id={axis: peer}, device_id_type=pl.DeviceIdType.MESH)
    pl.semaphore_wait(barrier, len(others))


def flipped(index, bit):
    return index + (1 - 2 * (index // bit % 2)) * bit


FIRST, SECOND = (0, 1, 2, 3), (4, 5)
TRADED = (2, 3, 4, 5)


def gather_kernel(
    rows_ref, select_ref, out_ref, in_ref, all_rows, all_select, all_out, all_in,
    local_sems, own_send, own_recv, pass_send, pass_recv, core_send, core_recv, trade_send, trade_recv,
):
    me = lax.axis_index("fsdp")
    mz = lax.axis_index("replica")
    a, b = flipped(me, 2), flipped(me, 4)
    corner = flipped(a, 4)
    twin = flipped(me, 1)
    mate = flipped(mz, 1)
    greet([("fsdp", a), ("fsdp", b), ("fsdp", twin), ("replica", mate)])
    kinds = ((rows_ref, all_rows), (select_ref, all_select), (out_ref, all_out), (in_ref, all_in))

    def span(piece, side):
        if piece < 2:
            return piece, 0, kinds[piece][0].shape[0]
        kind = 2 + piece % 2
        quarter = kinds[kind][0].shape[0] // 4
        return kind, side * (2 * quarter) + (quarter if piece in SECOND else 0), quarter

    def place(owner, piece, side):
        kind, start, count = span(piece, side)
        first = owner * kinds[kind][0].shape[0] + start
        return kinds[kind][1].at[pl.ds(pl.multiple_of(first, 16), count)]

    def mine(piece, side):
        kind, start, count = span(piece, side)
        return kinds[kind][0].at[pl.ds(pl.multiple_of(start, 16), count) if piece in TRADED else pl.ds(0, count)]

    side = mz % 2
    other = 1 - side
    started = []

    def start(copy):
        copy.start()
        started.append(copy)

    def own_copy(piece, k, peer, owner):
        return send(mine(piece, side), place(owner, piece, side), own_send.at[k, piece], own_recv.at[k, piece], peer)

    def pass_copy(piece, peer, owner, far=False):
        ref = place(owner, piece, other if far else side)
        at = piece + len(FIRST + SECOND) * far
        return send(ref, ref, pass_send.at[at], pass_recv.at[at], peer)

    def trade_copy(piece, k, owner, whose):
        ref = place(owner, piece, whose)
        return send(ref, ref, trade_send.at[k, piece], trade_recv.at[k, piece], mate, "replica")

    def core_copy(piece, k, owner, whose=None):
        if whose is None:
            return send(
                place(owner, piece, side), place(owner, piece, side), core_send.at[k, piece], core_recv.at[k, piece], twin
            )
        at = len(FIRST + SECOND) + piece
        ref = place(owner, piece, whose)
        return send(ref, ref, core_send.at[k, at], core_recv.at[k, at], twin)

    def whole_copy(kind, owner):
        src, dst = kinds[kind]
        count = src.shape[0]
        rows = dst.at[pl.ds(pl.multiple_of(owner * count, count), count)]
        return send(src, rows, core_send.at[3, kind], core_recv.at[3, kind], twin)

    for piece in FIRST + SECOND:
        start(own_copy(piece, 0, a, me))
    for piece in SECOND + (2, 3, 0, 1):
        start(own_copy(piece, 1, b, me))
    local = []
    for kind, (src, dst) in enumerate(kinds):
        start(whole_copy(kind, me))
        count = src.shape[0]
        rows = dst.at[pl.ds(pl.multiple_of(me * count, count), count)]
        copy = pltpu.make_async_copy(src, rows, local_sems.at[kind])
        copy.start()
        local.append(copy)
    owners = (a, b, corner)

    def arrived(piece, k):
        owner = owners[k]
        if k == 2:
            pass_copy(piece, a, owner).wait_recv()
        else:
            own_copy(piece, k, a, owner).wait_recv()
            if k == 0 and piece in FIRST:
                start(pass_copy(piece, b, owner))
            if k == 1 and piece in SECOND:
                start(pass_copy(piece, a, owner))
        if piece in TRADED and k < 2:
            start(trade_copy(piece, k, owner, side))
        start(core_copy(piece, k, owner))

    def traded(piece, k):
        owner = owners[k]
        trade_copy(piece, k, owner, other).wait_recv()
        if k == 0 and piece in FIRST:
            start(pass_copy(piece, b, owner, True))
        if k == 1 and piece in SECOND:
            start(pass_copy(piece, a, owner, True))
        start(core_copy(piece, k, owner, other))

    for piece, k in ((0, 0), (4, 1), (1, 0), (2, 0), (5, 1), (3, 0)):
        arrived(piece, k)
    traded(2, 0)
    traded(4, 1)
    arrived(4, 0)
    arrived(2, 1)
    traded(3, 0)
    traded(5, 1)
    for piece, k in ((5, 0), (3, 1), (0, 1), (1, 1), (0, 2), (1, 2), (2, 2), (4, 2), (3, 2), (5, 2)):
        arrived(piece, k)
    for piece, k in ((4, 0), (2, 1), (5, 0), (3, 1)):
        traded(piece, k)
    for piece in (2, 4, 3, 5):
        pass_copy(piece, a, corner, True).wait_recv()
        start(core_copy(piece, 2, corner, other))
    for kind in range(len(kinds)):
        whole_copy(kind, twin).wait_recv()
    for k, owner in enumerate((flipped(twin, 2), flipped(twin, 4), flipped(corner, 1))):
        for piece in FIRST + SECOND:
            core_copy(piece, k, owner).wait_recv()
        for piece in TRADED:
            core_copy(piece, k, owner, other).wait_recv()
    for copy in started:
        copy.wait_send()
    for copy in local:
        copy.wait()


def gather(*shards):
    size = lax.axis_size("fsdp")
    if size != 8 or lax.axis_size("replica") % 2:
        return [lax.all_gather(shard, "fsdp", axis=0, tiled=True) for shard in shards]
    vmem = pl.BlockSpec(memory_space=pltpu.VMEM)
    hbm = pl.BlockSpec(memory_space=pl.ANY)
    pieces = len(FIRST + SECOND)
    dma = pltpu.SemaphoreType.DMA
    return pl.pallas_call(
        gather_kernel,
        in_specs=[vmem] * 4,
        out_specs=[hbm] * 4,
        out_shape=[jax.ShapeDtypeStruct((size * shard.shape[0], shard.shape[1]), bf16) for shard in shards],
        scratch_shapes=[
            dma((len(shards),)), dma((2, pieces)), dma((2, pieces)), dma((2 * pieces,)), dma((2 * pieces,)),
            dma((4, 2 * pieces)), dma((4, 2 * pieces)), dma((3, pieces)), dma((3, pieces)),
        ],
        compiler_params=params(collective_id=2, has_side_effects=True),
        cost_estimate=cost(55),
        name="gather",
    )(*shards)


SMALL = (KERNEL, 1, 1, 1, STATES, RANK, RANK + 2 * STATES, 1)
SMALL_ROWS = 192


def xor(index, bits):
    for bit in (1, 2, 4, 8):
        if bits & bit:
            index = flipped(index, bit)
    return index


def tail_kernel(
    one_hot_ref, b0, b1, b2, b3, filter_ref, fbias_ref, sbias_ref, skip_ref, decay_ref, step_ref, select_ref,
    gain_ref, halo_ref, block_out, small_out, rim_out,
    total, to_z, from_z, part, parts, small_f, small_ref, got_small, small_z, small_from_z, small_part,
    small_parts, rim, child, got_rim, got_child,
    sems_s, sems_z, sems_p, sems_sz, sems_sp, sems_r, sems_cs, sems_cr,
):
    depth = lax.axis_size("replica")
    me, size = lax.axis_index("fsdp"), lax.axis_size("fsdp")
    mz = lax.axis_index("replica")
    last = size - 1
    near = [lax.rem(me + d, size) for d in range(1, size)]
    far = [lax.rem(mz + d, depth) for d in range(1, depth)]
    greet([("fsdp", peer) for peer in near] + [("replica", peer) for peer in far])

    def spread(src, dst, sems, peers, axis, index):
        copies = []
        for d, peer in enumerate(peers):
            source = src.at[peer] if src.shape[0] == len(peers) + 1 and len(src.shape) == len(dst.shape) else src
            copy = send(source, dst.at[index], sems.at[0, d], sems.at[1, d], peer, axis)
            copy.start()
            copies.append(copy)
        return copies

    width = small_f.shape[2]
    small_f[...] = jnp.zeros_like(small_f)
    refs = (filter_ref, fbias_ref, sbias_ref, skip_ref, decay_ref, step_ref, select_ref)
    for k in range(size):
        at = 0
        for ref, count in zip(refs, SMALL):
            small_f[k, at : at + count] = ref[0:count, k * width : (k + 1) * width]
            at += count
        some = gain_ref.shape[1] // size
        small_f[k, at : at + 1, 0:some] = gain_ref[:, k * some : (k + 1) * some]
    small_ref[...] = small_f[...].astype(bf16)
    sequels = one_hot_ref.shape[0]
    pieces = (SEQS - PROMPTS) // sequels
    for t in range(HALO):
        rim[t * PROMPTS : (t + 1) * PROMPTS] = halo_ref[t, 0:PROMPTS]
        for p in range(PROMPTS):
            sums = None
            for q in range(sequels):
                row = PROMPTS + q * pieces
                term = one_hot_ref[q, p] * halo_ref[t, row : row + 1]
                sums = term if q == 0 else sums + term
            child[t * PROMPTS + p : t * PROMPTS + p + 1] = sums
    block = b0[...].astype(f32) + b1[...].astype(f32) + b2[...].astype(f32) + b3[...].astype(f32)
    total[...] = block.reshape(total.shape)
    to_z[...] = total[...].astype(bf16)
    to_left = send(rim, got_rim, sems_r.at[0], sems_r.at[1], lax.rem(me + last, size))
    to_left.start()

    @pl.when(me != last)
    def _():
        send(child, got_child.at[me], sems_cs.at[me], sems_cr.at[me], last).start()

    copies = spread(small_ref, got_small, sems_s, near, "fsdp", me)
    z_copies = spread(to_z, from_z, sems_z, far, "replica", mz)
    small = small_ref[me].astype(f32)
    got_small[me] = jnp.zeros(got_small.shape[1:], bf16)
    from_z[mz] = jnp.zeros(from_z.shape[1:], bf16)
    small_from_z[mz] = jnp.zeros(small_from_z.shape[1:], bf16)
    for copy in copies:
        copy.wait()
    for k in range(size):
        small = small + got_small[k].astype(f32)
    small_z[...] = small.reshape(small_z.shape)
    small_to_z = small_part
    small_to_z[...] = small_z[...].astype(bf16)
    s_copies = spread(small_to_z, small_from_z, sems_sz, far, "replica", mz)
    for copy in z_copies:
        copy.wait()
    own = total[mz]
    for k in range(depth):
        own = own + from_z[k].astype(f32)
    part[...] = own.astype(bf16)
    p_copies = spread(part, parts, sems_p, far, "replica", mz)
    parts[mz] = part[...]
    for copy in s_copies:
        copy.wait()
    own = small_z[mz]
    for k in range(depth):
        own = own + small_from_z[k].astype(f32)
    small_parts[mz] = own.astype(bf16)
    small_own = small_to_z.at[mz]
    small_own[...] = own.astype(bf16)
    q_copies = []
    for d, peer in enumerate(far):
        copy = send(small_own, small_parts.at[mz], sems_sp.at[0, d], sems_sp.at[1, d], peer, "replica")
        copy.start()
        q_copies.append(copy)
    for copy in p_copies + q_copies:
        copy.wait()
    block_out[...] = parts[...].reshape(block_out.shape)
    small_out[...] = small_parts[...].reshape(small_out.shape)
    to_left.wait()

    @pl.when(me != last)
    def _():
        send(child, got_child.at[me], sems_cs.at[me], sems_cr.at[me], last).wait_send()
        rim_out[...] = got_rim[...]

    @pl.when(me == last)
    def _():
        sums = child[...]
        for k in range(size - 1):
            send(child, got_child.at[k], sems_cs.at[k], sems_cr.at[k], 0).wait_recv()
            sums = sums + got_child[k]
        rim_out[...] = sums


def tail(one_hot, blocks, small, halo_grad):
    size, depth = lax.axis_size("fsdp"), lax.axis_size("replica")
    vmem = pl.BlockSpec(memory_space=pltpu.VMEM)
    dma = pltpu.SemaphoreType.DMA
    while len(blocks) > 4:
        blocks = blocks[:3] + [summed(blocks[3], blocks[4:5]).astype(bf16)] + blocks[5:]
    rows, channels = blocks[0].shape
    features = small[-1].shape[1]
    width = channels // size
    cut = (depth, rows // depth, channels)
    by_owner = (size, SMALL_ROWS, width)
    small_cut = (depth, SMALL_ROWS // depth, width)
    rim = (HALO * PROMPTS, features)
    return pl.pallas_call(
        tail_kernel,
        in_specs=[pl.BlockSpec(memory_space=pltpu.SMEM)] + [vmem] * (4 + len(small) + 1),
        out_specs=[vmem] * 3,
        out_shape=[
            jax.ShapeDtypeStruct((rows, channels), bf16),
            jax.ShapeDtypeStruct((SMALL_ROWS, width), bf16),
            jax.ShapeDtypeStruct(rim, f32),
        ],
        scratch_shapes=[
            pltpu.VMEM(cut, f32), pltpu.VMEM(cut, bf16), pltpu.VMEM(cut, bf16),
            pltpu.VMEM(cut[1:], bf16), pltpu.VMEM(cut, bf16),
            pltpu.VMEM(by_owner, f32), pltpu.VMEM(by_owner, bf16), pltpu.VMEM(by_owner, bf16),
            pltpu.VMEM(small_cut, f32), pltpu.VMEM(small_cut, bf16),
            pltpu.VMEM(small_cut, bf16), pltpu.VMEM(small_cut, bf16),
            pltpu.VMEM(rim, f32), pltpu.VMEM(rim, f32), pltpu.VMEM(rim, f32), pltpu.VMEM((size,) + rim, f32),
            dma((2, size)), dma((2, depth)), dma((2, depth)), dma((2, depth)), dma((2, depth)),
            dma((2,)), dma((size,)), dma((size,)),
        ],
        compiler_params=params(collective_id=4, has_side_effects=True),
        cost_estimate=cost(30),
        name="tail",
    )(one_hot, *blocks, *small, halo_grad)


def deliver_kernel(block_ref, small_ref, rim_ref, prompt_ref, *rest):
    depth = lax.axis_size("replica")
    early_refs, outs = rest[:depth], rest[depth:-1]
    early = rest[-1]
    in_out, out_out, prompt_out = outs[:3]
    mz = lax.axis_index("replica")
    half = in_out.shape[1] // 2
    in_out[:, 0:half] = block_ref[...].astype(f32)
    small = small_ref[...].astype(f32)
    at = 0
    for out, count in zip(outs[3:], SMALL):
        rows = small[at : at + count]
        out[...] = rows[:, 0 : out.shape[1]]
        at += count
    for d, ref in enumerate(early_refs):
        count = ref.shape[0]
        early[pl.ds(pl.multiple_of(xor(mz, d) * count, count), count), :] = ref[...].astype(f32)
    rows = out_out.shape[0] // 2
    features = out_out.shape[1]
    out_out[0:rows, :] = early[0:rows, 0:features]
    out_out[rows:, :] = early[0:rows, features:]
    in_out[:, half:] = early[rows:, :]
    for p in range(PROMPTS):
        prompt_out[p, 0 : SEQS - HALO] = prompt_ref[p, 0 : SEQS - HALO]
        for t in range(HALO):
            row = SEQS - HALO + t
            prompt_out[p, row : row + 1] = (
                prompt_ref[p, row : row + 1] + rim_ref[t * PROMPTS + p : t * PROMPTS + p + 1]
            )


def deliver(block, small, rim, prompt_grad, early):
    size = lax.axis_size("fsdp")
    rows, channels = block.shape
    width = small.shape[1]
    features = prompt_grad.shape[2]
    vmem = pl.BlockSpec(memory_space=pltpu.VMEM)
    end = prompt_grad.shape[1] // SEQS - 1
    last = pl.BlockSpec((PROMPTS, SEQS, features), lambda i: (0, end, 0))
    shapes = [(count, width) for count in SMALL[:-1]] + [(1, features // size)]
    shapes = [(rows, 2 * channels), (2 * rows, features), prompt_grad.shape] + shapes
    return pl.pallas_call(
        deliver_kernel,
        grid=(1,),
        in_specs=[vmem, vmem, vmem, last] + [vmem] * len(early),
        out_specs=[vmem, vmem, last] + [vmem] * len(SMALL),
        out_shape=[jax.ShapeDtypeStruct(shape, f32) for shape in shapes],
        scratch_shapes=[pltpu.VMEM((2 * rows, channels), f32)],
        input_output_aliases={3: 2},
        compiler_params=params(),
        cost_estimate=cost(4),
        name="deliver",
    )(block, small, rim, prompt_grad, *early)


def contract_rows(left_side, right_side):
    return lax.dot_general(
        left_side, right_side, (((0,), (0,)), ((), ())), preferred_element_type=f32
    )


def contract_cols(left_side, right_side):
    return lax.dot_general(
        left_side, right_side, (((1,), (1,)), ((), ())), preferred_element_type=f32
    )


def exchanged(block, axis, distance):
    return lax.ppermute(block, axis, [(i, i ^ distance) for i in range(lax.axis_size(axis))])


def pick_row(block, index, axis=0):
    return lax.dynamic_index_in_dim(block, index, axis, keepdims=False)


def over_cores(blocks):
    blocks = blocks.reshape((-1, 2) + blocks.shape[1:])
    core = lax.axis_index("fsdp") % 2
    got = exchanged(pick_row(blocks, 1 - core, 1), "fsdp", 1)
    return (pick_row(blocks, core, 1).astype(f32) + got.astype(f32)).astype(bf16)


def to_chips(blocks):
    chip = lax.axis_index("fsdp") // 2
    got = [exchanged(pick_row(blocks, chip ^ d), "fsdp", 2 * d) for d in range(1, blocks.shape[0])]
    return pick_row(blocks, chip), got


def summed(own, got):
    total = own.astype(f32)
    for block in got:
        total = total + block.astype(f32)
    return total


def to_replicas(block):
    size, here = lax.axis_size("replica"), lax.axis_index("replica")
    parts = block.astype(bf16).reshape((size, -1) + block.shape[1:])
    own = pick_row(block.reshape(parts.shape), here)
    return own, [exchanged(pick_row(parts, here ^ d), "replica", d) for d in range(1, size)]


def from_replicas(part):
    return [part] + [exchanged(part, "replica", d) for d in range(1, lax.axis_size("replica"))]


def body(
    prompt_hidden, sequel_hidden, parents, prompt_cotangent, sequel_cotangent,
    norm_gain, input_weight, filter_weight, depthwise_filter_bias, select_weight,
    step_weight, step_bias, decay_log, skip_gain, output_weight,
):
    size, here = lax.axis_size("fsdp"), lax.axis_index("fsdp")
    prompts, steps = prompt_hidden.shape[:2]
    sequels, sequel_len = sequel_hidden.shape[:2]
    split = sequel_len // steps
    assert prompts == PROMPTS and sequels * split == SEQS - prompts
    rim = KERNEL - 1
    half = SEQS // 2
    rows = steps * SEQS

    after = lax.optimization_barrier
    width = step_bias.shape[0]
    tail_rows = prompt_hidden[:, steps - rim :]
    shard = jnp.concatenate(
        [
            step_weight,
            tail_rows.reshape(-1, width),
            filter_weight,
            depthwise_filter_bias[None],
            step_bias[None],
            skip_gain[None],
            jnp.pad(norm_gain, (0, width - norm_gain.shape[0]))[None],
        ],
        axis=0,
    )
    shard = jnp.pad(shard, ((0, -shard.shape[0] % 16), (0, 0)))
    lanes = jnp.concatenate([select_weight, decay_log], axis=1)
    lanes = jnp.pad(lanes, ((0, 0), (0, LANES - lanes.shape[1])))
    every, select_pad, full_output, full_input = gather(shard, lanes, output_weight, input_weight)
    every = every.reshape(size, shard.shape[0], width)
    at = RANK + tail_rows.size // width
    tails = every[:, RANK:at].reshape((size,) + tail_rows.shape)
    step_full = jnp.swapaxes(every[:, :RANK], 0, 1).reshape(RANK, -1)
    vectors = jnp.swapaxes(every[:, at : at + SEQS], 0, 1).astype(f32)
    gain = vectors[KERNEL + 3, :, : norm_gain.shape[0]].reshape(1, -1)
    vectors = vectors.reshape(SEQS, -1)
    fw, fb, sbias, skip = vectors[:KERNEL], vectors[4:5], vectors[5:6], vectors[6:7]
    first = RANK + 2 * STATES
    rate = -jnp.exp(select_pad[:, first : first + STATES].T.astype(f32)) * LOG2E
    step_pad = jnp.pad(step_full, ((0, LANES - RANK), (0, 0)))

    before = jnp.where(here > 0, tails[jnp.maximum(here - 1, 0)], jnp.zeros_like(tails[0]))
    cut = sequel_hidden.reshape(sequels, split, steps, D)
    inner = jnp.concatenate([tails[size - 1][parents][:, None], cut[:, :-1, steps - rim :]], axis=1)
    halo = jnp.concatenate([before, inner.reshape(-1, rim, D)], axis=0)
    halo = jnp.pad(jnp.swapaxes(halo, 0, 1), ((HALO - rim, 0), (0, 0), (0, 0))).reshape(-1, D).astype(f32)
    pieces = sequel_hidden.reshape(-1, steps, D)
    piece_cot = sequel_cotangent.reshape(-1, steps, D)
    scaled, cotangent = prepare(prompt_hidden, pieces, prompt_cotangent, piece_cot, halo, gain)

    mixture = product([scaled], full_input, bf16, part=0, parts=2, tiled=True)
    gate = product([scaled], full_input, f32, part=1, parts=2, tiled=True)
    mixture = mixture.reshape(-1, steps + HALO, SEQS, WIDE)
    gate = gate.reshape(-1, steps + HALO, SEQS, WIDE)
    gated_grad = product([cotangent], full_output, f32, across=True, tiled=True)
    gated_grad = gated_grad.reshape(-1, steps, SEQS, WIDE)
    act, bend, proj = front(mixture, fw, fb, select_pad, steps)
    groups = 1 if split == 1 else 2
    lane = jnp.arange(2 * STATES * LANES)[None, :]
    select = (jnp.arange(LANES)[:, None] == RANK + lane // LANES).astype(bf16)
    dt, sig, yg, silu, slope, ahead, behind, total = piece(
        proj, act, gate, gated_grad, step_pad, sbias, rate, select, groups
    )

    one_hot = (parents[:, None] == jnp.arange(PROMPTS, dtype=jnp.int32)[None, :]).astype(f32)
    own = total[half:].reshape(sequels, split, 1, INNER)
    own_behind = behind[half:].reshape(sequels, split, STATES, INNER)
    back = own_behind[:, split - 1]
    own_end = [jnp.zeros_like(back)]
    for p in range(split - 2, -1, -1):
        own_end.insert(0, back)
        back = own_behind[:, p] + jnp.exp2(rate * own[:, p]) * back
    joint = behind if split == 1 else jnp.concatenate([behind[:half], back], axis=0)
    start, end = chain(one_hot, ahead, joint, total, rate)
    if split > 1:
        state = start[half:]
        own_start = [state]
        for p in range(split - 1):
            state = jnp.exp2(rate * own[:, p]) * state + ahead[half:].reshape(own_behind.shape)[:, p]
            own_start.append(state)
        own_start = jnp.stack(own_start, axis=1).reshape(half, STATES, INNER)
        start = jnp.concatenate([start[:half], own_start], axis=0)
        end = jnp.concatenate([end[:half], jnp.stack(own_end, axis=1).reshape(half, STATES, INNER)], axis=0)

    gated, hist, gate_grad, skip_grad = forward(
        proj, dt, act, yg, silu, slope, rate, start, skip, select
    )
    gated = gated.reshape(rows, INNER)
    gate_grad = gate_grad.reshape(-1, INNER)
    output_grad = contract_rows(gated, cotangent).astype(bf16).reshape(size, -1, D)
    gate_weight_grad = contract_rows(scaled, gate_grad).astype(bf16)
    early = [over_cores(output_grad), over_cores(gate_weight_grad.reshape(size, -1, INNER))]
    wide = jnp.concatenate([early[0][:, : INNER // size // 2], early[0][:, INNER // size // 2 :]], axis=2)
    early = jnp.concatenate([wide, early[1]], axis=1)
    end, early = after((end, early))
    early = to_chips(early)

    rank_t = proj[:, :RANK].astype(bf16).T
    lane = jnp.arange(LANES)[None, None, :]
    which = jnp.arange(PAIRS)[:, None, None]
    source = jnp.arange(2 * LANES)[None, :, None]
    pick = (lane // 2 == jnp.where(source < LANES, RANK, RANK + STATES) // 2 + which).astype(bf16)
    act_grad, step_grad, bias_grad, decay_grad, projg = backward(
        proj, dt, sig, act, yg, rate, end, skip, hist, rank_t, step_pad.T, pick, select
    )
    projg, early = after((projg, early))
    early = summed(*early)
    projg, early = after((projg, early))
    early = to_replicas(early)
    filter_in_grad, select_grad, filter_grad, filter_bias_grad = filter_back(
        mixture, act, bend, act_grad, projg, projg.T, select_pad, fw
    )
    filter_in_grad, early = after((filter_in_grad, early))
    early = summed(*early).astype(bf16)
    filter_in_grad = filter_in_grad.reshape(-1, INNER)
    filter_weight_grad = contract_rows(scaled, filter_in_grad).astype(bf16)
    filter_weight_grad, early = after((filter_weight_grad, early))
    late = over_cores(filter_weight_grad.reshape(size, -1, INNER))
    early = from_replicas(early)
    mixed = jnp.dot(gated, full_output, preferred_element_type=f32)
    late, mixed, filter_in_grad = after((late, mixed, filter_in_grad))
    own_block, late = to_chips(late)
    scaled_grad = product([filter_in_grad, gate_grad], full_input, f32, across=True)
    prompt_out, piece_out, prompt_grad, piece_grad, halo_grad, gain_grad = finish(
        mixed, scaled_grad, prompt_hidden, pieces, prompt_cotangent, piece_cot, halo, gain
    )
    halo_grad, own_block, late = after((halo_grad, own_block, late))
    halo_grad = halo_grad.reshape(HALO, SEQS, D)
    small = [
        filter_grad, filter_bias_grad, bias_grad, skip_grad, decay_grad, step_grad, select_grad, gain_grad,
    ]
    block, small, following = tail(one_hot, [own_block] + late, small, halo_grad)
    (
        input_grad, output_grad, prompt_grad, g_filter, g_fbias, g_sbias, g_skip, g_decay, g_step, g_select, g_gain,
    ) = deliver(block, small, following, prompt_grad, early)
    if split > 1:
        own = jnp.swapaxes(halo_grad[:, half:], 0, 1).reshape(sequels, split, HALO, D)
        own = jnp.pad(own[:, 1:], ((0, 0), (0, 1), (0, 0), (0, 0))).reshape(half, HALO, D)
        piece_grad = piece_grad.at[:, steps - HALO :].add(own)
    return (
        prompt_out,
        piece_out.reshape(sequel_hidden.shape),
        prompt_grad,
        piece_grad.reshape(sequel_hidden.shape),
        g_gain[0],
        input_grad,
        g_filter,
        g_fbias[0],
        g_select.T,
        g_step,
        g_sbias[0],
        g_decay.T,
        g_skip[0],
        output_grad,
    )


def solution(mesh):
    rows = P("replica", "fsdp", None)
    own = P(("replica", "fsdp"), None, None)
    return jax.shard_map(
        body,
        mesh=mesh,
        in_specs=(
            rows, own, P(("replica", "fsdp")), rows, own,
            P("fsdp"), P("fsdp", None), P(None, "fsdp"), P("fsdp"), P("fsdp", None),
            P(None, "fsdp"), P("fsdp"), P("fsdp", None), P("fsdp"), P("fsdp", None),
        ),
        out_specs=(
            rows, own, rows, own,
            P("fsdp"), P("fsdp", None), P(None, "fsdp"), P("fsdp"), P("fsdp", None),
            P(None, "fsdp"), P("fsdp"), P("fsdp", None), P("fsdp"), P("fsdp", None),
        ),
        check_vma=False,
    )
```

```python
import functools
import math

import jax
import jax.numpy as jnp
from jax import lax
from jax.experimental import pallas as pl
from jax.experimental.pallas import tpu as pltpu
from jax.sharding import PartitionSpec as P

D = 1024
INNER = 2048
STATES = 16
RANK = 64
KERNEL = 4
PROMPTS = 4

SEQS = 8
HALO = 4
LANES = 128
WIDE = 256
LOG2E = math.log2(math.e)
LN2 = math.log(2.0)
f32 = jnp.float32
bf16 = jnp.bfloat16

VMEM_LIMIT = 62 * 1024 * 1024


def cost(microseconds):
    return pl.CostEstimate(flops=int(microseconds * 1e9), bytes_accessed=0, transcendentals=0)


def params(**kw):
    return pltpu.CompilerParams(vmem_limit_bytes=VMEM_LIMIT, **kw)


def sigmoid(x):
    return 1.0 / (1.0 + jnp.exp(-x))


def softplus(x):
    return jnp.maximum(x, 0.0) + jnp.log1p(jnp.exp(-jnp.abs(x)))


def product_kernel(across, *refs):
    lefts, rhs_ref, out_ref = refs[:-2], refs[-2], refs[-1]
    total = None
    at = 0
    for left in lefts:
        depth = left.shape[1]
        rhs = rhs_ref[:, at : at + depth] if across else rhs_ref[at : at + depth]
        dims = (((1,), (1 if across else 0,)), ((), ()))
        term = lax.dot_general(left[...], rhs, dims, preferred_element_type=f32)
        total = term if total is None else total + term
        at += depth
    if len(out_ref.shape) == 2:
        out_ref[...] = total.astype(out_ref.dtype)
    else:
        for k in range(out_ref.shape[0]):
            out_ref[k] = total[:, k * WIDE : (k + 1) * WIDE].astype(out_ref.dtype)


def product(lefts, rhs, kind, across=False, part=0, parts=1, tiled=False):
    rows = lefts[0].shape[0]
    depth = sum(left.shape[1] for left in lefts)
    tile = 2 * WIDE if len(lefts) == 1 else WIDE
    if across:
        columns = rhs.shape[0]
        rhs_spec = pl.BlockSpec((tile, depth), lambda j: (j, 0))
    else:
        columns = rhs.shape[1] // parts
        first = part * columns // tile
        rhs_spec = pl.BlockSpec((depth, tile), lambda j: (0, first + j))
    return pl.pallas_call(
        functools.partial(product_kernel, across),
        grid=(columns // tile,),
        in_specs=[pl.BlockSpec(left.shape, lambda j: (0, 0)) for left in lefts] + [rhs_spec],
        out_specs=pl.BlockSpec((tile // WIDE, rows, WIDE), lambda j: (j, 0, 0))
        if tiled
        else pl.BlockSpec((rows, tile), lambda j: (0, j)),
        out_shape=jax.ShapeDtypeStruct((columns // WIDE, rows, WIDE) if tiled else (rows, columns), kind),
        compiler_params=params(),
        cost_estimate=cost(0.01),
        name="product",
    )(*lefts, rhs)


def scale_of(rows):
    return lax.rsqrt(jnp.mean(rows * rows, axis=-1, keepdims=True) + 1e-05)


def by_time(prompt_ref, piece_ref):
    both_kinds = jnp.concatenate([prompt_ref[...], piece_ref[...]], axis=0).astype(f32)
    return jnp.swapaxes(both_kinds, 0, 1)


def prepare_kernel(prompt_ref, piece_ref, prompt_cot_ref, piece_cot_ref, halo_ref, gain_ref, scaled_ref, cot_ref):
    i = pl.program_id(0)
    gain = gain_ref[...]

    @pl.when(i == 0)
    def _():
        rows = halo_ref[...]
        scaled_ref[0 : HALO * SEQS, :] = (rows * scale_of(rows) * gain).astype(bf16)

    rows = by_time(prompt_ref, piece_ref)
    count = rows.shape[0] * SEQS
    rows = rows.reshape(count, D)
    at = pl.multiple_of(HALO * SEQS + i * count, HALO * SEQS)
    scaled_ref[pl.ds(at, count), :] = (rows * scale_of(rows) * gain).astype(bf16)
    cot_ref[...] = by_time(prompt_cot_ref, piece_cot_ref).reshape(count, D).astype(bf16)


CHUNK = 16
PREPARE_CHUNK = 32


def prepare(prompt, piece, prompt_cot, piece_cot, halo, gain):
    steps = prompt.shape[1]
    part = pl.BlockSpec((SEQS // 2, PREPARE_CHUNK, D), lambda i: (0, i, 0))
    rows = steps * SEQS
    return pl.pallas_call(
        prepare_kernel,
        grid=(steps // PREPARE_CHUNK,),
        in_specs=[
            part, part, part, part,
            pl.BlockSpec((HALO * SEQS, D), lambda i: (0, 0)),
            pl.BlockSpec((1, D), lambda i: (0, 0)),
        ],
        out_specs=[
            pl.BlockSpec((HALO * SEQS + rows, D), lambda i: (0, 0)),
            pl.BlockSpec((PREPARE_CHUNK * SEQS, D), lambda i: (i, 0)),
        ],
        out_shape=[
            jax.ShapeDtypeStruct((HALO * SEQS + rows, D), bf16),
            jax.ShapeDtypeStruct((rows, D), bf16),
        ],
        compiler_params=params(),
        cost_estimate=cost(5),
        name="prepare",
    )(prompt, piece, prompt_cot, piece_cot, halo, gain)


def norm_back(rows, scaled_grad, gain):
    inverse = scale_of(rows)
    unit = rows * inverse
    grad = scaled_grad * gain
    back = inverse * (grad - unit * jnp.mean(grad * unit, axis=-1, keepdims=True))
    return back, scaled_grad * unit


def finish_kernel(
    mixed_ref, grad_ref, grad_halo_ref,
    prompt_ref, piece_ref, prompt_cot_ref, piece_cot_ref, halo_ref, gain_ref,
    prompt_out, piece_out, prompt_grad, piece_grad, halo_grad, gain_grad,
):
    i = pl.program_id(0)
    gain = gain_ref[...]

    @pl.when(i == 0)
    def _():
        back, sums = norm_back(halo_ref[...], grad_halo_ref[...], gain)
        halo_grad[...] = back
        gain_grad[...] = jnp.sum(sums, axis=0, keepdims=True)

    half = SEQS // 2
    rows = by_time(prompt_ref, piece_ref)
    shape = rows.shape
    rows = rows.reshape(-1, D)
    back, sums = norm_back(rows, grad_ref[...], gain)
    gain_grad[...] += jnp.sum(sums, axis=0, keepdims=True)
    back = jnp.swapaxes(back.reshape(shape), 0, 1)
    prompt_grad[...] = back[:half] + prompt_cot_ref[...].astype(f32)
    piece_grad[...] = back[half:] + piece_cot_ref[...].astype(f32)
    mixed = jnp.swapaxes((mixed_ref[...] + rows).reshape(shape), 0, 1)
    prompt_out[...] = mixed[:half].astype(bf16)
    piece_out[...] = mixed[half:].astype(bf16)


def finish(mixed, grad, prompt, piece, prompt_cot, piece_cot, halo, gain):
    steps = prompt.shape[1]
    part = pl.BlockSpec((SEQS // 2, CHUNK, D), lambda i: (0, i, 0))
    first = pl.BlockSpec((HALO * SEQS, D), lambda i: (0, 0))
    shifted = pl.BlockSpec(
        (pl.Element(CHUNK * SEQS), pl.Element(D)),
        lambda i: (pl.multiple_of(HALO * SEQS + i * (CHUNK * SEQS), HALO * SEQS), 0),
    )
    return pl.pallas_call(
        finish_kernel,
        grid=(steps // CHUNK,),
        in_specs=[
            pl.BlockSpec((CHUNK * SEQS, D), lambda i: (i, 0)),
            shifted, first,
            part, part, part, part,
            first,
            pl.BlockSpec((1, D), lambda i: (0, 0)),
        ],
        out_specs=[part, part, part, part, first, pl.BlockSpec((1, D), lambda i: (0, 0))],
        out_shape=[
            jax.ShapeDtypeStruct(prompt.shape, bf16),
            jax.ShapeDtypeStruct(piece.shape, bf16),
            jax.ShapeDtypeStruct(prompt.shape, f32),
            jax.ShapeDtypeStruct(piece.shape, f32),
            jax.ShapeDtypeStruct((HALO * SEQS, D), f32),
            jax.ShapeDtypeStruct((1, D), f32),
        ],
        compiler_params=params(),
        cost_estimate=cost(0.01),
        name="finish",
    )(mixed, grad, grad, prompt, piece, prompt_cot, piece_cot, halo, gain)


def front_kernel(mix_ref, fw_ref, fb_ref, sel_ref, act_ref, bend_ref, proj_ref, low_scr):
    j = pl.program_id(0)
    steps = act_ref.shape[0]
    chunk = 16
    taps = [fw_ref[k : k + 1, :] for k in range(KERNEL)]
    bias = fb_ref[0:1, :]

    @pl.when(j == 0)
    def _():
        proj_ref[...] = jnp.zeros_like(proj_ref)

    def step(i, _):
        t = i * chunk
        x = mix_ref[pl.ds(t, chunk + HALO)].astype(f32)
        v = bias[None] + taps[0][None] * x[1 : 1 + chunk]
        for k in range(1, KERNEL):
            v = v + taps[k][None] * x[1 + k : 1 + k + chunk]
        sig = sigmoid(v)
        act = v * sig
        act_ref[pl.ds(t, chunk)] = act
        bend_ref[pl.ds(t, chunk)] = (sig + act * (1.0 - sig)).astype(bf16)
        r = pl.multiple_of(t * SEQS, chunk * SEQS)
        low_scr[pl.ds(r, chunk * SEQS), :] = act.reshape(chunk * SEQS, act.shape[-1]).astype(bf16)
        return 0

    lax.fori_loop(0, steps // chunk, step, 0)
    proj_ref[...] += jnp.dot(low_scr[...], sel_ref[...], preferred_element_type=f32)


def front(mixture, fw, fb, select_pad, steps):
    channels = fw.shape[1]
    return pl.pallas_call(
        front_kernel,
        grid=(channels // WIDE,),
        in_specs=[
            pl.BlockSpec((None, steps + HALO, SEQS, WIDE), lambda j: (j, 0, 0, 0)),
            pl.BlockSpec((KERNEL, WIDE), lambda j: (0, j)),
            pl.BlockSpec((1, WIDE), lambda j: (0, j)),
            pl.BlockSpec((WIDE, LANES), lambda j: (j, 0)),
        ],
        out_specs=[
            pl.BlockSpec((None, steps, SEQS, WIDE), lambda j: (j, 0, 0, 0)),
            pl.BlockSpec((None, steps, SEQS, WIDE), lambda j: (j, 0, 0, 0)),
            pl.BlockSpec((steps * SEQS, LANES), lambda j: (0, 0)),
        ],
        out_shape=[
            jax.ShapeDtypeStruct((channels // WIDE, steps, SEQS, WIDE), f32),
            jax.ShapeDtypeStruct((channels // WIDE, steps, SEQS, WIDE), bf16),
            jax.ShapeDtypeStruct((steps * SEQS, LANES), f32),
        ],
        scratch_shapes=[pltpu.VMEM((steps * SEQS, WIDE), bf16)],
        compiler_params=params(),
        cost_estimate=cost(16),
        name="front",
    )(mixture, fw, fb, select_pad)


def pair(a, b):
    return jnp.concatenate([a, b], axis=0).astype(bf16)


def both(v):
    return pair(v, v)


def halves(v):
    v = v.astype(f32)
    return v[:SEQS], v[SEQS:]


def folded(v):
    a, b = halves(v)
    return a + b


def spread_maps(proj_ref, select_ref, first, count, store):
    steps = proj_ref.shape[0] // SEQS
    chunk = 32

    def step(i, _):
        r = pl.multiple_of(i * chunk * SEQS, chunk * SEQS)
        rows = proj_ref[pl.ds(r, chunk * SEQS), :].astype(bf16)
        for n in range(0, count, 2):
            at = (first - RANK + n) * LANES
            wide = jnp.dot(rows, select_ref[:, at : at + 2 * LANES], preferred_element_type=f32)
            wide = wide.reshape(chunk, SEQS, 2 * LANES)
            store(i * chunk, chunk, n, wide[:, :, :LANES], wide[:, :, LANES:])
        return 0

    lax.fori_loop(0, steps // chunk, step, 0)


def store_plain(ref):
    def store(t, count, n, a, b):
        ref[pl.ds(t, count), n] = a
        ref[pl.ds(t, count), n + 1] = b

    return store


def store_pairs(ref):
    def store(t, count, n, a, b):
        ref[pl.ds(t, count), n // 2] = jnp.concatenate([a, b], axis=1).astype(bf16)

    return store


PAIRS = STATES // 2
RUN = 8


def piece_kernel(
    proj_ref, act_ref, gate_ref, gg_ref, stepw_ref, sbias_ref, rate_ref, select_ref,
    dt_ref, sig_ref, yg_ref, silu_ref, slope_ref, fwd_ref, bwd_ref, tot_ref,
    b_scr, c_scr, time_scr, acc_scr,
):
    j = pl.program_id(0)
    steps = dt_ref.shape[0]
    half = SEQS // 2
    groups = fwd_ref.shape[0] // half

    @pl.when(j == 0)
    def _():
        def store_groups(t, count, n, a, b):
            for group in range(groups):
                rows = slice(group * half, (group + 1) * half)
                parts = [a[:, rows], a[:, rows], b[:, rows], b[:, rows]]
                b_scr[group, pl.ds(t, count), n // 2] = jnp.concatenate(parts, axis=1).astype(bf16)

        spread_maps(proj_ref, select_ref, RANK, STATES, store_groups)
        spread_maps(proj_ref, select_ref, RANK + STATES, STATES, store_pairs(c_scr))

    chunk = 8
    sbias = sbias_ref[0:1, :]
    pre = jnp.dot(proj_ref[...].astype(bf16), stepw_ref[...], preferred_element_type=f32)
    time_scr[...] = pre.reshape(steps, SEQS, WIDE)

    def prep(i, total):
        t = i * chunk
        pre = time_scr[pl.ds(t, chunk)] + sbias[None]
        small = jnp.exp2(jnp.abs(pre) * -LOG2E)
        one = 1.0 + small
        inverse = 1.0 / one
        dt = jnp.maximum(pre, 0.0) + (jnp.log(one) + (small - (one - 1.0)) * inverse)
        dt_ref[pl.ds(t, chunk)] = dt
        sig_ref[pl.ds(t, chunk)] = jnp.where(pre >= 0.0, inverse, small * inverse).astype(bf16)
        gate = gate_ref[pl.ds(t + HALO, chunk)].astype(f32)
        gg = gg_ref[pl.ds(t, chunk)]
        sig = sigmoid(gate)
        silu = gate * sig
        yg_ref[pl.ds(t, chunk)] = gg * silu
        silu_ref[pl.ds(t, chunk)] = silu.astype(bf16)
        slope_ref[pl.ds(t, chunk)] = (gg * (sig + silu * (1.0 - sig))).astype(bf16)
        for k in range(chunk):
            total = total + dt[k]
            time_scr[t + k] = total
        return total

    total = lax.fori_loop(0, steps // chunk, prep, jnp.zeros((SEQS, WIDE), f32))
    tot_ref[...] = total

    units = []

    low = lax.broadcasted_iota(jnp.int32, (SEQS, LANES), 0) < half
    packed = [
        jnp.where(low, rate_ref[n : n + 1, :LANES], rate_ref[n : n + 1, LANES:])
        for n in range(STATES)
    ]
    packed = [pair(packed[2 * p], packed[2 * p + 1]) for p in range(PAIRS)]

    def forward_unit(group):
        rows = slice(group * half, (group + 1) * half)

        def pack(v):
            return jnp.concatenate([v[rows, :LANES], v[rows, LANES:]], axis=0)

        whole = pack(total)

        def vectors(t):
            return both(whole - pack(time_scr[t])), both(pack(dt_ref[t] * act_ref[t]))

        def out(n, value):
            fwd_ref[rows, n, :LANES] = value[:half]
            fwd_ref[rows, n, LANES:] = value[half:]

        return packed, vectors, lambda t, p: b_scr[group, t, p], out

    def backward_unit(cols):
        mine = [jnp.broadcast_to(rate_ref[n : n + 1, cols], (SEQS, LANES)) for n in range(STATES)]
        mine = [pair(mine[2 * p], mine[2 * p + 1]) for p in range(PAIRS)]

        def vectors(t):
            return both(time_scr[t, :, cols]), both(yg_ref[t, :, cols])

        def out(n, value):
            bwd_ref[:, n, cols] = value

        return mine, vectors, lambda t, p: c_scr[t, p], out

    for group in range(groups):
        units.append(forward_unit(group))
    for part in range(WIDE // LANES):
        units.append(backward_unit(slice(part * LANES, (part + 1) * LANES)))
    acc_scr[...] = jnp.zeros_like(acc_scr)

    def run(i, _):
        for k, (rates, vectors, map_at, _) in enumerate(units):
            sums = [None] * PAIRS
            for m in range(RUN):
                t = i * RUN + m
                time, drive = vectors(t)
                for p in range(PAIRS):
                    term = jnp.exp2(time * rates[p]) * drive * map_at(t, p)
                    sums[p] = term if m == 0 else sums[p] + term
            for p in range(PAIRS):
                a, b = halves(sums[p])
                acc_scr[k, 2 * p] += a
                acc_scr[k, 2 * p + 1] += b
        return 0

    lax.fori_loop(0, steps // RUN, run, 0)
    for k, (_, _, _, out) in enumerate(units):
        for n in range(STATES):
            out(n, acc_scr[k, n])


def piece(proj, act, gate, gated_grad, step_pad, sbias, rate, select, groups):
    grid, steps, _, _ = act.shape
    channels = grid * WIDE
    wide = lambda j: (0, 0, j)
    flat = pl.BlockSpec((None, steps, SEQS, WIDE), lambda j: (j, 0, 0, 0))
    shape = act.shape
    return pl.pallas_call(
        piece_kernel,
        grid=(grid,),
        in_specs=[
            pl.BlockSpec((steps * SEQS, LANES), lambda j: (0, 0)),
            flat,
            pl.BlockSpec((None, steps + HALO, SEQS, WIDE), lambda j: (j + grid, 0, 0, 0)),
            flat,
            pl.BlockSpec((LANES, WIDE), lambda j: (0, j)),
            pl.BlockSpec((1, WIDE), lambda j: (0, j)),
            pl.BlockSpec((STATES, WIDE), lambda j: (0, j)),
            pl.BlockSpec(select.shape, lambda j: (0, 0)),
        ],
        out_specs=[
            flat, flat, flat, flat, flat,
            pl.BlockSpec((groups * SEQS // 2, STATES, WIDE), wide),
            pl.BlockSpec((SEQS, STATES, WIDE), wide),
            pl.BlockSpec((SEQS, WIDE), lambda j: (0, j)),
        ],
        out_shape=[
            jax.ShapeDtypeStruct(shape, f32),
            jax.ShapeDtypeStruct(shape, bf16),
            jax.ShapeDtypeStruct(shape, f32),
            jax.ShapeDtypeStruct(shape, bf16),
            jax.ShapeDtypeStruct(shape, bf16),
            jax.ShapeDtypeStruct((groups * SEQS // 2, STATES, channels), f32),
            jax.ShapeDtypeStruct((SEQS, STATES, channels), f32),
            jax.ShapeDtypeStruct((SEQS, channels), f32),
        ],
        scratch_shapes=[
            pltpu.VMEM((groups, steps, PAIRS, 2 * SEQS, LANES), bf16),
            pltpu.VMEM((steps, PAIRS, 2 * SEQS, LANES), bf16),
            pltpu.VMEM((steps, SEQS, WIDE), f32),
            pltpu.VMEM((groups + WIDE // LANES, STATES, SEQS, LANES), f32),
        ],
        compiler_params=params(),
        cost_estimate=cost(60),
        name="piece",
    )(proj, act, gate, gated_grad, step_pad, sbias, rate, select)


def chain_kernel(
    one_hot_ref, ahead_ref, behind_ref, time_ref, rate_ref, start_out, end_out,
    moved_ref, got, got_time, back, done, sems, time_sems, back_sems,
):
    size = got.shape[0]
    width = got.shape[2]
    count = PROMPTS * STATES
    sequels = one_hot_ref.shape[0]
    me = lax.axis_index("fsdp")
    for p in range(PROMPTS):
        rows = slice(p * STATES, (p + 1) * STATES)
        total = one_hot_ref[0, p] * behind_ref[PROMPTS]
        for k in range(1, sequels):
            total = total + one_hot_ref[k, p] * behind_ref[PROMPTS + k]
        moved_ref[0 * count + p * STATES : 0 * count + (p + 1) * STATES] = ahead_ref[p].astype(bf16)
        moved_ref[1 * count + p * STATES : 1 * count + (p + 1) * STATES] = behind_ref[p].astype(bf16)
        moved_ref[2 * count + p * STATES : 2 * count + (p + 1) * STATES] = total.astype(bf16)
    barrier = pltpu.get_barrier_semaphore()
    for d in range(1, size):
        peer = lax.rem(me + d, size)
        pl.semaphore_signal(barrier, inc=1, device_id={"fsdp": peer}, device_id_type=pl.DeviceIdType.MESH)
    pl.semaphore_wait(barrier, size - 1)

    def columns(device):
        return pl.ds(pl.multiple_of(device * width, width), width)

    copies = []
    for d in range(1, size):
        peer = lax.rem(me + d, size)
        for src, dst, sem in ((moved_ref, got, sems), (time_ref, got_time, time_sems)):
            copy = pltpu.make_async_remote_copy(
                src_ref=src.at[:, columns(peer)],
                dst_ref=dst.at[me],
                send_sem=sem.at[0, d],
                recv_sem=sem.at[1, d],
                device_id={"fsdp": peer},
                device_id_type=pl.DeviceIdType.MESH,
            )
            copy.start()
            copies.append(copy)
    got[me] = moved_ref[:, columns(me)]
    got_time[me] = time_ref[:, columns(me)]
    for copy in copies:
        copy.wait()

    rate = jnp.concatenate([rate_ref[...]] * PROMPTS, axis=0)
    branch = jnp.zeros((count, width), f32)
    state = jnp.zeros((count, width), f32)
    decays = []
    for k in range(size):
        time = jnp.concatenate(
            [jnp.broadcast_to(got_time[k, p : p + 1, :], (STATES, width)) for p in range(PROMPTS)], axis=0
        )
        decays.append(jnp.exp2(rate * time))
        back[k, 0:count] = state.astype(bf16)
        state = decays[k] * state + got[k, 0:count].astype(f32)
        branch = branch + got[k, 2 * count : 3 * count].astype(f32)
    grad = branch
    for k in range(size - 1, -1, -1):
        back[k, count : 2 * count] = grad.astype(bf16)
        grad = decays[k] * grad + got[k, count : 2 * count].astype(f32)
    last = state.astype(bf16)
    for k in range(size):
        back[k, 2 * count : 3 * count] = last
    copies = []
    for d in range(1, size):
        peer = lax.rem(me + d, size)
        copy = pltpu.make_async_remote_copy(
            src_ref=back.at[peer],
            dst_ref=done.at[me],
            send_sem=back_sems.at[0, d],
            recv_sem=back_sems.at[1, d],
            device_id={"fsdp": peer},
            device_id_type=pl.DeviceIdType.MESH,
        )
        copy.start()
        copies.append(copy)
    done[me] = back[me]
    for copy in copies:
        copy.wait()
    for k in range(size):
        columns_k = slice(k * width, (k + 1) * width)
        last = []
        for p in range(PROMPTS):
            rows = slice(p * STATES, (p + 1) * STATES)
            start_out[p, :, columns_k] = done[k, rows].astype(f32)
            rows = slice(count + p * STATES, count + (p + 1) * STATES)
            end_out[p, :, columns_k] = done[k, rows].astype(f32)
            rows = slice(2 * count + p * STATES, 2 * count + (p + 1) * STATES)
            last.append(done[k, rows].astype(f32))
        for q in range(sequels):
            total = one_hot_ref[q, 0] * last[0]
            for p in range(1, PROMPTS):
                total = total + one_hot_ref[q, p] * last[p]
            start_out[PROMPTS + q, :, columns_k] = total
            end_out[PROMPTS + q, :, columns_k] = jnp.zeros_like(total)


def chain(one_hot, ahead, behind, time, rate):
    size = lax.axis_size("fsdp")
    channels = ahead.shape[2]
    rows = 3 * PROMPTS * STATES
    width = channels // size
    own = lax.dynamic_slice_in_dim(rate, lax.axis_index("fsdp") * width, width, 1)
    whole = pl.BlockSpec(memory_space=pltpu.VMEM)
    shape = (PROMPTS + one_hot.shape[0], STATES, channels)
    return pl.pallas_call(
        chain_kernel,
        in_specs=[pl.BlockSpec(memory_space=pltpu.SMEM)] + [whole] * 4,
        out_specs=[whole] * 2,
        out_shape=[jax.ShapeDtypeStruct(shape, f32)] * 2,
        scratch_shapes=[
            pltpu.VMEM((rows, channels), bf16),
            pltpu.VMEM((size, rows, width), bf16),
            pltpu.VMEM((size, SEQS, width), f32),
            pltpu.VMEM((size, rows, width), bf16),
            pltpu.VMEM((size, rows, width), bf16),
            pltpu.SemaphoreType.DMA((2, size)),
            pltpu.SemaphoreType.DMA((2, size)),
            pltpu.SemaphoreType.DMA((2, size)),
        ],
        compiler_params=params(collective_id=1, has_side_effects=True),
        cost_estimate=cost(25),
        name="chain",
    )(one_hot, ahead, behind, time, own)


TILES = [slice(k * LANES, (k + 1) * LANES) for k in range(WIDE // LANES)]


def forward_kernel(
    proj_ref, dt_ref, act_ref, yg_ref, silu_ref, slope_ref, rate_ref, start_ref, skip_ref, select_ref,
    gated_ref, hist_ref, gategrad_ref, skipg_ref,
    b_scr, c_scr,
):
    j = pl.program_id(0)
    steps = dt_ref.shape[0]

    @pl.when(j == 0)
    def _():
        spread_maps(proj_ref, select_ref, RANK, STATES, store_plain(b_scr))
        spread_maps(proj_ref, select_ref, RANK + STATES, STATES, store_pairs(c_scr))

    gategrad_ref[0:HALO] = jnp.zeros((HALO, SEQS, WIDE), bf16)
    unroll = 8

    for part, cols in enumerate(TILES):
        rates = [jnp.broadcast_to(rate_ref[n : n + 1, cols], (SEQS, LANES)) for n in range(STATES)]
        skip = jnp.broadcast_to(skip_ref[0:1, cols], (SEQS, LANES))

        def run(i, carry):
            h, skip_sum = carry
            for k in range(unroll):
                t = i * unroll + k
                dt = dt_ref[t, :, cols]
                act = act_ref[t, :, cols]
                u = dt * act
                new = []
                y = None
                for p in range(PAIRS):
                    for n in (2 * p, 2 * p + 1):
                        new.append(jnp.exp2(dt * rates[n]) * h[n] + u * b_scr[t, n])
                    low = pair(new[2 * p], new[2 * p + 1])
                    hist_ref[part, t + 1, p] = low
                    term = low * c_scr[t, p]
                    y = term if p == 0 else y + term
                h = tuple(new)
                mixed = folded(y) + skip * act
                gated_ref[t, :, cols] = (mixed * silu_ref[t, :, cols].astype(f32)).astype(bf16)
                gategrad_ref[t + HALO, :, cols] = (mixed * slope_ref[t, :, cols].astype(f32)).astype(bf16)
                skip_sum = skip_sum + yg_ref[t, :, cols] * act
            return h, skip_sum

        start = tuple(start_ref[:, n, cols] for n in range(STATES))
        for p in range(PAIRS):
            hist_ref[part, 0, p] = pair(start[2 * p], start[2 * p + 1])
        _, skip_sum = lax.fori_loop(0, steps // unroll, run, (start, jnp.zeros((SEQS, LANES), f32)))
        skipg_ref[:, cols] = jnp.sum(skip_sum, axis=0, keepdims=True)


def forward(proj, dt, act, yg, silu, slope, rate, start, skip, select):
    grid, steps, _, _ = act.shape
    channels = grid * WIDE
    tile = lambda j: (0, 0, j)
    flat = pl.BlockSpec((None, steps, SEQS, WIDE), lambda j: (j, 0, 0, 0))
    parts = len(TILES)
    return pl.pallas_call(
        forward_kernel,
        grid=(grid,),
        in_specs=[
            pl.BlockSpec((steps * SEQS, LANES), lambda j: (0, 0)),
            flat, flat, flat, flat, flat,
            pl.BlockSpec((STATES, WIDE), lambda j: (0, j)),
            pl.BlockSpec((SEQS, STATES, WIDE), tile),
            pl.BlockSpec((1, WIDE), lambda j: (0, j)),
            pl.BlockSpec(select.shape, lambda j: (0, 0)),
        ],
        out_specs=[
            pl.BlockSpec((steps, SEQS, WIDE), tile),
            pl.BlockSpec((None, parts, steps + 1, PAIRS, 2 * SEQS, LANES), lambda j: (j, 0, 0, 0, 0, 0)),
            pl.BlockSpec((steps + HALO, SEQS, WIDE), tile),
            pl.BlockSpec((1, WIDE), lambda j: (0, j)),
        ],
        out_shape=[
            jax.ShapeDtypeStruct((steps, SEQS, channels), bf16),
            jax.ShapeDtypeStruct((grid, parts, steps + 1, PAIRS, 2 * SEQS, LANES), bf16),
            jax.ShapeDtypeStruct((steps + HALO, SEQS, channels), bf16),
            jax.ShapeDtypeStruct((1, channels), f32),
        ],
        scratch_shapes=[
            pltpu.VMEM((steps, STATES, SEQS, LANES), f32),
            pltpu.VMEM((steps, PAIRS, 2 * SEQS, LANES), bf16),
        ],
        compiler_params=params(),
        cost_estimate=cost(50),
        name="forward_scan",
    )(proj, dt, act, yg, silu, slope, rate, start, skip, select)


def backward_kernel(
    proj_ref, dt_ref, sig_ref, act_ref, yg_ref, rate_ref, end_ref, skip_ref,
    hist_ref, rank_t_ref, stepw_t_ref, pick_ref, select_ref,
    act_grad_ref, stepg_ref, biasg_ref, decayg_ref, projg_ref,
    b_scr, c_scr, db_scr, dc_scr, pre_scr, acc_scr, decay_scr, ge_scr, sum_scr,
):
    j = pl.program_id(0)
    steps = dt_ref.shape[0]

    @pl.when(j == 0)
    def _():
        spread_maps(proj_ref, select_ref, RANK, STATES, store_pairs(b_scr))
        spread_maps(proj_ref, select_ref, RANK + STATES, STATES, store_plain(c_scr))

        def clear(t, _):
            for p in range(PAIRS):
                db_scr[t, p] = jnp.zeros((2 * SEQS, LANES), bf16)
                dc_scr[t, p] = jnp.zeros((2 * SEQS, LANES), bf16)
            return 0

        lax.fori_loop(0, steps, clear, 0)
        acc_scr[...] = jnp.zeros_like(acc_scr)

    decay_scr[...] = jnp.zeros_like(decay_scr)
    sum_scr[...] = jnp.zeros_like(sum_scr)
    for n in range(STATES):
        ge_scr[n] = end_ref[:, n, :]

    def run(i, _):
        base = steps - (i + 1) * RUN
        db = [[None] * PAIRS for _ in range(RUN)]
        dc = [[None] * PAIRS for _ in range(RUN)]
        for part, cols in enumerate(TILES):
            rates = [jnp.broadcast_to(rate_ref[n : n + 1, cols], (SEQS, LANES)) for n in range(STATES)]
            low_rates = [pair(rates[2 * p], rates[2 * p + 1]) for p in range(PAIRS)]
            skip = jnp.broadcast_to(skip_ref[0:1, cols], (SEQS, LANES))
            ge = [ge_scr[n, :, cols] for n in range(STATES)]
            bias_sum = jnp.zeros((SEQS, LANES), f32)
            decay = [None] * PAIRS
            for k in range(RUN - 1, -1, -1):
                t = base + k
                dt = dt_ref[t, :, cols]
                act = act_ref[t, :, cols]
                yg = yg_ref[t, :, cols]
                u2 = both(dt * act)
                dt2 = both(dt)
                yg2 = both(yg)
                du = None
                ddt = None
                for p in range(PAIRS):
                    g = [ge[n] + yg * c_scr[t, n] for n in (2 * p, 2 * p + 1)]
                    g2 = pair(*g)
                    term = yg2 * hist_ref[part, t + 1, p]
                    dc[k][p] = term if part == 0 else dc[k][p] + term
                    term = g2 * u2
                    db[k][p] = term if part == 0 else db[k][p] + term
                    term = g2 * b_scr[t, p]
                    du = term if p == 0 else du + term
                    gn = [jnp.exp2(dt * rates[2 * p + m]) * g[m] for m in (0, 1)]
                    ge[2 * p], ge[2 * p + 1] = gn
                    q = pair(*gn) * hist_ref[part, t, p]
                    term = q * dt2
                    decay[p] = term if decay[p] is None else decay[p] + term
                    term = q * low_rates[p]
                    ddt = term if p == 0 else ddt + term
                du = folded(du)
                pre_grad = (du * act + folded(ddt) * LN2) * sig_ref[t, :, cols].astype(f32)
                pre_scr[t, :, cols] = pre_grad.astype(bf16)
                act_grad_ref[t, :, cols] = yg * skip + du * dt
                bias_sum = bias_sum + pre_grad
                if part == len(TILES) - 1:
                    for p in range(PAIRS):
                        dc_scr[t, p] = dc[k][p] + dc_scr[t, p]
                        db_scr[t, p] = db[k][p] + db_scr[t, p]
            for p in range(PAIRS):
                a, b = halves(decay[p])
                decay_scr[2 * p, :, cols] += a
                decay_scr[2 * p + 1, :, cols] += b
            for n in range(STATES):
                ge_scr[n, :, cols] = ge[n]
            sum_scr[:, cols] += bias_sum
        return 0

    lax.fori_loop(0, steps // RUN, run, 0)
    for n in range(STATES):
        decayg_ref[n : n + 1, :] = jnp.sum(decay_scr[n] * rate_ref[n : n + 1, :], axis=0, keepdims=True) * LN2
    biasg_ref[...] = jnp.sum(sum_scr[...], axis=0, keepdims=True)

    pre_low = pre_scr[...].reshape(steps * SEQS, WIDE)
    stepg_ref[...] = jnp.dot(rank_t_ref[...], pre_low, preferred_element_type=f32)
    acc_scr[...] += jnp.dot(pre_low, stepw_t_ref[...], preferred_element_type=f32)

    @pl.when(j == pl.num_programs(0) - 1)
    def _():
        chunk = 32
        even = lax.broadcasted_iota(jnp.int32, (chunk, SEQS, LANES), 2) % 2 == 0

        def step(i, _):
            t = i * chunk
            total = jnp.zeros((chunk * 2 * SEQS, LANES), f32)
            for p in range(PAIRS):
                rows = jnp.concatenate([db_scr[pl.ds(t, chunk), p], dc_scr[pl.ds(t, chunk), p]], axis=2)
                rows = rows.reshape(chunk * 2 * SEQS, 2 * LANES)
                total = total + jnp.dot(rows, pick_ref[p], preferred_element_type=f32)
            total = total.reshape(chunk, 2 * SEQS, LANES)
            total = jnp.where(even, total[:, :SEQS], total[:, SEQS:]).reshape(chunk * SEQS, LANES)
            r = pl.multiple_of(t * SEQS, chunk * SEQS)
            projg_ref[pl.ds(r, chunk * SEQS), :] = (acc_scr[pl.ds(r, chunk * SEQS), :] + total).astype(bf16)
            return 0

        lax.fori_loop(0, steps // chunk, step, 0)


def backward(proj, dt, sig, act, yg, rate, end, skip, hist, rank_t, stepw_t, pick, select):
    grid, steps, _, _ = act.shape
    channels = grid * WIDE
    tile = lambda j: (0, 0, j)
    whole = lambda j: (0, 0)
    flat = pl.BlockSpec((None, steps, SEQS, WIDE), lambda j: (j, 0, 0, 0))
    sums = pltpu.VMEM((steps, PAIRS, 2 * SEQS, LANES), bf16)
    return pl.pallas_call(
        backward_kernel,
        grid=(grid,),
        in_specs=[
            pl.BlockSpec((steps * SEQS, LANES), whole),
            flat, flat, flat, flat,
            pl.BlockSpec((STATES, WIDE), lambda j: (0, j)),
            pl.BlockSpec((SEQS, STATES, WIDE), tile),
            pl.BlockSpec((1, WIDE), lambda j: (0, j)),
            pl.BlockSpec(
                (None, len(TILES), steps + 1, PAIRS, 2 * SEQS, LANES), lambda j: (j, 0, 0, 0, 0, 0)
            ),
            pl.BlockSpec((RANK, steps * SEQS), whole),
            pl.BlockSpec((WIDE, LANES), lambda j: (j, 0)),
            pl.BlockSpec(pick.shape, lambda j: (0, 0, 0)),
            pl.BlockSpec(select.shape, whole),
        ],
        out_specs=[
            flat,
            pl.BlockSpec((RANK, WIDE), lambda j: (0, j)),
            pl.BlockSpec((1, WIDE), lambda j: (0, j)),
            pl.BlockSpec((STATES, WIDE), lambda j: (0, j)),
            pl.BlockSpec((steps * SEQS, LANES), whole),
        ],
        out_shape=[
            jax.ShapeDtypeStruct(act.shape, f32),
            jax.ShapeDtypeStruct((RANK, channels), f32),
            jax.ShapeDtypeStruct((1, channels), f32),
            jax.ShapeDtypeStruct((STATES, channels), f32),
            jax.ShapeDtypeStruct((steps * SEQS, LANES), bf16),
        ],
        scratch_shapes=[
            sums,
            pltpu.VMEM((steps, STATES, SEQS, LANES), f32),
            sums, sums,
            pltpu.VMEM((steps, SEQS, WIDE), bf16),
            pltpu.VMEM((steps * SEQS, LANES), f32),
            pltpu.VMEM((STATES, SEQS, WIDE), f32),
            pltpu.VMEM((STATES, SEQS, WIDE), f32),
            pltpu.VMEM((SEQS, WIDE), f32),
        ],
        compiler_params=params(),
        cost_estimate=cost(90),
        name="backward_scan",
    )(proj, dt, sig, act, yg, rate, end, skip, hist, rank_t, stepw_t, pick, select)


def filter_back_kernel(
    mix_ref, act_ref, bend_ref, act_grad_ref, projg_ref, projg_t_ref, sel_ref, fw_ref,
    mixgrad_ref, selg_ref, fwg_ref, fbg_ref,
    dv_scr, more_scr,
):
    steps = act_ref.shape[0]
    chunk = 16
    taps = [fw_ref[k : k + 1, :] for k in range(KERNEL)]
    zero = jnp.zeros((HALO, SEQS, WIDE), f32)
    dv_scr[0:HALO] = zero
    dv_scr[steps + HALO :] = zero

    more = contract_cols(projg_ref[...], sel_ref[...])
    more_scr[...] = more.reshape(steps, SEQS, WIDE)

    def step(i, sums):
        t = i * chunk
        x = mix_ref[pl.ds(t, chunk + HALO)].astype(f32)
        total = act_grad_ref[pl.ds(t, chunk)] + more_scr[pl.ds(t, chunk)]
        dv = total * bend_ref[pl.ds(t, chunk)].astype(f32)
        dv_scr[pl.ds(t + HALO, chunk)] = dv
        new = [sums[0] + jnp.sum(dv, axis=0)]
        for k in range(KERNEL):
            new.append(sums[1 + k] + jnp.sum(dv * x[1 + k : 1 + k + chunk], axis=0))
        return tuple(new)

    sums = lax.fori_loop(
        0, steps // chunk, step, tuple(jnp.zeros((SEQS, WIDE), f32) for _ in range(KERNEL + 1))
    )
    fbg_ref[...] = jnp.sum(sums[0], axis=0, keepdims=True)
    for k in range(KERNEL):
        fwg_ref[k : k + 1, :] = jnp.sum(sums[1 + k], axis=0, keepdims=True)

    def spread(t, count):
        dv = dv_scr[pl.ds(t, count + HALO)]
        out = taps[KERNEL - 1][None] * dv[0:count]
        for k in range(KERNEL - 1):
            s = KERNEL - 1 - k
            out = out + taps[k][None] * dv[s : s + count]
        mixgrad_ref[pl.ds(t, count)] = out.astype(bf16)

    def out_step(i, _):
        spread(i * chunk, chunk)
        return 0

    lax.fori_loop(0, steps // chunk, out_step, 0)
    spread(steps, HALO)
    low = act_ref[...].reshape(steps * SEQS, WIDE).astype(bf16)
    selg_ref[...] = jnp.dot(projg_t_ref[...], low, preferred_element_type=f32)


def filter_back(mixture, act, bend, act_grad, projg, projg_t, select_pad, fw):
    grid, steps, _, _ = act.shape
    channels = grid * WIDE
    wide = lambda j: (0, 0, j)
    whole = lambda j: (0, 0)
    cols = lambda j: (0, j)
    return pl.pallas_call(
        filter_back_kernel,
        grid=(grid,),
        in_specs=[
            pl.BlockSpec((None, steps + HALO, SEQS, WIDE), lambda j: (j, 0, 0, 0)),
            pl.BlockSpec((None, steps, SEQS, WIDE), lambda j: (j, 0, 0, 0)),
            pl.BlockSpec((None, steps, SEQS, WIDE), lambda j: (j, 0, 0, 0)),
            pl.BlockSpec((None, steps, SEQS, WIDE), lambda j: (j, 0, 0, 0)),
            pl.BlockSpec((steps * SEQS, LANES), whole),
            pl.BlockSpec((LANES, steps * SEQS), whole),
            pl.BlockSpec((WIDE, LANES), lambda j: (j, 0)),
            pl.BlockSpec((KERNEL, WIDE), cols),
        ],
        out_specs=[
            pl.BlockSpec((steps + HALO, SEQS, WIDE), wide),
            pl.BlockSpec((LANES, WIDE), cols),
            pl.BlockSpec((KERNEL, WIDE), cols),
            pl.BlockSpec((1, WIDE), cols),
        ],
        out_shape=[
            jax.ShapeDtypeStruct((steps + HALO, SEQS, channels), bf16),
            jax.ShapeDtypeStruct((LANES, channels), f32),
            jax.ShapeDtypeStruct((KERNEL, channels), f32),
            jax.ShapeDtypeStruct((1, channels), f32),
        ],
        scratch_shapes=[
            pltpu.VMEM((steps + 2 * HALO, SEQS, WIDE), f32),
            pltpu.VMEM((steps, SEQS, WIDE), f32),
        ],
        compiler_params=params(),
        cost_estimate=cost(20),
        name="filter_back",
    )(mixture, act, bend, act_grad, projg, projg_t, select_pad, fw)


def send(src, dst, send_sem, recv_sem, peer, axis="fsdp"):
    return pltpu.make_async_remote_copy(
        src_ref=src,
        dst_ref=dst,
        send_sem=send_sem,
        recv_sem=recv_sem,
        device_id={axis: peer},
        device_id_type=pl.DeviceIdType.MESH,
    )


def greet(others):
    barrier = pltpu.get_barrier_semaphore()
    for axis, peer in others:
        pl.semaphore_signal(barrier, inc=1, device_id={axis: peer}, device_id_type=pl.DeviceIdType.MESH)
    pl.semaphore_wait(barrier, len(others))


def flipped(index, bit):
    return index + (1 - 2 * (index // bit % 2)) * bit


FIRST, SECOND = (0, 1, 2, 3), (4, 5)
TRADED = (2, 3, 4, 5)


def gather_kernel(
    rows_ref, select_ref, out_ref, in_ref, all_rows, all_select, all_out, all_in,
    local_sems, own_send, own_recv, pass_send, pass_recv, core_send, core_recv, trade_send, trade_recv,
):
    me = lax.axis_index("fsdp")
    mz = lax.axis_index("replica")
    a, b = flipped(me, 2), flipped(me, 4)
    corner = flipped(a, 4)
    twin = flipped(me, 1)
    mate = flipped(mz, 1)
    greet([("fsdp", a), ("fsdp", b), ("fsdp", twin), ("replica", mate)])
    kinds = ((rows_ref, all_rows), (select_ref, all_select), (out_ref, all_out), (in_ref, all_in))

    def span(piece, side):
        if piece < 2:
            return piece, 0, kinds[piece][0].shape[0]
        kind = 2 + piece % 2
        quarter = kinds[kind][0].shape[0] // 4
        return kind, side * (2 * quarter) + (quarter if piece in SECOND else 0), quarter

    def place(owner, piece, side):
        kind, start, count = span(piece, side)
        first = owner * kinds[kind][0].shape[0] + start
        return kinds[kind][1].at[pl.ds(pl.multiple_of(first, 16), count)]

    def mine(piece, side):
        kind, start, count = span(piece, side)
        return kinds[kind][0].at[pl.ds(pl.multiple_of(start, 16), count) if piece in TRADED else pl.ds(0, count)]

    side = mz % 2
    other = 1 - side
    started = []

    def start(copy):
        copy.start()
        started.append(copy)

    def own_copy(piece, k, peer, owner):
        return send(mine(piece, side), place(owner, piece, side), own_send.at[k, piece], own_recv.at[k, piece], peer)

    def pass_copy(piece, peer, owner, far=False):
        ref = place(owner, piece, other if far else side)
        at = piece + len(FIRST + SECOND) * far
        return send(ref, ref, pass_send.at[at], pass_recv.at[at], peer)

    def trade_copy(piece, k, owner, whose):
        ref = place(owner, piece, whose)
        return send(ref, ref, trade_send.at[k, piece], trade_recv.at[k, piece], mate, "replica")

    def core_copy(piece, k, owner, whose=None):
        if whose is None:
            return send(
                place(owner, piece, side), place(owner, piece, side), core_send.at[k, piece], core_recv.at[k, piece], twin
            )
        at = len(FIRST + SECOND) + piece
        ref = place(owner, piece, whose)
        return send(ref, ref, core_send.at[k, at], core_recv.at[k, at], twin)

    def whole_copy(kind, owner):
        src, dst = kinds[kind]
        count = src.shape[0]
        rows = dst.at[pl.ds(pl.multiple_of(owner * count, count), count)]
        return send(src, rows, core_send.at[3, kind], core_recv.at[3, kind], twin)

    for piece in FIRST + SECOND:
        start(own_copy(piece, 0, a, me))
    for piece in SECOND + (2, 3, 0, 1):
        start(own_copy(piece, 1, b, me))
    local = []
    for kind, (src, dst) in enumerate(kinds):
        start(whole_copy(kind, me))
        count = src.shape[0]
        rows = dst.at[pl.ds(pl.multiple_of(me * count, count), count)]
        copy = pltpu.make_async_copy(src, rows, local_sems.at[kind])
        copy.start()
        local.append(copy)
    owners = (a, b, corner)

    def arrived(piece, k):
        owner = owners[k]
        if k == 2:
            pass_copy(piece, a, owner).wait_recv()
        else:
            own_copy(piece, k, a, owner).wait_recv()
            if k == 0 and piece in FIRST:
                start(pass_copy(piece, b, owner))
            if k == 1 and piece in SECOND:
                start(pass_copy(piece, a, owner))
        if piece in TRADED and k < 2:
            start(trade_copy(piece, k, owner, side))
        start(core_copy(piece, k, owner))

    def traded(piece, k):
        owner = owners[k]
        trade_copy(piece, k, owner, other).wait_recv()
        if k == 0 and piece in FIRST:
            start(pass_copy(piece, b, owner, True))
        if k == 1 and piece in SECOND:
            start(pass_copy(piece, a, owner, True))
        start(core_copy(piece, k, owner, other))

    for piece, k in ((0, 0), (4, 1), (1, 0), (2, 0), (5, 1), (3, 0)):
        arrived(piece, k)
    traded(2, 0)
    traded(4, 1)
    arrived(4, 0)
    arrived(2, 1)
    traded(3, 0)
    traded(5, 1)
    for piece, k in ((5, 0), (3, 1), (0, 1), (1, 1), (0, 2), (1, 2), (2, 2), (4, 2), (3, 2), (5, 2)):
        arrived(piece, k)
    for piece, k in ((4, 0), (2, 1), (5, 0), (3, 1)):
        traded(piece, k)
    for piece in (2, 4, 3, 5):
        pass_copy(piece, a, corner, True).wait_recv()
        start(core_copy(piece, 2, corner, other))
    for kind in range(len(kinds)):
        whole_copy(kind, twin).wait_recv()
    for k, owner in enumerate((flipped(twin, 2), flipped(twin, 4), flipped(corner, 1))):
        for piece in FIRST + SECOND:
            core_copy(piece, k, owner).wait_recv()
        for piece in TRADED:
            core_copy(piece, k, owner, other).wait_recv()
    for copy in started:
        copy.wait_send()
    for copy in local:
        copy.wait()


def gather(*shards):
    size = lax.axis_size("fsdp")
    if size != 8 or lax.axis_size("replica") % 2:
        return [lax.all_gather(shard, "fsdp", axis=0, tiled=True) for shard in shards]
    vmem = pl.BlockSpec(memory_space=pltpu.VMEM)
    hbm = pl.BlockSpec(memory_space=pl.ANY)
    pieces = len(FIRST + SECOND)
    dma = pltpu.SemaphoreType.DMA
    return pl.pallas_call(
        gather_kernel,
        in_specs=[vmem] * 4,
        out_specs=[hbm] * 4,
        out_shape=[jax.ShapeDtypeStruct((size * shard.shape[0], shard.shape[1]), bf16) for shard in shards],
        scratch_shapes=[
            dma((len(shards),)), dma((2, pieces)), dma((2, pieces)), dma((2 * pieces,)), dma((2 * pieces,)),
            dma((4, 2 * pieces)), dma((4, 2 * pieces)), dma((3, pieces)), dma((3, pieces)),
        ],
        compiler_params=params(collective_id=2, has_side_effects=True),
        cost_estimate=cost(55),
        name="gather",
    )(*shards)


SMALL = (KERNEL, 1, 1, 1, STATES, RANK, RANK + 2 * STATES, 1)
SMALL_ROWS = 192


def xor(index, bits):
    for bit in (1, 2, 4, 8):
        if bits & bit:
            index = flipped(index, bit)
    return index


def tail_kernel(
    one_hot_ref, b0, b1, b2, b3, filter_ref, fbias_ref, sbias_ref, skip_ref, decay_ref, step_ref, select_ref,
    gain_ref, halo_ref, block_out, small_out, rim_out,
    total, to_z, from_z, part, parts, small_f, small_ref, got_small, small_z, small_from_z, small_part,
    small_parts, rim, child, got_rim, got_child,
    sems_s, sems_z, sems_p, sems_sz, sems_sp, sems_r, sems_cs, sems_cr,
):
    depth = lax.axis_size("replica")
    me, size = lax.axis_index("fsdp"), lax.axis_size("fsdp")
    mz = lax.axis_index("replica")
    last = size - 1
    near = [lax.rem(me + d, size) for d in range(1, size)]
    far = [lax.rem(mz + d, depth) for d in range(1, depth)]
    greet([("fsdp", peer) for peer in near] + [("replica", peer) for peer in far])

    def spread(src, dst, sems, peers, axis, index):
        copies = []
        for d, peer in enumerate(peers):
            source = src.at[peer] if src.shape[0] == len(peers) + 1 and len(src.shape) == len(dst.shape) else src
            copy = send(source, dst.at[index], sems.at[0, d], sems.at[1, d], peer, axis)
            copy.start()
            copies.append(copy)
        return copies

    width = small_f.shape[2]
    small_f[...] = jnp.zeros_like(small_f)
    refs = (filter_ref, fbias_ref, sbias_ref, skip_ref, decay_ref, step_ref, select_ref)
    for k in range(size):
        at = 0
        for ref, count in zip(refs, SMALL):
            small_f[k, at : at + count] = ref[0:count, k * width : (k + 1) * width]
            at += count
        some = gain_ref.shape[1] // size
        small_f[k, at : at + 1, 0:some] = gain_ref[:, k * some : (k + 1) * some]
    small_ref[...] = small_f[...].astype(bf16)
    sequels = one_hot_ref.shape[0]
    pieces = (SEQS - PROMPTS) // sequels
    for t in range(HALO):
        rim[t * PROMPTS : (t + 1) * PROMPTS] = halo_ref[t, 0:PROMPTS]
        for p in range(PROMPTS):
            sums = None
            for q in range(sequels):
                row = PROMPTS + q * pieces
                term = one_hot_ref[q, p] * halo_ref[t, row : row + 1]
                sums = term if q == 0 else sums + term
            child[t * PROMPTS + p : t * PROMPTS + p + 1] = sums
    block = b0[...].astype(f32) + b1[...].astype(f32) + b2[...].astype(f32) + b3[...].astype(f32)
    total[...] = block.reshape(total.shape)
    to_z[...] = total[...].astype(bf16)
    to_left = send(rim, got_rim, sems_r.at[0], sems_r.at[1], lax.rem(me + last, size))
    to_left.start()

    @pl.when(me != last)
    def _():
        send(child, got_child.at[me], sems_cs.at[me], sems_cr.at[me], last).start()

    copies = spread(small_ref, got_small, sems_s, near, "fsdp", me)
    z_copies = spread(to_z, from_z, sems_z, far, "replica", mz)
    small = small_ref[me].astype(f32)
    got_small[me] = jnp.zeros(got_small.shape[1:], bf16)
    from_z[mz] = jnp.zeros(from_z.shape[1:], bf16)
    small_from_z[mz] = jnp.zeros(small_from_z.shape[1:], bf16)
    for copy in copies:
        copy.wait()
    for k in range(size):
        small = small + got_small[k].astype(f32)
    small_z[...] = small.reshape(small_z.shape)
    small_to_z = small_part
    small_to_z[...] = small_z[...].astype(bf16)
    s_copies = spread(small_to_z, small_from_z, sems_sz, far, "replica", mz)
    for copy in z_copies:
        copy.wait()
    own = total[mz]
    for k in range(depth):
        own = own + from_z[k].astype(f32)
    part[...] = own.astype(bf16)
    p_copies = spread(part, parts, sems_p, far, "replica", mz)
    parts[mz] = part[...]
    for copy in s_copies:
        copy.wait()
    own = small_z[mz]
    for k in range(depth):
        own = own + small_from_z[k].astype(f32)
    small_parts[mz] = own.astype(bf16)
    small_own = small_to_z.at[mz]
    small_own[...] = own.astype(bf16)
    q_copies = []
    for d, peer in enumerate(far):
        copy = send(small_own, small_parts.at[mz], sems_sp.at[0, d], sems_sp.at[1, d], peer, "replica")
        copy.start()
        q_copies.append(copy)
    for copy in p_copies + q_copies:
        copy.wait()
    block_out[...] = parts[...].reshape(block_out.shape)
    small_out[...] = small_parts[...].reshape(small_out.shape)
    to_left.wait()

    @pl.when(me != last)
    def _():
        send(child, got_child.at[me], sems_cs.at[me], sems_cr.at[me], last).wait_send()
        rim_out[...] = got_rim[...]

    @pl.when(me == last)
    def _():
        sums = child[...]
        for k in range(size - 1):
            send(child, got_child.at[k], sems_cs.at[k], sems_cr.at[k], 0).wait_recv()
            sums = sums + got_child[k]
        rim_out[...] = sums


def tail(one_hot, blocks, small, halo_grad):
    size, depth = lax.axis_size("fsdp"), lax.axis_size("replica")
    vmem = pl.BlockSpec(memory_space=pltpu.VMEM)
    dma = pltpu.SemaphoreType.DMA
    while len(blocks) > 4:
        blocks = blocks[:3] + [summed(blocks[3], blocks[4:5]).astype(bf16)] + blocks[5:]
    rows, channels = blocks[0].shape
    features = small[-1].shape[1]
    width = channels // size
    cut = (depth, rows // depth, channels)
    by_owner = (size, SMALL_ROWS, width)
    small_cut = (depth, SMALL_ROWS // depth, width)
    rim = (HALO * PROMPTS, features)
    return pl.pallas_call(
        tail_kernel,
        in_specs=[pl.BlockSpec(memory_space=pltpu.SMEM)] + [vmem] * (4 + len(small) + 1),
        out_specs=[vmem] * 3,
        out_shape=[
            jax.ShapeDtypeStruct((rows, channels), bf16),
            jax.ShapeDtypeStruct((SMALL_ROWS, width), bf16),
            jax.ShapeDtypeStruct(rim, f32),
        ],
        scratch_shapes=[
            pltpu.VMEM(cut, f32), pltpu.VMEM(cut, bf16), pltpu.VMEM(cut, bf16),
            pltpu.VMEM(cut[1:], bf16), pltpu.VMEM(cut, bf16),
            pltpu.VMEM(by_owner, f32), pltpu.VMEM(by_owner, bf16), pltpu.VMEM(by_owner, bf16),
            pltpu.VMEM(small_cut, f32), pltpu.VMEM(small_cut, bf16),
            pltpu.VMEM(small_cut, bf16), pltpu.VMEM(small_cut, bf16),
            pltpu.VMEM(rim, f32), pltpu.VMEM(rim, f32), pltpu.VMEM(rim, f32), pltpu.VMEM((size,) + rim, f32),
            dma((2, size)), dma((2, depth)), dma((2, depth)), dma((2, depth)), dma((2, depth)),
            dma((2,)), dma((size,)), dma((size,)),
        ],
        compiler_params=params(collective_id=4, has_side_effects=True),
        cost_estimate=cost(30),
        name="tail",
    )(one_hot, *blocks, *small, halo_grad)


def deliver_kernel(block_ref, small_ref, rim_ref, prompt_ref, *rest):
    depth = lax.axis_size("replica")
    early_refs, outs = rest[:depth], rest[depth:-1]
    early = rest[-1]
    in_out, out_out, prompt_out = outs[:3]
    mz = lax.axis_index("replica")
    half = in_out.shape[1] // 2
    in_out[:, 0:half] = block_ref[...].astype(f32)
    small = small_ref[...].astype(f32)
    at = 0
    for out, count in zip(outs[3:], SMALL):
        rows = small[at : at + count]
        out[...] = rows[:, 0 : out.shape[1]]
        at += count
    for d, ref in enumerate(early_refs):
        count = ref.shape[0]
        early[pl.ds(pl.multiple_of(xor(mz, d) * count, count), count), :] = ref[...].astype(f32)
    rows = out_out.shape[0] // 2
    features = out_out.shape[1]
    out_out[0:rows, :] = early[0:rows, 0:features]
    out_out[rows:, :] = early[0:rows, features:]
    in_out[:, half:] = early[rows:, :]
    for p in range(PROMPTS):
        prompt_out[p, 0 : SEQS - HALO] = prompt_ref[p, 0 : SEQS - HALO]
        for t in range(HALO):
            row = SEQS - HALO + t
            prompt_out[p, row : row + 1] = (
                prompt_ref[p, row : row + 1] + rim_ref[t * PROMPTS + p : t * PROMPTS + p + 1]
            )


def deliver(block, small, rim, prompt_grad, early):
    size = lax.axis_size("fsdp")
    rows, channels = block.shape
    width = small.shape[1]
    features = prompt_grad.shape[2]
    vmem = pl.BlockSpec(memory_space=pltpu.VMEM)
    end = prompt_grad.shape[1] // SEQS - 1
    last = pl.BlockSpec((PROMPTS, SEQS, features), lambda i: (0, end, 0))
    shapes = [(count, width) for count in SMALL[:-1]] + [(1, features // size)]
    shapes = [(rows, 2 * channels), (2 * rows, features), prompt_grad.shape] + shapes
    return pl.pallas_call(
        deliver_kernel,
        grid=(1,),
        in_specs=[vmem, vmem, vmem, last] + [vmem] * len(early),
        out_specs=[vmem, vmem, last] + [vmem] * len(SMALL),
        out_shape=[jax.ShapeDtypeStruct(shape, f32) for shape in shapes],
        scratch_shapes=[pltpu.VMEM((2 * rows, channels), f32)],
        input_output_aliases={3: 2},
        compiler_params=params(),
        cost_estimate=cost(4),
        name="deliver",
    )(block, small, rim, prompt_grad, *early)


def contract_rows(left_side, right_side):
    return lax.dot_general(
        left_side, right_side, (((0,), (0,)), ((), ())), preferred_element_type=f32
    )


def contract_cols(left_side, right_side):
    return lax.dot_general(
        left_side, right_side, (((1,), (1,)), ((), ())), preferred_element_type=f32
    )


def exchanged(block, axis, distance):
    return lax.ppermute(block, axis, [(i, i ^ distance) for i in range(lax.axis_size(axis))])


def pick_row(block, index, axis=0):
    return lax.dynamic_index_in_dim(block, index, axis, keepdims=False)


def over_cores(blocks):
    blocks = blocks.reshape((-1, 2) + blocks.shape[1:])
    core = lax.axis_index("fsdp") % 2
    got = exchanged(pick_row(blocks, 1 - core, 1), "fsdp", 1)
    return (pick_row(blocks, core, 1).astype(f32) + got.astype(f32)).astype(bf16)


def to_chips(blocks):
    chip = lax.axis_index("fsdp") // 2
    got = [exchanged(pick_row(blocks, chip ^ d), "fsdp", 2 * d) for d in range(1, blocks.shape[0])]
    return pick_row(blocks, chip), got


def summed(own, got):
    total = own.astype(f32)
    for block in got:
        total = total + block.astype(f32)
    return total


def to_replicas(block):
    size, here = lax.axis_size("replica"), lax.axis_index("replica")
    parts = block.astype(bf16).reshape((size, -1) + block.shape[1:])
    own = pick_row(block.reshape(parts.shape), here)
    return own, [exchanged(pick_row(parts, here ^ d), "replica", d) for d in range(1, size)]


def from_replicas(part):
    return [part] + [exchanged(part, "replica", d) for d in range(1, lax.axis_size("replica"))]


def body(
    prompt_hidden, sequel_hidden, parents, prompt_cotangent, sequel_cotangent,
    norm_gain, input_weight, filter_weight, depthwise_filter_bias, select_weight,
    step_weight, step_bias, decay_log, skip_gain, output_weight,
):
    size, here = lax.axis_size("fsdp"), lax.axis_index("fsdp")
    prompts, steps = prompt_hidden.shape[:2]
    sequels, sequel_len = sequel_hidden.shape[:2]
    split = sequel_len // steps
    assert prompts == PROMPTS and sequels * split == SEQS - prompts
    rim = KERNEL - 1
    half = SEQS // 2
    rows = steps * SEQS

    after = lax.optimization_barrier
    width = step_bias.shape[0]
    tail_rows = prompt_hidden[:, steps - rim :]
    shard = jnp.concatenate(
        [
            step_weight,
            tail_rows.reshape(-1, width),
            filter_weight,
            depthwise_filter_bias[None],
            step_bias[None],
            skip_gain[None],
            jnp.pad(norm_gain, (0, width - norm_gain.shape[0]))[None],
        ],
        axis=0,
    )
    shard = jnp.pad(shard, ((0, -shard.shape[0] % 16), (0, 0)))
    lanes = jnp.concatenate([select_weight, decay_log], axis=1)
    lanes = jnp.pad(lanes, ((0, 0), (0, LANES - lanes.shape[1])))
    every, select_pad, full_output, full_input = gather(shard, lanes, output_weight, input_weight)
    every = every.reshape(size, shard.shape[0], width)
    at = RANK + tail_rows.size // width
    tails = every[:, RANK:at].reshape((size,) + tail_rows.shape)
    step_full = jnp.swapaxes(every[:, :RANK], 0, 1).reshape(RANK, -1)
    vectors = jnp.swapaxes(every[:, at : at + SEQS], 0, 1).astype(f32)
    gain = vectors[KERNEL + 3, :, : norm_gain.shape[0]].reshape(1, -1)
    vectors = vectors.reshape(SEQS, -1)
    fw, fb, sbias, skip = vectors[:KERNEL], vectors[4:5], vectors[5:6], vectors[6:7]
    first = RANK + 2 * STATES
    rate = -jnp.exp(select_pad[:, first : first + STATES].T.astype(f32)) * LOG2E
    step_pad = jnp.pad(step_full, ((0, LANES - RANK), (0, 0)))

    before = jnp.where(here > 0, tails[jnp.maximum(here - 1, 0)], jnp.zeros_like(tails[0]))
    cut = sequel_hidden.reshape(sequels, split, steps, D)
    inner = jnp.concatenate([tails[size - 1][parents][:, None], cut[:, :-1, steps - rim :]], axis=1)
    halo = jnp.concatenate([before, inner.reshape(-1, rim, D)], axis=0)
    halo = jnp.pad(jnp.swapaxes(halo, 0, 1), ((HALO - rim, 0), (0, 0), (0, 0))).reshape(-1, D).astype(f32)
    pieces = sequel_hidden.reshape(-1, steps, D)
    piece_cot = sequel_cotangent.reshape(-1, steps, D)
    scaled, cotangent = prepare(prompt_hidden, pieces, prompt_cotangent, piece_cot, halo, gain)

    mixture = product([scaled], full_input, bf16, tiled=True)
    mixture = mixture.reshape(-1, steps + HALO, SEQS, WIDE)
    gated_grad = product([cotangent], full_output, f32, across=True, tiled=True)
    gated_grad = gated_grad.reshape(-1, steps, SEQS, WIDE)
    act, bend, proj = front(mixture, fw, fb, select_pad, steps)
    groups = 1 if split == 1 else 2
    lane = jnp.arange(2 * STATES * LANES)[None, :]
    select = (jnp.arange(LANES)[:, None] == RANK + lane // LANES).astype(bf16)
    dt, sig, yg, silu, slope, ahead, behind, total = piece(
        proj, act, mixture, gated_grad, step_pad, sbias, rate, select, groups
    )

    one_hot = (parents[:, None] == jnp.arange(PROMPTS, dtype=jnp.int32)[None, :]).astype(f32)
    own = total[half:].reshape(sequels, split, 1, INNER)
    own_behind = behind[half:].reshape(sequels, split, STATES, INNER)
    back = own_behind[:, split - 1]
    own_end = [jnp.zeros_like(back)]
    for p in range(split - 2, -1, -1):
        own_end.insert(0, back)
        back = own_behind[:, p] + jnp.exp2(rate * own[:, p]) * back
    joint = behind if split == 1 else jnp.concatenate([behind[:half], back], axis=0)
    start, end = chain(one_hot, ahead, joint, total, rate)
    if split > 1:
        state = start[half:]
        own_start = [state]
        for p in range(split - 1):
            state = jnp.exp2(rate * own[:, p]) * state + ahead[half:].reshape(own_behind.shape)[:, p]
            own_start.append(state)
        own_start = jnp.stack(own_start, axis=1).reshape(half, STATES, INNER)
        start = jnp.concatenate([start[:half], own_start], axis=0)
        end = jnp.concatenate([end[:half], jnp.stack(own_end, axis=1).reshape(half, STATES, INNER)], axis=0)

    gated, hist, gate_grad, skip_grad = forward(
        proj, dt, act, yg, silu, slope, rate, start, skip, select
    )
    gated = gated.reshape(rows, INNER)
    gate_grad = gate_grad.reshape(-1, INNER)
    output_grad = contract_rows(gated, cotangent).astype(bf16).reshape(size, -1, D)
    gate_weight_grad = contract_rows(scaled, gate_grad).astype(bf16)
    early = [over_cores(output_grad), over_cores(gate_weight_grad.reshape(size, -1, INNER))]
    wide = jnp.concatenate([early[0][:, : INNER // size // 2], early[0][:, INNER // size // 2 :]], axis=2)
    early = jnp.concatenate([wide, early[1]], axis=1)
    end, early = after((end, early))
    early = to_chips(early)

    rank_t = proj[:, :RANK].astype(bf16).T
    lane = jnp.arange(LANES)[None, None, :]
    which = jnp.arange(PAIRS)[:, None, None]
    source = jnp.arange(2 * LANES)[None, :, None]
    pick = (lane // 2 == jnp.where(source < LANES, RANK, RANK + STATES) // 2 + which).astype(bf16)
    act_grad, step_grad, bias_grad, decay_grad, projg = backward(
        proj, dt, sig, act, yg, rate, end, skip, hist, rank_t, step_pad.T, pick, select
    )
    projg, early = after((projg, early))
    early = summed(*early)
    projg, early = after((projg, early))
    early = to_replicas(early)
    filter_in_grad, select_grad, filter_grad, filter_bias_grad = filter_back(
        mixture, act, bend, act_grad, projg, projg.T, select_pad, fw
    )
    filter_in_grad, early = after((filter_in_grad, early))
    early = summed(*early).astype(bf16)
    filter_in_grad = filter_in_grad.reshape(-1, INNER)
    filter_weight_grad = contract_rows(scaled, filter_in_grad).astype(bf16)
    filter_weight_grad, early = after((filter_weight_grad, early))
    late = over_cores(filter_weight_grad.reshape(size, -1, INNER))
    early = from_replicas(early)
    mixed = jnp.dot(gated, full_output, preferred_element_type=f32)
    late, mixed, filter_in_grad = after((late, mixed, filter_in_grad))
    own_block, late = to_chips(late)
    scaled_grad = product([filter_in_grad, gate_grad], full_input, f32, across=True)
    prompt_out, piece_out, prompt_grad, piece_grad, halo_grad, gain_grad = finish(
        mixed, scaled_grad, prompt_hidden, pieces, prompt_cotangent, piece_cot, halo, gain
    )
    halo_grad, own_block, late = after((halo_grad, own_block, late))
    halo_grad = halo_grad.reshape(HALO, SEQS, D)
    small = [
        filter_grad, filter_bias_grad, bias_grad, skip_grad, decay_grad, step_grad, select_grad, gain_grad,
    ]
    block, small, following = tail(one_hot, [own_block] + late, small, halo_grad)
    (
        input_grad, output_grad, prompt_grad, g_filter, g_fbias, g_sbias, g_skip, g_decay, g_step, g_select, g_gain,
    ) = deliver(block, small, following, prompt_grad, early)
    if split > 1:
        own = jnp.swapaxes(halo_grad[:, half:], 0, 1).reshape(sequels, split, HALO, D)
        own = jnp.pad(own[:, 1:], ((0, 0), (0, 1), (0, 0), (0, 0))).reshape(half, HALO, D)
        piece_grad = piece_grad.at[:, steps - HALO :].add(own)
    return (
        prompt_out,
        piece_out.reshape(sequel_hidden.shape),
        prompt_grad,
        piece_grad.reshape(sequel_hidden.shape),
        g_gain[0],
        input_grad,
        g_filter,
        g_fbias[0],
        g_select.T,
        g_step,
        g_sbias[0],
        g_decay.T,
        g_skip[0],
        output_grad,
    )


def solution(mesh):
    rows = P("replica", "fsdp", None)
    own = P(("replica", "fsdp"), None, None)
    return jax.shard_map(
        body,
        mesh=mesh,
        in_specs=(
            rows, own, P(("replica", "fsdp")), rows, own,
            P("fsdp"), P("fsdp", None), P(None, "fsdp"), P("fsdp"), P("fsdp", None),
            P(None, "fsdp"), P("fsdp"), P("fsdp", None), P("fsdp"), P("fsdp", None),
        ),
        out_specs=(
            rows, own, rows, own,
            P("fsdp"), P("fsdp", None), P(None, "fsdp"), P("fsdp"), P("fsdp", None),
            P(None, "fsdp"), P("fsdp"), P("fsdp", None), P("fsdp"), P("fsdp", None),
        ),
        check_vma=False,
    )
```

```python
import functools
import math

import jax
import jax.numpy as jnp
from jax import lax
from jax.experimental import pallas as pl
from jax.experimental.pallas import tpu as pltpu
from jax.sharding import PartitionSpec as P

D = 1024
INNER = 2048
STATES = 16
RANK = 64
KERNEL = 4
PROMPTS = 4

SEQS = 8
HALO = 4
LANES = 128
WIDE = 256
LOG2E = math.log2(math.e)
LN2 = math.log(2.0)
f32 = jnp.float32
bf16 = jnp.bfloat16

VMEM_LIMIT = 62 * 1024 * 1024


def cost(microseconds):
    return pl.CostEstimate(flops=int(microseconds * 1e9), bytes_accessed=0, transcendentals=0)


def params(**kw):
    return pltpu.CompilerParams(vmem_limit_bytes=VMEM_LIMIT, **kw)


def sigmoid(x):
    return 1.0 / (1.0 + jnp.exp(-x))


def softplus(x):
    return jnp.maximum(x, 0.0) + jnp.log1p(jnp.exp(-jnp.abs(x)))


def product_kernel(across, *refs):
    lefts, rhs_ref, out_ref = refs[:-2], refs[-2], refs[-1]
    total = None
    at = 0
    for left in lefts:
        depth = left.shape[1]
        rhs = rhs_ref[:, at : at + depth] if across else rhs_ref[at : at + depth]
        dims = (((1,), (1 if across else 0,)), ((), ()))
        term = lax.dot_general(left[...], rhs, dims, preferred_element_type=f32)
        total = term if total is None else total + term
        at += depth
    if len(out_ref.shape) == 2:
        out_ref[...] = total.astype(out_ref.dtype)
    else:
        for k in range(out_ref.shape[0]):
            out_ref[k] = total[:, k * WIDE : (k + 1) * WIDE].astype(out_ref.dtype)


def product(lefts, rhs, kind, across=False, part=0, parts=1, tiled=False):
    rows = lefts[0].shape[0]
    depth = sum(left.shape[1] for left in lefts)
    tile = 2 * WIDE if len(lefts) == 1 else WIDE
    if across:
        columns = rhs.shape[0]
        rhs_spec = pl.BlockSpec((tile, depth), lambda j: (j, 0))
    else:
        columns = rhs.shape[1] // parts
        first = part * columns // tile
        rhs_spec = pl.BlockSpec((depth, tile), lambda j: (0, first + j))
    return pl.pallas_call(
        functools.partial(product_kernel, across),
        grid=(columns // tile,),
        in_specs=[pl.BlockSpec(left.shape, lambda j: (0, 0)) for left in lefts] + [rhs_spec],
        out_specs=pl.BlockSpec((tile // WIDE, rows, WIDE), lambda j: (j, 0, 0))
        if tiled
        else pl.BlockSpec((rows, tile), lambda j: (0, j)),
        out_shape=jax.ShapeDtypeStruct((columns // WIDE, rows, WIDE) if tiled else (rows, columns), kind),
        compiler_params=params(),
        cost_estimate=cost(0.01),
        name="product",
    )(*lefts, rhs)


def scale_of(rows):
    return lax.rsqrt(jnp.mean(rows * rows, axis=-1, keepdims=True) + 1e-05)


def by_time(prompt_ref, piece_ref):
    both_kinds = jnp.concatenate([prompt_ref[...], piece_ref[...]], axis=0).astype(f32)
    return jnp.swapaxes(both_kinds, 0, 1)


def prepare_kernel(prompt_ref, piece_ref, prompt_cot_ref, piece_cot_ref, halo_ref, gain_ref, scaled_ref, cot_ref):
    i = pl.program_id(0)
    gain = gain_ref[...]

    @pl.when(i == 0)
    def _():
        rows = halo_ref[...]
        scaled_ref[0 : HALO * SEQS, :] = (rows * scale_of(rows) * gain).astype(bf16)

    rows = by_time(prompt_ref, piece_ref)
    count = rows.shape[0] * SEQS
    rows = rows.reshape(count, D)
    at = pl.multiple_of(HALO * SEQS + i * count, HALO * SEQS)
    scaled_ref[pl.ds(at, count), :] = (rows * scale_of(rows) * gain).astype(bf16)
    cot_ref[...] = by_time(prompt_cot_ref, piece_cot_ref).reshape(count, D).astype(bf16)


CHUNK = 32
PREPARE_CHUNK = 32


def prepare(prompt, piece, prompt_cot, piece_cot, halo, gain):
    steps = prompt.shape[1]
    part = pl.BlockSpec((SEQS // 2, PREPARE_CHUNK, D), lambda i: (0, i, 0))
    rows = steps * SEQS
    return pl.pallas_call(
        prepare_kernel,
        grid=(steps // PREPARE_CHUNK,),
        in_specs=[
            part, part, part, part,
            pl.BlockSpec((HALO * SEQS, D), lambda i: (0, 0)),
            pl.BlockSpec((1, D), lambda i: (0, 0)),
        ],
        out_specs=[
            pl.BlockSpec((HALO * SEQS + rows, D), lambda i: (0, 0)),
            pl.BlockSpec((PREPARE_CHUNK * SEQS, D), lambda i: (i, 0)),
        ],
        out_shape=[
            jax.ShapeDtypeStruct((HALO * SEQS + rows, D), bf16),
            jax.ShapeDtypeStruct((rows, D), bf16),
        ],
        compiler_params=params(),
        cost_estimate=cost(5),
        name="prepare",
    )(prompt, piece, prompt_cot, piece_cot, halo, gain)


def norm_back(rows, scaled_grad, gain):
    inverse = scale_of(rows)
    unit = rows * inverse
    grad = scaled_grad * gain
    back = inverse * (grad - unit * jnp.mean(grad * unit, axis=-1, keepdims=True))
    return back, scaled_grad * unit


def finish_kernel(
    mixed_ref, grad_ref, grad_halo_ref,
    prompt_ref, piece_ref, prompt_cot_ref, piece_cot_ref, halo_ref, gain_ref,
    prompt_out, piece_out, prompt_grad, piece_grad, halo_grad, gain_grad,
):
    i = pl.program_id(0)
    gain = gain_ref[...]

    @pl.when(i == 0)
    def _():
        back, sums = norm_back(halo_ref[...], grad_halo_ref[...], gain)
        halo_grad[...] = back
        gain_grad[...] = jnp.sum(sums, axis=0, keepdims=True)

    half = SEQS // 2
    rows = by_time(prompt_ref, piece_ref)
    shape = rows.shape
    rows = rows.reshape(-1, D)
    back, sums = norm_back(rows, grad_ref[...], gain)
    gain_grad[...] += jnp.sum(sums, axis=0, keepdims=True)
    back = jnp.swapaxes(back.reshape(shape), 0, 1)
    prompt_grad[...] = back[:half] + prompt_cot_ref[...].astype(f32)
    piece_grad[...] = back[half:] + piece_cot_ref[...].astype(f32)
    mixed = jnp.swapaxes((mixed_ref[...] + rows).reshape(shape), 0, 1)
    prompt_out[...] = mixed[:half].astype(bf16)
    piece_out[...] = mixed[half:].astype(bf16)


def finish(mixed, grad, prompt, piece, prompt_cot, piece_cot, halo, gain):
    steps = prompt.shape[1]
    part = pl.BlockSpec((SEQS // 2, CHUNK, D), lambda i: (0, i, 0))
    first = pl.BlockSpec((HALO * SEQS, D), lambda i: (0, 0))
    shifted = pl.BlockSpec(
        (pl.Element(CHUNK * SEQS), pl.Element(D)),
        lambda i: (pl.multiple_of(HALO * SEQS + i * (CHUNK * SEQS), HALO * SEQS), 0),
    )
    return pl.pallas_call(
        finish_kernel,
        grid=(steps // CHUNK,),
        in_specs=[
            pl.BlockSpec((CHUNK * SEQS, D), lambda i: (i, 0)),
            shifted, first,
            part, part, part, part,
            first,
            pl.BlockSpec((1, D), lambda i: (0, 0)),
        ],
        out_specs=[part, part, part, part, first, pl.BlockSpec((1, D), lambda i: (0, 0))],
        out_shape=[
            jax.ShapeDtypeStruct(prompt.shape, bf16),
            jax.ShapeDtypeStruct(piece.shape, bf16),
            jax.ShapeDtypeStruct(prompt.shape, f32),
            jax.ShapeDtypeStruct(piece.shape, f32),
            jax.ShapeDtypeStruct((HALO * SEQS, D), f32),
            jax.ShapeDtypeStruct((1, D), f32),
        ],
        compiler_params=params(),
        cost_estimate=cost(0.01),
        name="finish",
    )(mixed, grad, grad, prompt, piece, prompt_cot, piece_cot, halo, gain)


def front_kernel(mix_ref, fw_ref, fb_ref, sel_ref, act_ref, bend_ref, proj_ref, low_scr):
    j = pl.program_id(0)
    steps = act_ref.shape[0]
    chunk = 16
    taps = [fw_ref[k : k + 1, :] for k in range(KERNEL)]
    bias = fb_ref[0:1, :]

    @pl.when(j == 0)
    def _():
        proj_ref[...] = jnp.zeros_like(proj_ref)

    def step(i, _):
        t = i * chunk
        x = mix_ref[pl.ds(t, chunk + HALO)].astype(f32)
        v = bias[None] + taps[0][None] * x[1 : 1 + chunk]
        for k in range(1, KERNEL):
            v = v + taps[k][None] * x[1 + k : 1 + k + chunk]
        sig = sigmoid(v)
        act = v * sig
        act_ref[pl.ds(t, chunk)] = act
        bend_ref[pl.ds(t, chunk)] = (sig + act * (1.0 - sig)).astype(bf16)
        r = pl.multiple_of(t * SEQS, chunk * SEQS)
        low_scr[pl.ds(r, chunk * SEQS), :] = act.reshape(chunk * SEQS, act.shape[-1]).astype(bf16)
        return 0

    lax.fori_loop(0, steps // chunk, step, 0)
    proj_ref[...] += jnp.dot(low_scr[...], sel_ref[...], preferred_element_type=f32)


def front(mixture, fw, fb, select_pad, steps):
    channels = fw.shape[1]
    return pl.pallas_call(
        front_kernel,
        grid=(channels // WIDE,),
        in_specs=[
            pl.BlockSpec((None, steps + HALO, SEQS, WIDE), lambda j: (j, 0, 0, 0)),
            pl.BlockSpec((KERNEL, WIDE), lambda j: (0, j)),
            pl.BlockSpec((1, WIDE), lambda j: (0, j)),
            pl.BlockSpec((WIDE, LANES), lambda j: (j, 0)),
        ],
        out_specs=[
            pl.BlockSpec((None, steps, SEQS, WIDE), lambda j: (j, 0, 0, 0)),
            pl.BlockSpec((None, steps, SEQS, WIDE), lambda j: (j, 0, 0, 0)),
            pl.BlockSpec((steps * SEQS, LANES), lambda j: (0, 0)),
        ],
        out_shape=[
            jax.ShapeDtypeStruct((channels // WIDE, steps, SEQS, WIDE), f32),
            jax.ShapeDtypeStruct((channels // WIDE, steps, SEQS, WIDE), bf16),
            jax.ShapeDtypeStruct((steps * SEQS, LANES), f32),
        ],
        scratch_shapes=[pltpu.VMEM((steps * SEQS, WIDE), bf16)],
        compiler_params=params(),
        cost_estimate=cost(16),
        name="front",
    )(mixture, fw, fb, select_pad)


def pair(a, b):
    return jnp.concatenate([a, b], axis=0).astype(bf16)


def both(v):
    return pair(v, v)


def halves(v):
    v = v.astype(f32)
    return v[:SEQS], v[SEQS:]


def folded(v):
    a, b = halves(v)
    return a + b


def spread_maps(proj_ref, select_ref, first, count, store):
    steps = proj_ref.shape[0] // SEQS
    chunk = 32

    def step(i, _):
        r = pl.multiple_of(i * chunk * SEQS, chunk * SEQS)
        rows = proj_ref[pl.ds(r, chunk * SEQS), :].astype(bf16)
        for n in range(0, count, 2):
            at = (first - RANK + n) * LANES
            wide = jnp.dot(rows, select_ref[:, at : at + 2 * LANES], preferred_element_type=f32)
            wide = wide.reshape(chunk, SEQS, 2 * LANES)
            store(i * chunk, chunk, n, wide[:, :, :LANES], wide[:, :, LANES:])
        return 0

    lax.fori_loop(0, steps // chunk, step, 0)


def store_plain(ref):
    def store(t, count, n, a, b):
        ref[pl.ds(t, count), n] = a
        ref[pl.ds(t, count), n + 1] = b

    return store


def store_pairs(ref):
    def store(t, count, n, a, b):
        ref[pl.ds(t, count), n // 2] = jnp.concatenate([a, b], axis=1).astype(bf16)

    return store


PAIRS = STATES // 2
RUN = 8


def piece_kernel(
    proj_ref, act_ref, gate_ref, gg_ref, stepw_ref, sbias_ref, rate_ref, select_ref,
    dt_ref, sig_ref, yg_ref, silu_ref, slope_ref, fwd_ref, bwd_ref, tot_ref,
    b_scr, c_scr, time_scr, acc_scr,
):
    j = pl.program_id(0)
    steps = dt_ref.shape[0]
    half = SEQS // 2
    groups = fwd_ref.shape[0] // half

    @pl.when(j == 0)
    def _():
        def store_groups(t, count, n, a, b):
            for group in range(groups):
                rows = slice(group * half, (group + 1) * half)
                parts = [a[:, rows], a[:, rows], b[:, rows], b[:, rows]]
                b_scr[group, pl.ds(t, count), n // 2] = jnp.concatenate(parts, axis=1).astype(bf16)

        spread_maps(proj_ref, select_ref, RANK, STATES, store_groups)
        spread_maps(proj_ref, select_ref, RANK + STATES, STATES, store_pairs(c_scr))

    chunk = 8
    sbias = sbias_ref[0:1, :]
    pre = jnp.dot(proj_ref[...].astype(bf16), stepw_ref[...], preferred_element_type=f32)
    time_scr[...] = pre.reshape(steps, SEQS, WIDE)

    def prep(i, total):
        t = i * chunk
        pre = time_scr[pl.ds(t, chunk)] + sbias[None]
        small = jnp.exp2(jnp.abs(pre) * -LOG2E)
        one = 1.0 + small
        inverse = 1.0 / one
        dt = jnp.maximum(pre, 0.0) + (jnp.log(one) + (small - (one - 1.0)) * inverse)
        dt_ref[pl.ds(t, chunk)] = dt
        sig_ref[pl.ds(t, chunk)] = jnp.where(pre >= 0.0, inverse, small * inverse).astype(bf16)
        gate = gate_ref[pl.ds(t + HALO, chunk)].astype(f32)
        gg = gg_ref[pl.ds(t, chunk)].astype(f32)
        sig = sigmoid(gate)
        silu = gate * sig
        yg_ref[pl.ds(t, chunk)] = gg * silu
        silu_ref[pl.ds(t, chunk)] = silu.astype(bf16)
        slope_ref[pl.ds(t, chunk)] = (gg * (sig + silu * (1.0 - sig))).astype(bf16)
        for k in range(chunk):
            total = total + dt[k]
            time_scr[t + k] = total
        return total

    total = lax.fori_loop(0, steps // chunk, prep, jnp.zeros((SEQS, WIDE), f32))
    tot_ref[...] = total

    units = []

    low = lax.broadcasted_iota(jnp.int32, (SEQS, LANES), 0) < half
    packed = [
        jnp.where(low, rate_ref[n : n + 1, :LANES], rate_ref[n : n + 1, LANES:])
        for n in range(STATES)
    ]
    packed = [pair(packed[2 * p], packed[2 * p + 1]) for p in range(PAIRS)]

    def forward_unit(group):
        rows = slice(group * half, (group + 1) * half)

        def pack(v):
            return jnp.concatenate([v[rows, :LANES], v[rows, LANES:]], axis=0)

        whole = pack(total)

        def vectors(t):
            return both(whole - pack(time_scr[t])), both(pack(dt_ref[t] * act_ref[t]))

        def out(n, value):
            fwd_ref[rows, n, :LANES] = value[:half]
            fwd_ref[rows, n, LANES:] = value[half:]

        return packed, vectors, lambda t, p: b_scr[group, t, p], out

    def backward_unit(cols):
        mine = [jnp.broadcast_to(rate_ref[n : n + 1, cols], (SEQS, LANES)) for n in range(STATES)]
        mine = [pair(mine[2 * p], mine[2 * p + 1]) for p in range(PAIRS)]

        def vectors(t):
            return both(time_scr[t, :, cols]), both(yg_ref[t, :, cols])

        def out(n, value):
            bwd_ref[:, n, cols] = value

        return mine, vectors, lambda t, p: c_scr[t, p], out

    for group in range(groups):
        units.append(forward_unit(group))
    for part in range(WIDE // LANES):
        units.append(backward_unit(slice(part * LANES, (part + 1) * LANES)))
    acc_scr[...] = jnp.zeros_like(acc_scr)

    def run(i, _):
        for k, (rates, vectors, map_at, _) in enumerate(units):
            sums = [None] * PAIRS
            for m in range(RUN):
                t = i * RUN + m
                time, drive = vectors(t)
                for p in range(PAIRS):
                    term = jnp.exp2(time * rates[p]) * drive * map_at(t, p)
                    sums[p] = term if m == 0 else sums[p] + term
            for p in range(PAIRS):
                a, b = halves(sums[p])
                acc_scr[k, 2 * p] += a
                acc_scr[k, 2 * p + 1] += b
        return 0

    lax.fori_loop(0, steps // RUN, run, 0)
    for k, (_, _, _, out) in enumerate(units):
        for n in range(STATES):
            out(n, acc_scr[k, n])


def piece(proj, act, gate, gated_grad, step_pad, sbias, rate, select, groups):
    grid, steps, _, _ = act.shape
    channels = grid * WIDE
    wide = lambda j: (0, 0, j)
    flat = pl.BlockSpec((None, steps, SEQS, WIDE), lambda j: (j, 0, 0, 0))
    shape = act.shape
    return pl.pallas_call(
        piece_kernel,
        grid=(grid,),
        in_specs=[
            pl.BlockSpec((steps * SEQS, LANES), lambda j: (0, 0)),
            flat,
            pl.BlockSpec((None, steps + HALO, SEQS, WIDE), lambda j: (j + grid, 0, 0, 0)),
            flat,
            pl.BlockSpec((LANES, WIDE), lambda j: (0, j)),
            pl.BlockSpec((1, WIDE), lambda j: (0, j)),
            pl.BlockSpec((STATES, WIDE), lambda j: (0, j)),
            pl.BlockSpec(select.shape, lambda j: (0, 0)),
        ],
        out_specs=[
            flat, flat, flat, flat, flat,
            pl.BlockSpec((groups * SEQS // 2, STATES, WIDE), wide),
            pl.BlockSpec((SEQS, STATES, WIDE), wide),
            pl.BlockSpec((SEQS, WIDE), lambda j: (0, j)),
        ],
        out_shape=[
            jax.ShapeDtypeStruct(shape, f32),
            jax.ShapeDtypeStruct(shape, bf16),
            jax.ShapeDtypeStruct(shape, f32),
            jax.ShapeDtypeStruct(shape, bf16),
            jax.ShapeDtypeStruct(shape, bf16),
            jax.ShapeDtypeStruct((groups * SEQS // 2, STATES, channels), f32),
            jax.ShapeDtypeStruct((SEQS, STATES, channels), f32),
            jax.ShapeDtypeStruct((SEQS, channels), f32),
        ],
        scratch_shapes=[
            pltpu.VMEM((groups, steps, PAIRS, 2 * SEQS, LANES), bf16),
            pltpu.VMEM((steps, PAIRS, 2 * SEQS, LANES), bf16),
            pltpu.VMEM((steps, SEQS, WIDE), f32),
            pltpu.VMEM((groups + WIDE // LANES, STATES, SEQS, LANES), f32),
        ],
        compiler_params=params(),
        cost_estimate=cost(60),
        name="piece",
    )(proj, act, gate, gated_grad, step_pad, sbias, rate, select)


def chain_kernel(
    one_hot_ref, ahead_ref, behind_ref, time_ref, rate_ref, start_out, end_out,
    moved_ref, got, got_time, back, done, sems, time_sems, back_sems,
):
    size = got.shape[0]
    width = got.shape[2]
    count = PROMPTS * STATES
    sequels = one_hot_ref.shape[0]
    me = lax.axis_index("fsdp")
    for p in range(PROMPTS):
        rows = slice(p * STATES, (p + 1) * STATES)
        total = one_hot_ref[0, p] * behind_ref[PROMPTS]
        for k in range(1, sequels):
            total = total + one_hot_ref[k, p] * behind_ref[PROMPTS + k]
        moved_ref[0 * count + p * STATES : 0 * count + (p + 1) * STATES] = ahead_ref[p].astype(bf16)
        moved_ref[1 * count + p * STATES : 1 * count + (p + 1) * STATES] = behind_ref[p].astype(bf16)
        moved_ref[2 * count + p * STATES : 2 * count + (p + 1) * STATES] = total.astype(bf16)
    barrier = pltpu.get_barrier_semaphore()
    for d in range(1, size):
        peer = lax.rem(me + d, size)
        pl.semaphore_signal(barrier, inc=1, device_id={"fsdp": peer}, device_id_type=pl.DeviceIdType.MESH)
    pl.semaphore_wait(barrier, size - 1)

    def columns(device):
        return pl.ds(pl.multiple_of(device * width, width), width)

    copies = []
    for d in range(1, size):
        peer = lax.rem(me + d, size)
        for src, dst, sem in ((moved_ref, got, sems), (time_ref, got_time, time_sems)):
            copy = pltpu.make_async_remote_copy(
                src_ref=src.at[:, columns(peer)],
                dst_ref=dst.at[me],
                send_sem=sem.at[0, d],
                recv_sem=sem.at[1, d],
                device_id={"fsdp": peer},
                device_id_type=pl.DeviceIdType.MESH,
            )
            copy.start()
            copies.append(copy)
    got[me] = moved_ref[:, columns(me)]
    got_time[me] = time_ref[:, columns(me)]
    for copy in copies:
        copy.wait()

    rate = jnp.concatenate([rate_ref[...]] * PROMPTS, axis=0)
    branch = jnp.zeros((count, width), f32)
    state = jnp.zeros((count, width), f32)
    decays = []
    for k in range(size):
        time = jnp.concatenate(
            [jnp.broadcast_to(got_time[k, p : p + 1, :], (STATES, width)) for p in range(PROMPTS)], axis=0
        )
        decays.append(jnp.exp2(rate * time))
        back[k, 0:count] = state.astype(bf16)
        state = decays[k] * state + got[k, 0:count].astype(f32)
        branch = branch + got[k, 2 * count : 3 * count].astype(f32)
    grad = branch
    for k in range(size - 1, -1, -1):
        back[k, count : 2 * count] = grad.astype(bf16)
        grad = decays[k] * grad + got[k, count : 2 * count].astype(f32)
    last = state.astype(bf16)
    for k in range(size):
        back[k, 2 * count : 3 * count] = last
    copies = []
    for d in range(1, size):
        peer = lax.rem(me + d, size)
        copy = pltpu.make_async_remote_copy(
            src_ref=back.at[peer],
            dst_ref=done.at[me],
            send_sem=back_sems.at[0, d],
            recv_sem=back_sems.at[1, d],
            device_id={"fsdp": peer},
            device_id_type=pl.DeviceIdType.MESH,
        )
        copy.start()
        copies.append(copy)
    done[me] = back[me]
    for copy in copies:
        copy.wait()
    for k in range(size):
        columns_k = slice(k * width, (k + 1) * width)
        last = []
        for p in range(PROMPTS):
            rows = slice(p * STATES, (p + 1) * STATES)
            start_out[p, :, columns_k] = done[k, rows].astype(f32)
            rows = slice(count + p * STATES, count + (p + 1) * STATES)
            end_out[p, :, columns_k] = done[k, rows].astype(f32)
            rows = slice(2 * count + p * STATES, 2 * count + (p + 1) * STATES)
            last.append(done[k, rows].astype(f32))
        for q in range(sequels):
            total = one_hot_ref[q, 0] * last[0]
            for p in range(1, PROMPTS):
                total = total + one_hot_ref[q, p] * last[p]
            start_out[PROMPTS + q, :, columns_k] = total
            end_out[PROMPTS + q, :, columns_k] = jnp.zeros_like(total)


def chain(one_hot, ahead, behind, time, rate):
    size = lax.axis_size("fsdp")
    channels = ahead.shape[2]
    rows = 3 * PROMPTS * STATES
    width = channels // size
    own = lax.dynamic_slice_in_dim(rate, lax.axis_index("fsdp") * width, width, 1)
    whole = pl.BlockSpec(memory_space=pltpu.VMEM)
    shape = (PROMPTS + one_hot.shape[0], STATES, channels)
    return pl.pallas_call(
        chain_kernel,
        in_specs=[pl.BlockSpec(memory_space=pltpu.SMEM)] + [whole] * 4,
        out_specs=[whole] * 2,
        out_shape=[jax.ShapeDtypeStruct(shape, f32)] * 2,
        scratch_shapes=[
            pltpu.VMEM((rows, channels), bf16),
            pltpu.VMEM((size, rows, width), bf16),
            pltpu.VMEM((size, SEQS, width), f32),
            pltpu.VMEM((size, rows, width), bf16),
            pltpu.VMEM((size, rows, width), bf16),
            pltpu.SemaphoreType.DMA((2, size)),
            pltpu.SemaphoreType.DMA((2, size)),
            pltpu.SemaphoreType.DMA((2, size)),
        ],
        compiler_params=params(collective_id=1, has_side_effects=True),
        cost_estimate=cost(25),
        name="chain",
    )(one_hot, ahead, behind, time, own)


TILES = [slice(k * LANES, (k + 1) * LANES) for k in range(WIDE // LANES)]


def forward_kernel(
    proj_ref, dt_ref, act_ref, yg_ref, silu_ref, slope_ref, rate_ref, start_ref, skip_ref, select_ref,
    gated_ref, hist_ref, gategrad_ref, skipg_ref,
    b_scr, c_scr,
):
    j = pl.program_id(0)
    steps = dt_ref.shape[0]

    @pl.when(j == 0)
    def _():
        spread_maps(proj_ref, select_ref, RANK, STATES, store_plain(b_scr))
        spread_maps(proj_ref, select_ref, RANK + STATES, STATES, store_pairs(c_scr))

    gategrad_ref[0:HALO] = jnp.zeros((HALO, SEQS, WIDE), bf16)
    unroll = 8

    for part, cols in enumerate(TILES):
        rates = [jnp.broadcast_to(rate_ref[n : n + 1, cols], (SEQS, LANES)) for n in range(STATES)]
        skip = jnp.broadcast_to(skip_ref[0:1, cols], (SEQS, LANES))

        def run(i, carry):
            h, skip_sum = carry
            for k in range(unroll):
                t = i * unroll + k
                dt = dt_ref[t, :, cols]
                act = act_ref[t, :, cols]
                u = dt * act
                new = []
                y = None
                for p in range(PAIRS):
                    for n in (2 * p, 2 * p + 1):
                        new.append(jnp.exp2(dt * rates[n]) * h[n] + u * b_scr[t, n])
                    low = pair(new[2 * p], new[2 * p + 1])
                    hist_ref[part, t + 1, p] = low
                    term = low * c_scr[t, p]
                    y = term if p == 0 else y + term
                h = tuple(new)
                mixed = folded(y) + skip * act
                gated_ref[t, :, cols] = (mixed * silu_ref[t, :, cols].astype(f32)).astype(bf16)
                gategrad_ref[t + HALO, :, cols] = (mixed * slope_ref[t, :, cols].astype(f32)).astype(bf16)
                skip_sum = skip_sum + yg_ref[t, :, cols] * act
            return h, skip_sum

        start = tuple(start_ref[:, n, cols] for n in range(STATES))
        for p in range(PAIRS):
            hist_ref[part, 0, p] = pair(start[2 * p], start[2 * p + 1])
        _, skip_sum = lax.fori_loop(0, steps // unroll, run, (start, jnp.zeros((SEQS, LANES), f32)))
        skipg_ref[:, cols] = jnp.sum(skip_sum, axis=0, keepdims=True)


def forward(proj, dt, act, yg, silu, slope, rate, start, skip, select):
    grid, steps, _, _ = act.shape
    channels = grid * WIDE
    tile = lambda j: (0, 0, j)
    flat = pl.BlockSpec((None, steps, SEQS, WIDE), lambda j: (j, 0, 0, 0))
    parts = len(TILES)
    return pl.pallas_call(
        forward_kernel,
        grid=(grid,),
        in_specs=[
            pl.BlockSpec((steps * SEQS, LANES), lambda j: (0, 0)),
            flat, flat, flat, flat, flat,
            pl.BlockSpec((STATES, WIDE), lambda j: (0, j)),
            pl.BlockSpec((SEQS, STATES, WIDE), tile),
            pl.BlockSpec((1, WIDE), lambda j: (0, j)),
            pl.BlockSpec(select.shape, lambda j: (0, 0)),
        ],
        out_specs=[
            pl.BlockSpec((steps, SEQS, WIDE), tile),
            pl.BlockSpec((None, parts, steps + 1, PAIRS, 2 * SEQS, LANES), lambda j: (j, 0, 0, 0, 0, 0)),
            pl.BlockSpec((steps + HALO, SEQS, WIDE), tile),
            pl.BlockSpec((1, WIDE), lambda j: (0, j)),
        ],
        out_shape=[
            jax.ShapeDtypeStruct((steps, SEQS, channels), bf16),
            jax.ShapeDtypeStruct((grid, parts, steps + 1, PAIRS, 2 * SEQS, LANES), bf16),
            jax.ShapeDtypeStruct((steps + HALO, SEQS, channels), bf16),
            jax.ShapeDtypeStruct((1, channels), f32),
        ],
        scratch_shapes=[
            pltpu.VMEM((steps, STATES, SEQS, LANES), f32),
            pltpu.VMEM((steps, PAIRS, 2 * SEQS, LANES), bf16),
        ],
        compiler_params=params(),
        cost_estimate=cost(50),
        name="forward_scan",
    )(proj, dt, act, yg, silu, slope, rate, start, skip, select)


def backward_kernel(
    proj_ref, dt_ref, sig_ref, act_ref, yg_ref, rate_ref, end_ref, skip_ref,
    hist_ref, rank_t_ref, stepw_t_ref, pick_ref, select_ref,
    act_grad_ref, stepg_ref, biasg_ref, decayg_ref, projg_ref,
    b_scr, c_scr, db_scr, dc_scr, pre_scr, acc_scr, decay_scr, ge_scr, sum_scr,
):
    j = pl.program_id(0)
    steps = dt_ref.shape[0]

    @pl.when(j == 0)
    def _():
        spread_maps(proj_ref, select_ref, RANK, STATES, store_pairs(b_scr))
        spread_maps(proj_ref, select_ref, RANK + STATES, STATES, store_plain(c_scr))

        def clear(t, _):
            for p in range(PAIRS):
                db_scr[t, p] = jnp.zeros((2 * SEQS, LANES), bf16)
                dc_scr[t, p] = jnp.zeros((2 * SEQS, LANES), bf16)
            return 0

        lax.fori_loop(0, steps, clear, 0)
        acc_scr[...] = jnp.zeros_like(acc_scr)

    decay_scr[...] = jnp.zeros_like(decay_scr)
    sum_scr[...] = jnp.zeros_like(sum_scr)
    for n in range(STATES):
        ge_scr[n] = end_ref[:, n, :]

    def run(i, _):
        base = steps - (i + 1) * RUN
        db = [[None] * PAIRS for _ in range(RUN)]
        dc = [[None] * PAIRS for _ in range(RUN)]
        for part, cols in enumerate(TILES):
            rates = [jnp.broadcast_to(rate_ref[n : n + 1, cols], (SEQS, LANES)) for n in range(STATES)]
            low_rates = [pair(rates[2 * p], rates[2 * p + 1]) for p in range(PAIRS)]
            skip = jnp.broadcast_to(skip_ref[0:1, cols], (SEQS, LANES))
            ge = [ge_scr[n, :, cols] for n in range(STATES)]
            bias_sum = jnp.zeros((SEQS, LANES), f32)
            decay = [None] * PAIRS
            for k in range(RUN - 1, -1, -1):
                t = base + k
                dt = dt_ref[t, :, cols]
                act = act_ref[t, :, cols]
                yg = yg_ref[t, :, cols]
                u2 = both(dt * act)
                dt2 = both(dt)
                yg2 = both(yg)
                du = None
                ddt = None
                for p in range(PAIRS):
                    g = [ge[n] + yg * c_scr[t, n] for n in (2 * p, 2 * p + 1)]
                    g2 = pair(*g)
                    term = yg2 * hist_ref[part, t + 1, p]
                    dc[k][p] = term if part == 0 else dc[k][p] + term
                    term = g2 * u2
                    db[k][p] = term if part == 0 else db[k][p] + term
                    term = g2 * b_scr[t, p]
                    du = term if p == 0 else du + term
                    gn = [jnp.exp2(dt * rates[2 * p + m]) * g[m] for m in (0, 1)]
                    ge[2 * p], ge[2 * p + 1] = gn
                    q = pair(*gn) * hist_ref[part, t, p]
                    term = q * dt2
                    decay[p] = term if decay[p] is None else decay[p] + term
                    term = q * low_rates[p]
                    ddt = term if p == 0 else ddt + term
                du = folded(du)
                pre_grad = (du * act + folded(ddt) * LN2) * sig_ref[t, :, cols].astype(f32)
                pre_scr[t, :, cols] = pre_grad.astype(bf16)
                act_grad_ref[t, :, cols] = yg * skip + du * dt
                bias_sum = bias_sum + pre_grad
                if part == len(TILES) - 1:
                    for p in range(PAIRS):
                        dc_scr[t, p] = dc[k][p] + dc_scr[t, p]
                        db_scr[t, p] = db[k][p] + db_scr[t, p]
            for p in range(PAIRS):
                a, b = halves(decay[p])
                decay_scr[2 * p, :, cols] += a
                decay_scr[2 * p + 1, :, cols] += b
            for n in range(STATES):
                ge_scr[n, :, cols] = ge[n]
            sum_scr[:, cols] += bias_sum
        return 0

    lax.fori_loop(0, steps // RUN, run, 0)
    for n in range(STATES):
        decayg_ref[n : n + 1, :] = jnp.sum(decay_scr[n] * rate_ref[n : n + 1, :], axis=0, keepdims=True) * LN2
    biasg_ref[...] = jnp.sum(sum_scr[...], axis=0, keepdims=True)

    pre_low = pre_scr[...].reshape(steps * SEQS, WIDE)
    stepg_ref[...] = jnp.dot(rank_t_ref[...], pre_low, preferred_element_type=f32)
    acc_scr[...] += jnp.dot(pre_low, stepw_t_ref[...], preferred_element_type=f32)

    @pl.when(j == pl.num_programs(0) - 1)
    def _():
        chunk = 32
        even = lax.broadcasted_iota(jnp.int32, (chunk, SEQS, LANES), 2) % 2 == 0

        def step(i, _):
            t = i * chunk
            total = jnp.zeros((chunk * 2 * SEQS, LANES), f32)
            for p in range(PAIRS):
                rows = jnp.concatenate([db_scr[pl.ds(t, chunk), p], dc_scr[pl.ds(t, chunk), p]], axis=2)
                rows = rows.reshape(chunk * 2 * SEQS, 2 * LANES)
                total = total + jnp.dot(rows, pick_ref[p], preferred_element_type=f32)
            total = total.reshape(chunk, 2 * SEQS, LANES)
            total = jnp.where(even, total[:, :SEQS], total[:, SEQS:]).reshape(chunk * SEQS, LANES)
            r = pl.multiple_of(t * SEQS, chunk * SEQS)
            projg_ref[pl.ds(r, chunk * SEQS), :] = (acc_scr[pl.ds(r, chunk * SEQS), :] + total).astype(bf16)
            return 0

        lax.fori_loop(0, steps // chunk, step, 0)


def backward(proj, dt, sig, act, yg, rate, end, skip, hist, rank_t, stepw_t, pick, select):
    grid, steps, _, _ = act.shape
    channels = grid * WIDE
    tile = lambda j: (0, 0, j)
    whole = lambda j: (0, 0)
    flat = pl.BlockSpec((None, steps, SEQS, WIDE), lambda j: (j, 0, 0, 0))
    sums = pltpu.VMEM((steps, PAIRS, 2 * SEQS, LANES), bf16)
    return pl.pallas_call(
        backward_kernel,
        grid=(grid,),
        in_specs=[
            pl.BlockSpec((steps * SEQS, LANES), whole),
            flat, flat, flat, flat,
            pl.BlockSpec((STATES, WIDE), lambda j: (0, j)),
            pl.BlockSpec((SEQS, STATES, WIDE), tile),
            pl.BlockSpec((1, WIDE), lambda j: (0, j)),
            pl.BlockSpec(
                (None, len(TILES), steps + 1, PAIRS, 2 * SEQS, LANES), lambda j: (j, 0, 0, 0, 0, 0)
            ),
            pl.BlockSpec((RANK, steps * SEQS), whole),
            pl.BlockSpec((WIDE, LANES), lambda j: (j, 0)),
            pl.BlockSpec(pick.shape, lambda j: (0, 0, 0)),
            pl.BlockSpec(select.shape, whole),
        ],
        out_specs=[
            flat,
            pl.BlockSpec((RANK, WIDE), lambda j: (0, j)),
            pl.BlockSpec((1, WIDE), lambda j: (0, j)),
            pl.BlockSpec((STATES, WIDE), lambda j: (0, j)),
            pl.BlockSpec((steps * SEQS, LANES), whole),
        ],
        out_shape=[
            jax.ShapeDtypeStruct(act.shape, f32),
            jax.ShapeDtypeStruct((RANK, channels), f32),
            jax.ShapeDtypeStruct((1, channels), f32),
            jax.ShapeDtypeStruct((STATES, channels), f32),
            jax.ShapeDtypeStruct((steps * SEQS, LANES), bf16),
        ],
        scratch_shapes=[
            sums,
            pltpu.VMEM((steps, STATES, SEQS, LANES), f32),
            sums, sums,
            pltpu.VMEM((steps, SEQS, WIDE), bf16),
            pltpu.VMEM((steps * SEQS, LANES), f32),
            pltpu.VMEM((STATES, SEQS, WIDE), f32),
            pltpu.VMEM((STATES, SEQS, WIDE), f32),
            pltpu.VMEM((SEQS, WIDE), f32),
        ],
        compiler_params=params(),
        cost_estimate=cost(90),
        name="backward_scan",
    )(proj, dt, sig, act, yg, rate, end, skip, hist, rank_t, stepw_t, pick, select)


def filter_back_kernel(
    mix_ref, act_ref, bend_ref, act_grad_ref, projg_ref, projg_t_ref, sel_ref, fw_ref,
    mixgrad_ref, selg_ref, fwg_ref, fbg_ref,
    dv_scr, more_scr,
):
    steps = act_ref.shape[0]
    chunk = 16
    taps = [fw_ref[k : k + 1, :] for k in range(KERNEL)]
    zero = jnp.zeros((HALO, SEQS, WIDE), f32)
    dv_scr[0:HALO] = zero
    dv_scr[steps + HALO :] = zero

    more = contract_cols(projg_ref[...], sel_ref[...])
    more_scr[...] = more.reshape(steps, SEQS, WIDE)

    def step(i, sums):
        t = i * chunk
        x = mix_ref[pl.ds(t, chunk + HALO)].astype(f32)
        total = act_grad_ref[pl.ds(t, chunk)] + more_scr[pl.ds(t, chunk)]
        dv = total * bend_ref[pl.ds(t, chunk)].astype(f32)
        dv_scr[pl.ds(t + HALO, chunk)] = dv
        new = [sums[0] + jnp.sum(dv, axis=0)]
        for k in range(KERNEL):
            new.append(sums[1 + k] + jnp.sum(dv * x[1 + k : 1 + k + chunk], axis=0))
        return tuple(new)

    sums = lax.fori_loop(
        0, steps // chunk, step, tuple(jnp.zeros((SEQS, WIDE), f32) for _ in range(KERNEL + 1))
    )
    fbg_ref[...] = jnp.sum(sums[0], axis=0, keepdims=True)
    for k in range(KERNEL):
        fwg_ref[k : k + 1, :] = jnp.sum(sums[1 + k], axis=0, keepdims=True)

    def spread(t, count):
        dv = dv_scr[pl.ds(t, count + HALO)]
        out = taps[KERNEL - 1][None] * dv[0:count]
        for k in range(KERNEL - 1):
            s = KERNEL - 1 - k
            out = out + taps[k][None] * dv[s : s + count]
        mixgrad_ref[pl.ds(t, count)] = out.astype(bf16)

    def out_step(i, _):
        spread(i * chunk, chunk)
        return 0

    lax.fori_loop(0, steps // chunk, out_step, 0)
    spread(steps, HALO)
    low = act_ref[...].reshape(steps * SEQS, WIDE).astype(bf16)
    selg_ref[...] = jnp.dot(projg_t_ref[...], low, preferred_element_type=f32)


def filter_back(mixture, act, bend, act_grad, projg, projg_t, select_pad, fw):
    grid, steps, _, _ = act.shape
    channels = grid * WIDE
    wide = lambda j: (0, 0, j)
    whole = lambda j: (0, 0)
    cols = lambda j: (0, j)
    return pl.pallas_call(
        filter_back_kernel,
        grid=(grid,),
        in_specs=[
            pl.BlockSpec((None, steps + HALO, SEQS, WIDE), lambda j: (j, 0, 0, 0)),
            pl.BlockSpec((None, steps, SEQS, WIDE), lambda j: (j, 0, 0, 0)),
            pl.BlockSpec((None, steps, SEQS, WIDE), lambda j: (j, 0, 0, 0)),
            pl.BlockSpec((None, steps, SEQS, WIDE), lambda j: (j, 0, 0, 0)),
            pl.BlockSpec((steps * SEQS, LANES), whole),
            pl.BlockSpec((LANES, steps * SEQS), whole),
            pl.BlockSpec((WIDE, LANES), lambda j: (j, 0)),
            pl.BlockSpec((KERNEL, WIDE), cols),
        ],
        out_specs=[
            pl.BlockSpec((steps + HALO, SEQS, WIDE), wide),
            pl.BlockSpec((LANES, WIDE), cols),
            pl.BlockSpec((KERNEL, WIDE), cols),
            pl.BlockSpec((1, WIDE), cols),
        ],
        out_shape=[
            jax.ShapeDtypeStruct((steps + HALO, SEQS, channels), bf16),
            jax.ShapeDtypeStruct((LANES, channels), f32),
            jax.ShapeDtypeStruct((KERNEL, channels), f32),
            jax.ShapeDtypeStruct((1, channels), f32),
        ],
        scratch_shapes=[
            pltpu.VMEM((steps + 2 * HALO, SEQS, WIDE), f32),
            pltpu.VMEM((steps, SEQS, WIDE), f32),
        ],
        compiler_params=params(),
        cost_estimate=cost(20),
        name="filter_back",
    )(mixture, act, bend, act_grad, projg, projg_t, select_pad, fw)


def send(src, dst, send_sem, recv_sem, peer, axis="fsdp"):
    return pltpu.make_async_remote_copy(
        src_ref=src,
        dst_ref=dst,
        send_sem=send_sem,
        recv_sem=recv_sem,
        device_id={axis: peer},
        device_id_type=pl.DeviceIdType.MESH,
    )


def greet(others):
    barrier = pltpu.get_barrier_semaphore()
    for axis, peer in others:
        pl.semaphore_signal(barrier, inc=1, device_id={axis: peer}, device_id_type=pl.DeviceIdType.MESH)
    pl.semaphore_wait(barrier, len(others))


def flipped(index, bit):
    return index + (1 - 2 * (index // bit % 2)) * bit


FIRST, SECOND = (0, 1, 2, 3), (4, 5)
TRADED = (2, 3, 4, 5)


def gather_kernel(
    rows_ref, select_ref, out_ref, in_ref, all_rows, all_select, all_out, all_in,
    local_sems, own_send, own_recv, pass_send, pass_recv, core_send, core_recv, trade_send, trade_recv,
):
    me = lax.axis_index("fsdp")
    mz = lax.axis_index("replica")
    a, b = flipped(me, 2), flipped(me, 4)
    corner = flipped(a, 4)
    twin = flipped(me, 1)
    mate = flipped(mz, 1)
    greet([("fsdp", a), ("fsdp", b), ("fsdp", twin), ("replica", mate)])
    kinds = ((rows_ref, all_rows), (select_ref, all_select), (out_ref, all_out), (in_ref, all_in))

    def span(piece, side):
        if piece < 2:
            return piece, 0, kinds[piece][0].shape[0]
        kind = 2 + piece % 2
        quarter = kinds[kind][0].shape[0] // 4
        return kind, side * (2 * quarter) + (quarter if piece in SECOND else 0), quarter

    def place(owner, piece, side):
        kind, start, count = span(piece, side)
        first = owner * kinds[kind][0].shape[0] + start
        return kinds[kind][1].at[pl.ds(pl.multiple_of(first, 16), count)]

    def mine(piece, side):
        kind, start, count = span(piece, side)
        return kinds[kind][0].at[pl.ds(pl.multiple_of(start, 16), count) if piece in TRADED else pl.ds(0, count)]

    side = mz % 2
    other = 1 - side
    started = []

    def start(copy):
        copy.start()
        started.append(copy)

    def own_copy(piece, k, peer, owner):
        return send(mine(piece, side), place(owner, piece, side), own_send.at[k, piece], own_recv.at[k, piece], peer)

    def pass_copy(piece, peer, owner, far=False):
        ref = place(owner, piece, other if far else side)
        at = piece + len(FIRST + SECOND) * far
        return send(ref, ref, pass_send.at[at], pass_recv.at[at], peer)

    def trade_copy(piece, k, owner, whose):
        ref = place(owner, piece, whose)
        return send(ref, ref, trade_send.at[k, piece], trade_recv.at[k, piece], mate, "replica")

    def core_copy(piece, k, owner, whose=None):
        if whose is None:
            return send(
                place(owner, piece, side), place(owner, piece, side), core_send.at[k, piece], core_recv.at[k, piece], twin
            )
        at = len(FIRST + SECOND) + piece
        ref = place(owner, piece, whose)
        return send(ref, ref, core_send.at[k, at], core_recv.at[k, at], twin)

    def whole_copy(kind, owner):
        src, dst = kinds[kind]
        count = src.shape[0]
        rows = dst.at[pl.ds(pl.multiple_of(owner * count, count), count)]
        return send(src, rows, core_send.at[3, kind], core_recv.at[3, kind], twin)

    for piece in FIRST + SECOND:
        start(own_copy(piece, 0, a, me))
    for piece in SECOND + (2, 3, 0, 1):
        start(own_copy(piece, 1, b, me))
    local = []
    for kind, (src, dst) in enumerate(kinds):
        start(whole_copy(kind, me))
        count = src.shape[0]
        rows = dst.at[pl.ds(pl.multiple_of(me * count, count), count)]
        copy = pltpu.make_async_copy(src, rows, local_sems.at[kind])
        copy.start()
        local.append(copy)
    owners = (a, b, corner)

    def arrived(piece, k):
        owner = owners[k]
        if k == 2:
            pass_copy(piece, a, owner).wait_recv()
        else:
            own_copy(piece, k, a, owner).wait_recv()
            if k == 0 and piece in FIRST:
                start(pass_copy(piece, b, owner))
            if k == 1 and piece in SECOND:
                start(pass_copy(piece, a, owner))
        if piece in TRADED and k < 2:
            start(trade_copy(piece, k, owner, side))
        start(core_copy(piece, k, owner))

    def traded(piece, k):
        owner = owners[k]
        trade_copy(piece, k, owner, other).wait_recv()
        if k == 0 and piece in FIRST:
            start(pass_copy(piece, b, owner, True))
        if k == 1 and piece in SECOND:
            start(pass_copy(piece, a, owner, True))
        start(core_copy(piece, k, owner, other))

    for piece, k in ((0, 0), (4, 1), (1, 0), (2, 0), (5, 1), (3, 0)):
        arrived(piece, k)
    traded(2, 0)
    traded(4, 1)
    arrived(4, 0)
    arrived(2, 1)
    traded(3, 0)
    traded(5, 1)
    for piece, k in ((5, 0), (3, 1), (0, 1), (1, 1), (0, 2), (1, 2), (2, 2), (4, 2), (3, 2), (5, 2)):
        arrived(piece, k)
    for piece, k in ((4, 0), (2, 1), (5, 0), (3, 1)):
        traded(piece, k)
    for piece in (2, 4, 3, 5):
        pass_copy(piece, a, corner, True).wait_recv()
        start(core_copy(piece, 2, corner, other))
    for kind in range(len(kinds)):
        whole_copy(kind, twin).wait_recv()
    for k, owner in enumerate((flipped(twin, 2), flipped(twin, 4), flipped(corner, 1))):
        for piece in FIRST + SECOND:
            core_copy(piece, k, owner).wait_recv()
        for piece in TRADED:
            core_copy(piece, k, owner, other).wait_recv()
    for copy in started:
        copy.wait_send()
    for copy in local:
        copy.wait()


def gather(*shards):
    size = lax.axis_size("fsdp")
    if size != 8 or lax.axis_size("replica") % 2:
        return [lax.all_gather(shard, "fsdp", axis=0, tiled=True) for shard in shards]
    vmem = pl.BlockSpec(memory_space=pltpu.VMEM)
    hbm = pl.BlockSpec(memory_space=pl.ANY)
    pieces = len(FIRST + SECOND)
    dma = pltpu.SemaphoreType.DMA
    return pl.pallas_call(
        gather_kernel,
        in_specs=[vmem] * 4,
        out_specs=[hbm] * 4,
        out_shape=[jax.ShapeDtypeStruct((size * shard.shape[0], shard.shape[1]), bf16) for shard in shards],
        scratch_shapes=[
            dma((len(shards),)), dma((2, pieces)), dma((2, pieces)), dma((2 * pieces,)), dma((2 * pieces,)),
            dma((4, 2 * pieces)), dma((4, 2 * pieces)), dma((3, pieces)), dma((3, pieces)),
        ],
        compiler_params=params(collective_id=2, has_side_effects=True),
        cost_estimate=cost(55),
        name="gather",
    )(*shards)


SMALL = (KERNEL, 1, 1, 1, STATES, RANK, RANK + 2 * STATES, 1)
SMALL_ROWS = 192


def xor(index, bits):
    for bit in (1, 2, 4, 8):
        if bits & bit:
            index = flipped(index, bit)
    return index


def tail_kernel(
    one_hot_ref, b0, b1, b2, b3, filter_ref, fbias_ref, sbias_ref, skip_ref, decay_ref, step_ref, select_ref,
    gain_ref, halo_ref, block_out, small_out, rim_out,
    total, to_z, from_z, part, parts, small_f, small_ref, got_small, small_z, small_from_z, small_part,
    small_parts, rim, child, got_rim, got_child,
    sems_s, sems_z, sems_p, sems_sz, sems_sp, sems_r, sems_cs, sems_cr,
):
    depth = lax.axis_size("replica")
    me, size = lax.axis_index("fsdp"), lax.axis_size("fsdp")
    mz = lax.axis_index("replica")
    last = size - 1
    near = [lax.rem(me + d, size) for d in range(1, size)]
    far = [lax.rem(mz + d, depth) for d in range(1, depth)]
    greet([("fsdp", peer) for peer in near] + [("replica", peer) for peer in far])

    def spread(src, dst, sems, peers, axis, index):
        copies = []
        for d, peer in enumerate(peers):
            source = src.at[peer] if src.shape[0] == len(peers) + 1 and len(src.shape) == len(dst.shape) else src
            copy = send(source, dst.at[index], sems.at[0, d], sems.at[1, d], peer, axis)
            copy.start()
            copies.append(copy)
        return copies

    width = small_f.shape[2]
    small_f[...] = jnp.zeros_like(small_f)
    refs = (filter_ref, fbias_ref, sbias_ref, skip_ref, decay_ref, step_ref, select_ref)
    for k in range(size):
        at = 0
        for ref, count in zip(refs, SMALL):
            small_f[k, at : at + count] = ref[0:count, k * width : (k + 1) * width]
            at += count
        some = gain_ref.shape[1] // size
        small_f[k, at : at + 1, 0:some] = gain_ref[:, k * some : (k + 1) * some]
    small_ref[...] = small_f[...].astype(bf16)
    sequels = one_hot_ref.shape[0]
    pieces = (SEQS - PROMPTS) // sequels
    for t in range(HALO):
        rim[t * PROMPTS : (t + 1) * PROMPTS] = halo_ref[t, 0:PROMPTS]
        for p in range(PROMPTS):
            sums = None
            for q in range(sequels):
                row = PROMPTS + q * pieces
                term = one_hot_ref[q, p] * halo_ref[t, row : row + 1]
                sums = term if q == 0 else sums + term
            child[t * PROMPTS + p : t * PROMPTS + p + 1] = sums
    block = b0[...].astype(f32) + b1[...].astype(f32) + b2[...].astype(f32) + b3[...].astype(f32)
    total[...] = block.reshape(total.shape)
    to_z[...] = total[...].astype(bf16)
    to_left = send(rim, got_rim, sems_r.at[0], sems_r.at[1], lax.rem(me + last, size))
    to_left.start()

    @pl.when(me != last)
    def _():
        send(child, got_child.at[me], sems_cs.at[me], sems_cr.at[me], last).start()

    copies = spread(small_ref, got_small, sems_s, near, "fsdp", me)
    z_copies = spread(to_z, from_z, sems_z, far, "replica", mz)
    small = small_ref[me].astype(f32)
    got_small[me] = jnp.zeros(got_small.shape[1:], bf16)
    from_z[mz] = jnp.zeros(from_z.shape[1:], bf16)
    small_from_z[mz] = jnp.zeros(small_from_z.shape[1:], bf16)
    for copy in copies:
        copy.wait()
    for k in range(size):
        small = small + got_small[k].astype(f32)
    small_z[...] = small.reshape(small_z.shape)
    small_to_z = small_part
    small_to_z[...] = small_z[...].astype(bf16)
    s_copies = spread(small_to_z, small_from_z, sems_sz, far, "replica", mz)
    for copy in z_copies:
        copy.wait()
    own = total[mz]
    for k in range(depth):
        own = own + from_z[k].astype(f32)
    part[...] = own.astype(bf16)
    p_copies = spread(part, parts, sems_p, far, "replica", mz)
    parts[mz] = part[...]
    for copy in s_copies:
        copy.wait()
    own = small_z[mz]
    for k in range(depth):
        own = own + small_from_z[k].astype(f32)
    small_parts[mz] = own.astype(bf16)
    small_own = small_to_z.at[mz]
    small_own[...] = own.astype(bf16)
    q_copies = []
    for d, peer in enumerate(far):
        copy = send(small_own, small_parts.at[mz], sems_sp.at[0, d], sems_sp.at[1, d], peer, "replica")
        copy.start()
        q_copies.append(copy)
    for copy in p_copies + q_copies:
        copy.wait()
    block_out[...] = parts[...].reshape(block_out.shape)
    small_out[...] = small_parts[...].reshape(small_out.shape)
    to_left.wait()

    @pl.when(me != last)
    def _():
        send(child, got_child.at[me], sems_cs.at[me], sems_cr.at[me], last).wait_send()
        rim_out[...] = got_rim[...]

    @pl.when(me == last)
    def _():
        sums = child[...]
        for k in range(size - 1):
            send(child, got_child.at[k], sems_cs.at[k], sems_cr.at[k], 0).wait_recv()
            sums = sums + got_child[k]
        rim_out[...] = sums


def tail(one_hot, blocks, small, halo_grad):
    size, depth = lax.axis_size("fsdp"), lax.axis_size("replica")
    vmem = pl.BlockSpec(memory_space=pltpu.VMEM)
    dma = pltpu.SemaphoreType.DMA
    while len(blocks) > 4:
        blocks = blocks[:3] + [summed(blocks[3], blocks[4:5]).astype(bf16)] + blocks[5:]
    rows, channels = blocks[0].shape
    features = small[-1].shape[1]
    width = channels // size
    cut = (depth, rows // depth, channels)
    by_owner = (size, SMALL_ROWS, width)
    small_cut = (depth, SMALL_ROWS // depth, width)
    rim = (HALO * PROMPTS, features)
    return pl.pallas_call(
        tail_kernel,
        in_specs=[pl.BlockSpec(memory_space=pltpu.SMEM)] + [vmem] * (4 + len(small) + 1),
        out_specs=[vmem] * 3,
        out_shape=[
            jax.ShapeDtypeStruct((rows, channels), bf16),
            jax.ShapeDtypeStruct((SMALL_ROWS, width), bf16),
            jax.ShapeDtypeStruct(rim, f32),
        ],
        scratch_shapes=[
            pltpu.VMEM(cut, f32), pltpu.VMEM(cut, bf16), pltpu.VMEM(cut, bf16),
            pltpu.VMEM(cut[1:], bf16), pltpu.VMEM(cut, bf16),
            pltpu.VMEM(by_owner, f32), pltpu.VMEM(by_owner, bf16), pltpu.VMEM(by_owner, bf16),
            pltpu.VMEM(small_cut, f32), pltpu.VMEM(small_cut, bf16),
            pltpu.VMEM(small_cut, bf16), pltpu.VMEM(small_cut, bf16),
            pltpu.VMEM(rim, f32), pltpu.VMEM(rim, f32), pltpu.VMEM(rim, f32), pltpu.VMEM((size,) + rim, f32),
            dma((2, size)), dma((2, depth)), dma((2, depth)), dma((2, depth)), dma((2, depth)),
            dma((2,)), dma((size,)), dma((size,)),
        ],
        compiler_params=params(collective_id=4, has_side_effects=True),
        cost_estimate=cost(30),
        name="tail",
    )(one_hot, *blocks, *small, halo_grad)


def deliver_kernel(block_ref, small_ref, rim_ref, prompt_ref, *rest):
    depth = lax.axis_size("replica")
    early_refs, outs = rest[:depth], rest[depth:-1]
    early = rest[-1]
    in_out, out_out, prompt_out = outs[:3]
    mz = lax.axis_index("replica")
    half = in_out.shape[1] // 2
    in_out[:, 0:half] = block_ref[...].astype(f32)
    small = small_ref[...].astype(f32)
    at = 0
    for out, count in zip(outs[3:], SMALL):
        rows = small[at : at + count]
        out[...] = rows[:, 0 : out.shape[1]]
        at += count
    for d, ref in enumerate(early_refs):
        count = ref.shape[0]
        early[pl.ds(pl.multiple_of(xor(mz, d) * count, count), count), :] = ref[...].astype(f32)
    rows = out_out.shape[0] // 2
    features = out_out.shape[1]
    out_out[0:rows, :] = early[0:rows, 0:features]
    out_out[rows:, :] = early[0:rows, features:]
    in_out[:, half:] = early[rows:, :]
    for p in range(PROMPTS):
        prompt_out[p, 0 : SEQS - HALO] = prompt_ref[p, 0 : SEQS - HALO]
        for t in range(HALO):
            row = SEQS - HALO + t
            prompt_out[p, row : row + 1] = (
                prompt_ref[p, row : row + 1] + rim_ref[t * PROMPTS + p : t * PROMPTS + p + 1]
            )


def deliver(block, small, rim, prompt_grad, early):
    size = lax.axis_size("fsdp")
    rows, channels = block.shape
    width = small.shape[1]
    features = prompt_grad.shape[2]
    vmem = pl.BlockSpec(memory_space=pltpu.VMEM)
    end = prompt_grad.shape[1] // SEQS - 1
    last = pl.BlockSpec((PROMPTS, SEQS, features), lambda i: (0, end, 0))
    shapes = [(count, width) for count in SMALL[:-1]] + [(1, features // size)]
    shapes = [(rows, 2 * channels), (2 * rows, features), prompt_grad.shape] + shapes
    return pl.pallas_call(
        deliver_kernel,
        grid=(1,),
        in_specs=[vmem, vmem, vmem, last] + [vmem] * len(early),
        out_specs=[vmem, vmem, last] + [vmem] * len(SMALL),
        out_shape=[jax.ShapeDtypeStruct(shape, f32) for shape in shapes],
        scratch_shapes=[pltpu.VMEM((2 * rows, channels), f32)],
        input_output_aliases={3: 2},
        compiler_params=params(),
        cost_estimate=cost(4),
        name="deliver",
    )(block, small, rim, prompt_grad, *early)


def contract_rows(left_side, right_side):
    return lax.dot_general(
        left_side, right_side, (((0,), (0,)), ((), ())), preferred_element_type=f32
    )


def contract_cols(left_side, right_side):
    return lax.dot_general(
        left_side, right_side, (((1,), (1,)), ((), ())), preferred_element_type=f32
    )


def exchanged(block, axis, distance):
    return lax.ppermute(block, axis, [(i, i ^ distance) for i in range(lax.axis_size(axis))])


def pick_row(block, index, axis=0):
    return lax.dynamic_index_in_dim(block, index, axis, keepdims=False)


def over_cores(blocks):
    blocks = blocks.reshape((-1, 2) + blocks.shape[1:])
    core = lax.axis_index("fsdp") % 2
    got = exchanged(pick_row(blocks, 1 - core, 1), "fsdp", 1)
    return (pick_row(blocks, core, 1).astype(f32) + got.astype(f32)).astype(bf16)


def to_chips(blocks):
    chip = lax.axis_index("fsdp") // 2
    got = [exchanged(pick_row(blocks, chip ^ d), "fsdp", 2 * d) for d in range(1, blocks.shape[0])]
    return pick_row(blocks, chip), got


def summed(own, got):
    total = own.astype(f32)
    for block in got:
        total = total + block.astype(f32)
    return total


def to_replicas(block):
    size, here = lax.axis_size("replica"), lax.axis_index("replica")
    parts = block.astype(bf16).reshape((size, -1) + block.shape[1:])
    own = pick_row(block.reshape(parts.shape), here)
    return own, [exchanged(pick_row(parts, here ^ d), "replica", d) for d in range(1, size)]


def from_replicas(part):
    return [part] + [exchanged(part, "replica", d) for d in range(1, lax.axis_size("replica"))]


def body(
    prompt_hidden, sequel_hidden, parents, prompt_cotangent, sequel_cotangent,
    norm_gain, input_weight, filter_weight, depthwise_filter_bias, select_weight,
    step_weight, step_bias, decay_log, skip_gain, output_weight,
):
    size, here = lax.axis_size("fsdp"), lax.axis_index("fsdp")
    prompts, steps = prompt_hidden.shape[:2]
    sequels, sequel_len = sequel_hidden.shape[:2]
    split = sequel_len // steps
    assert prompts == PROMPTS and sequels * split == SEQS - prompts
    rim = KERNEL - 1
    half = SEQS // 2
    rows = steps * SEQS

    after = lax.optimization_barrier
    width = step_bias.shape[0]
    tail_rows = prompt_hidden[:, steps - rim :]
    shard = jnp.concatenate(
        [
            step_weight,
            tail_rows.reshape(-1, width),
            filter_weight,
            depthwise_filter_bias[None],
            step_bias[None],
            skip_gain[None],
            jnp.pad(norm_gain, (0, width - norm_gain.shape[0]))[None],
        ],
        axis=0,
    )
    shard = jnp.pad(shard, ((0, -shard.shape[0] % 16), (0, 0)))
    lanes = jnp.concatenate([select_weight, decay_log], axis=1)
    lanes = jnp.pad(lanes, ((0, 0), (0, LANES - lanes.shape[1])))
    every, select_pad, full_output, full_input = gather(shard, lanes, output_weight, input_weight)
    every = every.reshape(size, shard.shape[0], width)
    at = RANK + tail_rows.size // width
    tails = every[:, RANK:at].reshape((size,) + tail_rows.shape)
    step_full = jnp.swapaxes(every[:, :RANK], 0, 1).reshape(RANK, -1)
    vectors = jnp.swapaxes(every[:, at : at + SEQS], 0, 1).astype(f32)
    gain = vectors[KERNEL + 3, :, : norm_gain.shape[0]].reshape(1, -1)
    vectors = vectors.reshape(SEQS, -1)
    fw, fb, sbias, skip = vectors[:KERNEL], vectors[4:5], vectors[5:6], vectors[6:7]
    first = RANK + 2 * STATES
    rate = -jnp.exp(select_pad[:, first : first + STATES].T.astype(f32)) * LOG2E
    step_pad = jnp.pad(step_full, ((0, LANES - RANK), (0, 0)))

    before = jnp.where(here > 0, tails[jnp.maximum(here - 1, 0)], jnp.zeros_like(tails[0]))
    cut = sequel_hidden.reshape(sequels, split, steps, D)
    inner = jnp.concatenate([tails[size - 1][parents][:, None], cut[:, :-1, steps - rim :]], axis=1)
    halo = jnp.concatenate([before, inner.reshape(-1, rim, D)], axis=0)
    halo = jnp.pad(jnp.swapaxes(halo, 0, 1), ((HALO - rim, 0), (0, 0), (0, 0))).reshape(-1, D).astype(f32)
    pieces = sequel_hidden.reshape(-1, steps, D)
    piece_cot = sequel_cotangent.reshape(-1, steps, D)
    scaled, cotangent = prepare(prompt_hidden, pieces, prompt_cotangent, piece_cot, halo, gain)

    mixture = product([scaled], full_input, bf16, tiled=True)
    mixture = mixture.reshape(-1, steps + HALO, SEQS, WIDE)
    gated_grad = product([cotangent], full_output, bf16, across=True, tiled=True)
    gated_grad = gated_grad.reshape(-1, steps, SEQS, WIDE)
    act, bend, proj = front(mixture, fw, fb, select_pad, steps)
    groups = 1 if split == 1 else 2
    lane = jnp.arange(2 * STATES * LANES)[None, :]
    select = (jnp.arange(LANES)[:, None] == RANK + lane // LANES).astype(bf16)
    dt, sig, yg, silu, slope, ahead, behind, total = piece(
        proj, act, mixture, gated_grad, step_pad, sbias, rate, select, groups
    )

    one_hot = (parents[:, None] == jnp.arange(PROMPTS, dtype=jnp.int32)[None, :]).astype(f32)
    own = total[half:].reshape(sequels, split, 1, INNER)
    own_behind = behind[half:].reshape(sequels, split, STATES, INNER)
    back = own_behind[:, split - 1]
    own_end = [jnp.zeros_like(back)]
    for p in range(split - 2, -1, -1):
        own_end.insert(0, back)
        back = own_behind[:, p] + jnp.exp2(rate * own[:, p]) * back
    joint = behind if split == 1 else jnp.concatenate([behind[:half], back], axis=0)
    start, end = chain(one_hot, ahead, joint, total, rate)
    if split > 1:
        state = start[half:]
        own_start = [state]
        for p in range(split - 1):
            state = jnp.exp2(rate * own[:, p]) * state + ahead[half:].reshape(own_behind.shape)[:, p]
            own_start.append(state)
        own_start = jnp.stack(own_start, axis=1).reshape(half, STATES, INNER)
        start = jnp.concatenate([start[:half], own_start], axis=0)
        end = jnp.concatenate([end[:half], jnp.stack(own_end, axis=1).reshape(half, STATES, INNER)], axis=0)

    gated, hist, gate_grad, skip_grad = forward(
        proj, dt, act, yg, silu, slope, rate, start, skip, select
    )
    gated = gated.reshape(rows, INNER)
    gate_grad = gate_grad.reshape(-1, INNER)
    output_grad = contract_rows(gated, cotangent).astype(bf16).reshape(size, -1, D)
    gate_weight_grad = contract_rows(scaled, gate_grad).astype(bf16)
    early = [over_cores(output_grad), over_cores(gate_weight_grad.reshape(size, -1, INNER))]
    wide = jnp.concatenate([early[0][:, : INNER // size // 2], early[0][:, INNER // size // 2 :]], axis=2)
    early = jnp.concatenate([wide, early[1]], axis=1)
    end, early = after((end, early))
    early = to_chips(early)

    rank_t = proj[:, :RANK].astype(bf16).T
    lane = jnp.arange(LANES)[None, None, :]
    which = jnp.arange(PAIRS)[:, None, None]
    source = jnp.arange(2 * LANES)[None, :, None]
    pick = (lane // 2 == jnp.where(source < LANES, RANK, RANK + STATES) // 2 + which).astype(bf16)
    act_grad, step_grad, bias_grad, decay_grad, projg = backward(
        proj, dt, sig, act, yg, rate, end, skip, hist, rank_t, step_pad.T, pick, select
    )
    projg, early = after((projg, early))
    early = summed(*early)
    projg, early = after((projg, early))
    early = to_replicas(early)
    filter_in_grad, select_grad, filter_grad, filter_bias_grad = filter_back(
        mixture, act, bend, act_grad, projg, projg.T, select_pad, fw
    )
    filter_in_grad, early = after((filter_in_grad, early))
    early = summed(*early).astype(bf16)
    filter_in_grad = filter_in_grad.reshape(-1, INNER)
    filter_weight_grad = contract_rows(scaled, filter_in_grad).astype(bf16)
    filter_weight_grad, early = after((filter_weight_grad, early))
    late = over_cores(filter_weight_grad.reshape(size, -1, INNER))
    early = from_replicas(early)
    mixed = jnp.dot(gated, full_output, preferred_element_type=f32)
    late, mixed, filter_in_grad = after((late, mixed, filter_in_grad))
    own_block, late = to_chips(late)
    scaled_grad = product([filter_in_grad, gate_grad], full_input, f32, across=True)
    prompt_out, piece_out, prompt_grad, piece_grad, halo_grad, gain_grad = finish(
        mixed, scaled_grad, prompt_hidden, pieces, prompt_cotangent, piece_cot, halo, gain
    )
    halo_grad, own_block, late = after((halo_grad, own_block, late))
    halo_grad = halo_grad.reshape(HALO, SEQS, D)
    small = [
        filter_grad, filter_bias_grad, bias_grad, skip_grad, decay_grad, step_grad, select_grad, gain_grad,
    ]
    block, small, following = tail(one_hot, [own_block] + late, small, halo_grad)
    (
        input_grad, output_grad, prompt_grad, g_filter, g_fbias, g_sbias, g_skip, g_decay, g_step, g_select, g_gain,
    ) = deliver(block, small, following, prompt_grad, early)
    if split > 1:
        own = jnp.swapaxes(halo_grad[:, half:], 0, 1).reshape(sequels, split, HALO, D)
        own = jnp.pad(own[:, 1:], ((0, 0), (0, 1), (0, 0), (0, 0))).reshape(half, HALO, D)
        piece_grad = piece_grad.at[:, steps - HALO :].add(own)
    return (
        prompt_out,
        piece_out.reshape(sequel_hidden.shape),
        prompt_grad,
        piece_grad.reshape(sequel_hidden.shape),
        g_gain[0],
        input_grad,
        g_filter,
        g_fbias[0],
        g_select.T,
        g_step,
        g_sbias[0],
        g_decay.T,
        g_skip[0],
        output_grad,
    )


def solution(mesh):
    rows = P("replica", "fsdp", None)
    own = P(("replica", "fsdp"), None, None)
    return jax.shard_map(
        body,
        mesh=mesh,
        in_specs=(
            rows, own, P(("replica", "fsdp")), rows, own,
            P("fsdp"), P("fsdp", None), P(None, "fsdp"), P("fsdp"), P("fsdp", None),
            P(None, "fsdp"), P("fsdp"), P("fsdp", None), P("fsdp"), P("fsdp", None),
        ),
        out_specs=(
            rows, own, rows, own,
            P("fsdp"), P("fsdp", None), P(None, "fsdp"), P("fsdp"), P("fsdp", None),
            P(None, "fsdp"), P("fsdp"), P("fsdp", None), P("fsdp"), P("fsdp", None),
        ),
        check_vma=False,
    )
```
